32 devices in a mesh: seq: 8 (over y, x, core), doc: 4 (over z).
Axes of the slice: x: 2, y: 2, z: 4, core: 2. Of those that a mesh axis runs over, the one named last changes fastest.
Arguments:
- tokens: bfloat16 [4, 4096, 1024], P('doc', 'seq'), may hold values from -6 to 6
- cotangent: bfloat16 [4, 4096, 1024], P('doc', 'seq'), may hold values from -6 to 6
- attn_gain: bfloat16 [1024], replicated, may hold values from 0.5 to 1.5
- w_query: bfloat16 [1024, 1024], replicated, may hold values from -0.1875 to 0.1875
- w_key: bfloat16 [1024, 1024], replicated, may hold values from -0.1875 to 0.1875
- w_value: bfloat16 [1024, 1024], replicated, may hold values from -0.1875 to 0.1875
- w_out: bfloat16 [1024, 1024], replicated, may hold values from -3 to 3
- ffn_gain: bfloat16 [1024], replicated, may hold values from 0.5 to 1.5
- w_gate: bfloat16 [1024, 2816], replicated, may hold values from -0.1875 to 0.1875
- w_up: bfloat16 [1024, 2816], replicated, may hold values from -0.1875 to 0.1875
- w_down: bfloat16 [2816, 1024], replicated, may hold values from -0.109375 to 0.109375
- mem_keys: bfloat16 [4, 4096, 1024], P('doc', 'seq'), may hold values from -6 to 6
- mem_values: bfloat16 [4, 4096, 1024], P('doc', 'seq'), may hold values from -6 to 6
- seg_len: int32 [4, 2], P('doc'), may hold values from 512 to 2048, as said below
- mem_idx: int32 [4, 8, 128], P('doc', 'seq'), may hold values from 0 to 4095, as said below
Outputs:
- layer_out: bfloat16 [4, 4096, 1024], P('doc', 'seq')
- grad_tokens: bfloat16 [4, 4096, 1024], P('doc', 'seq')
- grad_attn_gain: float32 [1024], P(('seq', 'doc'))
- grad_query: float32 [1024, 1024], P(('seq', 'doc'))
- grad_key: float32 [1024, 1024], P(('seq', 'doc'))
- grad_value: float32 [1024, 1024], P(('seq', 'doc'))
- grad_out: float32 [1024, 1024], P(('seq', 'doc'))
- grad_ffn_gain: float32 [1024], P(('seq', 'doc'))
- grad_gate: float32 [1024, 2816], P(('seq', 'doc'))
- grad_up: float32 [1024, 2816], P(('seq', 'doc'))
- grad_down: float32 [2816, 1024], P(('seq', 'doc'))
- grad_mem_keys: float32 [4, 4096, 1024], P('doc', 'seq')
- grad_mem_values: float32 [4, 4096, 1024], P('doc', 'seq')
The draws below stay inside these ranges and needn't reach their ends.
Inputs may be any that keep to these rules, and one draw needn't show every extreme that they name: Positions at or beyond seg_len in a segment are padding; in every stream some segment has all 2048 positions valid. `mem_idx`: memory row r of a stream lies on seq index r // 512. Each query block names exactly 32 distinct rows of each of half of the seq indices and none of the others; which indices is drawn afresh for every block.
All inputs are finite; a program needn't handle non-finite values.
Results may differ from the reference program's by a relative error of at most 0.014.
Values may be sent and summed in bfloat16 or wider, within the bound.
A program may use at most 320 MiB of HBM per device.

```python
import jax
import jax.numpy as jnp
from jax import lax

D = 1024
HEADS = 8
HEAD_DIM = 128
FF = 2816
HD = 1024
TOPK = 128
BLK = 512
BPS = 4
SEG = 2048
MEM_DEV = 512
CAP = 32
STREAMS = 4
LEN = 4096
NSEGS = 2
MEM = 4096
N_SEQ = 8


def draw_seg_len(key, part):
    len_key, full_key = jax.random.split(key)
    drawn = jax.random.randint(len_key, (STREAMS, NSEGS), SEG // 4, SEG + 1)
    chosen = jax.random.randint(full_key, (STREAMS, 1), 0, NSEGS)
    columns = jnp.arange(NSEGS)[None, :]
    return jnp.where(columns == chosen, SEG, drawn).astype(jnp.int32)


def draw_owner_rows(row_seed):
    return jax.random.permutation(row_seed, MEM_DEV)[:CAP]


def draw_block_rows(block_key):
    owner_key, row_key = jax.random.split(block_key)
    owner_count = N_SEQ // 2
    owners = jax.random.permutation(owner_key, N_SEQ)[:owner_count]
    row_keys = jax.random.split(row_key, owner_count)
    picked = jax.vmap(draw_owner_rows)(row_keys)
    return (owners[:, None] * MEM_DEV + picked).reshape(owner_count * CAP)


def draw_mem_idx(key, part):
    block_keys = jax.random.split(key, STREAMS * N_SEQ)
    return jax.vmap(draw_block_rows)(block_keys).reshape(STREAMS, N_SEQ, TOPK).astype(jnp.int32)


def shard_levels(rng, shape, pieces, low, largest):
    def one(dim, parts):
        steps = jax.random.uniform(jax.random.fold_in(jax.random.fold_in(rng, 6), dim), (parts,), jnp.float32, low / len(pieces), largest / len(pieces))
        return jnp.repeat(jnp.exp(steps), shape[dim] // parts).reshape((-1,) + (1,) * (len(shape) - dim - 1))

    level = one(*pieces[0])
    for cut in pieces[1:]:
        level = level * one(*cut)
    return level


def centred(key, extent, spread, reach, pieces=(), held_as=jnp.bfloat16):
    result = jax.random.normal(key, extent, jnp.float32) * spread
    if len(pieces) > 0:
        result = shard_levels(key, extent, pieces, -0.22, 0.18) * result
    return jnp.clip(result, min=-reach, max=reach).astype(held_as)


def setup_inputs(seed: int = 0) -> dict:
    arg_keys = jax.random.split(jax.random.key(seed), 16)
    return {
        "tokens": centred(arg_keys[0], (STREAMS, LEN, D), 1.0, 6.0, ((0, 4), (1, 8))),
        "cotangent": centred(arg_keys[1], (STREAMS, LEN, D), 1.0, 6.0, ((0, 4), (1, 8))),
        "attn_gain": jnp.clip(1.0 + 0.1 * jax.random.normal(arg_keys[2], (D,), jnp.float32), 0.5, 1.5).astype(jnp.bfloat16),
        "w_query": centred(arg_keys[3], (D, HD), D ** -0.5, 0.1875),
        "w_key": centred(arg_keys[4], (D, HD), D ** -0.5, 0.1875),
        "w_value": centred(arg_keys[5], (D, HD), D ** -0.5, 0.1875),
        "w_out": centred(arg_keys[6], (HD, D), (D // 256) ** -0.5, 3.0),
        "ffn_gain": jnp.clip(1.0 + 0.1 * jax.random.normal(arg_keys[7], (D,), jnp.float32), 0.5, 1.5).astype(jnp.bfloat16),
        "w_gate": centred(arg_keys[8], (D, FF), D ** -0.5, 0.1875),
        "w_up": centred(arg_keys[9], (D, FF), D ** -0.5, 0.1875),
        "w_down": centred(arg_keys[10], (FF, D), FF ** -0.5, 0.109375),
        "mem_keys": centred(arg_keys[11], (STREAMS, MEM, HD), 1.0, 6.0, ((0, 4), (1, 8))),
        "mem_values": centred(arg_keys[12], (STREAMS, MEM, HD), 1.0, 6.0, ((0, 4), (1, 8))),
        "seg_len": draw_seg_len(jax.random.fold_in(arg_keys[15], 71), 0),
        "mem_idx": draw_mem_idx(jax.random.fold_in(arg_keys[15], 71), 0),
    }


EPS = 1e-05
NEG = -1000000000.0
PRECISE = lax.Precision.HIGHEST

@jax.custom_vjp
def low(v):
    return lax.optimization_barrier(v.astype(jnp.bfloat16)).astype(jnp.float32)

@jax.custom_vjp
def low_back(v):
    return v

def low_keep(v):
    return (low(v), None)

def low_pass(kept, grad):
    return (grad,)

def back_keep(v):
    return (v, None)

def back_low(kept, grad):
    return (low(grad),)
low.defvjp(low_keep, low_pass)
low_back.defvjp(back_keep, back_low)

def matmul(left, right):
    return jnp.dot(left, right, precision=PRECISE)

def rms_scaled(values, gain):
    factor = lax.rsqrt(lax.optimization_barrier(jnp.mean(values * values, axis=-1, keepdims=True)) + EPS)
    return values * factor * gain

def attend(queries, key_rows, value_rows, allowed):
    count = queries.shape[0]
    qheads = queries.reshape(count, HEADS, HEAD_DIM)
    kheads = key_rows.reshape(key_rows.shape[0], HEADS, HEAD_DIM)
    vheads = value_rows.reshape(value_rows.shape[0], HEADS, HEAD_DIM)
    logits_raw = jnp.einsum('qhd,khd->hqk', qheads, kheads, precision=PRECISE) * HEAD_DIM ** (-0.5)
    scores = jnp.where(allowed[None], low_back(logits_raw), NEG)
    row_max = lax.optimization_barrier(jnp.max(scores, axis=-1, keepdims=True))
    exponent = jnp.exp(scores - row_max)
    weights = exponent / lax.optimization_barrier(jnp.sum(exponent, axis=-1, keepdims=True))
    attended = jnp.einsum('hqk,khd->qhd', low(weights), vheads, precision=PRECISE)
    return attended.reshape(count, HD)

def stream_forward(params, tokens_f, mem_k, mem_v, lengths, indices):
    attn_gain, w_query, w_key, w_value, w_out, ffn_gain, w_gate, w_up, w_down = params
    normed = low(rms_scaled(tokens_f, attn_gain))
    queries = low(low_back(matmul(normed, w_query)))
    key_all = low(low_back(matmul(normed, w_key)))
    value_all = low(low_back(matmul(normed, w_value)))

    def block_attention(block_id):
        segment = block_id // BPS
        seg_start = (segment * SEG).astype(jnp.int32)
        seg_keys = lax.dynamic_slice_in_dim(key_all, seg_start, SEG, 0)
        seg_values = lax.dynamic_slice_in_dim(value_all, seg_start, SEG, 0)
        block_queries = lax.dynamic_slice_in_dim(queries, (block_id * BLK).astype(jnp.int32), BLK, 0)
        chosen = lax.dynamic_index_in_dim(indices, block_id, 0, keepdims=False)
        memory_keys = jnp.take(mem_k, chosen, axis=0)
        memory_values = jnp.take(mem_v, chosen, axis=0)
        query_pos = block_id % BPS * BLK + jnp.arange(BLK, dtype=jnp.int32)
        key_pos = jnp.arange(SEG, dtype=jnp.int32)
        length = lax.dynamic_index_in_dim(lengths, segment, 0, keepdims=False)
        local_ok = (key_pos[None, :] <= query_pos[:, None]) & (key_pos[None, :] < length)
        allowed = jnp.concatenate([local_ok, jnp.ones((BLK, TOPK), dtype=bool)], axis=1)
        return attend(block_queries, jnp.concatenate([seg_keys, memory_keys], axis=0), jnp.concatenate([seg_values, memory_values], axis=0), allowed)
    attended = lax.map(jax.checkpoint(block_attention), jnp.arange(N_SEQ, dtype=jnp.int32))
    attended = low(low_back(attended.reshape(LEN, HD)))
    middle = tokens_f + low_back(matmul(attended, w_out))
    normed_two = low(rms_scaled(middle, ffn_gain))
    gate = low_back(matmul(normed_two, w_gate))
    upper = low_back(matmul(normed_two, w_up))
    hidden = low(jax.nn.silu(gate) * upper)
    return middle + low_back(matmul(hidden, w_down))

def reference(tokens, cotangent, attn_gain, w_query, w_key, w_value, w_out, ffn_gain, w_gate, w_up, w_down, mem_keys, mem_values, seg_len, mem_idx):
    params = tuple((w.astype(jnp.float32) for w in (attn_gain, w_query, w_key, w_value, w_out, ffn_gain, w_gate, w_up, w_down)))

    def per_stream(totals, inputs):
        stream_tokens, stream_grad, stream_mk, stream_mv, lengths, indices = inputs

        def forward(weights, tokens_f, mem_k, mem_v):
            return stream_forward(weights, tokens_f, mem_k, mem_v, lengths, indices)
        output, pullback = jax.vjp(forward, params, stream_tokens.astype(jnp.float32), stream_mk.astype(jnp.float32), stream_mv.astype(jnp.float32))
        grad_params, grad_input, grad_mk, grad_mv = pullback(stream_grad.astype(jnp.float32))
        totals = jax.tree.map(lambda acc, new_grad: acc + new_grad, totals, grad_params)
        return (totals, (output.astype(jnp.bfloat16), grad_input.astype(jnp.bfloat16), grad_mk, grad_mv))
    zeros = jax.tree.map(jnp.zeros_like, params)
    totals, (outputs, grad_inputs, grad_mks, grad_mvs) = lax.scan(per_stream, zeros, (tokens, cotangent, mem_keys, mem_values, seg_len, mem_idx))
    return (outputs, grad_inputs, totals[0], totals[1], totals[2], totals[3], totals[4], totals[5], totals[6], totals[7], totals[8], grad_mks, grad_mvs)
```

```python
import jax
import jax.numpy as jnp
from jax import lax
from jax.experimental import pallas as pl
from jax.experimental.pallas import tpu as pltpu
from jax.sharding import PartitionSpec as P

HEADS = 8
HEAD_DIM = 128
TOPK = 128
BPS = 4


EPS = 1e-05
NEG = -1000000000.0


def from_behind(value, axis, steps):
    count = lax.axis_size(axis)
    leading, last = (max(0, -steps), min(count, count - steps))
    return lax.ppermute(value, axis, [(source, source + steps) for source in range(leading, last)])


def rms_factor(values):
    return lax.rsqrt(jnp.mean(values * values, axis=-1, keepdims=True) + EPS)


def neighbour_blocks(kv_own):
    pieces = []
    for distance in range(BPS - 1, 0, -1):
        pieces.append(from_behind(kv_own, "seq", distance))
    pieces.append(kv_own)
    return jnp.concatenate(pieces, axis=2)


def take_rows(table, row_ids):
    return jnp.take(table, row_ids, axis=0)


def add_rows(table, row_ids, updates):
    return table.at[row_ids].add(updates)


def fetch_rows(mem_keys, mem_values, row_ids, owner_count, capacity):
    stream_count = mem_keys.shape[0]
    key_rows = jax.vmap(take_rows)(mem_keys, row_ids)
    value_rows = jax.vmap(take_rows)(mem_values, row_ids)
    stacked = jnp.stack((key_rows, value_rows), axis=1)
    stacked = stacked.reshape(stack_shape(stream_count, owner_count, capacity, mem_keys.shape[2]))
    arrived = lax.all_to_all(stacked, "seq", split_axis=2, concat_axis=2, tiled=True)
    return arrived.reshape(stream_count, 2, owner_count * capacity, mem_keys.shape[2])


def stack_shape(stream_count, owner_count, capacity, attn_width):
    return (stream_count, 2, owner_count, capacity, attn_width)


def attention_scores(queries, kv_seg, mem_kv, allowed):
    count = queries.shape[0]
    key_rows = jnp.concatenate((kv_seg[0], mem_kv[0]), axis=0)
    value_rows = jnp.concatenate((kv_seg[1], mem_kv[1]), axis=0)
    qheads = queries.reshape(count, HEADS, HEAD_DIM)
    kheads = key_rows.reshape(key_rows.shape[0], HEADS, HEAD_DIM)
    vheads = value_rows.reshape(value_rows.shape[0], HEADS, HEAD_DIM)
    logits = jnp.einsum(
        "qhd,khd->hqk", qheads, kheads, preferred_element_type=jnp.float32
    ) * HEAD_DIM ** (-0.5)
    return (jnp.where(allowed[None], logits, NEG), qheads, kheads, vheads)


def attend_forward(operands):
    queries, kv_seg, mem_kv, allowed = operands
    scores, qheads, kheads, vheads = attention_scores(queries, kv_seg, mem_kv, allowed)
    row_max = jnp.max(scores, axis=-1, keepdims=True)
    exponent = jnp.exp(scores - row_max)
    total = jnp.sum(exponent, axis=-1, keepdims=True)
    weights = (exponent / total).astype(jnp.bfloat16)
    attended = jnp.einsum("hqk,khd->qhd", weights, vheads, preferred_element_type=jnp.float32)
    return (attended.reshape(queries.shape[0], -1), (row_max + jnp.log(total))[..., 0])


def attend_backward(operands):
    queries, kv_seg, mem_kv, allowed, log_total, grad_rows = operands
    scores, qheads, kheads, vheads = attention_scores(queries, kv_seg, mem_kv, allowed)
    weights = jnp.exp(scores - log_total[..., None])
    grad_heads = grad_rows.reshape(grad_rows.shape[0], HEADS, HEAD_DIM)
    grad_weights = jnp.einsum(
        "qhd,khd->hqk", grad_heads, vheads, preferred_element_type=jnp.float32
    )
    inner = jnp.sum(weights * grad_weights, axis=-1, keepdims=True)
    grad_scores = (weights * (grad_weights - inner)).astype(jnp.bfloat16)
    scale = HEAD_DIM ** (-0.5)
    grad_queries = (
        jnp.einsum("hqk,khd->qhd", grad_scores, kheads, preferred_element_type=jnp.float32) * scale
    )
    grad_keys = (
        jnp.einsum("hqk,qhd->khd", grad_scores, qheads, preferred_element_type=jnp.float32) * scale
    )
    grad_values = jnp.einsum(
        "hqk,qhd->khd", weights.astype(jnp.bfloat16), grad_heads, preferred_element_type=jnp.float32
    )
    attn_width = queries.shape[1]
    return (
        grad_queries.reshape(queries.shape[0], attn_width),
        grad_keys.reshape(-1, attn_width),
        grad_values.reshape(-1, attn_width),
    )


MESH = pl.DeviceIdType.MESH
UNIT = 256
SKEW = 2

def flip(value, bit):
    return value + bit - 2 * bit * ((value // bit) % 2)


def partners():
    seq, doc = lax.axis_index("seq"), lax.axis_index("doc")
    return {
        "core": (flip(seq, 1), doc),
        "x": (flip(seq, 2), doc),
        "y": (flip(seq, 4), doc),
        "low": (seq, flip(doc, 1)),
        "high": (seq, flip(doc, 2)),
    }


ORDERS = (("x", "y", "low", "high"), ("y", "x", "low", "high"), ("low", "high", "x", "y"))


def rs_kernel(plan, every, names, refs_in, gains_in, refs_out, gains_out, own, stages, gain_buf, sems):
    seq, doc = lax.axis_index("seq"), lax.axis_index("doc")
    bits = {
        "core": seq % 2,
        "x": (seq // 2) % 2,
        "y": (seq // 4) % 2,
        "low": doc % 2,
        "high": (doc // 2) % 2,
    }
    peer = partners()
    local_sem, send_sem, recv_sem, gain_send, gain_recv = sems
    barrier = pltpu.get_barrier_semaphore()
    for name in ("core", "x", "y", "low", "high"):
        pl.semaphore_signal(barrier, inc=1, device_id=peer[name], device_id_type=MESH)
    pl.semaphore_wait(barrier, 5)

    def pick(cls, level, unit, side):
        order = ORDERS[cls]
        ref = stages[cls][level]
        name = order[level]
        where = (1 - bits[name]) if side == "send" else bits[name]
        left = [axis for axis in ("y", "x", "high", "low") if axis not in order[:level]]
        index = (unit,) + (slice(None),) * left.index(name) + (where,)
        return ref, index

    def first(cls, unit, array, column):
        source = refs_in[array]
        lanes = pl.ds(column, UNIT)
        there = source.at[:, :, 1 - bits["core"], :, :, :, lanes]
        here = source.at[:, :, bits["core"], :, :, :, lanes]
        local = pltpu.make_async_copy(here, own[cls].at[unit], local_sem[cls].at[unit])
        remote = pltpu.make_async_remote_copy(
            src_ref=there, dst_ref=stages[cls][0].at[unit],
            send_sem=send_sem[cls].at[0, unit], recv_sem=recv_sem[cls].at[0, unit],
            device_id=peer["core"], device_id_type=MESH)
        return local, remote

    def later(cls, level, unit):
        ref, index = pick(cls, level - 1, unit, "send")
        return pltpu.make_async_remote_copy(
            src_ref=ref.at[index], dst_ref=stages[cls][level].at[unit],
            send_sem=send_sem[cls].at[level, unit], recv_sem=recv_sem[cls].at[level, unit],
            device_id=peer[ORDERS[cls][level - 1]], device_id_type=MESH)

    def gain_copy(level):
        name = ("core", "x", "y", "low", "high")[level]
        return pltpu.make_async_remote_copy(
            src_ref=gain_buf.at[0, level], dst_ref=gain_buf.at[1, level],
            send_sem=gain_send.at[level], recv_sem=gain_recv.at[level],
            device_id=peer[name], device_id_type=MESH)

    gain_buf[0, 0] = gains_in[...]
    gain_copy(0).start()
    longest = max(len(units) * every[c] for c, units in enumerate(plan))
    for step in range(longest):
        for cls, units in enumerate(plan):
            if step % every[cls] == 0 and step // every[cls] < len(units):
                array, column = units[step // every[cls]]
                local, remote = first(cls, step // every[cls], array, column)
                remote.start()
                local.start()

    def arrive(cls, level, unit):
        array, column = plan[cls][0]
        ref = stages[cls][level]
        if level == 0:
            local, remote = first(cls, unit, array, column)
            remote.wait_recv()
            local.wait()
            ref[unit] = ref[unit] + own[cls][unit]
        else:
            later(cls, level, unit).wait_recv()
            prev, index = pick(cls, level - 1, unit, "keep")
            if level < 4:
                ref[unit] = ref[unit] + prev[index]
            else:
                refs_out[cls][unit] = ref[unit].astype(jnp.float32) + prev[index].astype(jnp.float32)
        if level < 4:
            later(cls, level + 1, unit).start()

    def body(step, carry):
        for level in range(4, -1, -1):
            for cls, units in enumerate(plan):
                at = step - level * SKEW
                unit = at // every[cls]
                ok = (at >= 0) & (unit < len(units))
                if every[cls] > 1:
                    ok = ok & (at % every[cls] == 0)

                @pl.when(ok)
                def _():
                    arrive(cls, level, unit)
        for level in range(5):
            @pl.when(step == 3 * level + 2)
            def _():
                gain_copy(level).wait_recv()
                total = gain_buf[0, level] + gain_buf[1, level]
                if level < 4:
                    gain_buf[0, level + 1] = total
                    gain_copy(level + 1).start()
                else:
                    gains_out[...] = total
        return carry

    steps = max(longest, 15 - 4 * SKEW) + 4 * SKEW
    lax.fori_loop(0, steps, body, 0)
    for level in range(5):
        gain_copy(level).wait_send()
    for cls, units in enumerate(plan):
        def drain(unit, carry):
            first(cls, unit, *plan[cls][0])[1].wait_send()
            for level in range(1, 5):
                later(cls, level, unit).wait_send()
            return carry
        lax.fori_loop(0, len(units), drain, 0)


def make_rs(plan, every, n_in):
    rows = (32, 32, 88)
    n = [len(p) for p in plan]
    def shapes(cls):
        u, r = n[cls], rows[cls]
        return [(u,) + (2,) * k + (r, UNIT) for k in (4, 3, 2, 1, 0)]

    def kernel(*refs):
        refs_in = refs[:n_in]
        gains_in = refs[n_in]
        refs_out = refs[n_in + 1 : n_in + 4]
        gains_out = refs[n_in + 4]
        k = n_in + 5
        own = refs[k : k + 3]
        k += 3
        stages = [refs[k + 5 * c : k + 5 * c + 5] for c in range(3)]
        k += 15
        gain_buf = refs[k]
        k += 1
        sems = (refs[k : k + 3], refs[k + 3 : k + 6], refs[k + 6 : k + 9], refs[k + 9], refs[k + 10])
        rs_kernel(plan, every, None, refs_in, gains_in, refs_out, gains_out, own, stages, gain_buf, sems)

    scratch = [pltpu.VMEM(shapes(c)[0], jnp.bfloat16) for c in range(3)]
    for c in range(3):
        scratch += [pltpu.VMEM(s, jnp.bfloat16) for s in shapes(c)]
    scratch.append(pltpu.VMEM((2, 5, 16, 128), jnp.float32))
    scratch += [pltpu.SemaphoreType.DMA((n[c],)) for c in range(3)]
    scratch += [pltpu.SemaphoreType.DMA((5, n[c])) for c in range(3)]
    scratch += [pltpu.SemaphoreType.DMA((5, n[c])) for c in range(3)]
    scratch += [pltpu.SemaphoreType.DMA((5,)), pltpu.SemaphoreType.DMA((5,))]
    return pl.pallas_call(
        kernel,
        out_shape=tuple(jax.ShapeDtypeStruct((n[c], rows[c], UNIT), jnp.float32) for c in range(3))
        + (jax.ShapeDtypeStruct((16, 128), jnp.float32),),
        in_specs=[pl.BlockSpec(memory_space=pl.ANY)] * n_in + [pl.BlockSpec(memory_space=pltpu.VMEM)],
        out_specs=tuple(pl.BlockSpec(memory_space=pltpu.VMEM) for _ in range(4)),
        scratch_shapes=scratch,
        name="weight_sums",
        compiler_params=pltpu.CompilerParams(collective_id=0, has_side_effects=True, vmem_limit_bytes=58 * 2**20),
    )


def weight_plan():
    a = [(0, 256 * i) for i in range(11)] + [(2, 256 * i) for i in range(4)] + [(3, 256 * i) for i in range(4)]
    b = [(1, 256 * i) for i in range(11)] + [(4, 256 * i) for i in range(4)] + [(5, 256 * i) for i in range(4)]
    c = [(6, 256 * i) for i in range(4)]
    return (a, b, c), (1, 1, 4)


def reduce_weights(gate, up, query, key, value, out, down, gain_one, gain_two):
    plan, every = weight_plan()
    def wide(g):
        return g.reshape(2, 2, 2, 2, 2, g.shape[0] // 32, g.shape[1])
    gains = jnp.concatenate((gain_one, gain_two)).reshape(16, 128)
    ins = [wide(gate), wide(up), wide(query), wide(key), wide(value), wide(out), wide(down), gains]
    a, b, c, gsum = make_rs(plan, every, 7)(*ins)
    def cols(x):
        return x.transpose(1, 0, 2).reshape(x.shape[1], -1)
    index = lax.axis_index("seq") * lax.axis_size("doc") + lax.axis_index("doc")
    gsum = gsum.reshape(2, 32, 32)
    mine = lax.dynamic_index_in_dim(gsum, index, 1, keepdims=False)
    return (cols(a[:11]), cols(b[:11]), cols(a[11:15]), cols(a[15:19]), cols(b[11:15]), cols(b[15:19]), cols(c), mine[0], mine[1])

def sum_weights(weights, gains):
    if (lax.axis_size("seq"), lax.axis_size("doc")) == (8, 4):
        return reduce_weights(*[grad.astype(jnp.bfloat16) for grad in weights], *gains)
    return tuple(
        lax.psum_scatter(grad, ("seq", "doc"), scatter_dimension=0, tiled=True)
        for grad in weights + gains
    )


def on_device(
    tokens,
    cotangent,
    attn_gain,
    w_query,
    w_key,
    w_value,
    w_out,
    ffn_gain,
    w_gate,
    w_up,
    w_down,
    mem_keys,
    mem_values,
    seg_len,
    mem_idx,
):
    stream_count, block_len, model_width = tokens.shape
    attn_width = w_query.shape[1]
    mem_rows = mem_keys.shape[1]
    seq_count = lax.axis_size("seq")
    place = lax.axis_index("seq")
    part_pos = place % BPS
    segment = place // BPS
    capacity = 2 * TOPK // seq_count
    slot_count = seq_count * capacity
    seg_width = BPS * block_len
    lengths = lax.dynamic_index_in_dim(seg_len, segment, 1, keepdims=False)
    tokens_f = tokens.astype(jnp.float32).reshape(-1, model_width)
    gain_one = attn_gain.astype(jnp.float32)
    gain_two = ffn_gain.astype(jnp.float32)
    factor_one = rms_factor(tokens_f)
    unit_one = tokens_f * factor_one
    normed_one = (unit_one * gain_one).astype(jnp.bfloat16)
    queries = jnp.dot(normed_one, w_query, preferred_element_type=jnp.float32).astype(jnp.bfloat16)
    keys_own = jnp.dot(normed_one, w_key, preferred_element_type=jnp.float32).astype(jnp.bfloat16)
    values_own = jnp.dot(normed_one, w_value, preferred_element_type=jnp.float32).astype(
        jnp.bfloat16
    )
    kv_own = jnp.stack(
        (
            keys_own.reshape(stream_count, block_len, attn_width),
            values_own.reshape(stream_count, block_len, attn_width),
        ),
        axis=1,
    )
    kv_seg = neighbour_blocks(kv_own)
    chosen = mem_idx[:, 0, :]
    owner = chosen // mem_rows
    local_row = chosen % mem_rows
    order = jnp.arange(TOPK)
    same_before = (owner[:, :, None] == owner[:, None, :]) & (
        order[None, None, :] < order[None, :, None]
    )
    rank = jnp.sum(same_before.astype(jnp.int32), axis=2)
    slot = owner * capacity + rank
    slot_ids = jnp.arange(slot_count)
    matched = slot[:, :, None] == slot_ids[None, None, :]
    request = jnp.sum(jnp.where(matched, local_row[:, :, None] + 1, 0), axis=1) - 1
    valid = request >= 0
    requested_in = lax.all_to_all(
        request.reshape(stream_count, seq_count, capacity),
        "seq",
        split_axis=1,
        concat_axis=1,
        tiled=True,
    )
    row_ids = jnp.maximum(requested_in, 0).reshape(stream_count, slot_count)
    mem_kv = fetch_rows(mem_keys, mem_values, row_ids, seq_count, capacity)
    key_pos = (part_pos - (BPS - 1)) * block_len + jnp.arange(seg_width)
    query_pos = part_pos * block_len + jnp.arange(block_len)
    local_ok = (
        (key_pos[None, None, :] >= 0)
        & (key_pos[None, None, :] <= query_pos[None, :, None])
        & (key_pos[None, None, :] < lengths[:, None, None])
    )
    memory_ok = jnp.broadcast_to(valid[:, None, :], (stream_count, block_len, slot_count))
    allowed = jnp.concatenate((local_ok, memory_ok), axis=2)
    query_blocks = queries.reshape(stream_count, block_len, attn_width)
    attended, log_total = lax.map(attend_forward, (query_blocks, kv_seg, mem_kv, allowed))
    attended_low = attended.astype(jnp.bfloat16).reshape(-1, attn_width)
    middle = tokens_f + jnp.dot(attended_low, w_out, preferred_element_type=jnp.float32)
    factor_two = rms_factor(middle)
    unit_two = middle * factor_two
    normed_two = (unit_two * gain_two).astype(jnp.bfloat16)
    gate = jnp.dot(normed_two, w_gate, preferred_element_type=jnp.float32)
    upper = jnp.dot(normed_two, w_up, preferred_element_type=jnp.float32)
    sigma = jax.nn.sigmoid(gate)
    hidden = (gate * sigma * upper).astype(jnp.bfloat16)
    layer_out = (middle + jnp.dot(hidden, w_down, preferred_element_type=jnp.float32)).astype(
        jnp.bfloat16
    )
    grad_y = cotangent.astype(jnp.float32).reshape(-1, model_width)
    grad_y_low = grad_y.astype(jnp.bfloat16)
    grad_down = jnp.einsum("nf,nd->fd", hidden, grad_y_low, preferred_element_type=jnp.float32)
    grad_hidden = jnp.einsum("nd,fd->nf", grad_y_low, w_down, preferred_element_type=jnp.float32)
    grad_gate_act = (grad_hidden * upper * sigma * (1.0 + gate * (1.0 - sigma))).astype(
        jnp.bfloat16
    )
    grad_up_act = (grad_hidden * gate * sigma).astype(jnp.bfloat16)
    grad_gate = jnp.einsum(
        "nd,nf->df", normed_two, grad_gate_act, preferred_element_type=jnp.float32
    )
    grad_up = jnp.einsum("nd,nf->df", normed_two, grad_up_act, preferred_element_type=jnp.float32)
    grad_normed_two = jnp.einsum(
        "nf,df->nd", grad_gate_act, w_gate, preferred_element_type=jnp.float32
    ) + jnp.einsum("nf,df->nd", grad_up_act, w_up, preferred_element_type=jnp.float32)
    grad_ffn_gain = jnp.sum(grad_normed_two * unit_two, axis=0)
    scaled_two = gain_two * grad_normed_two
    grad_middle = grad_y + factor_two * (
        scaled_two - unit_two * jnp.mean(scaled_two * unit_two, axis=-1, keepdims=True)
    )
    grad_branch = grad_middle.astype(jnp.bfloat16)
    grad_out = jnp.einsum(
        "nh,nd->hd", attended_low, grad_branch, preferred_element_type=jnp.float32
    )
    grad_attended = jnp.einsum(
        "nd,hd->nh", grad_branch, w_out, preferred_element_type=jnp.float32
    ).astype(jnp.bfloat16)
    kv_back = neighbour_blocks(kv_own)
    mem_back = fetch_rows(mem_keys, mem_values, row_ids, seq_count, capacity)
    grad_queries, grad_keys_all, grad_values_all = lax.map(
        attend_backward,
        (
            query_blocks,
            kv_back,
            mem_back,
            allowed,
            log_total,
            grad_attended.reshape(stream_count, block_len, attn_width),
        ),
    )
    grad_local = jnp.stack((grad_keys_all[:, :seg_width], grad_values_all[:, :seg_width]), axis=1)
    grad_memory = jnp.stack((grad_keys_all[:, seg_width:], grad_values_all[:, seg_width:]), axis=1)
    own_grad = grad_local[:, :, (BPS - 1) * block_len :]
    for distance in range(1, BPS):
        offset = (BPS - 1 - distance) * block_len
        piece = grad_local[:, :, offset : offset + block_len]
        own_grad = own_grad + from_behind(piece.astype(jnp.bfloat16), "seq", -distance).astype(
            piece.dtype
        )
    grad_memory = jnp.where(valid[:, None, :, None], grad_memory, 0.0)
    returned = lax.all_to_all(
        grad_memory.reshape(stack_shape(stream_count, seq_count, capacity, attn_width)).astype(
            jnp.bfloat16
        ),
        "seq",
        split_axis=2,
        concat_axis=2,
        tiled=True,
    ).astype(jnp.float32)
    returned = returned.reshape(stream_count, 2, slot_count, attn_width)
    empty_table = jnp.zeros((stream_count, mem_rows, attn_width), jnp.float32)
    grad_mem_keys = jax.vmap(add_rows)(empty_table, row_ids, returned[:, 0])
    grad_mem_values = jax.vmap(add_rows)(empty_table, row_ids, returned[:, 1])
    grad_q_low = grad_queries.astype(jnp.bfloat16).reshape(-1, attn_width)
    grad_k_low = own_grad[:, 0].astype(jnp.bfloat16).reshape(-1, attn_width)
    grad_v_low = own_grad[:, 1].astype(jnp.bfloat16).reshape(-1, attn_width)
    grad_query = jnp.einsum("nd,nh->dh", normed_one, grad_q_low, preferred_element_type=jnp.float32)
    grad_key = jnp.einsum("nd,nh->dh", normed_one, grad_k_low, preferred_element_type=jnp.float32)
    grad_value = jnp.einsum("nd,nh->dh", normed_one, grad_v_low, preferred_element_type=jnp.float32)
    grad_normed_one = (
        jnp.einsum("nh,dh->nd", grad_q_low, w_query, preferred_element_type=jnp.float32)
        + jnp.einsum("nh,dh->nd", grad_k_low, w_key, preferred_element_type=jnp.float32)
        + jnp.einsum("nh,dh->nd", grad_v_low, w_value, preferred_element_type=jnp.float32)
    )
    grad_attn_gain = jnp.sum(grad_normed_one * unit_one, axis=0)
    scaled_one = gain_one * grad_normed_one
    grad_input = grad_middle + factor_one * (
        scaled_one - unit_one * jnp.mean(scaled_one * unit_one, axis=-1, keepdims=True)
    )
    grad_tokens = grad_input.astype(jnp.bfloat16).reshape(stream_count, block_len, model_width)
    summed = sum_weights(
        (grad_gate, grad_up, grad_query, grad_key, grad_value, grad_out, grad_down),
        (grad_attn_gain, grad_ffn_gain),
    )
    return (
        layer_out.reshape(stream_count, block_len, model_width),
        grad_tokens,
        summed[7],
        summed[2],
        summed[3],
        summed[4],
        summed[5],
        summed[8],
        summed[0],
        summed[1],
        summed[6],
        grad_mem_keys,
        grad_mem_values,
    )


def solution(mesh):
    in_specs = (
        P("doc", "seq", None),
        P("doc", "seq", None),
        P(),
        P(),
        P(),
        P(),
        P(),
        P(),
        P(),
        P(),
        P(),
        P("doc", "seq", None),
        P("doc", "seq", None),
        P("doc", None),
        P("doc", "seq", None),
    )
    out_specs = (
        P("doc", "seq", None),
        P("doc", "seq", None),
        P(("seq", "doc")),
        P(("seq", "doc"), None),
        P(("seq", "doc"), None),
        P(("seq", "doc"), None),
        P(("seq", "doc"), None),
        P(("seq", "doc")),
        P(("seq", "doc"), None),
        P(("seq", "doc"), None),
        P(("seq", "doc"), None),
        P("doc", "seq", None),
        P("doc", "seq", None),
    )
    return jax.shard_map(
        on_device, mesh=mesh, in_specs=in_specs, out_specs=out_specs, check_vma=False
    )
```

```python
import functools
import math

import jax
import jax.numpy as jnp
from jax import lax
from jax.experimental import pallas as pl
from jax.experimental.pallas import tpu as pltpu
from jax.sharding import PartitionSpec as P

HEADS = 8
HEAD_DIM = 128
TOPK = 128
BPS = 4
NEG = -1000000000.0
MESH = pl.DeviceIdType.MESH
UNIT = 256
SKEW = 2

def flip(value, bit):
    return value + bit - 2 * bit * ((value // bit) % 2)


def partners():
    seq, doc = lax.axis_index("seq"), lax.axis_index("doc")
    return {
        "core": (flip(seq, 1), doc),
        "x": (flip(seq, 2), doc),
        "y": (flip(seq, 4), doc),
        "low": (seq, flip(doc, 1)),
        "high": (seq, flip(doc, 2)),
    }


ORDERS = (("x", "y", "low", "high"), ("y", "x", "low", "high"), ("low", "high", "x", "y"))


def rs_kernel(plan, every, names, refs_in, gains_in, refs_out, gains_out, own, stages, gain_buf, sems):
    seq, doc = lax.axis_index("seq"), lax.axis_index("doc")
    bits = {
        "core": seq % 2,
        "x": (seq // 2) % 2,
        "y": (seq // 4) % 2,
        "low": doc % 2,
        "high": (doc // 2) % 2,
    }
    peer = partners()
    local_sem, send_sem, recv_sem, gain_send, gain_recv = sems
    barrier = pltpu.get_barrier_semaphore()
    for name in ("core", "x", "y", "low", "high"):
        pl.semaphore_signal(barrier, inc=1, device_id=peer[name], device_id_type=MESH)
    pl.semaphore_wait(barrier, 5)

    def pick(cls, level, unit, side):
        order = ORDERS[cls]
        ref = stages[cls][level]
        name = order[level]
        where = (1 - bits[name]) if side == "send" else bits[name]
        left = [axis for axis in ("y", "x", "high", "low") if axis not in order[:level]]
        index = (unit,) + (slice(None),) * left.index(name) + (where,)
        return ref, index

    def first(cls, unit, array, column):
        source = refs_in[array]
        lanes = pl.ds(column, UNIT)
        there = source.at[:, :, 1 - bits["core"], :, :, :, lanes]
        here = source.at[:, :, bits["core"], :, :, :, lanes]
        local = pltpu.make_async_copy(here, own[cls].at[unit], local_sem[cls].at[unit])
        remote = pltpu.make_async_remote_copy(
            src_ref=there, dst_ref=stages[cls][0].at[unit],
            send_sem=send_sem[cls].at[0, unit], recv_sem=recv_sem[cls].at[0, unit],
            device_id=peer["core"], device_id_type=MESH)
        return local, remote

    def later(cls, level, unit):
        ref, index = pick(cls, level - 1, unit, "send")
        return pltpu.make_async_remote_copy(
            src_ref=ref.at[index], dst_ref=stages[cls][level].at[unit],
            send_sem=send_sem[cls].at[level, unit], recv_sem=recv_sem[cls].at[level, unit],
            device_id=peer[ORDERS[cls][level - 1]], device_id_type=MESH)

    def gain_copy(level):
        name = ("core", "x", "y", "low", "high")[level]
        return pltpu.make_async_remote_copy(
            src_ref=gain_buf.at[0, level], dst_ref=gain_buf.at[1, level],
            send_sem=gain_send.at[level], recv_sem=gain_recv.at[level],
            device_id=peer[name], device_id_type=MESH)

    gain_buf[0, 0] = gains_in[...]
    gain_copy(0).start()
    longest = max(len(units) * every[c] for c, units in enumerate(plan))
    for step in range(longest):
        for cls, units in enumerate(plan):
            if step % every[cls] == 0 and step // every[cls] < len(units):
                array, column = units[step // every[cls]]
                local, remote = first(cls, step // every[cls], array, column)
                remote.start()
                local.start()

    def arrive(cls, level, unit):
        array, column = plan[cls][0]
        ref = stages[cls][level]
        if level == 0:
            local, remote = first(cls, unit, array, column)
            remote.wait_recv()
            local.wait()
            ref[unit] = ref[unit] + own[cls][unit]
        else:
            later(cls, level, unit).wait_recv()
            prev, index = pick(cls, level - 1, unit, "keep")
            if level < 4:
                ref[unit] = ref[unit] + prev[index]
            else:
                refs_out[cls][unit] = ref[unit].astype(jnp.float32) + prev[index].astype(jnp.float32)
        if level < 4:
            later(cls, level + 1, unit).start()

    def body(step, carry):
        for level in range(4, -1, -1):
            for cls, units in enumerate(plan):
                at = step - level * SKEW
                unit = at // every[cls]
                ok = (at >= 0) & (unit < len(units))
                if every[cls] > 1:
                    ok = ok & (at % every[cls] == 0)

                @pl.when(ok)
                def _():
                    arrive(cls, level, unit)
        for level in range(5):
            @pl.when(step == 3 * level + 2)
            def _():
                gain_copy(level).wait_recv()
                total = gain_buf[0, level] + gain_buf[1, level]
                if level < 4:
                    gain_buf[0, level + 1] = total
                    gain_copy(level + 1).start()
                else:
                    gains_out[...] = total
        return carry

    steps = max(longest, 15 - 4 * SKEW) + 4 * SKEW
    lax.fori_loop(0, steps, body, 0)
    for level in range(5):
        gain_copy(level).wait_send()
    for cls, units in enumerate(plan):
        def drain(unit, carry):
            first(cls, unit, *plan[cls][0])[1].wait_send()
            for level in range(1, 5):
                later(cls, level, unit).wait_send()
            return carry
        lax.fori_loop(0, len(units), drain, 0)


def make_rs(plan, every, n_in):
    rows = (32, 32, 88)
    n = [len(p) for p in plan]
    def shapes(cls):
        u, r = n[cls], rows[cls]
        return [(u,) + (2,) * k + (r, UNIT) for k in (4, 3, 2, 1, 0)]

    def kernel(*refs):
        refs_in = refs[:n_in]
        gains_in = refs[n_in]
        refs_out = refs[n_in + 1 : n_in + 4]
        gains_out = refs[n_in + 4]
        k = n_in + 5
        own = refs[k : k + 3]
        k += 3
        stages = [refs[k + 5 * c : k + 5 * c + 5] for c in range(3)]
        k += 15
        gain_buf = refs[k]
        k += 1
        sems = (refs[k : k + 3], refs[k + 3 : k + 6], refs[k + 6 : k + 9], refs[k + 9], refs[k + 10])
        rs_kernel(plan, every, None, refs_in, gains_in, refs_out, gains_out, own, stages, gain_buf, sems)

    scratch = [pltpu.VMEM(shapes(c)[0], jnp.bfloat16) for c in range(3)]
    for c in range(3):
        scratch += [pltpu.VMEM(s, jnp.bfloat16) for s in shapes(c)]
    scratch.append(pltpu.VMEM((2, 5, 16, 128), jnp.float32))
    scratch += [pltpu.SemaphoreType.DMA((n[c],)) for c in range(3)]
    scratch += [pltpu.SemaphoreType.DMA((5, n[c])) for c in range(3)]
    scratch += [pltpu.SemaphoreType.DMA((5, n[c])) for c in range(3)]
    scratch += [pltpu.SemaphoreType.DMA((5,)), pltpu.SemaphoreType.DMA((5,))]
    return pl.pallas_call(
        kernel,
        out_shape=tuple(jax.ShapeDtypeStruct((n[c], rows[c], UNIT), jnp.float32) for c in range(3))
        + (jax.ShapeDtypeStruct((16, 128), jnp.float32),),
        in_specs=[pl.BlockSpec(memory_space=pl.ANY)] * n_in + [pl.BlockSpec(memory_space=pltpu.VMEM)],
        out_specs=tuple(pl.BlockSpec(memory_space=pltpu.VMEM) for _ in range(4)),
        scratch_shapes=scratch,
        name="weight_sums",
        compiler_params=pltpu.CompilerParams(collective_id=0, has_side_effects=True, vmem_limit_bytes=58 * 2**20),
    )


def weight_plan():
    a = [(0, 256 * i) for i in range(11)] + [(2, 256 * i) for i in range(4)] + [(3, 256 * i) for i in range(4)]
    b = [(1, 256 * i) for i in range(11)] + [(4, 256 * i) for i in range(4)] + [(5, 256 * i) for i in range(4)]
    c = [(6, 256 * i) for i in range(4)]
    return (a, b, c), (1, 1, 4)


def reduce_weights(gate, up, query, key, value, out, down, gain_one, gain_two):
    plan, every = weight_plan()
    def wide(g):
        return g.reshape(2, 2, 2, 2, 2, g.shape[0] // 32, g.shape[1])
    gains = jnp.concatenate((gain_one, gain_two)).reshape(16, 128)
    ins = [wide(gate), wide(up), wide(query), wide(key), wide(value), wide(out), wide(down), gains]
    a, b, c, gsum = make_rs(plan, every, 7)(*ins)
    def cols(x):
        return x.transpose(1, 0, 2).reshape(x.shape[1], -1)
    index = lax.axis_index("seq") * lax.axis_size("doc") + lax.axis_index("doc")
    gsum = gsum.reshape(2, 32, 32)
    mine = lax.dynamic_index_in_dim(gsum, index, 1, keepdims=False)
    return (cols(a[:11]), cols(b[:11]), cols(a[11:15]), cols(a[15:19]), cols(b[11:15]), cols(b[15:19]), cols(c), mine[0], mine[1])


HALF = HEADS // 2
LOG2E = math.log2(math.e)
SCALE = HEAD_DIM ** (-0.5)
NT = (((1,), (1,)), ((), ()))
TN = (((0,), (0,)), ((), ()))
NN = (((1,), (0,)), ((), ()))


def matmul(left, right, dims):
    return lax.dot_general(left, right, dims, preferred_element_type=jnp.float32)


def seats():
    seq, doc = lax.axis_index("seq"), lax.axis_index("doc")
    core, chip = seq % 2, (seq // 2) % 2
    mate = (flip(seq, 1), doc)
    across = (flip(seq, 2), doc)
    diagonal = (flip(flip(seq, 2), 1), doc)
    return core, chip, mate, across, diagonal


def meet(peers):
    barrier = pltpu.get_barrier_semaphore()
    for peer in peers:
        pl.semaphore_signal(barrier, inc=1, device_id=peer, device_id_type=MESH)
    pl.semaphore_wait(barrier, len(peers))


def head_lanes(core, head):
    return pl.ds(pl.multiple_of((core * HALF + head) * HEAD_DIM, HEAD_DIM), HEAD_DIM)


def remote(src, dst, send, recv, peer):
    return pltpu.make_async_remote_copy(
        src_ref=src, dst_ref=dst, send_sem=send, recv_sem=recv, device_id=peer, device_id_type=MESH
    )


def share_heads(sources, boxes, core, mate, local_sem, send_sem, recv_sem):
    copies = []
    for i, (source, box) in enumerate(zip(sources, boxes)):
        for head in range(HALF):
            copies.append(
                remote(
                    source.at[:, head_lanes(1 - core, head)],
                    box.at[core, head],
                    send_sem.at[i, head],
                    recv_sem.at[i, head],
                    mate,
                )
            )
            copies[-1].start()
    for i, (source, box) in enumerate(zip(sources, boxes)):
        for head in range(HALF):
            copies.append(
                pltpu.make_async_copy(
                    source.at[:, head_lanes(core, head)], box.at[core, head], local_sem.at[i, head]
                )
            )
            copies[-1].start()
    return copies


def masked(scores, first_key, limit, diagonal):
    key = lax.broadcasted_iota(jnp.int32, scores.shape, 0)
    ok = key + first_key < limit
    if diagonal:
        ok = ok & (key <= lax.broadcasted_iota(jnp.int32, scores.shape, 1))
    return jnp.where(ok, scores, NEG)


def soften(parts):
    top = functools.reduce(
        jnp.maximum, [jnp.max(scores, axis=0, keepdims=True) for scores, _ in parts]
    )
    total, mixed = 0.0, 0.0
    for scores, values in parts:
        exponent = jnp.exp2(scores - top)
        total = total + jnp.sum(exponent, axis=0, keepdims=True)
        mixed = mixed + matmul(values, exponent.astype(jnp.bfloat16), TN)
    return mixed / total, top + jnp.log(total) * LOG2E


def forward_kernel(
    limit_ref, q, k, v, mk, mv,
    attended, qb, kb, vb, qx, mkb, mvb, ob, lse,
    mixed_own, mixed_out, mixed_in, lse_out, lse_in,
    local_sem, mate_send, mate_recv, far_send, far_recv, back_send, back_recv, end_sem,
):
    core, chip, mate, across, diagonal = seats()
    block = q.shape[0]
    limit = limit_ref[0]
    meet((mate, across, diagonal))

    def query_copy(head, own):
        return remote(
            q.at[:, head_lanes(core if own else 1 - core, head)],
            qx.at[core, head],
            far_send.at[0 if own else 1, head],
            far_recv.at[core, head],
            across if own else diagonal,
        )

    def arrived_query(far, head):
        return remote(
            q.at[:, head_lanes(core, head)], qx.at[far, head], far_send.at[0, head], far_recv.at[far, head], across
        )

    @pl.when(chip == 1)
    def _():
        for head in range(HALF):
            query_copy(head, True).start()
            query_copy(head, False).start()

    copies = share_heads((q, k, v, mk, mv), (qb, kb, vb, mkb, mvb), core, mate, local_sem, mate_send, mate_recv)
    for copy in copies:
        copy.wait()

    def own_part(blk, head):
        query = qb[blk, head]
        parts = []
        for kblk in range(blk + 1):
            scores = matmul(kb[kblk, head], query, NT) * (SCALE * LOG2E)
            scores = masked(scores, (2 * chip + kblk) * block, limit, kblk == blk)
            parts.append((scores, vb[kblk, head]))
        parts.append((matmul(mkb[blk, head], query, NT) * (SCALE * LOG2E), mvb[blk, head]))
        return soften(parts)

    for blk in range(2):
        def own_head(head, carry):
            mixed, level = own_part(blk, head)
            mixed_own[blk, head] = mixed
            lse[blk, head] = level
            return carry
        lax.fori_loop(0, HALF, own_head, 0)

    def back_copy(blk, head):
        return (
            remote(mixed_out.at[blk, head], mixed_in.at[blk, head], back_send.at[0, blk, head], back_recv.at[0, blk, head], across),
            remote(lse_out.at[blk, head], lse_in.at[blk, head], back_send.at[1, blk, head], back_recv.at[1, blk, head], across),
        )

    @pl.when(chip == 0)
    def _():
        def cross(i, carry):
            head, blk = i // 2, i % 2
            arrived_query(blk, head).wait_recv()
            query = qx[blk, head]
            parts = []
            for kblk in range(2):
                scores = matmul(kb[kblk, head], query, NT) * (SCALE * LOG2E)
                parts.append((masked(scores, kblk * block, limit, False), vb[kblk, head]))
            mixed, level = soften(parts)
            mixed_out[blk, head] = mixed.astype(jnp.bfloat16)
            lse_out[blk, head] = level
            for copy in back_copy(blk, head):
                copy.start()
            return carry
        lax.fori_loop(0, 2 * HALF, cross, 0)

        def finish(i, carry):
            head, blk = i // 2, i % 2
            ob[blk, head] = mixed_own[blk, head].T.astype(jnp.bfloat16)
            return carry
        lax.fori_loop(0, 2 * HALF, finish, 0)

    @pl.when(chip == 1)
    def _():
        def merge(i, carry):
            head, blk = i // 2, i % 2
            for copy in back_copy(blk, head):
                copy.wait_recv()
            near, far = lse[blk, head], lse_in[blk, head]
            top = jnp.maximum(near, far)
            near, far = jnp.exp2(near - top), jnp.exp2(far - top)
            total = near + far
            mixed = (mixed_own[blk, head] * near + mixed_in[blk, head].astype(jnp.float32) * far) / total
            ob[blk, head] = mixed.T.astype(jnp.bfloat16)
            lse[blk, head] = top + jnp.log(total) * LOG2E
            return carry
        lax.fori_loop(0, 2 * HALF, merge, 0)

    ends = []
    for head in range(HALF):
        ends.append(
            remote(ob.at[1 - core, head], attended.at[:, head_lanes(core, head)], end_sem.at[0, head], end_sem.at[1, head], mate)
        )
        ends.append(
            pltpu.make_async_copy(ob.at[core, head], attended.at[:, head_lanes(core, head)], end_sem.at[2, head])
        )
    for copy in ends:
        copy.start()
    for copy in ends:
        copy.wait()

    @pl.when(chip == 0)
    def _():
        for head in range(HALF):
            for blk in range(2):
                for copy in back_copy(blk, head):
                    copy.wait_send()

    @pl.when(chip == 1)
    def _():
        for head in range(HALF):
            query_copy(head, True).wait_send()
            query_copy(head, False).wait_send()


def attend_forward(limit, queries, keys, values, mem_keys, mem_values):
    block, width = queries.shape
    topk = mem_keys.shape[0]
    low, full = jnp.bfloat16, jnp.float32
    box = (2, HALF, block, HEAD_DIM)
    mem_box = (2, HALF, topk, HEAD_DIM)
    flat = (2, HALF, HEAD_DIM, block)
    row = (2, HALF, 1, block)
    dma = pltpu.SemaphoreType.DMA
    hbm, vmem = pl.BlockSpec(memory_space=pl.ANY), pl.BlockSpec(memory_space=pltpu.VMEM)
    struct = jax.ShapeDtypeStruct
    return pl.pallas_call(
        forward_kernel,
        out_shape=(
            struct((block, width), low),
            struct(box, low), struct(box, low), struct(box, low), struct(box, low),
            struct(mem_box, low), struct(mem_box, low), struct(box, low), struct(row, full),
        ),
        in_specs=[pl.BlockSpec(memory_space=pltpu.SMEM)] + [hbm] * 5,
        out_specs=(hbm,) + (vmem,) * 8,
        scratch_shapes=[
            pltpu.VMEM(flat, full), pltpu.VMEM(flat, low), pltpu.VMEM(flat, low),
            pltpu.VMEM(row, full), pltpu.VMEM(row, full),
            dma((5, HALF)), dma((5, HALF)), dma((5, HALF)),
            dma((2, HALF)), dma((2, HALF)), dma((2, 2, HALF)), dma((2, 2, HALF)), dma((3, HALF)),
        ],
        name="attend_forward",
        compiler_params=pltpu.CompilerParams(collective_id=1, has_side_effects=True, vmem_limit_bytes=56 * 2**20),
    )(limit, queries, keys, values, mem_keys, mem_values)


def backward_kernel(
    limit_ref, grad, qb, kb, vb, qx, mkb, mvb, ob, lse,
    dq, dk, dv, dmk, dmv,
    gb, gx, delta, lse_in, delta_in, dq_own, dq_out, dq_in, dk_sum, dv_sum, dmk_low, dmv_low, dqb, dkb, dvb,
    local_sem, mate_send, mate_recv, far_send, far_recv, row_send, row_recv, back_send, back_recv,
    end_local, end_send, end_recv,
):
    core, chip, mate, across, diagonal = seats()
    block = grad.shape[0]
    limit = limit_ref[0]
    meet((mate, across, diagonal))

    def grad_copy(head, own):
        return remote(
            grad.at[:, head_lanes(core if own else 1 - core, head)],
            gx.at[core, head],
            far_send.at[0 if own else 1, head],
            far_recv.at[core, head],
            across if own else diagonal,
        )

    def arrived_grad(far, head):
        return remote(
            grad.at[:, head_lanes(core, head)], gx.at[far, head], far_send.at[0, head], far_recv.at[far, head], across
        )

    def row_copies():
        return (
            remote(lse, lse_in, row_send.at[0], row_recv.at[0], across),
            remote(delta, delta_in, row_send.at[1], row_recv.at[1], across),
        )

    @pl.when(chip == 1)
    def _():
        for head in range(HALF):
            grad_copy(head, True).start()
            grad_copy(head, False).start()

    copies = share_heads((grad,), (gb,), core, mate, local_sem, mate_send, mate_recv)
    for copy in copies:
        copy.wait()

    def rows(i, carry):
        head, blk = i // 2, i % 2
        product = gb[blk, head].astype(jnp.float32) * ob[blk, head].astype(jnp.float32)
        delta[blk, head] = jnp.sum(product.T, axis=0, keepdims=True)
        return carry

    lax.fori_loop(0, 2 * HALF, rows, 0)

    @pl.when(chip == 1)
    def _():
        for copy in row_copies():
            copy.start()

    def pull(key_rows, value_rows, query, grad_rows, level, inner, where):
        scores = matmul(key_rows, query, NT) * (SCALE * LOG2E)
        if where is not None:
            scores = masked(scores, where[0], limit, where[1])
        weights = jnp.exp2(scores - level)
        grad_weights = matmul(value_rows, grad_rows, NT)
        grad_scores = (weights * (grad_weights - inner)).astype(jnp.bfloat16)
        return (
            matmul(grad_scores, query, NN),
            matmul(weights.astype(jnp.bfloat16), grad_rows, NN),
            matmul(key_rows, grad_scores, TN),
        )

    for blk in range(2):
        def own_head(head, carry):
            query, grad_rows = qb[blk, head], gb[blk, head]
            level, inner = lse[blk, head], delta[blk, head]
            total = 0.0
            for kblk in range(blk + 1):
                gk, gv, gq = pull(
                    kb[kblk, head], vb[kblk, head], query, grad_rows, level, inner,
                    ((2 * chip + kblk) * block, kblk == blk),
                )
                if kblk == blk:
                    dk_sum[kblk, head], dv_sum[kblk, head] = gk, gv
                else:
                    dk_sum[kblk, head] += gk
                    dv_sum[kblk, head] += gv
                total = total + gq
            gk, gv, gq = pull(mkb[blk, head], mvb[blk, head], query, grad_rows, level, inner, None)
            dmk_low[blk, head] = (gk * SCALE).astype(jnp.bfloat16)
            dmv_low[blk, head] = gv.astype(jnp.bfloat16)
            dq_own[blk, head] = total + gq
            return carry
        lax.fori_loop(0, HALF, own_head, 0)

    def back_copy(blk, head):
        return remote(dq_out.at[blk, head], dq_in.at[blk, head], back_send.at[blk, head], back_recv.at[blk, head], across)

    @pl.when(chip == 0)
    def _():
        for copy in row_copies():
            copy.wait_recv()

        def cross(i, carry):
            head, blk = i // 2, i % 2
            arrived_grad(blk, head).wait_recv()
            query, grad_rows = qx[blk, head], gx[blk, head]
            level, inner = lse_in[blk, head], delta_in[blk, head]
            total = 0.0
            for kblk in range(2):
                gk, gv, gq = pull(
                    kb[kblk, head], vb[kblk, head], query, grad_rows, level, inner, (kblk * block, False)
                )
                dk_sum[kblk, head] += gk
                dv_sum[kblk, head] += gv
                total = total + gq
            dq_out[blk, head] = total.astype(jnp.bfloat16)
            back_copy(blk, head).start()
            return carry
        lax.fori_loop(0, 2 * HALF, cross, 0)

    def finish(i, carry):
        head, blk = i // 2, i % 2
        dqb[blk, head] = (dq_own[blk, head].T * SCALE).astype(jnp.bfloat16)
        dkb[blk, head] = (dk_sum[blk, head] * SCALE).astype(jnp.bfloat16)
        dvb[blk, head] = dv_sum[blk, head].astype(jnp.bfloat16)
        return carry

    @pl.when(chip == 1)
    def _():
        def merge(i, carry):
            head, blk = i // 2, i % 2
            back_copy(blk, head).wait_recv()
            dq_own[blk, head] += dq_in[blk, head].astype(jnp.float32)
            return finish(i, carry)
        lax.fori_loop(0, 2 * HALF, merge, 0)

    @pl.when(chip == 0)
    def _():
        lax.fori_loop(0, 2 * HALF, finish, 0)

    ends = []
    for i, (box, out) in enumerate(((dqb, dq), (dkb, dk), (dvb, dv), (dmk_low, dmk), (dmv_low, dmv))):
        for head in range(HALF):
            lanes = head_lanes(core, head)
            ends.append(remote(box.at[1 - core, head], out.at[:, lanes], end_send.at[i, head], end_recv.at[i, head], mate))
            ends.append(pltpu.make_async_copy(box.at[core, head], out.at[:, lanes], end_local.at[i, head]))
    for copy in ends:
        copy.start()
    for copy in ends:
        copy.wait()

    @pl.when(chip == 0)
    def _():
        for head in range(HALF):
            for blk in range(2):
                back_copy(blk, head).wait_send()

    @pl.when(chip == 1)
    def _():
        for copy in row_copies():
            copy.wait_send()
        for head in range(HALF):
            grad_copy(head, True).wait_send()
            grad_copy(head, False).wait_send()


def attend_backward(limit, grad, saved):
    block, width = grad.shape
    topk = saved[4].shape[2]
    low, full = jnp.bfloat16, jnp.float32
    box = (2, HALF, block, HEAD_DIM)
    mem_box = (2, HALF, topk, HEAD_DIM)
    flat = (2, HALF, HEAD_DIM, block)
    row = (2, HALF, 1, block)
    dma = pltpu.SemaphoreType.DMA
    hbm, vmem = pl.BlockSpec(memory_space=pl.ANY), pl.BlockSpec(memory_space=pltpu.VMEM)
    struct = jax.ShapeDtypeStruct
    return pl.pallas_call(
        backward_kernel,
        out_shape=(struct((block, width), low),) * 3 + (struct((topk, width), low),) * 2,
        in_specs=[pl.BlockSpec(memory_space=pltpu.SMEM), hbm] + [vmem] * 8,
        out_specs=(hbm,) * 5,
        scratch_shapes=[
            pltpu.VMEM(box, low), pltpu.VMEM(box, low),
            pltpu.VMEM(row, full), pltpu.VMEM(row, full), pltpu.VMEM(row, full),
            pltpu.VMEM(flat, full), pltpu.VMEM(flat, low), pltpu.VMEM(flat, low),
            pltpu.VMEM(box, full), pltpu.VMEM(box, full),
            pltpu.VMEM(mem_box, low), pltpu.VMEM(mem_box, low),
            pltpu.VMEM(box, low), pltpu.VMEM(box, low), pltpu.VMEM(box, low),
            dma((1, HALF)), dma((1, HALF)), dma((1, HALF)),
            dma((2, HALF)), dma((2, HALF)), dma((2,)), dma((2,)),
            dma((2, HALF)), dma((2, HALF)),
            dma((5, HALF)), dma((5, HALF)), dma((5, HALF)),
        ],
        name="attend_backward",
        compiler_params=pltpu.CompilerParams(collective_id=2, has_side_effects=True, vmem_limit_bytes=56 * 2**20),
    )(limit, grad, *saved)


EPS = 1e-05


def rms_factor(values):
    return lax.rsqrt(jnp.mean(values * values, axis=-1, keepdims=True) + EPS)


def dot32(left, right):
    return jnp.dot(left, right, preferred_element_type=jnp.float32)


def sum_weights(weights, gains):
    if (lax.axis_size("seq"), lax.axis_size("doc")) == (8, 4):
        return reduce_weights(*[grad.astype(jnp.bfloat16) for grad in weights], *gains)
    return tuple(
        lax.psum_scatter(grad, ("seq", "doc"), scatter_dimension=0, tiled=True)
        for grad in weights + gains
    )


def exchange(rows, owner_count, capacity):
    parts, _, width = rows.shape
    shaped = rows.reshape(parts, owner_count, capacity, width)
    moved = lax.all_to_all(shaped, "seq", split_axis=1, concat_axis=1, tiled=True)
    return moved.reshape(parts, owner_count * capacity, width)


def on_device(
    tokens,
    cotangent,
    attn_gain,
    w_query,
    w_key,
    w_value,
    w_out,
    ffn_gain,
    w_gate,
    w_up,
    w_down,
    mem_keys,
    mem_values,
    seg_len,
    mem_idx,
):
    low = jnp.bfloat16
    stream_count, block_len, model_width = tokens.shape
    mem_rows = mem_keys.shape[1]
    seq_count = lax.axis_size("seq")
    segment = lax.axis_index("seq") // BPS
    capacity = 2 * TOPK // seq_count
    slot_count = seq_count * capacity
    limit = lax.dynamic_index_in_dim(seg_len, segment, 1, keepdims=False)

    chosen = mem_idx[0, 0]
    owner = chosen // mem_rows
    order = jnp.arange(TOPK)
    same_before = (owner[:, None] == owner[None, :]) & (order[None, :] < order[:, None])
    slot = owner * capacity + jnp.sum(same_before.astype(jnp.int32), axis=1)
    placed = slot[:, None] == jnp.arange(slot_count)[None, :]
    request = jnp.sum(jnp.where(placed, (chosen % mem_rows)[:, None] + 1, 0), axis=0) - 1
    requested = lax.all_to_all(
        request.reshape(seq_count, capacity), "seq", split_axis=0, concat_axis=0, tiled=True
    ).reshape(slot_count)
    picked = (requested[:, None] == jnp.arange(mem_rows)[None, :]).astype(low)
    placed = placed.astype(low)
    sent = jnp.stack((dot32(picked, mem_keys[0]).astype(low), dot32(picked, mem_values[0]).astype(low)))
    arrived = exchange(sent, seq_count, capacity)
    mem_key_rows = dot32(placed, arrived[0]).astype(low)
    mem_value_rows = dot32(placed, arrived[1]).astype(low)

    tokens_f = tokens[0].astype(jnp.float32)
    gain_one = attn_gain.astype(jnp.float32)
    gain_two = ffn_gain.astype(jnp.float32)
    factor_one = rms_factor(tokens_f)
    unit_one = tokens_f * factor_one
    normed_one = (unit_one * gain_one).astype(low)
    queries = dot32(normed_one, w_query).astype(low)
    keys = dot32(normed_one, w_key).astype(low)
    values = dot32(normed_one, w_value).astype(low)
    attended, *saved = attend_forward(limit, queries, keys, values, mem_key_rows, mem_value_rows)
    middle = tokens_f + dot32(attended, w_out)
    factor_two = rms_factor(middle)
    unit_two = middle * factor_two
    normed_two = (unit_two * gain_two).astype(low)
    gate = dot32(normed_two, w_gate)
    upper = dot32(normed_two, w_up)
    sigma = jax.nn.sigmoid(gate)
    hidden = (gate * sigma * upper).astype(low)
    layer_out = (middle + dot32(hidden, w_down)).astype(low)

    grad_y_low = cotangent[0]
    grad_y = grad_y_low.astype(jnp.float32)
    grad_down = dot32(hidden.T, grad_y_low)
    grad_hidden = dot32(grad_y_low, w_down.T)
    grad_gate_act = (grad_hidden * upper * sigma * (1.0 + gate * (1.0 - sigma))).astype(low)
    grad_up_act = (grad_hidden * gate * sigma).astype(low)
    grad_gate = dot32(normed_two.T, grad_gate_act)
    grad_up = dot32(normed_two.T, grad_up_act)
    grad_normed_two = dot32(grad_gate_act, w_gate.T) + dot32(grad_up_act, w_up.T)
    grad_ffn_gain = jnp.sum(grad_normed_two * unit_two, axis=0)
    scaled_two = gain_two * grad_normed_two
    grad_middle = grad_y + factor_two * (
        scaled_two - unit_two * jnp.mean(scaled_two * unit_two, axis=-1, keepdims=True)
    )
    grad_branch = grad_middle.astype(low)
    grad_out = dot32(attended.T, grad_branch)
    grad_attended = dot32(grad_branch, w_out.T).astype(low)
    grad_q, grad_k, grad_v, grad_mk, grad_mv = attend_backward(limit, grad_attended, saved)

    back = jnp.stack((dot32(placed.T, grad_mk).astype(low), dot32(placed.T, grad_mv).astype(low)))
    returned = exchange(back, seq_count, capacity)
    grad_mem_keys = dot32(picked.T, returned[0])
    grad_mem_values = dot32(picked.T, returned[1])
    grad_query = dot32(normed_one.T, grad_q)
    grad_key = dot32(normed_one.T, grad_k)
    grad_value = dot32(normed_one.T, grad_v)
    grad_normed_one = dot32(grad_q, w_query.T) + dot32(grad_k, w_key.T) + dot32(grad_v, w_value.T)
    grad_attn_gain = jnp.sum(grad_normed_one * unit_one, axis=0)
    scaled_one = gain_one * grad_normed_one
    grad_input = grad_middle + factor_one * (
        scaled_one - unit_one * jnp.mean(scaled_one * unit_one, axis=-1, keepdims=True)
    )
    grad_tokens = grad_input.astype(low)
    gate_rows, up_rows, query_rows, key_rows, value_rows, out_rows, down_rows, attn_row, ffn_row = sum_weights(
        (grad_gate, grad_up, grad_query, grad_key, grad_value, grad_out, grad_down),
        (grad_attn_gain, grad_ffn_gain),
    )
    return (
        layer_out[None],
        grad_tokens[None],
        attn_row,
        query_rows,
        key_rows,
        value_rows,
        out_rows,
        ffn_row,
        gate_rows,
        up_rows,
        down_rows,
        grad_mem_keys[None],
        grad_mem_values[None],
    )


def solution(mesh):
    in_specs = (
        P("doc", "seq", None),
        P("doc", "seq", None),
        P(),
        P(),
        P(),
        P(),
        P(),
        P(),
        P(),
        P(),
        P(),
        P("doc", "seq", None),
        P("doc", "seq", None),
        P("doc", None),
        P("doc", "seq", None),
    )
    out_specs = (
        P("doc", "seq", None),
        P("doc", "seq", None),
        P(("seq", "doc")),
        P(("seq", "doc"), None),
        P(("seq", "doc"), None),
        P(("seq", "doc"), None),
        P(("seq", "doc"), None),
        P(("seq", "doc")),
        P(("seq", "doc"), None),
        P(("seq", "doc"), None),
        P(("seq", "doc"), None),
        P("doc", "seq", None),
        P("doc", "seq", None),
    )
    return jax.shard_map(
        on_device, mesh=mesh, in_specs=in_specs, out_specs=out_specs, check_vma=False
    )
```

```python
import functools
import math

import jax
import jax.numpy as jnp
from jax import lax
from jax.experimental import pallas as pl
from jax.experimental.pallas import tpu as pltpu
from jax.sharding import PartitionSpec as P

HEADS = 8
HEAD_DIM = 128
TOPK = 128
BPS = 4
NEG = -1000000000.0
MESH = pl.DeviceIdType.MESH
EPS = 1e-05
UNIT = 256
SKEW = 2


def flip(value, bit):
    return value + bit - 2 * bit * ((value // bit) % 2)


HALF = HEADS // 2
LOG2E = math.log2(math.e)
SCALE = HEAD_DIM ** (-0.5)
NT = (((1,), (1,)), ((), ()))
TN = (((0,), (0,)), ((), ()))
NN = (((1,), (0,)), ((), ()))


def matmul(left, right, dims):
    return lax.dot_general(left, right, dims, preferred_element_type=jnp.float32)


def seats():
    seq, doc = lax.axis_index("seq"), lax.axis_index("doc")
    core, chip = seq % 2, (seq // 2) % 2
    mate = (flip(seq, 1), doc)
    across = (flip(seq, 2), doc)
    diagonal = (flip(flip(seq, 2), 1), doc)
    return core, chip, mate, across, diagonal


def meet(peers):
    barrier = pltpu.get_barrier_semaphore()
    for peer in peers:
        pl.semaphore_signal(barrier, inc=1, device_id=peer, device_id_type=MESH)
    pl.semaphore_wait(barrier, len(peers))


def head_lanes(core, head):
    return pl.ds(pl.multiple_of((core * HALF + head) * HEAD_DIM, HEAD_DIM), HEAD_DIM)


def remote(src, dst, send, recv, peer):
    return pltpu.make_async_remote_copy(
        src_ref=src, dst_ref=dst, send_sem=send, recv_sem=recv, device_id=peer, device_id_type=MESH
    )


def share_heads(sources, boxes, core, mate, local_sem, send_sem, recv_sem):
    copies = []
    for i, (source, box) in enumerate(zip(sources, boxes)):
        for head in range(HALF):
            copies.append(
                remote(
                    source.at[:, head_lanes(1 - core, head)],
                    box.at[core, head],
                    send_sem.at[i, head],
                    recv_sem.at[i, head],
                    mate,
                )
            )
            copies[-1].start()
    for i, (source, box) in enumerate(zip(sources, boxes)):
        for head in range(HALF):
            copies.append(
                pltpu.make_async_copy(
                    source.at[:, head_lanes(core, head)], box.at[core, head], local_sem.at[i, head]
                )
            )
            copies[-1].start()
    return copies


def masked(scores, first_key, limit, diagonal):
    key = lax.broadcasted_iota(jnp.int32, scores.shape, 0)
    ok = key + first_key < limit
    if diagonal:
        ok = ok & (key <= lax.broadcasted_iota(jnp.int32, scores.shape, 1))
    return jnp.where(ok, scores, NEG)


def soften(parts):
    top = functools.reduce(
        jnp.maximum, [jnp.max(scores, axis=0, keepdims=True) for scores, _ in parts]
    )
    total, mixed = 0.0, 0.0
    for scores, values in parts:
        exponent = jnp.exp2(scores - top)
        total = total + jnp.sum(exponent, axis=0, keepdims=True)
        mixed = mixed + matmul(values, exponent.astype(jnp.bfloat16), TN)
    return mixed / total, top + jnp.log(total) * LOG2E


def forward_kernel(
    limit_ref, q, k, v, mk, mv,
    attended, qb, kb, vb, qx, mkb, mvb, ob, lse,
    mixed_own, mixed_out, mixed_in, lse_out, lse_in,
    local_sem, mate_send, mate_recv, far_send, far_recv, back_send, back_recv, end_sem,
):
    core, chip, mate, across, diagonal = seats()
    block = q.shape[0]
    limit = limit_ref[0]
    meet((mate, across, diagonal))

    def query_copy(head, own):
        return remote(
            q.at[:, head_lanes(core if own else 1 - core, head)],
            qx.at[core, head],
            far_send.at[0 if own else 1, head],
            far_recv.at[core, head],
            across if own else diagonal,
        )

    def arrived_query(far, head):
        return remote(
            q.at[:, head_lanes(core, head)], qx.at[far, head], far_send.at[0, head], far_recv.at[far, head], across
        )

    @pl.when(chip == 1)
    def _():
        for head in range(HALF):
            query_copy(head, True).start()
            query_copy(head, False).start()

    copies = share_heads((q, k, v, mk, mv), (qb, kb, vb, mkb, mvb), core, mate, local_sem, mate_send, mate_recv)
    for copy in copies:
        copy.wait()

    def own_part(blk, head):
        query = qb[blk, head]
        parts = []
        for kblk in range(blk + 1):
            scores = matmul(kb[kblk, head], query, NT) * (SCALE * LOG2E)
            scores = masked(scores, (2 * chip + kblk) * block, limit, kblk == blk)
            parts.append((scores, vb[kblk, head]))
        parts.append((matmul(mkb[blk, head], query, NT) * (SCALE * LOG2E), mvb[blk, head]))
        return soften(parts)

    for blk in range(2):
        def own_head(head, carry):
            mixed, level = own_part(blk, head)
            mixed_own[blk, head] = mixed
            lse[blk, head] = level
            return carry
        lax.fori_loop(0, HALF, own_head, 0)

    def back_copy(blk, head):
        return (
            remote(mixed_out.at[blk, head], mixed_in.at[blk, head], back_send.at[0, blk, head], back_recv.at[0, blk, head], across),
            remote(lse_out.at[blk, head], lse_in.at[blk, head], back_send.at[1, blk, head], back_recv.at[1, blk, head], across),
        )

    @pl.when(chip == 0)
    def _():
        def cross(i, carry):
            head, blk = i // 2, i % 2
            arrived_query(blk, head).wait_recv()
            query = qx[blk, head]
            parts = []
            for kblk in range(2):
                scores = matmul(kb[kblk, head], query, NT) * (SCALE * LOG2E)
                parts.append((masked(scores, kblk * block, limit, False), vb[kblk, head]))
            mixed, level = soften(parts)
            mixed_out[blk, head] = mixed.astype(jnp.bfloat16)
            lse_out[blk, head] = level
            for copy in back_copy(blk, head):
                copy.start()
            return carry
        lax.fori_loop(0, 2 * HALF, cross, 0)

        def finish(i, carry):
            head, blk = i // 2, i % 2
            ob[blk, head] = mixed_own[blk, head].T.astype(jnp.bfloat16)
            return carry
        lax.fori_loop(0, 2 * HALF, finish, 0)

    @pl.when(chip == 1)
    def _():
        def merge(i, carry):
            head, blk = i // 2, i % 2
            for copy in back_copy(blk, head):
                copy.wait_recv()
            near, far = lse[blk, head], lse_in[blk, head]
            top = jnp.maximum(near, far)
            near, far = jnp.exp2(near - top), jnp.exp2(far - top)
            total = near + far
            mixed = (mixed_own[blk, head] * near + mixed_in[blk, head].astype(jnp.float32) * far) / total
            ob[blk, head] = mixed.T.astype(jnp.bfloat16)
            lse[blk, head] = top + jnp.log(total) * LOG2E
            return carry
        lax.fori_loop(0, 2 * HALF, merge, 0)

    ends = []
    for head in range(HALF):
        ends.append(
            remote(ob.at[1 - core, head], attended.at[:, head_lanes(core, head)], end_sem.at[0, head], end_sem.at[1, head], mate)
        )
        ends.append(
            pltpu.make_async_copy(ob.at[core, head], attended.at[:, head_lanes(core, head)], end_sem.at[2, head])
        )
    for copy in ends:
        copy.start()
    for copy in ends:
        copy.wait()

    @pl.when(chip == 0)
    def _():
        for head in range(HALF):
            for blk in range(2):
                for copy in back_copy(blk, head):
                    copy.wait_send()

    @pl.when(chip == 1)
    def _():
        for head in range(HALF):
            query_copy(head, True).wait_send()
            query_copy(head, False).wait_send()


def attend_forward(limit, queries, keys, values, mem_keys, mem_values):
    block, width = queries.shape
    topk = mem_keys.shape[0]
    low, full = jnp.bfloat16, jnp.float32
    box = (2, HALF, block, HEAD_DIM)
    mem_box = (2, HALF, topk, HEAD_DIM)
    flat = (2, HALF, HEAD_DIM, block)
    row = (2, HALF, 1, block)
    dma = pltpu.SemaphoreType.DMA
    hbm, vmem = pl.BlockSpec(memory_space=pl.ANY), pl.BlockSpec(memory_space=pltpu.VMEM)
    struct = jax.ShapeDtypeStruct
    return pl.pallas_call(
        forward_kernel,
        out_shape=(
            struct((block, width), low),
            struct(box, low), struct(box, low), struct(box, low), struct(box, low),
            struct(mem_box, low), struct(mem_box, low), struct(box, low), struct(row, full),
        ),
        in_specs=[pl.BlockSpec(memory_space=pltpu.SMEM)] + [hbm] * 5,
        out_specs=(hbm,) + (vmem,) * 8,
        scratch_shapes=[
            pltpu.VMEM(flat, full), pltpu.VMEM(flat, low), pltpu.VMEM(flat, low),
            pltpu.VMEM(row, full), pltpu.VMEM(row, full),
            dma((5, HALF)), dma((5, HALF)), dma((5, HALF)),
            dma((2, HALF)), dma((2, HALF)), dma((2, 2, HALF)), dma((2, 2, HALF)), dma((3, HALF)),
        ],
        name="attend_forward",
        compiler_params=pltpu.CompilerParams(collective_id=1, has_side_effects=True, vmem_limit_bytes=56 * 2**20),
    )(limit, queries, keys, values, mem_keys, mem_values)


def backward_kernel(
    limit_ref, grad, qb, kb, vb, qx, mkb, mvb, ob, lse,
    dq, dk, dv, dmk, dmv,
    gb, gx, delta, lse_in, delta_in, dq_own, dq_out, dq_in, dk_sum, dv_sum, dmk_low, dmv_low, dqb, dkb, dvb,
    local_sem, mate_send, mate_recv, far_send, far_recv, row_send, row_recv, back_send, back_recv,
    end_local, end_send, end_recv,
):
    core, chip, mate, across, diagonal = seats()
    block = grad.shape[0]
    limit = limit_ref[0]
    meet((mate, across, diagonal))

    def grad_copy(head, own):
        return remote(
            grad.at[:, head_lanes(core if own else 1 - core, head)],
            gx.at[core, head],
            far_send.at[0 if own else 1, head],
            far_recv.at[core, head],
            across if own else diagonal,
        )

    def arrived_grad(far, head):
        return remote(
            grad.at[:, head_lanes(core, head)], gx.at[far, head], far_send.at[0, head], far_recv.at[far, head], across
        )

    def row_copies():
        return (
            remote(lse, lse_in, row_send.at[0], row_recv.at[0], across),
            remote(delta, delta_in, row_send.at[1], row_recv.at[1], across),
        )

    @pl.when(chip == 1)
    def _():
        for head in range(HALF):
            grad_copy(head, True).start()
            grad_copy(head, False).start()

    copies = share_heads((grad,), (gb,), core, mate, local_sem, mate_send, mate_recv)
    for copy in copies:
        copy.wait()

    def rows(i, carry):
        head, blk = i // 2, i % 2
        product = gb[blk, head].astype(jnp.float32) * ob[blk, head].astype(jnp.float32)
        delta[blk, head] = jnp.sum(product.T, axis=0, keepdims=True)
        return carry

    lax.fori_loop(0, 2 * HALF, rows, 0)

    @pl.when(chip == 1)
    def _():
        for copy in row_copies():
            copy.start()

    def pull(key_rows, value_rows, query, grad_rows, level, inner, where):
        scores = matmul(key_rows, query, NT) * (SCALE * LOG2E)
        if where is not None:
            scores = masked(scores, where[0], limit, where[1])
        weights = jnp.exp2(scores - level)
        grad_weights = matmul(value_rows, grad_rows, NT)
        grad_scores = (weights * (grad_weights - inner)).astype(jnp.bfloat16)
        return (
            matmul(grad_scores, query, NN),
            matmul(weights.astype(jnp.bfloat16), grad_rows, NN),
            matmul(key_rows, grad_scores, TN),
        )

    for blk in range(2):
        def own_head(head, carry):
            query, grad_rows = qb[blk, head], gb[blk, head]
            level, inner = lse[blk, head], delta[blk, head]
            total = 0.0
            for kblk in range(blk + 1):
                gk, gv, gq = pull(
                    kb[kblk, head], vb[kblk, head], query, grad_rows, level, inner,
                    ((2 * chip + kblk) * block, kblk == blk),
                )
                if kblk == blk:
                    dk_sum[kblk, head], dv_sum[kblk, head] = gk, gv
                else:
                    dk_sum[kblk, head] += gk
                    dv_sum[kblk, head] += gv
                total = total + gq
            gk, gv, gq = pull(mkb[blk, head], mvb[blk, head], query, grad_rows, level, inner, None)
            dmk_low[blk, head] = (gk * SCALE).astype(jnp.bfloat16)
            dmv_low[blk, head] = gv.astype(jnp.bfloat16)
            dq_own[blk, head] = total + gq
            return carry
        lax.fori_loop(0, HALF, own_head, 0)

    def back_copy(blk, head):
        return remote(dq_out.at[blk, head], dq_in.at[blk, head], back_send.at[blk, head], back_recv.at[blk, head], across)

    @pl.when(chip == 0)
    def _():
        for copy in row_copies():
            copy.wait_recv()

        def cross(i, carry):
            head, blk = i // 2, i % 2
            arrived_grad(blk, head).wait_recv()
            query, grad_rows = qx[blk, head], gx[blk, head]
            level, inner = lse_in[blk, head], delta_in[blk, head]
            total = 0.0
            for kblk in range(2):
                gk, gv, gq = pull(
                    kb[kblk, head], vb[kblk, head], query, grad_rows, level, inner, (kblk * block, False)
                )
                dk_sum[kblk, head] += gk
                dv_sum[kblk, head] += gv
                total = total + gq
            dq_out[blk, head] = total.astype(jnp.bfloat16)
            back_copy(blk, head).start()
            return carry
        lax.fori_loop(0, 2 * HALF, cross, 0)

    def finish(i, carry):
        head, blk = i // 2, i % 2
        dqb[blk, head] = (dq_own[blk, head].T * SCALE).astype(jnp.bfloat16)
        dkb[blk, head] = (dk_sum[blk, head] * SCALE).astype(jnp.bfloat16)
        dvb[blk, head] = dv_sum[blk, head].astype(jnp.bfloat16)
        return carry

    @pl.when(chip == 1)
    def _():
        def merge(i, carry):
            head, blk = i // 2, i % 2
            back_copy(blk, head).wait_recv()
            dq_own[blk, head] += dq_in[blk, head].astype(jnp.float32)
            return finish(i, carry)
        lax.fori_loop(0, 2 * HALF, merge, 0)

    @pl.when(chip == 0)
    def _():
        lax.fori_loop(0, 2 * HALF, finish, 0)

    ends = []
    for i, (box, out) in enumerate(((dqb, dq), (dkb, dk), (dvb, dv), (dmk_low, dmk), (dmv_low, dmv))):
        for head in range(HALF):
            lanes = head_lanes(core, head)
            ends.append(remote(box.at[1 - core, head], out.at[:, lanes], end_send.at[i, head], end_recv.at[i, head], mate))
            ends.append(pltpu.make_async_copy(box.at[core, head], out.at[:, lanes], end_local.at[i, head]))
    for copy in ends:
        copy.start()
    for copy in ends:
        copy.wait()

    @pl.when(chip == 0)
    def _():
        for head in range(HALF):
            for blk in range(2):
                back_copy(blk, head).wait_send()

    @pl.when(chip == 1)
    def _():
        for copy in row_copies():
            copy.wait_send()
        for head in range(HALF):
            grad_copy(head, True).wait_send()
            grad_copy(head, False).wait_send()


def attend_backward(limit, grad, saved):
    block, width = grad.shape
    topk = saved[4].shape[2]
    low, full = jnp.bfloat16, jnp.float32
    box = (2, HALF, block, HEAD_DIM)
    mem_box = (2, HALF, topk, HEAD_DIM)
    flat = (2, HALF, HEAD_DIM, block)
    row = (2, HALF, 1, block)
    dma = pltpu.SemaphoreType.DMA
    hbm, vmem = pl.BlockSpec(memory_space=pl.ANY), pl.BlockSpec(memory_space=pltpu.VMEM)
    struct = jax.ShapeDtypeStruct
    return pl.pallas_call(
        backward_kernel,
        out_shape=(struct((block, width), low),) * 3 + (struct((topk, width), low),) * 2,
        in_specs=[pl.BlockSpec(memory_space=pltpu.SMEM), hbm] + [vmem] * 8,
        out_specs=(hbm,) * 5,
        scratch_shapes=[
            pltpu.VMEM(box, low), pltpu.VMEM(box, low),
            pltpu.VMEM(row, full), pltpu.VMEM(row, full), pltpu.VMEM(row, full),
            pltpu.VMEM(flat, full), pltpu.VMEM(flat, low), pltpu.VMEM(flat, low),
            pltpu.VMEM(box, full), pltpu.VMEM(box, full),
            pltpu.VMEM(mem_box, low), pltpu.VMEM(mem_box, low),
            pltpu.VMEM(box, low), pltpu.VMEM(box, low), pltpu.VMEM(box, low),
            dma((1, HALF)), dma((1, HALF)), dma((1, HALF)),
            dma((2, HALF)), dma((2, HALF)), dma((2,)), dma((2,)),
            dma((2, HALF)), dma((2, HALF)),
            dma((5, HALF)), dma((5, HALF)), dma((5, HALF)),
        ],
        name="attend_backward",
        compiler_params=pltpu.CompilerParams(collective_id=2, has_side_effects=True, vmem_limit_bytes=56 * 2**20),
    )(limit, grad, *saved)


SUM_ORDERS = (("x", "y", "low", "high"), ("y", "x", "low", "high"), ("low", "high", "y", "x"))
EARLY = (8, 18, 4)
UNITS = (12, 26, 4)
ROWS = (32, 32, 88)
SLOTS = (2, 4, 2)
FIRST_LATE = 18
STEPS = 26


def when(condition, body):
    if isinstance(condition, bool):
        if condition:
            body()
    else:
        pl.when(condition)(body)


def turn(cls, at):
    if cls == 0:
        early = (at % 2 == 0) & (at >= 0) & (at < 16)
        late = (at % 2 == 0) & (at >= FIRST_LATE) & (at < STEPS)
        return early, at // 2, late, at // 2 - 1
    if cls == 1:
        return (at >= 0) & (at < FIRST_LATE), at, (at >= FIRST_LATE) & (at < STEPS), at
    return (at % 4 == 0) & (at >= 0) & (at < 16), at // 4, None, None


class Sums:
    def __init__(self, gate, up, out, down, own, stages, sums, local_sem, send_sem, recv_sem, peers):
        self.grads = {"gate": gate, "up": up, "out": out, "down": down}
        self.own, self.stages, self.sums = own, stages, sums
        self.local_sem, self.send_sem, self.recv_sem = local_sem, send_sem, recv_sem
        self.peers = peers
        seq, doc = lax.axis_index("seq"), lax.axis_index("doc")
        self.bits = {
            "core": seq % 2,
            "x": (seq // 2) % 2,
            "y": (seq // 4) % 2,
            "low": doc % 2,
            "high": (doc // 2) % 2,
        }
        self.ranges = (
            ((0, 8, "gate", 0),),
            ((0, 3, "gate", 8 * UNIT), (3, 14, "up", 0), (14, 18, "out", 0)),
            ((0, 4, "down", 0),),
        )

    def part(self, name, column, core):
        return self.grads[name].at[:, :, core, :, :, :, pl.ds(pl.multiple_of(column, UNIT), UNIT)]

    def core_copy(self, cls, unit, source):
        return remote(
            source,
            self.stages[cls][0].at[unit],
            self.send_sem[cls].at[0, unit],
            self.recv_sem[cls].at[0, unit],
            self.peers["core"],
        )

    def own_copy(self, cls, unit, name, column):
        slot = unit % SLOTS[cls]
        return pltpu.make_async_copy(
            self.part(name, column, self.bits["core"]), self.own[cls].at[slot], self.local_sem[cls].at[slot]
        )

    def load_own(self, cls, unit):
        for first, end, name, column in self.ranges[cls]:
            when(
                (unit >= first) & (unit < end),
                lambda: self.own_copy(cls, unit, name, (unit - first) * UNIT + column).start(),
            )

    def begin(self):
        for step in range(FIRST_LATE):
            for cls in range(3):
                due, unit, _, _ = turn(cls, step)
                if due:
                    for first, end, name, column in self.ranges[cls]:
                        if first <= unit < end:
                            source = self.part(name, (unit - first) * UNIT + column, 1 - self.bits["core"])
                            self.core_copy(cls, unit, source).start()
                    if unit < SLOTS[cls]:
                        self.load_own(cls, unit)

    def half(self, cls, level, unit, mine):
        order = SUM_ORDERS[cls]
        name = order[level]
        left = [axis for axis in ("y", "x", "high", "low") if axis not in order[:level]]
        side = self.bits[name] if mine else 1 - self.bits[name]
        return self.stages[cls][level], (unit,) + (slice(None),) * left.index(name) + (side,)

    def copy(self, cls, level, unit):
        ref, index = self.half(cls, level - 1, unit, False)
        return remote(
            ref.at[index],
            self.stages[cls][level].at[unit],
            self.send_sem[cls].at[level, unit],
            self.recv_sem[cls].at[level, unit],
            self.peers[SUM_ORDERS[cls][level - 1]],
        )

    def arrive(self, cls, level, unit, fresh=None):
        ref = self.stages[cls][level]
        if level == 0:
            _, _, name, column = self.ranges[cls][0]
            self.core_copy(cls, unit, self.part(name, column, 1 - self.bits["core"])).wait_recv()
            if fresh is None:
                self.own_copy(cls, unit, name, column).wait()
                ref[unit] = ref[unit] + self.own[cls][unit % SLOTS[cls]]
                when(unit + SLOTS[cls] < EARLY[cls], lambda: self.load_own(cls, unit + SLOTS[cls]))
            else:
                ref[unit] = ref[unit] + fresh()
        else:
            self.copy(cls, level, unit).wait_recv()
            kept, index = self.half(cls, level - 1, unit, True)
            if level < 4:
                ref[unit] = ref[unit] + kept[index]
            else:
                self.sums[cls][unit] = ref[unit].astype(jnp.float32) + kept[index].astype(jnp.float32)
        if level < 4:
            self.copy(cls, level + 1, unit).start()

    def tick(self, step, fresh=None):
        for level in range(4, -1, -1):
            for cls in range(3):
                early, unit, late, late_unit = turn(cls, step - level * SKEW)
                if level > 0 and late is not None:
                    when(early | late, lambda: self.arrive(cls, level, jnp.where(late, late_unit, unit)))
                elif level > 0 or fresh is None:
                    when(early, lambda: self.arrive(cls, level, unit))
                elif late is not None:
                    when(late, lambda: self.arrive(cls, level, late_unit, lambda: fresh(cls, late_unit)))

    def drain(self):
        for cls in range(3):
            _, _, name, column = self.ranges[cls][0]

            def one(unit, carry):
                self.core_copy(cls, unit, self.part(name, column, 1 - self.bits["core"])).wait_send()
                for level in range(1, 5):
                    self.copy(cls, level, unit).wait_send()
                return carry

            lax.fori_loop(0, UNITS[cls], one, 0)


def back_kernel(
    limit_ref, grad, qb_in, kb_in, vb_in, qx_in, mkb_in, mvb_in, ob_in, lse_in0,
    gate, up, out, down, w_query, w_key, w_value, normed_t, tokens, grad_middle, gain, ffn_row, placed_t, picked_t,
    grad_tokens, gate_rows, up_rows, query_rows, key_rows, value_rows, out_rows, down_rows, gains_out, grad_mk, grad_mv,
    gb, gx, lse, delta, lse_in, delta_in, dq_cross, dqkv, dqkv_mate, spots, mem_out, mem_in, gain_buf,
    own_a, own_b, own_c, *rest,
):
    stages = [rest[5 * c : 5 * c + 5] for c in range(3)]
    sums = rest[15:18]
    rest = rest[18:]
    local_sems, send_sems, recv_sems, rest = rest[0:3], rest[3:6], rest[6:9], rest[9:]
    (
        in_sem, gb_local, gb_send, gb_recv, spot_sem, far_send, far_recv, row_send, row_recv, back_send, back_recv,
        mate_send, mate_recv, mem_local, mem_send, mem_recv, gain_send, gain_recv, load_sem, weight_sem, done_sem, table_sem,
    ) = rest
    core, chip, mate, across, diagonal = seats()
    seq, doc = lax.axis_index("seq"), lax.axis_index("doc")
    seq_count = mem_in.shape[0]
    block = grad.shape[0]
    limit = limit_ref[0]
    peers = {
        "core": mate,
        "x": across,
        "y": (flip(seq, 4), doc),
        "low": (seq, flip(doc, 1)),
        "high": (seq, flip(doc, 2)),
    }
    others = [(lax.rem(seq + away, seq_count), doc) for away in range(1, seq_count)]
    meet(others + [peers["low"], peers["high"]])
    engine = Sums(
        gate, up, out, down, (own_a, own_b, own_c), stages, sums, local_sems, send_sems, recv_sems, peers
    )

    def grad_copy(head, own):
        return remote(
            grad.at[:, head_lanes(core if own else 1 - core, head)],
            gx.at[core, head],
            far_send.at[0 if own else 1, head],
            far_recv.at[core, head],
            across if own else diagonal,
        )

    def arrived_grad(far, head):
        return remote(
            grad.at[:, head_lanes(core, head)], gx.at[far, head], far_send.at[0, head], far_recv.at[far, head], across
        )

    def row_copies():
        return (
            remote(lse, lse_in, row_send.at[0], row_recv.at[0], across),
            remote(delta, delta_in, row_send.at[1], row_recv.at[1], across),
        )

    def back_copy(blk, head):
        return remote(dq_cross.at[blk, head], dq_cross.at[blk, head], back_send.at[blk, head], back_recv.at[blk, head], across)

    def mate_copy(i, head):
        lanes = head_lanes(core, head)
        return remote(dqkv_mate.at[i, head], dqkv.at[i, :, lanes], mate_send.at[i, head], mate_recv.at[i, head], mate)

    def mate_arrival(i, head):
        lanes = head_lanes(1 - core, head)
        return remote(dqkv_mate.at[i, head], dqkv.at[i, :, lanes], mate_send.at[i, head], mate_recv.at[i, head], mate)

    def mem_copy(away):
        peer = lax.rem(seq + away, seq_count)
        return remote(mem_out.at[peer], mem_in.at[seq], mem_send.at[away - 1], mem_recv.at[away - 1], (peer, doc))

    @pl.when(chip == 1)
    def _():
        for head in range(HALF):
            grad_copy(head, True).start()
            grad_copy(head, False).start()

    def attention(qb, kb, vb, qx, mkb, mvb, ob, dq_own, dk_sum, dv_sum, dm):
        inputs = [
            pltpu.make_async_copy(src, dst, in_sem.at[i])
            for i, (src, dst) in enumerate(
                ((qb_in, qb), (kb_in, kb), (vb_in, vb), (mkb_in, mkb), (mvb_in, mvb), (ob_in, ob), (lse_in0, lse), (qx_in, qx))
            )
        ]
        spot_copies = [
            remote(placed_t, spots.at[core], spot_sem.at[0], spot_sem.at[1], mate),
            pltpu.make_async_copy(placed_t, spots.at[core], spot_sem.at[2]),
        ]
        copies = share_heads((grad,), (gb,), core, mate, gb_local, gb_send, gb_recv)
        for copy in inputs + spot_copies:
            copy.start()
        engine.begin()
        for copy in copies + inputs + spot_copies:
            copy.wait()

        def rows(i, carry):
            head, blk = i // 2, i % 2
            product = gb[blk, head].astype(jnp.float32) * ob[blk, head].astype(jnp.float32)
            delta[blk, head] = jnp.sum(product.T, axis=0, keepdims=True)
            return carry

        lax.fori_loop(0, 2 * HALF, rows, 0)

        @pl.when(chip == 1)
        def _():
            for copy in row_copies():
                copy.start()

        def pull(key_rows, value_rows, query, grad_rows, level, inner, where):
            scores = matmul(key_rows, query, NT) * (SCALE * LOG2E)
            if where is not None:
                scores = masked(scores, where[0], limit, where[1])
            weights = jnp.exp2(scores - level)
            grad_weights = matmul(value_rows, grad_rows, NT)
            grad_scores = (weights * (grad_weights - inner)).astype(jnp.bfloat16)
            return (
                matmul(grad_scores, query, NN),
                matmul(weights.astype(jnp.bfloat16), grad_rows, NN),
                matmul(key_rows, grad_scores, TN),
            )

        def own_head(head, carry):
            lanes = pl.ds(pl.multiple_of(head * HEAD_DIM, HEAD_DIM), HEAD_DIM)
            for blk in range(2):
                query, grad_rows = qb[blk, head], gb[blk, head]
                level, inner = lse[blk, head], delta[blk, head]
                total = 0.0
                for kblk in range(blk + 1):
                    gk, gv, gq = pull(
                        kb[kblk, head], vb[kblk, head], query, grad_rows, level, inner,
                        ((2 * chip + kblk) * block, kblk == blk),
                    )
                    if kblk == blk:
                        dk_sum[kblk, head], dv_sum[kblk, head] = gk, gv
                    else:
                        dk_sum[kblk, head] += gk
                        dv_sum[kblk, head] += gv
                    total = total + gq
                gk, gv, gq = pull(mkb[blk, head], mvb[blk, head], query, grad_rows, level, inner, None)
                dm[blk, 0, :, lanes] = (gk * SCALE).astype(jnp.bfloat16)
                dm[blk, 1, :, lanes] = gv.astype(jnp.bfloat16)
                dq_own[blk, head] = total + gq
            engine.tick(head)
            return carry

        lax.fori_loop(0, HALF, own_head, 0)

        for blk in range(2):
            for kind in range(2):
                rows_out = matmul(spots[blk], dm[blk, kind], NN).astype(jnp.bfloat16)
                mem_out[:, blk, kind] = rows_out.reshape(mem_out.shape[0], mem_out.shape[3], mem_out.shape[4])
        for away in range(1, seq_count):
            mem_copy(away).start()
        pltpu.make_async_copy(mem_out.at[seq], mem_in.at[seq], mem_local.at[0]).start()

        @pl.when(chip == 0)
        def _():
            for copy in row_copies():
                copy.wait_recv()

            def cross(i, carry):
                head, blk = i // 2, i % 2
                arrived_grad(blk, head).wait_recv()
                query, grad_rows = qx[blk, head], gx[blk, head]
                level, inner = lse_in[blk, head], delta_in[blk, head]
                total = 0.0
                for kblk in range(2):
                    gk, gv, gq = pull(
                        kb[kblk, head], vb[kblk, head], query, grad_rows, level, inner, (kblk * block, False)
                    )
                    dk_sum[kblk, head] += gk
                    dv_sum[kblk, head] += gv
                    total = total + gq
                dq_cross[blk, head] = total.astype(jnp.bfloat16)
                back_copy(blk, head).start()
                engine.tick(HALF + i)
                return carry

            lax.fori_loop(0, 2 * HALF, cross, 0)

        @pl.when(chip == 1)
        def _():
            def merge(i, carry):
                head, blk = i // 2, i % 2
                engine.tick(HALF + i)
                back_copy(blk, head).wait_recv()
                dq_own[blk, head] += dq_cross[blk, head].astype(jnp.float32)
                return carry

            lax.fori_loop(0, 2 * HALF, merge, 0)

        def results(blk, head):
            return (
                (dq_own[blk, head].T * SCALE).astype(jnp.bfloat16),
                (dk_sum[blk, head] * SCALE).astype(jnp.bfloat16),
                dv_sum[blk, head].astype(jnp.bfloat16),
            )

        def for_mate(head, carry):
            for i, value in enumerate(results(1 - core, head)):
                dqkv_mate[i, head] = value
                mate_copy(i, head).start()
            return carry

        def for_own(head, carry):
            for i, value in enumerate(results(core, head)):
                dqkv[i, :, head_lanes(core, head)] = value
            return carry

        lax.fori_loop(0, HALF, for_mate, 0)
        lax.fori_loop(0, HALF, for_own, 0)

    box = (2, HALF, block, HEAD_DIM)
    mem_box = mkb_in.shape
    low, full = jnp.bfloat16, jnp.float32
    pl.run_scoped(
        attention,
        pltpu.VMEM(box, low), pltpu.VMEM(box, low), pltpu.VMEM(box, low), pltpu.VMEM(box, low),
        pltpu.VMEM(mem_box, low), pltpu.VMEM(mem_box, low), pltpu.VMEM(box, low),
        pltpu.VMEM((2, HALF, HEAD_DIM, block), full), pltpu.VMEM(box, full), pltpu.VMEM(box, full),
        pltpu.VMEM((2, 2, mem_box[2], HALF * HEAD_DIM), low),
    )

    def tail(normed, pick, dx, middle, rows, weights, made, table):
        width = dx.shape[1]
        chunk = weights.shape[2]
        loads = [
            pltpu.make_async_copy(normed_t, normed, load_sem.at[0]),
            pltpu.make_async_copy(tokens, rows, load_sem.at[1]),
            pltpu.make_async_copy(grad_middle, middle, load_sem.at[2]),
            pltpu.make_async_copy(picked_t, pick, load_sem.at[3]),
        ]

        def weight_copies(j):
            at = pl.ds(pl.multiple_of(j * chunk, chunk), chunk)
            return [
                pltpu.make_async_copy(w.at[at, :], weights.at[j % 2, i], weight_sem.at[j % 2, i])
                for i, w in enumerate((w_query, w_key, w_value))
            ]

        for copy in loads + weight_copies(0):
            copy.start()
        for i in range(3):
            for head in range(HALF):
                mate_arrival(i, head).wait_recv()
        loads[0].wait()

        def made_copy(cls, unit, w):
            return engine.core_copy(cls, unit, made.at[w, :, :, 1 - core])

        def make(w):
            i = w // 4
            lanes = pl.ds(pl.multiple_of((w % 4) * UNIT, UNIT), UNIT)
            value = matmul(normed[...], dqkv[i, :, lanes], NN).astype(jnp.bfloat16)
            made[w] = value.reshape(made.shape[1:])
            pl.when(w < 4)(lambda: made_copy(0, EARLY[0] + w, w).start())
            pl.when(w >= 4)(lambda: made_copy(1, EARLY[1] + w - 4, w).start())

        def build(j, carry):
            make(2 * j)
            make(2 * j + 1)

            @pl.when(j < 4)
            def _():
                for copy in weight_copies(j):
                    copy.wait()

                @pl.when(j < 3)
                def _():
                    for copy in weight_copies(j + 1):
                        copy.start()

                total = 0.0
                for i in range(3):
                    total = total + matmul(dqkv[i], weights[j % 2, i], NT)
                dx[:, pl.ds(pl.multiple_of(j * chunk, chunk), chunk)] = total

            engine.tick(FIRST_LATE - 6 + j)
            return carry

        lax.fori_loop(0, 6, build, 0)
        for copy in loads[1:]:
            copy.wait()

        part = 64

        def norm_back(i, carry):
            at = pl.ds(pl.multiple_of(i * part, part), part)
            x = rows[at, :].astype(jnp.float32)
            factor = lax.rsqrt(jnp.mean(x * x, axis=-1, keepdims=True) + EPS)
            unit = x * factor
            grad_normed = dx[at, :]
            scaled = gain[...] * grad_normed
            inner = jnp.mean(scaled * unit, axis=-1, keepdims=True)
            rows[at, :] = (middle[at, :] + factor * (scaled - unit * inner)).astype(jnp.bfloat16)
            return carry + jnp.sum(grad_normed * unit, axis=0, keepdims=True)

        gain_row = lax.fori_loop(0, block // part, norm_back, jnp.zeros((1, width), jnp.float32))
        gain_buf[0, 0, 0] = gain_row
        gain_buf[0, 0, 1] = ffn_row[...]
        out_copy = pltpu.make_async_copy(rows, grad_tokens, load_sem.at[1])
        out_copy.start()

        def gain_copy(level):
            name = ("core", "x", "y", "low", "high")[level]
            return remote(
                gain_buf.at[0, level], gain_buf.at[1, level], gain_send.at[level], gain_recv.at[level], peers[name]
            )

        gain_copy(0).start()

        def mem_chunk(m):
            kind, lane = m // 4, pl.ds(pl.multiple_of((m % 4) * UNIT, UNIT), UNIT)
            pieces = []
            for src in range(seq_count // 2):
                for blk in range(2):
                    pieces.append((src, blk))
            half = (m % 4) // 2
            inside = pl.ds(pl.multiple_of((m % 2) * UNIT, UNIT), UNIT)
            values = jnp.concatenate(
                [mem_in[2 * src + half, blk, kind, :, inside] for src, blk in pieces], axis=0
            )
            table[m % 2] = matmul(pick[...], values, NN)
            pl.when(kind == 0)(lambda: pltpu.make_async_copy(table.at[m % 2], grad_mk.at[:, lane], table_sem.at[m % 2]).start())
            pl.when(kind == 1)(lambda: pltpu.make_async_copy(table.at[m % 2], grad_mv.at[:, lane], table_sem.at[m % 2]).start())

        def table_done(m):
            pltpu.make_async_copy(table.at[m % 2], grad_mk.at[:, pl.ds(0, UNIT)], table_sem.at[m % 2]).wait()

        for away in range(1, seq_count):
            source = lax.rem(seq + seq_count - away, seq_count)
            remote(mem_out.at[source], mem_in.at[source], mem_send.at[away - 1], mem_recv.at[away - 1], (source, doc)).wait_recv()
        pltpu.make_async_copy(mem_out.at[seq], mem_in.at[seq], mem_local.at[0]).wait()

        def fresh(cls, unit):
            w = unit - EARLY[0] if cls == 0 else unit - EARLY[1] + 4
            return made[w, :, :, core]

        def rest_of(step, carry):
            m = step - FIRST_LATE

            @pl.when(m < 8)
            def _():
                pl.when(m >= 2)(lambda: table_done(m))
                mem_chunk(m)

            for level in range(5):
                @pl.when(m == 2 * level + 2)
                def _():
                    gain_copy(level).wait_recv()
                    total = gain_buf[0, level] + gain_buf[1, level]
                    if level < 4:
                        gain_buf[0, level + 1] = total
                        gain_copy(level + 1).start()
                    else:
                        gains_out[...] = total

            engine.tick(step, fresh)
            return carry

        lax.fori_loop(FIRST_LATE, STEPS + 4 * SKEW, rest_of, 0)

        outs = []
        homes = [(0, u, gate_rows, u * UNIT) for u in range(8)]
        homes += [(0, 8 + u, query_rows, u * UNIT) for u in range(4)]
        homes += [(1, u, gate_rows, (8 + u) * UNIT) for u in range(3)]
        homes += [(1, 3 + u, up_rows, u * UNIT) for u in range(11)]
        homes += [(1, 14 + u, out_rows, u * UNIT) for u in range(4)]
        homes += [(1, 18 + u, key_rows, u * UNIT) for u in range(4)]
        homes += [(1, 22 + u, value_rows, u * UNIT) for u in range(4)]
        homes += [(2, u, down_rows, u * UNIT) for u in range(4)]
        for i, (cls, unit, ref, column) in enumerate(homes):
            outs.append(pltpu.make_async_copy(sums[cls].at[unit], ref.at[:, pl.ds(column, UNIT)], done_sem.at[i]))
            outs[-1].start()
        engine.drain()
        for level in range(5):
            gain_copy(level).wait_send()
        table_done(0)
        table_done(1)
        for copy in outs + [out_copy]:
            copy.wait()

    width = w_query.shape[0]
    pl.run_scoped(
        tail,
        pltpu.VMEM(normed_t.shape, low), pltpu.VMEM(picked_t.shape, low),
        pltpu.VMEM((block, width), full), pltpu.VMEM((block, width), full), pltpu.VMEM((block, width), low),
        pltpu.VMEM((2, 3, UNIT, width), low), pltpu.VMEM((12, 2, 2, 2, 2, 2, 32, UNIT), low),
        pltpu.VMEM((2, picked_t.shape[0], UNIT), full),
    )

    for away in range(1, seq_count):
        mem_copy(away).wait_send()
    for i in range(3):
        for head in range(HALF):
            mate_copy(i, head).wait_send()

    @pl.when(chip == 0)
    def _():
        for head in range(HALF):
            for blk in range(2):
                back_copy(blk, head).wait_send()

    @pl.when(chip == 1)
    def _():
        for copy in row_copies():
            copy.wait_send()
        for head in range(HALF):
            grad_copy(head, True).wait_send()
            grad_copy(head, False).wait_send()


def go_back(limit, grad, saved, weight_grads, projections, normed_t, tokens, grad_middle, gain, ffn_row, placed_t, picked_t):
    block, width = grad.shape
    low, full = jnp.bfloat16, jnp.float32
    box = (2, HALF, block, HEAD_DIM)
    row = (2, HALF, 1, block)
    seq_count = lax.axis_size("seq")
    capacity = 2 * TOPK // seq_count
    dma = pltpu.SemaphoreType.DMA
    hbm, vmem = pl.BlockSpec(memory_space=pl.ANY), pl.BlockSpec(memory_space=pltpu.VMEM)
    struct = jax.ShapeDtypeStruct

    def wide(g):
        return g.reshape(2, 2, 2, 2, 2, g.shape[0] // 32, g.shape[1])

    mem = (seq_count, 2, 2, capacity, HALF * HEAD_DIM)
    scratch = [
        pltpu.VMEM(box, low), pltpu.VMEM(box, low),
        pltpu.VMEM(row, full), pltpu.VMEM(row, full), pltpu.VMEM(row, full), pltpu.VMEM(row, full),
        pltpu.VMEM((2, HALF, HEAD_DIM, block), low),
        pltpu.VMEM((3, block, width), low), pltpu.VMEM((3, HALF, block, HEAD_DIM), low),
        pltpu.VMEM((2,) + placed_t.shape, low), pltpu.VMEM(mem, low), pltpu.VMEM(mem, low),
        pltpu.VMEM((2, 5, 2, 1, width), full),
    ]
    scratch += [pltpu.VMEM((SLOTS[c], 2, 2, 2, 2, ROWS[c], UNIT), low) for c in range(3)]
    for c in range(3):
        scratch += [pltpu.VMEM((UNITS[c],) + (2,) * k + (ROWS[c], UNIT), low) for k in (4, 3, 2, 1, 0)]
    scratch += [pltpu.VMEM((UNITS[c], ROWS[c], UNIT), full) for c in range(3)]
    scratch += [dma((SLOTS[c],)) for c in range(3)]
    scratch += [dma((5, UNITS[c])) for c in range(3)] * 2
    scratch += [
        dma((8,)), dma((1, HALF)), dma((1, HALF)), dma((1, HALF)), dma((3,)),
        dma((2, HALF)), dma((2, HALF)), dma((2,)), dma((2,)), dma((2, HALF)), dma((2, HALF)),
        dma((3, HALF)), dma((3, HALF)), dma((1,)), dma((seq_count - 1,)), dma((seq_count - 1,)),
        dma((5,)), dma((5,)), dma((4,)), dma((2, 3)), dma((sum(UNITS),)), dma((2,)),
    ]
    gate, up, out, down = weight_grads
    rows = struct((32, width), full)
    mem_rows = picked_t.shape[0]
    return pl.pallas_call(
        back_kernel,
        out_shape=(
            struct((block, width), low),
            struct((32, gate.shape[1]), full), struct((32, up.shape[1]), full),
            rows, rows, rows, rows,
            struct((88, width), full), struct((2, 1, width), full),
            struct((mem_rows, width), full), struct((mem_rows, width), full),
        ),
        in_specs=[pl.BlockSpec(memory_space=pltpu.SMEM)] + [hbm] * 19 + [vmem] * 2 + [hbm] * 2,
        out_specs=(hbm,) * 8 + (vmem,) + (hbm,) * 2,
        scratch_shapes=scratch,
        name="go_back",
        compiler_params=pltpu.CompilerParams(collective_id=3, has_side_effects=True, vmem_limit_bytes=60 * 2**20),
    )(
        limit, grad, *saved, wide(gate), wide(up), wide(out), wide(down), *projections,
        normed_t, tokens, grad_middle, gain, ffn_row, placed_t, picked_t,
    )


def rms_factor(values):
    return lax.rsqrt(jnp.mean(values * values, axis=-1, keepdims=True) + EPS)


def dot32(left, right):
    return jnp.dot(left, right, preferred_element_type=jnp.float32)


def fitting():
    return (lax.axis_size("seq"), lax.axis_size("doc")) == (8, 4)


def exchange(rows, owner_count, capacity):
    parts, _, width = rows.shape
    shaped = rows.reshape(parts, owner_count, capacity, width)
    moved = lax.all_to_all(shaped, "seq", split_axis=1, concat_axis=1, tiled=True)
    return moved.reshape(parts, owner_count * capacity, width)


def on_device(
    tokens,
    cotangent,
    attn_gain,
    w_query,
    w_key,
    w_value,
    w_out,
    ffn_gain,
    w_gate,
    w_up,
    w_down,
    mem_keys,
    mem_values,
    seg_len,
    mem_idx,
):
    low = jnp.bfloat16
    stream_count, block_len, model_width = tokens.shape
    mem_rows = mem_keys.shape[1]
    seq_count = lax.axis_size("seq")
    segment = lax.axis_index("seq") // BPS
    capacity = 2 * TOPK // seq_count
    slot_count = seq_count * capacity
    limit = lax.dynamic_index_in_dim(seg_len, segment, 1, keepdims=False)

    chosen = mem_idx[0, 0]
    owner = chosen // mem_rows
    order = jnp.arange(TOPK)
    same_before = (owner[:, None] == owner[None, :]) & (order[None, :] < order[:, None])
    slot = owner * capacity + jnp.sum(same_before.astype(jnp.int32), axis=1)
    placed = slot[:, None] == jnp.arange(slot_count)[None, :]
    request = jnp.sum(jnp.where(placed, (chosen % mem_rows)[:, None] + 1, 0), axis=0) - 1
    requested = lax.all_to_all(
        request.reshape(seq_count, capacity), "seq", split_axis=0, concat_axis=0, tiled=True
    ).reshape(slot_count)
    picked = (requested[:, None] == jnp.arange(mem_rows)[None, :]).astype(low)
    placed = placed.astype(low)
    sent = jnp.stack((dot32(picked, mem_keys[0]).astype(low), dot32(picked, mem_values[0]).astype(low)))
    arrived = exchange(sent, seq_count, capacity)
    mem_key_rows = dot32(placed, arrived[0]).astype(low)
    mem_value_rows = dot32(placed, arrived[1]).astype(low)

    tokens_f = tokens[0].astype(jnp.float32)
    gain_one = attn_gain.astype(jnp.float32)
    gain_two = ffn_gain.astype(jnp.float32)
    factor_one = rms_factor(tokens_f)
    unit_one = tokens_f * factor_one
    normed_one = (unit_one * gain_one).astype(low)
    queries = dot32(normed_one, w_query).astype(low)
    keys = dot32(normed_one, w_key).astype(low)
    values = dot32(normed_one, w_value).astype(low)
    attended, *saved = attend_forward(limit, queries, keys, values, mem_key_rows, mem_value_rows)
    middle = tokens_f + dot32(attended, w_out)
    factor_two = rms_factor(middle)
    unit_two = middle * factor_two
    normed_two = (unit_two * gain_two).astype(low)
    gate = dot32(normed_two, w_gate)
    upper = dot32(normed_two, w_up)
    sigma = jax.nn.sigmoid(gate)
    hidden = (gate * sigma * upper).astype(low)
    layer_out = (middle + dot32(hidden, w_down)).astype(low)

    grad_y_low = cotangent[0]
    grad_y = grad_y_low.astype(jnp.float32)
    grad_down = dot32(hidden.T, grad_y_low)
    grad_hidden = dot32(grad_y_low, w_down.T)
    grad_gate_act = (grad_hidden * upper * sigma * (1.0 + gate * (1.0 - sigma))).astype(low)
    grad_up_act = (grad_hidden * gate * sigma).astype(low)
    grad_gate = dot32(normed_two.T, grad_gate_act)
    grad_up = dot32(normed_two.T, grad_up_act)
    grad_normed_two = dot32(grad_gate_act, w_gate.T) + dot32(grad_up_act, w_up.T)
    grad_ffn_gain = jnp.sum(grad_normed_two * unit_two, axis=0)
    scaled_two = gain_two * grad_normed_two
    grad_middle = grad_y + factor_two * (
        scaled_two - unit_two * jnp.mean(scaled_two * unit_two, axis=-1, keepdims=True)
    )
    grad_branch = grad_middle.astype(low)
    grad_out = dot32(attended.T, grad_branch)
    grad_attended = dot32(grad_branch, w_out.T).astype(low)
    if fitting():
        grad_tokens, gate_rows, up_rows, query_rows, key_rows, value_rows, out_rows, down_rows, gains, grad_mem_keys, grad_mem_values = go_back(
            limit,
            grad_attended,
            saved,
            [grad.astype(low) for grad in (grad_gate, grad_up, grad_out, grad_down)],
            (w_query, w_key, w_value),
            normed_one.T,
            tokens[0],
            grad_middle,
            gain_one[None],
            grad_ffn_gain[None],
            placed.T,
            picked.T,
        )
        index = lax.axis_index("seq") * lax.axis_size("doc") + lax.axis_index("doc")
        parts = gains.reshape(2, seq_count * lax.axis_size("doc"), -1)
        attn_row, ffn_row = lax.dynamic_index_in_dim(parts, index, 1, keepdims=False)
    else:
        grad_q, grad_k, grad_v, grad_mk, grad_mv = attend_backward(limit, grad_attended, saved)
        back = jnp.stack((dot32(placed.T, grad_mk).astype(low), dot32(placed.T, grad_mv).astype(low)))
        returned = exchange(back, seq_count, capacity)
        grad_mem_keys = dot32(picked.T, returned[0])
        grad_mem_values = dot32(picked.T, returned[1])
        grad_query = dot32(normed_one.T, grad_q)
        grad_key = dot32(normed_one.T, grad_k)
        grad_value = dot32(normed_one.T, grad_v)
        grad_normed_one = dot32(grad_q, w_query.T) + dot32(grad_k, w_key.T) + dot32(grad_v, w_value.T)
        grad_attn_gain = jnp.sum(grad_normed_one * unit_one, axis=0)
        scaled_one = gain_one * grad_normed_one
        grad_input = grad_middle + factor_one * (
            scaled_one - unit_one * jnp.mean(scaled_one * unit_one, axis=-1, keepdims=True)
        )
        grad_tokens = grad_input.astype(low)
        gate_rows, up_rows, query_rows, key_rows, value_rows, out_rows, down_rows, attn_row, ffn_row = [
            lax.psum_scatter(grad, ("seq", "doc"), scatter_dimension=0, tiled=True)
            for grad in (
                grad_gate, grad_up, grad_query, grad_key, grad_value, grad_out, grad_down, grad_attn_gain, grad_ffn_gain
            )
        ]
    return (
        layer_out[None],
        grad_tokens[None],
        attn_row,
        query_rows,
        key_rows,
        value_rows,
        out_rows,
        ffn_row,
        gate_rows,
        up_rows,
        down_rows,
        grad_mem_keys[None],
        grad_mem_values[None],
    )


def solution(mesh):
    in_specs = (
        P("doc", "seq", None),
        P("doc", "seq", None),
        P(),
        P(),
        P(),
        P(),
        P(),
        P(),
        P(),
        P(),
        P(),
        P("doc", "seq", None),
        P("doc", "seq", None),
        P("doc", None),
        P("doc", "seq", None),
    )
    out_specs = (
        P("doc", "seq", None),
        P("doc", "seq", None),
        P(("seq", "doc")),
        P(("seq", "doc"), None),
        P(("seq", "doc"), None),
        P(("seq", "doc"), None),
        P(("seq", "doc"), None),
        P(("seq", "doc")),
        P(("seq", "doc"), None),
        P(("seq", "doc"), None),
        P(("seq", "doc"), None),
        P("doc", "seq", None),
        P("doc", "seq", None),
    )
    return jax.shard_map(
        on_device, mesh=mesh, in_specs=in_specs, out_specs=out_specs, check_vma=False
    )
```

```python
import functools
import math

import jax
import jax.numpy as jnp
from jax import lax
from jax.experimental import pallas as pl
from jax.experimental.pallas import tpu as pltpu
from jax.sharding import PartitionSpec as P

HEADS = 8
HEAD_DIM = 128
TOPK = 128
BPS = 4
NEG = -1000000000.0
MESH = pl.DeviceIdType.MESH
EPS = 1e-05
UNIT = 256
SKEW = 4


def flip(value, bit):
    return value + bit - 2 * bit * ((value // bit) % 2)


HALF = HEADS // 2
LOG2E = math.log2(math.e)
SCALE = HEAD_DIM ** (-0.5)
NT = (((1,), (1,)), ((), ()))
TN = (((0,), (0,)), ((), ()))
NN = (((1,), (0,)), ((), ()))


def matmul(left, right, dims):
    return lax.dot_general(left, right, dims, preferred_element_type=jnp.float32)


def seats():
    seq, doc = lax.axis_index("seq"), lax.axis_index("doc")
    core, chip = seq % 2, (seq // 2) % 2
    mate = (flip(seq, 1), doc)
    across = (flip(seq, 2), doc)
    diagonal = (flip(flip(seq, 2), 1), doc)
    return core, chip, mate, across, diagonal


def meet(peers):
    barrier = pltpu.get_barrier_semaphore()
    for peer in peers:
        pl.semaphore_signal(barrier, inc=1, device_id=peer, device_id_type=MESH)
    pl.semaphore_wait(barrier, len(peers))


def head_lanes(core, head):
    return pl.ds(pl.multiple_of((core * HALF + head) * HEAD_DIM, HEAD_DIM), HEAD_DIM)


def remote(src, dst, send, recv, peer):
    return pltpu.make_async_remote_copy(
        src_ref=src, dst_ref=dst, send_sem=send, recv_sem=recv, device_id=peer, device_id_type=MESH
    )


def share_heads(sources, boxes, core, mate, local_sem, send_sem, recv_sem):
    copies = []
    for i, (source, box) in enumerate(zip(sources, boxes)):
        for head in range(HALF):
            copies.append(
                remote(
                    source.at[:, head_lanes(1 - core, head)],
                    box.at[core, head],
                    send_sem.at[i, head],
                    recv_sem.at[i, head],
                    mate,
                )
            )
            copies[-1].start()
    for i, (source, box) in enumerate(zip(sources, boxes)):
        for head in range(HALF):
            copies.append(
                pltpu.make_async_copy(
                    source.at[:, head_lanes(core, head)], box.at[core, head], local_sem.at[i, head]
                )
            )
            copies[-1].start()
    return copies


def masked(scores, first_key, limit, diagonal):
    key = lax.broadcasted_iota(jnp.int32, scores.shape, 0)
    ok = key + first_key < limit
    if diagonal:
        ok = ok & (key <= lax.broadcasted_iota(jnp.int32, scores.shape, 1))
    return jnp.where(ok, scores, NEG)


def soften(parts):
    top = functools.reduce(
        jnp.maximum, [jnp.max(scores, axis=0, keepdims=True) for scores, _ in parts]
    )
    total, mixed = 0.0, 0.0
    for scores, values in parts:
        exponent = jnp.exp2(scores - top)
        total = total + jnp.sum(exponent, axis=0, keepdims=True)
        mixed = mixed + matmul(values, exponent.astype(jnp.bfloat16), TN)
    return mixed / total, top + jnp.log(total) * LOG2E


def forward_kernel(
    limit_ref, q, k, v, mk, mv,
    attended, qb, kb, vb, qx, mkb, mvb, ob, lse,
    mixed_own, mixed_out, mixed_in, lse_out, lse_in,
    local_sem, mate_send, mate_recv, far_send, far_recv, back_send, back_recv, end_sem,
):
    core, chip, mate, across, diagonal = seats()
    block = q.shape[0]
    limit = limit_ref[0]
    meet((mate, across, diagonal))

    def query_copy(head, own):
        return remote(
            q.at[:, head_lanes(core if own else 1 - core, head)],
            qx.at[core, head],
            far_send.at[0 if own else 1, head],
            far_recv.at[core, head],
            across if own else diagonal,
        )

    def arrived_query(far, head):
        return remote(
            q.at[:, head_lanes(core, head)], qx.at[far, head], far_send.at[0, head], far_recv.at[far, head], across
        )

    @pl.when(chip == 1)
    def _():
        for head in range(HALF):
            query_copy(head, True).start()
            query_copy(head, False).start()

    copies = share_heads((q, k, v, mk, mv), (qb, kb, vb, mkb, mvb), core, mate, local_sem, mate_send, mate_recv)
    for copy in copies:
        copy.wait()

    def own_part(blk, head):
        query = qb[blk, head]
        parts = []
        for kblk in range(blk + 1):
            scores = matmul(kb[kblk, head], query, NT) * (SCALE * LOG2E)
            scores = masked(scores, (2 * chip + kblk) * block, limit, kblk == blk)
            parts.append((scores, vb[kblk, head]))
        parts.append((matmul(mkb[blk, head], query, NT) * (SCALE * LOG2E), mvb[blk, head]))
        return soften(parts)

    for blk in range(2):
        def own_head(head, carry):
            mixed, level = own_part(blk, head)
            mixed_own[blk, head] = mixed
            lse[blk, head] = level
            return carry
        lax.fori_loop(0, HALF, own_head, 0)

    def back_copy(blk, head):
        return (
            remote(mixed_out.at[blk, head], mixed_in.at[blk, head], back_send.at[0, blk, head], back_recv.at[0, blk, head], across),
            remote(lse_out.at[blk, head], lse_in.at[blk, head], back_send.at[1, blk, head], back_recv.at[1, blk, head], across),
        )

    @pl.when(chip == 0)
    def _():
        def cross(i, carry):
            head, blk = i // 2, i % 2
            arrived_query(blk, head).wait_recv()
            query = qx[blk, head]
            parts = []
            for kblk in range(2):
                scores = matmul(kb[kblk, head], query, NT) * (SCALE * LOG2E)
                parts.append((masked(scores, kblk * block, limit, False), vb[kblk, head]))
            mixed, level = soften(parts)
            mixed_out[blk, head] = mixed.astype(jnp.bfloat16)
            lse_out[blk, head] = level
            for copy in back_copy(blk, head):
                copy.start()
            return carry
        lax.fori_loop(0, 2 * HALF, cross, 0)

        def finish(i, carry):
            head, blk = i // 2, i % 2
            ob[blk, head] = mixed_own[blk, head].T.astype(jnp.bfloat16)
            return carry
        lax.fori_loop(0, 2 * HALF, finish, 0)

    @pl.when(chip == 1)
    def _():
        def merge(i, carry):
            head, blk = i // 2, i % 2
            for copy in back_copy(blk, head):
                copy.wait_recv()
            near, far = lse[blk, head], lse_in[blk, head]
            top = jnp.maximum(near, far)
            near, far = jnp.exp2(near - top), jnp.exp2(far - top)
            total = near + far
            mixed = (mixed_own[blk, head] * near + mixed_in[blk, head].astype(jnp.float32) * far) / total
            ob[blk, head] = mixed.T.astype(jnp.bfloat16)
            lse[blk, head] = top + jnp.log(total) * LOG2E
            return carry
        lax.fori_loop(0, 2 * HALF, merge, 0)

    ends = []
    for head in range(HALF):
        ends.append(
            remote(ob.at[1 - core, head], attended.at[:, head_lanes(core, head)], end_sem.at[0, head], end_sem.at[1, head], mate)
        )
        ends.append(
            pltpu.make_async_copy(ob.at[core, head], attended.at[:, head_lanes(core, head)], end_sem.at[2, head])
        )
    for copy in ends:
        copy.start()
    for copy in ends:
        copy.wait()

    @pl.when(chip == 0)
    def _():
        for head in range(HALF):
            for blk in range(2):
                for copy in back_copy(blk, head):
                    copy.wait_send()

    @pl.when(chip == 1)
    def _():
        for head in range(HALF):
            query_copy(head, True).wait_send()
            query_copy(head, False).wait_send()


def attend_forward(limit, queries, keys, values, mem_keys, mem_values):
    block, width = queries.shape
    topk = mem_keys.shape[0]
    low, full = jnp.bfloat16, jnp.float32
    box = (2, HALF, block, HEAD_DIM)
    mem_box = (2, HALF, topk, HEAD_DIM)
    flat = (2, HALF, HEAD_DIM, block)
    row = (2, HALF, 1, block)
    dma = pltpu.SemaphoreType.DMA
    hbm, vmem = pl.BlockSpec(memory_space=pl.ANY), pl.BlockSpec(memory_space=pltpu.VMEM)
    struct = jax.ShapeDtypeStruct
    return pl.pallas_call(
        forward_kernel,
        out_shape=(
            struct((block, width), low),
            struct(box, low), struct(box, low), struct(box, low), struct(box, low),
            struct(mem_box, low), struct(mem_box, low), struct(box, low), struct(row, full),
        ),
        in_specs=[pl.BlockSpec(memory_space=pltpu.SMEM)] + [hbm] * 5,
        out_specs=(hbm,) + (vmem,) * 8,
        scratch_shapes=[
            pltpu.VMEM(flat, full), pltpu.VMEM(flat, low), pltpu.VMEM(flat, low),
            pltpu.VMEM(row, full), pltpu.VMEM(row, full),
            dma((5, HALF)), dma((5, HALF)), dma((5, HALF)),
            dma((2, HALF)), dma((2, HALF)), dma((2, 2, HALF)), dma((2, 2, HALF)), dma((3, HALF)),
        ],
        name="attend_forward",
        compiler_params=pltpu.CompilerParams(collective_id=1, has_side_effects=True, vmem_limit_bytes=56 * 2**20),
    )(limit, queries, keys, values, mem_keys, mem_values)


def backward_kernel(
    limit_ref, grad, qb, kb, vb, qx, mkb, mvb, ob, lse,
    dq, dk, dv, dmk, dmv,
    gb, gx, delta, lse_in, delta_in, dq_own, dq_out, dq_in, dk_sum, dv_sum, dmk_low, dmv_low, dqb, dkb, dvb,
    local_sem, mate_send, mate_recv, far_send, far_recv, row_send, row_recv, back_send, back_recv,
    end_local, end_send, end_recv,
):
    core, chip, mate, across, diagonal = seats()
    block = grad.shape[0]
    limit = limit_ref[0]
    meet((mate, across, diagonal))

    def grad_copy(head, own):
        return remote(
            grad.at[:, head_lanes(core if own else 1 - core, head)],
            gx.at[core, head],
            far_send.at[0 if own else 1, head],
            far_recv.at[core, head],
            across if own else diagonal,
        )

    def arrived_grad(far, head):
        return remote(
            grad.at[:, head_lanes(core, head)], gx.at[far, head], far_send.at[0, head], far_recv.at[far, head], across
        )

    def row_copies():
        return (
            remote(lse, lse_in, row_send.at[0], row_recv.at[0], across),
            remote(delta, delta_in, row_send.at[1], row_recv.at[1], across),
        )

    @pl.when(chip == 1)
    def _():
        for head in range(HALF):
            grad_copy(head, True).start()
            grad_copy(head, False).start()

    copies = share_heads((grad,), (gb,), core, mate, local_sem, mate_send, mate_recv)
    for copy in copies:
        copy.wait()

    def rows(i, carry):
        head, blk = i // 2, i % 2
        product = gb[blk, head].astype(jnp.float32) * ob[blk, head].astype(jnp.float32)
        delta[blk, head] = jnp.sum(product.T, axis=0, keepdims=True)
        return carry

    lax.fori_loop(0, 2 * HALF, rows, 0)

    @pl.when(chip == 1)
    def _():
        for copy in row_copies():
            copy.start()

    def pull(key_rows, value_rows, query, grad_rows, level, inner, where):
        scores = matmul(key_rows, query, NT) * (SCALE * LOG2E)
        if where is not None:
            scores = masked(scores, where[0], limit, where[1])
        weights = jnp.exp2(scores - level)
        grad_weights = matmul(value_rows, grad_rows, NT)
        grad_scores = (weights * (grad_weights - inner)).astype(jnp.bfloat16)
        return (
            matmul(grad_scores, query, NN),
            matmul(weights.astype(jnp.bfloat16), grad_rows, NN),
            matmul(key_rows, grad_scores, TN),
        )

    for blk in range(2):
        def own_head(head, carry):
            query, grad_rows = qb[blk, head], gb[blk, head]
            level, inner = lse[blk, head], delta[blk, head]
            total = 0.0
            for kblk in range(blk + 1):
                gk, gv, gq = pull(
                    kb[kblk, head], vb[kblk, head], query, grad_rows, level, inner,
                    ((2 * chip + kblk) * block, kblk == blk),
                )
                if kblk == blk:
                    dk_sum[kblk, head], dv_sum[kblk, head] = gk, gv
                else:
                    dk_sum[kblk, head] += gk
                    dv_sum[kblk, head] += gv
                total = total + gq
            gk, gv, gq = pull(mkb[blk, head], mvb[blk, head], query, grad_rows, level, inner, None)
            dmk_low[blk, head] = (gk * SCALE).astype(jnp.bfloat16)
            dmv_low[blk, head] = gv.astype(jnp.bfloat16)
            dq_own[blk, head] = total + gq
            return carry
        lax.fori_loop(0, HALF, own_head, 0)

    def back_copy(blk, head):
        return remote(dq_out.at[blk, head], dq_in.at[blk, head], back_send.at[blk, head], back_recv.at[blk, head], across)

    @pl.when(chip == 0)
    def _():
        for copy in row_copies():
            copy.wait_recv()

        def cross(i, carry):
            head, blk = i // 2, i % 2
            arrived_grad(blk, head).wait_recv()
            query, grad_rows = qx[blk, head], gx[blk, head]
            level, inner = lse_in[blk, head], delta_in[blk, head]
            total = 0.0
            for kblk in range(2):
                gk, gv, gq = pull(
                    kb[kblk, head], vb[kblk, head], query, grad_rows, level, inner, (kblk * block, False)
                )
                dk_sum[kblk, head] += gk
                dv_sum[kblk, head] += gv
                total = total + gq
            dq_out[blk, head] = total.astype(jnp.bfloat16)
            back_copy(blk, head).start()
            return carry
        lax.fori_loop(0, 2 * HALF, cross, 0)

    def finish(i, carry):
        head, blk = i // 2, i % 2
        dqb[blk, head] = (dq_own[blk, head].T * SCALE).astype(jnp.bfloat16)
        dkb[blk, head] = (dk_sum[blk, head] * SCALE).astype(jnp.bfloat16)
        dvb[blk, head] = dv_sum[blk, head].astype(jnp.bfloat16)
        return carry

    @pl.when(chip == 1)
    def _():
        def merge(i, carry):
            head, blk = i // 2, i % 2
            back_copy(blk, head).wait_recv()
            dq_own[blk, head] += dq_in[blk, head].astype(jnp.float32)
            return finish(i, carry)
        lax.fori_loop(0, 2 * HALF, merge, 0)

    @pl.when(chip == 0)
    def _():
        lax.fori_loop(0, 2 * HALF, finish, 0)

    ends = []
    for i, (box, out) in enumerate(((dqb, dq), (dkb, dk), (dvb, dv), (dmk_low, dmk), (dmv_low, dmv))):
        for head in range(HALF):
            lanes = head_lanes(core, head)
            ends.append(remote(box.at[1 - core, head], out.at[:, lanes], end_send.at[i, head], end_recv.at[i, head], mate))
            ends.append(pltpu.make_async_copy(box.at[core, head], out.at[:, lanes], end_local.at[i, head]))
    for copy in ends:
        copy.start()
    for copy in ends:
        copy.wait()

    @pl.when(chip == 0)
    def _():
        for head in range(HALF):
            for blk in range(2):
                back_copy(blk, head).wait_send()

    @pl.when(chip == 1)
    def _():
        for copy in row_copies():
            copy.wait_send()
        for head in range(HALF):
            grad_copy(head, True).wait_send()
            grad_copy(head, False).wait_send()


def attend_backward(limit, grad, saved):
    block, width = grad.shape
    topk = saved[4].shape[2]
    low, full = jnp.bfloat16, jnp.float32
    box = (2, HALF, block, HEAD_DIM)
    mem_box = (2, HALF, topk, HEAD_DIM)
    flat = (2, HALF, HEAD_DIM, block)
    row = (2, HALF, 1, block)
    dma = pltpu.SemaphoreType.DMA
    hbm, vmem = pl.BlockSpec(memory_space=pl.ANY), pl.BlockSpec(memory_space=pltpu.VMEM)
    struct = jax.ShapeDtypeStruct
    return pl.pallas_call(
        backward_kernel,
        out_shape=(struct((block, width), low),) * 3 + (struct((topk, width), low),) * 2,
        in_specs=[pl.BlockSpec(memory_space=pltpu.SMEM), hbm] + [vmem] * 8,
        out_specs=(hbm,) * 5,
        scratch_shapes=[
            pltpu.VMEM(box, low), pltpu.VMEM(box, low),
            pltpu.VMEM(row, full), pltpu.VMEM(row, full), pltpu.VMEM(row, full),
            pltpu.VMEM(flat, full), pltpu.VMEM(flat, low), pltpu.VMEM(flat, low),
            pltpu.VMEM(box, full), pltpu.VMEM(box, full),
            pltpu.VMEM(mem_box, low), pltpu.VMEM(mem_box, low),
            pltpu.VMEM(box, low), pltpu.VMEM(box, low), pltpu.VMEM(box, low),
            dma((1, HALF)), dma((1, HALF)), dma((1, HALF)),
            dma((2, HALF)), dma((2, HALF)), dma((2,)), dma((2,)),
            dma((2, HALF)), dma((2, HALF)),
            dma((5, HALF)), dma((5, HALF)), dma((5, HALF)),
        ],
        name="attend_backward",
        compiler_params=pltpu.CompilerParams(collective_id=2, has_side_effects=True, vmem_limit_bytes=56 * 2**20),
    )(limit, grad, *saved)


def keep_order(rank_of):
    before = lax.broadcasted_iota(jnp.int32, (rank_of, rank_of), 0)
    return (before < lax.broadcasted_iota(jnp.int32, (rank_of, rank_of), 1)).astype(jnp.bfloat16)


def front_kernel(
    limit_ref, tokens, gain, w_query, w_key, w_value, mem_keys, mem_values, wanted,
    attended, qb, kb, vb, qx, mkb, mvb, ob, lse, spots, pick_t,
    rows, weights, normed, qkv, tables, every, pick, mem_out, mem_in,
    mixed_own, mixed_out, mixed_in, lse_out, lse_in,
    load_sem, want_send, want_recv, mem_send, mem_recv, mem_local,
    local_sem, mate_send, mate_recv, far_send, far_recv, back_send, back_recv, end_sem,
):
    core, chip, mate, across, diagonal = seats()
    seq, doc = lax.axis_index("seq"), lax.axis_index("doc")
    seq_count, capacity = mem_in.shape[0], mem_in.shape[3]
    block, width = tokens.shape
    mem_rows, topk = tables.shape[1], every.shape[2]
    limit = limit_ref[0]

    loads = [
        pltpu.make_async_copy(src, dst, load_sem.at[i])
        for i, (src, dst) in enumerate(
            (
                (wanted, every.at[seq]), (tokens, rows), (w_query, weights.at[0]), (w_key, weights.at[1]),
                (w_value, weights.at[2]), (mem_keys, tables.at[0]), (mem_values, tables.at[1]),
            )
        )
    ]
    for copy in loads:
        copy.start()
    meet([(lax.rem(seq + away, seq_count), doc) for away in range(1, seq_count)])
    loads[0].wait()

    def want_copy(away):
        return remote(
            every.at[seq], every.at[seq], want_send.at[away - 1], want_recv.at[away - 1],
            (lax.rem(seq + away, seq_count), doc),
        )

    def want_arrival(away):
        source = lax.rem(seq + seq_count - away, seq_count)
        return remote(every.at[source], every.at[source], want_send.at[away - 1], want_recv.at[away - 1], (source, doc))

    def mem_copy(away):
        peer = lax.rem(seq + away, seq_count)
        return remote(mem_out.at[peer], mem_in.at[seq], mem_send.at[away - 1], mem_recv.at[away - 1], (peer, doc))

    def mem_arrival(away):
        source = lax.rem(seq + seq_count - away, seq_count)
        return remote(mem_out.at[source], mem_in.at[source], mem_send.at[away - 1], mem_recv.at[away - 1], (source, doc))

    for away in range(1, seq_count):
        want_copy(away).start()
    loads[1].wait()
    part = 64

    def norm(i, carry):
        at = pl.ds(pl.multiple_of(i * part, part), part)
        x = rows[at, :].astype(jnp.float32)
        factor = lax.rsqrt(jnp.mean(x * x, axis=-1, keepdims=True) + EPS)
        normed[at, :] = (x * factor * gain[...]).astype(jnp.bfloat16)
        return carry

    lax.fori_loop(0, block // part, norm, 0)

    def project(i):
        loads[2 + i].wait()

        def one(j, carry):
            lanes = pl.ds(pl.multiple_of(j * UNIT, UNIT), UNIT)
            qkv[i, :, lanes] = matmul(normed[...], weights[i, :, lanes], NN).astype(jnp.bfloat16)
            return carry

        lax.fori_loop(0, width // UNIT, one, 0)

    project(0)

    def query_copy(head, own):
        return remote(
            qkv.at[0, :, head_lanes(core if own else 1 - core, head)],
            qx.at[core, head],
            far_send.at[0 if own else 1, head],
            far_recv.at[core, head],
            across if own else diagonal,
        )

    def arrived_query(far, head):
        return remote(
            qkv.at[0, :, head_lanes(core, head)], qx.at[far, head], far_send.at[0, head], far_recv.at[far, head], across
        )

    @pl.when(chip == 1)
    def _():
        for head in range(HALF):
            query_copy(head, True).start()
            query_copy(head, False).start()

    project(1)
    project(2)
    copies = share_heads(
        (qkv.at[0], qkv.at[1], qkv.at[2]), (qb, kb, vb), core, mate, local_sem, mate_send, mate_recv
    )

    for away in range(1, seq_count):
        want_arrival(away).wait_recv()
    triangle = keep_order(topk)
    asked = every[:, 0, :]
    here = asked - seq * mem_rows
    mine = (here >= 0) & (here < mem_rows)
    before = matmul(mine.astype(jnp.bfloat16), triangle, NN).astype(jnp.int32)
    place = lax.broadcasted_iota(jnp.int32, (capacity, topk), 0)
    line = lax.broadcasted_iota(jnp.int32, (mem_rows, topk), 0)
    for b in range(seq_count):
        at_place = jnp.where((before[b : b + 1] == place) & (here[b : b + 1] >= 0) & (here[b : b + 1] < mem_rows), 1.0, 0.0)
        at_line = jnp.where(here[b : b + 1] == line, 1.0, 0.0)
        pick[b * capacity : (b + 1) * capacity, :] = matmul(
            at_place.astype(jnp.bfloat16), at_line.astype(jnp.bfloat16), NT
        ).astype(jnp.bfloat16)
    half = HALF * HEAD_DIM
    for kind in range(2):
        loads[5 + kind].wait()
        for side in range(2):
            found = matmul(pick[...], tables[kind, :, side * half : (side + 1) * half], NN).astype(jnp.bfloat16)
            for b in range(seq_count):
                mem_out[2 * (b // 2) + side, b % 2, kind] = found[b * capacity : (b + 1) * capacity]
    for away in range(1, seq_count):
        mem_copy(away).start()
    own_rows = pltpu.make_async_copy(mem_out.at[seq], mem_in.at[seq], mem_local.at[0])
    own_rows.start()
    pick_t[...] = pick[...].astype(jnp.float32).T.astype(jnp.bfloat16)
    seat = lax.broadcasted_iota(jnp.int32, (seq_count, topk), 0)
    slot_at = lax.broadcasted_iota(jnp.int32, (seq_count * capacity, topk), 0)
    for blk in range(2):
        away_rows = every[2 * (seq // 2) + blk] - seat * mem_rows
        owner = (away_rows >= 0) & (away_rows < mem_rows)
        rank = matmul(owner.astype(jnp.bfloat16), triangle, NN).astype(jnp.int32)
        slot = jnp.sum(jnp.where(owner, seat * capacity + rank, 0), axis=0, keepdims=True)
        spots[blk] = jnp.where(slot == slot_at, 1.0, 0.0).astype(jnp.bfloat16)

    for copy in copies:
        copy.wait()

    def own_head(blk, head):
        query = qb[blk, head]
        parts = []
        for kblk in range(blk + 1):
            scores = matmul(kb[kblk, head], query, NT) * (SCALE * LOG2E)
            scores = masked(scores, (2 * chip + kblk) * block, limit, kblk == blk)
            parts.append((scores, vb[kblk, head]))
        mixed_own[blk, head], lse[blk, head] = soften(parts)

    def back_copy(blk, head):
        return (
            remote(mixed_out.at[blk, head], mixed_in.at[blk, head], back_send.at[0, blk, head], back_recv.at[0, blk, head], across),
            remote(lse_out.at[blk, head], lse_in.at[blk, head], back_send.at[1, blk, head], back_recv.at[1, blk, head], across),
        )

    def heads(head, carry):
        @pl.when(chip == 0)
        def _():
            def cross(blk, carry):
                arrived_query(blk, head).wait_recv()
                query = qx[blk, head]
                parts = []
                for kblk in range(2):
                    scores = matmul(kb[kblk, head], query, NT) * (SCALE * LOG2E)
                    parts.append((masked(scores, kblk * block, limit, False), vb[kblk, head]))
                mixed, level = soften(parts)
                mixed_out[blk, head] = mixed.astype(jnp.bfloat16)
                lse_out[blk, head] = level
                for copy in back_copy(blk, head):
                    copy.start()
                return carry

            lax.fori_loop(0, 2, cross, 0)

        own_head(0, head)
        own_head(1, head)
        return carry

    lax.fori_loop(0, HALF, heads, 0)

    for away in range(1, seq_count):
        mem_arrival(away).wait_recv()
    own_rows.wait()
    for blk in range(2):
        for kind, box in enumerate((mkb, mvb)):
            found = mem_in[:, blk, kind].reshape(seq_count * capacity, half)
            found = matmul(spots[blk], found, TN).astype(jnp.bfloat16)
            for head in range(HALF):
                box[blk, head] = found[:, head * HEAD_DIM : (head + 1) * HEAD_DIM]

    def blend(pieces):
        top = functools.reduce(jnp.maximum, [level for _, level in pieces])
        total, mixed = 0.0, 0.0
        for value, level in pieces:
            share = jnp.exp2(level - top)
            total = total + share
            mixed = mixed + value * share
        return mixed / total, top + jnp.log(total) * LOG2E

    def finish(i, carry):
        head, blk = i // 2, i % 2
        scores = matmul(mkb[blk, head], qb[blk, head], NT) * (SCALE * LOG2E)
        pieces = [(mixed_own[blk, head], lse[blk, head]), soften([(scores, mvb[blk, head])])]

        @pl.when(chip == 0)
        def _():
            mixed, lse[blk, head] = blend(pieces)
            ob[blk, head] = mixed.T.astype(jnp.bfloat16)

        @pl.when(chip == 1)
        def _():
            for copy in back_copy(blk, head):
                copy.wait_recv()
            far = (mixed_in[blk, head].astype(jnp.float32), lse_in[blk, head])
            mixed, lse[blk, head] = blend(pieces + [far])
            ob[blk, head] = mixed.T.astype(jnp.bfloat16)

        return carry

    lax.fori_loop(0, 2 * HALF, finish, 0)

    ends = []
    for head in range(HALF):
        ends.append(
            remote(ob.at[1 - core, head], attended.at[:, head_lanes(core, head)], end_sem.at[0, head], end_sem.at[1, head], mate)
        )
        ends.append(
            pltpu.make_async_copy(ob.at[core, head], attended.at[:, head_lanes(core, head)], end_sem.at[2, head])
        )
    for copy in ends:
        copy.start()
    for copy in ends:
        copy.wait()
    for away in range(1, seq_count):
        want_copy(away).wait_send()
        mem_copy(away).wait_send()

    @pl.when(chip == 0)
    def _():
        for head in range(HALF):
            for blk in range(2):
                for copy in back_copy(blk, head):
                    copy.wait_send()

    @pl.when(chip == 1)
    def _():
        for head in range(HALF):
            query_copy(head, True).wait_send()
            query_copy(head, False).wait_send()


def go_forward(limit, tokens, gain, projections, mem_keys, mem_values, wanted):
    block, width = tokens.shape
    mem_rows, topk = mem_keys.shape[0], wanted.shape[1]
    seq_count = lax.axis_size("seq")
    capacity = 2 * topk // seq_count
    slots = seq_count * capacity
    low, full = jnp.bfloat16, jnp.float32
    box = (2, HALF, block, HEAD_DIM)
    mem_box = (2, HALF, topk, HEAD_DIM)
    flat = (2, HALF, HEAD_DIM, block)
    row = (2, HALF, 1, block)
    mem = (seq_count, 2, 2, capacity, HALF * HEAD_DIM)
    dma = pltpu.SemaphoreType.DMA
    hbm, vmem = pl.BlockSpec(memory_space=pl.ANY), pl.BlockSpec(memory_space=pltpu.VMEM)
    struct = jax.ShapeDtypeStruct
    return pl.pallas_call(
        front_kernel,
        out_shape=(
            struct((block, width), low),
            struct(box, low), struct(box, low), struct(box, low), struct(box, low),
            struct(mem_box, low), struct(mem_box, low), struct(box, low), struct(row, full),
            struct((2, slots, topk), low), struct((mem_rows, slots), low),
        ),
        in_specs=[pl.BlockSpec(memory_space=pltpu.SMEM), hbm, vmem] + [hbm] * 6,
        out_specs=(hbm,) + (vmem,) * 10,
        scratch_shapes=[
            pltpu.VMEM((block, width), low), pltpu.VMEM((3, width, width), low), pltpu.VMEM((block, width), low),
            pltpu.VMEM((3, block, width), low), pltpu.VMEM((2, mem_rows, width), low),
            pltpu.VMEM((seq_count, 1, topk), jnp.int32), pltpu.VMEM((slots, mem_rows), low),
            pltpu.VMEM(mem, low), pltpu.VMEM(mem, low),
            pltpu.VMEM(flat, full), pltpu.VMEM(flat, low), pltpu.VMEM(flat, low),
            pltpu.VMEM(row, full), pltpu.VMEM(row, full),
            dma((7,)), dma((seq_count - 1,)), dma((seq_count - 1,)), dma((seq_count - 1,)), dma((seq_count - 1,)), dma((1,)),
            dma((3, HALF)), dma((3, HALF)), dma((3, HALF)),
            dma((2, HALF)), dma((2, HALF)), dma((2, 2, HALF)), dma((2, 2, HALF)), dma((3, HALF)),
        ],
        name="go_forward",
        compiler_params=pltpu.CompilerParams(collective_id=4, has_side_effects=True, vmem_limit_bytes=56 * 2**20),
    )(limit, tokens, gain, *projections, mem_keys, mem_values, wanted)


SUM_ORDERS = (("x", "y", "low", "high"), ("y", "x", "low", "high"), ("low", "high", "y", "x"))
EARLY = (8, 18, 4)
UNITS = (12, 26, 4)
ROWS = (32, 32, 88)
SLOTS = (2, 4, 2)
FIRST_LATE = 18
STEPS = 26


def when(condition, body):
    if isinstance(condition, bool):
        if condition:
            body()
    else:
        pl.when(condition)(body)


def turn(cls, at):
    if cls == 0:
        early = (at % 2 == 0) & (at >= 0) & (at < 16)
        late = (at % 2 == 0) & (at >= FIRST_LATE) & (at < STEPS)
        return early, at // 2, late, at // 2 - 1
    if cls == 1:
        return (at >= 0) & (at < FIRST_LATE), at, (at >= FIRST_LATE) & (at < STEPS), at
    return (at % 4 == 0) & (at >= 0) & (at < 16), at // 4, None, None


class Sums:
    def __init__(self, gate, up, out, down, own, stages, sums, local_sem, send_sem, recv_sem, peers):
        self.grads = {"gate": gate, "up": up, "out": out, "down": down}
        self.own, self.stages, self.sums = own, stages, sums
        self.local_sem, self.send_sem, self.recv_sem = local_sem, send_sem, recv_sem
        self.peers = peers
        seq, doc = lax.axis_index("seq"), lax.axis_index("doc")
        self.bits = {
            "core": seq % 2,
            "x": (seq // 2) % 2,
            "y": (seq // 4) % 2,
            "low": doc % 2,
            "high": (doc // 2) % 2,
        }
        self.ranges = (
            ((0, 8, "gate", 0),),
            ((0, 3, "gate", 8 * UNIT), (3, 14, "up", 0), (14, 18, "out", 0)),
            ((0, 4, "down", 0),),
        )

    def part(self, name, column, core):
        return self.grads[name].at[:, :, core, :, :, :, pl.ds(pl.multiple_of(column, UNIT), UNIT)]

    def core_copy(self, cls, unit, source):
        return remote(
            source,
            self.stages[cls][0].at[unit],
            self.send_sem[cls].at[0, unit],
            self.recv_sem[cls].at[0, unit],
            self.peers["core"],
        )

    def own_copy(self, cls, unit, name, column):
        slot = unit % SLOTS[cls]
        return pltpu.make_async_copy(
            self.part(name, column, self.bits["core"]), self.own[cls].at[slot], self.local_sem[cls].at[slot]
        )

    def load_own(self, cls, unit):
        for first, end, name, column in self.ranges[cls]:
            when(
                (unit >= first) & (unit < end),
                lambda: self.own_copy(cls, unit, name, (unit - first) * UNIT + column).start(),
            )

    def begin(self):
        for step in range(FIRST_LATE):
            for cls in range(3):
                due, unit, _, _ = turn(cls, step)
                if due:
                    for first, end, name, column in self.ranges[cls]:
                        if first <= unit < end:
                            source = self.part(name, (unit - first) * UNIT + column, 1 - self.bits["core"])
                            self.core_copy(cls, unit, source).start()
                    if unit < SLOTS[cls]:
                        self.load_own(cls, unit)

    def half(self, cls, level, unit, mine):
        order = SUM_ORDERS[cls]
        name = order[level]
        left = [axis for axis in ("y", "x", "high", "low") if axis not in order[:level]]
        side = self.bits[name] if mine else 1 - self.bits[name]
        return self.stages[cls][level], (unit,) + (slice(None),) * left.index(name) + (side,)

    def copy(self, cls, level, unit):
        ref, index = self.half(cls, level - 1, unit, False)
        return remote(
            ref.at[index],
            self.stages[cls][level].at[unit],
            self.send_sem[cls].at[level, unit],
            self.recv_sem[cls].at[level, unit],
            self.peers[SUM_ORDERS[cls][level - 1]],
        )

    def arrive(self, cls, level, unit, fresh=None):
        ref = self.stages[cls][level]
        if level == 0:
            _, _, name, column = self.ranges[cls][0]
            self.core_copy(cls, unit, self.part(name, column, 1 - self.bits["core"])).wait_recv()
            if fresh is None:
                self.own_copy(cls, unit, name, column).wait()
                ref[unit] = ref[unit] + self.own[cls][unit % SLOTS[cls]]
                when(unit + SLOTS[cls] < EARLY[cls], lambda: self.load_own(cls, unit + SLOTS[cls]))
            else:
                ref[unit] = ref[unit] + fresh()
        else:
            self.copy(cls, level, unit).wait_recv()
            kept, index = self.half(cls, level - 1, unit, True)
            if level < 4:
                ref[unit] = ref[unit] + kept[index]
            else:
                self.sums[cls][unit] = ref[unit].astype(jnp.float32) + kept[index].astype(jnp.float32)
        if level < 4:
            self.copy(cls, level + 1, unit).start()

    def tick(self, step, fresh=None):
        for level in range(4, -1, -1):
            for cls in range(3):
                early, unit, late, late_unit = turn(cls, step - level * SKEW)
                if level > 0 and late is not None:
                    when(early | late, lambda: self.arrive(cls, level, jnp.where(late, late_unit, unit)))
                elif level > 0 or fresh is None:
                    when(early, lambda: self.arrive(cls, level, unit))
                elif late is not None:
                    when(late, lambda: self.arrive(cls, level, late_unit, lambda: fresh(cls, late_unit)))

    def drain(self):
        for cls in range(3):
            _, _, name, column = self.ranges[cls][0]

            def one(unit, carry):
                self.core_copy(cls, unit, self.part(name, column, 1 - self.bits["core"])).wait_send()
                for level in range(1, 5):
                    self.copy(cls, level, unit).wait_send()
                return carry

            lax.fori_loop(0, UNITS[cls], one, 0)


def back_kernel(
    limit_ref, grad, qb_in, kb_in, vb_in, qx_in, mkb_in, mvb_in, ob_in, lse_in0,
    gate, up, out, down, w_query, w_key, w_value, tokens, grad_middle, gain, ffn_row, spots_in, picked_t,
    grad_tokens, gate_rows, up_rows, query_rows, key_rows, value_rows, out_rows, down_rows, gains_out, grad_mk, grad_mv,
    gb, gx, lse, delta, lse_in, delta_in, dq_cross, dqkv, dqkv_mate, spots, mem_out, mem_in, gain_buf,
    own_a, own_b, own_c, *rest,
):
    stages = [rest[5 * c : 5 * c + 5] for c in range(3)]
    sums = rest[15:18]
    rest = rest[18:]
    local_sems, send_sems, recv_sems, rest = rest[0:3], rest[3:6], rest[6:9], rest[9:]
    (
        in_sem, gb_local, gb_send, gb_recv, spot_sem, far_send, far_recv, row_send, row_recv, back_send, back_recv,
        mate_send, mate_recv, mem_local, mem_send, mem_recv, gain_send, gain_recv, load_sem, weight_sem, done_sem, table_sem,
    ) = rest
    core, chip, mate, across, diagonal = seats()
    seq, doc = lax.axis_index("seq"), lax.axis_index("doc")
    seq_count = mem_in.shape[0]
    block = grad.shape[0]
    limit = limit_ref[0]
    peers = {
        "core": mate,
        "x": across,
        "y": (flip(seq, 4), doc),
        "low": (seq, flip(doc, 1)),
        "high": (seq, flip(doc, 2)),
    }
    others = [(lax.rem(seq + away, seq_count), doc) for away in range(1, seq_count)]
    meet(others + [peers["low"], peers["high"]])
    engine = Sums(
        gate, up, out, down, (own_a, own_b, own_c), stages, sums, local_sems, send_sems, recv_sems, peers
    )

    def grad_copy(head, own):
        return remote(
            grad.at[:, head_lanes(core if own else 1 - core, head)],
            gx.at[core, head],
            far_send.at[0 if own else 1, head],
            far_recv.at[core, head],
            across if own else diagonal,
        )

    def arrived_grad(far, head):
        return remote(
            grad.at[:, head_lanes(core, head)], gx.at[far, head], far_send.at[0, head], far_recv.at[far, head], across
        )

    def row_copies():
        return (
            remote(lse, lse_in, row_send.at[0], row_recv.at[0], across),
            remote(delta, delta_in, row_send.at[1], row_recv.at[1], across),
        )

    def back_copy(blk, head):
        return remote(dq_cross.at[blk, head], dq_cross.at[blk, head], back_send.at[blk, head], back_recv.at[blk, head], across)

    def mate_copy(i, head):
        lanes = head_lanes(core, head)
        return remote(dqkv_mate.at[i, head], dqkv.at[i, :, lanes], mate_send.at[i, head], mate_recv.at[i, head], mate)

    def mate_arrival(i, head):
        lanes = head_lanes(1 - core, head)
        return remote(dqkv_mate.at[i, head], dqkv.at[i, :, lanes], mate_send.at[i, head], mate_recv.at[i, head], mate)

    def mem_copy(away):
        peer = lax.rem(seq + away, seq_count)
        return remote(mem_out.at[peer], mem_in.at[seq], mem_send.at[away - 1], mem_recv.at[away - 1], (peer, doc))

    @pl.when(chip == 1)
    def _():
        for head in range(HALF):
            grad_copy(head, True).start()
            grad_copy(head, False).start()

    def attention(qb, kb, vb, qx, mkb, mvb, ob, dq_own, dk_sum, dv_sum, dm):
        inputs = [
            pltpu.make_async_copy(src, dst, in_sem.at[i])
            for i, (src, dst) in enumerate(
                ((qb_in, qb), (kb_in, kb), (vb_in, vb), (mkb_in, mkb), (mvb_in, mvb), (ob_in, ob), (lse_in0, lse), (qx_in, qx))
            )
        ]
        spot_copies = [pltpu.make_async_copy(spots_in, spots, spot_sem.at[0])]
        copies = share_heads((grad,), (gb,), core, mate, gb_local, gb_send, gb_recv)
        for copy in inputs + spot_copies:
            copy.start()
        engine.begin()
        for copy in copies + inputs + spot_copies:
            copy.wait()

        def rows(i, carry):
            head, blk = i // 2, i % 2
            product = gb[blk, head].astype(jnp.float32) * ob[blk, head].astype(jnp.float32)
            delta[blk, head] = jnp.sum(product.T, axis=0, keepdims=True)
            return carry

        lax.fori_loop(0, 2 * HALF, rows, 0)

        @pl.when(chip == 1)
        def _():
            for copy in row_copies():
                copy.start()

        def pull(key_rows, value_rows, query, grad_rows, level, inner, where):
            scores = matmul(key_rows, query, NT) * (SCALE * LOG2E)
            if where is not None:
                scores = masked(scores, where[0], limit, where[1])
            weights = jnp.exp2(scores - level)
            grad_weights = matmul(value_rows, grad_rows, NT)
            grad_scores = (weights * (grad_weights - inner)).astype(jnp.bfloat16)
            return (
                matmul(grad_scores, query, NN),
                matmul(weights.astype(jnp.bfloat16), grad_rows, NN),
                matmul(key_rows, grad_scores, TN),
            )

        def own_head(head, carry):
            lanes = pl.ds(pl.multiple_of(head * HEAD_DIM, HEAD_DIM), HEAD_DIM)
            for blk in range(2):
                query, grad_rows = qb[blk, head], gb[blk, head]
                level, inner = lse[blk, head], delta[blk, head]
                total = 0.0
                for kblk in range(blk + 1):
                    gk, gv, gq = pull(
                        kb[kblk, head], vb[kblk, head], query, grad_rows, level, inner,
                        ((2 * chip + kblk) * block, kblk == blk),
                    )
                    if kblk == blk:
                        dk_sum[kblk, head], dv_sum[kblk, head] = gk, gv
                    else:
                        dk_sum[kblk, head] += gk
                        dv_sum[kblk, head] += gv
                    total = total + gq
                gk, gv, gq = pull(mkb[blk, head], mvb[blk, head], query, grad_rows, level, inner, None)
                dm[blk, 0, :, lanes] = (gk * SCALE).astype(jnp.bfloat16)
                dm[blk, 1, :, lanes] = gv.astype(jnp.bfloat16)
                dq_own[blk, head] = total + gq
            engine.tick(head)
            return carry

        lax.fori_loop(0, HALF, own_head, 0)

        for blk in range(2):
            for kind in range(2):
                rows_out = matmul(spots[blk], dm[blk, kind], NN).astype(jnp.bfloat16)
                mem_out[:, blk, kind] = rows_out.reshape(mem_out.shape[0], mem_out.shape[3], mem_out.shape[4])
        for away in range(1, seq_count):
            mem_copy(away).start()
        pltpu.make_async_copy(mem_out.at[seq], mem_in.at[seq], mem_local.at[0]).start()

        @pl.when(chip == 0)
        def _():
            for copy in row_copies():
                copy.wait_recv()

            def cross(i, carry):
                head, blk = i // 2, i % 2
                arrived_grad(blk, head).wait_recv()
                query, grad_rows = qx[blk, head], gx[blk, head]
                level, inner = lse_in[blk, head], delta_in[blk, head]
                total = 0.0
                for kblk in range(2):
                    gk, gv, gq = pull(
                        kb[kblk, head], vb[kblk, head], query, grad_rows, level, inner, (kblk * block, False)
                    )
                    dk_sum[kblk, head] += gk
                    dv_sum[kblk, head] += gv
                    total = total + gq
                dq_cross[blk, head] = total.astype(jnp.bfloat16)
                back_copy(blk, head).start()
                engine.tick(HALF + i)
                return carry

            lax.fori_loop(0, 2 * HALF, cross, 0)

        @pl.when(chip == 1)
        def _():
            def merge(i, carry):
                head, blk = i // 2, i % 2
                engine.tick(HALF + i)
                back_copy(blk, head).wait_recv()
                dq_own[blk, head] += dq_cross[blk, head].astype(jnp.float32)
                return carry

            lax.fori_loop(0, 2 * HALF, merge, 0)

        def results(blk, head):
            return (
                (dq_own[blk, head].T * SCALE).astype(jnp.bfloat16),
                (dk_sum[blk, head] * SCALE).astype(jnp.bfloat16),
                dv_sum[blk, head].astype(jnp.bfloat16),
            )

        def for_mate(head, carry):
            for i, value in enumerate(results(1 - core, head)):
                dqkv_mate[i, head] = value
                mate_copy(i, head).start()
            return carry

        def for_own(head, carry):
            for i, value in enumerate(results(core, head)):
                dqkv[i, :, head_lanes(core, head)] = value
            return carry

        lax.fori_loop(0, HALF, for_mate, 0)
        lax.fori_loop(0, HALF, for_own, 0)

    box = (2, HALF, block, HEAD_DIM)
    mem_box = mkb_in.shape
    low, full = jnp.bfloat16, jnp.float32
    pl.run_scoped(
        attention,
        pltpu.VMEM(box, low), pltpu.VMEM(box, low), pltpu.VMEM(box, low), pltpu.VMEM(box, low),
        pltpu.VMEM(mem_box, low), pltpu.VMEM(mem_box, low), pltpu.VMEM(box, low),
        pltpu.VMEM((2, HALF, HEAD_DIM, block), full), pltpu.VMEM(box, full), pltpu.VMEM(box, full),
        pltpu.VMEM((2, 2, mem_box[2], HALF * HEAD_DIM), low),
    )

    def tail(normed, pick, dx, middle, rows, weights, made, table):
        width = dx.shape[1]
        chunk = weights.shape[2]
        loads = [
            pltpu.make_async_copy(tokens, rows, load_sem.at[1]),
            pltpu.make_async_copy(grad_middle, middle, load_sem.at[2]),
            pltpu.make_async_copy(picked_t, pick, load_sem.at[3]),
        ]

        def weight_copies(j):
            at = pl.ds(pl.multiple_of(j * chunk, chunk), chunk)
            return [
                pltpu.make_async_copy(w.at[at, :], weights.at[j % 2, i], weight_sem.at[j % 2, i])
                for i, w in enumerate((w_query, w_key, w_value))
            ]

        for copy in loads + weight_copies(0):
            copy.start()
        for i in range(3):
            for head in range(HALF):
                mate_arrival(i, head).wait_recv()
        loads[0].wait()
        part = 64

        def norm(i, carry):
            at = pl.ds(pl.multiple_of(i * 2 * part, 2 * part), 2 * part)
            x = rows[at, :].astype(jnp.float32)
            factor = lax.rsqrt(jnp.mean(x * x, axis=-1, keepdims=True) + EPS)
            normed[:, at] = (x * factor * gain[...]).T.astype(jnp.bfloat16)
            return carry

        lax.fori_loop(0, block // (2 * part), norm, 0)

        def made_copy(cls, unit, w):
            return engine.core_copy(cls, unit, made.at[w, :, :, 1 - core])

        def make(w):
            i = w // 4
            lanes = pl.ds(pl.multiple_of((w % 4) * UNIT, UNIT), UNIT)
            value = matmul(normed[...], dqkv[i, :, lanes], NN).astype(jnp.bfloat16)
            made[w] = value.reshape(made.shape[1:])
            pl.when(w < 4)(lambda: made_copy(0, EARLY[0] + w, w).start())
            pl.when(w >= 4)(lambda: made_copy(1, EARLY[1] + w - 4, w).start())

        def build(j, carry):
            make(2 * j)
            make(2 * j + 1)

            @pl.when(j < 4)
            def _():
                for copy in weight_copies(j):
                    copy.wait()

                @pl.when(j < 3)
                def _():
                    for copy in weight_copies(j + 1):
                        copy.start()

                total = 0.0
                for i in range(3):
                    total = total + matmul(dqkv[i], weights[j % 2, i], NT)
                dx[:, pl.ds(pl.multiple_of(j * chunk, chunk), chunk)] = total

            engine.tick(FIRST_LATE - 6 + j)
            return carry

        lax.fori_loop(0, 6, build, 0)
        for copy in loads[1:]:
            copy.wait()

        def norm_back(i, carry):
            at = pl.ds(pl.multiple_of(i * part, part), part)
            x = rows[at, :].astype(jnp.float32)
            factor = lax.rsqrt(jnp.mean(x * x, axis=-1, keepdims=True) + EPS)
            unit = x * factor
            grad_normed = dx[at, :]
            scaled = gain[...] * grad_normed
            inner = jnp.mean(scaled * unit, axis=-1, keepdims=True)
            rows[at, :] = (middle[at, :] + factor * (scaled - unit * inner)).astype(jnp.bfloat16)
            return carry + jnp.sum(grad_normed * unit, axis=0, keepdims=True)

        gain_row = lax.fori_loop(0, block // part, norm_back, jnp.zeros((1, width), jnp.float32))
        gain_buf[0, 0, 0] = gain_row
        gain_buf[0, 0, 1] = ffn_row[...]
        out_copy = pltpu.make_async_copy(rows, grad_tokens, load_sem.at[1])
        out_copy.start()

        def gain_copy(level):
            name = ("core", "x", "y", "low", "high")[level]
            return remote(
                gain_buf.at[0, level], gain_buf.at[1, level], gain_send.at[level], gain_recv.at[level], peers[name]
            )

        gain_copy(0).start()

        def mem_chunk(m):
            kind, lane = m // 4, pl.ds(pl.multiple_of((m % 4) * UNIT, UNIT), UNIT)
            pieces = []
            for src in range(seq_count // 2):
                for blk in range(2):
                    pieces.append((src, blk))
            half = (m % 4) // 2
            inside = pl.ds(pl.multiple_of((m % 2) * UNIT, UNIT), UNIT)
            values = jnp.concatenate(
                [mem_in[2 * src + half, blk, kind, :, inside] for src, blk in pieces], axis=0
            )
            table[m % 2] = matmul(pick[...], values, NN)
            pl.when(kind == 0)(lambda: pltpu.make_async_copy(table.at[m % 2], grad_mk.at[:, lane], table_sem.at[m % 2]).start())
            pl.when(kind == 1)(lambda: pltpu.make_async_copy(table.at[m % 2], grad_mv.at[:, lane], table_sem.at[m % 2]).start())

        def table_done(m):
            pltpu.make_async_copy(table.at[m % 2], grad_mk.at[:, pl.ds(0, UNIT)], table_sem.at[m % 2]).wait()

        for away in range(1, seq_count):
            source = lax.rem(seq + seq_count - away, seq_count)
            remote(mem_out.at[source], mem_in.at[source], mem_send.at[away - 1], mem_recv.at[away - 1], (source, doc)).wait_recv()
        pltpu.make_async_copy(mem_out.at[seq], mem_in.at[seq], mem_local.at[0]).wait()

        def fresh(cls, unit):
            w = unit - EARLY[0] if cls == 0 else unit - EARLY[1] + 4
            return made[w, :, :, core]

        def rest_of(step, carry):
            m = step - FIRST_LATE

            @pl.when(m < 8)
            def _():
                pl.when(m >= 2)(lambda: table_done(m))
                mem_chunk(m)

            for level in range(5):
                @pl.when(m == 2 * level + 2)
                def _():
                    gain_copy(level).wait_recv()
                    total = gain_buf[0, level] + gain_buf[1, level]
                    if level < 4:
                        gain_buf[0, level + 1] = total
                        gain_copy(level + 1).start()
                    else:
                        gains_out[...] = total

            engine.tick(step, fresh)
            return carry

        lax.fori_loop(FIRST_LATE, STEPS + 4 * SKEW, rest_of, 0)

        outs = []
        homes = [(0, u, gate_rows, u * UNIT) for u in range(8)]
        homes += [(0, 8 + u, query_rows, u * UNIT) for u in range(4)]
        homes += [(1, u, gate_rows, (8 + u) * UNIT) for u in range(3)]
        homes += [(1, 3 + u, up_rows, u * UNIT) for u in range(11)]
        homes += [(1, 14 + u, out_rows, u * UNIT) for u in range(4)]
        homes += [(1, 18 + u, key_rows, u * UNIT) for u in range(4)]
        homes += [(1, 22 + u, value_rows, u * UNIT) for u in range(4)]
        homes += [(2, u, down_rows, u * UNIT) for u in range(4)]
        for i, (cls, unit, ref, column) in enumerate(homes):
            outs.append(pltpu.make_async_copy(sums[cls].at[unit], ref.at[:, pl.ds(column, UNIT)], done_sem.at[i]))
            outs[-1].start()
        engine.drain()
        for level in range(5):
            gain_copy(level).wait_send()
        table_done(0)
        table_done(1)
        for copy in outs + [out_copy]:
            copy.wait()

    width = w_query.shape[0]
    pl.run_scoped(
        tail,
        pltpu.VMEM((width, block), low), pltpu.VMEM(picked_t.shape, low),
        pltpu.VMEM((block, width), full), pltpu.VMEM((block, width), full), pltpu.VMEM((block, width), low),
        pltpu.VMEM((2, 3, UNIT, width), low), pltpu.VMEM((12, 2, 2, 2, 2, 2, 32, UNIT), low),
        pltpu.VMEM((2, picked_t.shape[0], UNIT), full),
    )

    for away in range(1, seq_count):
        mem_copy(away).wait_send()
    for i in range(3):
        for head in range(HALF):
            mate_copy(i, head).wait_send()

    @pl.when(chip == 0)
    def _():
        for head in range(HALF):
            for blk in range(2):
                back_copy(blk, head).wait_send()

    @pl.when(chip == 1)
    def _():
        for copy in row_copies():
            copy.wait_send()
        for head in range(HALF):
            grad_copy(head, True).wait_send()
            grad_copy(head, False).wait_send()


def go_back(limit, grad, saved, weight_grads, projections, tokens, grad_middle, gain, ffn_row, placed_t, picked_t):
    block, width = grad.shape
    low, full = jnp.bfloat16, jnp.float32
    box = (2, HALF, block, HEAD_DIM)
    row = (2, HALF, 1, block)
    seq_count = lax.axis_size("seq")
    capacity = 2 * TOPK // seq_count
    dma = pltpu.SemaphoreType.DMA
    hbm, vmem = pl.BlockSpec(memory_space=pl.ANY), pl.BlockSpec(memory_space=pltpu.VMEM)
    struct = jax.ShapeDtypeStruct

    def wide(g):
        return g.reshape(2, 2, 2, 2, 2, g.shape[0] // 32, g.shape[1])

    mem = (seq_count, 2, 2, capacity, HALF * HEAD_DIM)
    scratch = [
        pltpu.VMEM(box, low), pltpu.VMEM(box, low),
        pltpu.VMEM(row, full), pltpu.VMEM(row, full), pltpu.VMEM(row, full), pltpu.VMEM(row, full),
        pltpu.VMEM((2, HALF, HEAD_DIM, block), low),
        pltpu.VMEM((3, block, width), low), pltpu.VMEM((3, HALF, block, HEAD_DIM), low),
        pltpu.VMEM(placed_t.shape, low), pltpu.VMEM(mem, low), pltpu.VMEM(mem, low),
        pltpu.VMEM((2, 5, 2, 1, width), full),
    ]
    scratch += [pltpu.VMEM((SLOTS[c], 2, 2, 2, 2, ROWS[c], UNIT), low) for c in range(3)]
    for c in range(3):
        scratch += [pltpu.VMEM((UNITS[c],) + (2,) * k + (ROWS[c], UNIT), low) for k in (4, 3, 2, 1, 0)]
    scratch += [pltpu.VMEM((UNITS[c], ROWS[c], UNIT), full) for c in range(3)]
    scratch += [dma((SLOTS[c],)) for c in range(3)]
    scratch += [dma((5, UNITS[c])) for c in range(3)] * 2
    scratch += [
        dma((8,)), dma((1, HALF)), dma((1, HALF)), dma((1, HALF)), dma((1,)),
        dma((2, HALF)), dma((2, HALF)), dma((2,)), dma((2,)), dma((2, HALF)), dma((2, HALF)),
        dma((3, HALF)), dma((3, HALF)), dma((1,)), dma((seq_count - 1,)), dma((seq_count - 1,)),
        dma((5,)), dma((5,)), dma((4,)), dma((2, 3)), dma((sum(UNITS),)), dma((2,)),
    ]
    gate, up, out, down = weight_grads
    rows = struct((32, width), full)
    mem_rows = picked_t.shape[0]
    return pl.pallas_call(
        back_kernel,
        out_shape=(
            struct((block, width), low),
            struct((32, gate.shape[1]), full), struct((32, up.shape[1]), full),
            rows, rows, rows, rows,
            struct((88, width), full), struct((2, 1, width), full),
            struct((mem_rows, width), full), struct((mem_rows, width), full),
        ),
        in_specs=[pl.BlockSpec(memory_space=pltpu.SMEM)] + [hbm] * 18 + [vmem] * 2 + [hbm] * 2,
        out_specs=(hbm,) * 8 + (vmem,) + (hbm,) * 2,
        scratch_shapes=scratch,
        name="go_back",
        compiler_params=pltpu.CompilerParams(collective_id=3, has_side_effects=True, vmem_limit_bytes=60 * 2**20),
    )(
        limit, grad, *saved, wide(gate), wide(up), wide(out), wide(down), *projections,
        tokens, grad_middle, gain, ffn_row, placed_t, picked_t,
    )


def rms_factor(values):
    return lax.rsqrt(jnp.mean(values * values, axis=-1, keepdims=True) + EPS)


def dot32(left, right):
    return jnp.dot(left, right, preferred_element_type=jnp.float32)


def fitting():
    return (lax.axis_size("seq"), lax.axis_size("doc")) == (8, 4)


def exchange(rows, owner_count, capacity):
    parts, _, width = rows.shape
    shaped = rows.reshape(parts, owner_count, capacity, width)
    moved = lax.all_to_all(shaped, "seq", split_axis=1, concat_axis=1, tiled=True)
    return moved.reshape(parts, owner_count * capacity, width)


def on_device(
    tokens,
    cotangent,
    attn_gain,
    w_query,
    w_key,
    w_value,
    w_out,
    ffn_gain,
    w_gate,
    w_up,
    w_down,
    mem_keys,
    mem_values,
    seg_len,
    mem_idx,
):
    low = jnp.bfloat16
    stream_count, block_len, model_width = tokens.shape
    mem_rows = mem_keys.shape[1]
    seq_count = lax.axis_size("seq")
    segment = lax.axis_index("seq") // BPS
    capacity = 2 * TOPK // seq_count
    slot_count = seq_count * capacity
    limit = lax.dynamic_index_in_dim(seg_len, segment, 1, keepdims=False)

    tokens_f = tokens[0].astype(jnp.float32)
    gain_one = attn_gain.astype(jnp.float32)
    gain_two = ffn_gain.astype(jnp.float32)
    factor_one = rms_factor(tokens_f)
    unit_one = tokens_f * factor_one
    normed_one = (unit_one * gain_one).astype(low)
    if fitting():
        attended, *saved, placed_t, picked_t = go_forward(
            limit, tokens[0], gain_one[None], (w_query, w_key, w_value), mem_keys[0], mem_values[0], mem_idx[0]
        )
    else:
        chosen = mem_idx[0, 0]
        owner = chosen // mem_rows
        order = jnp.arange(TOPK)
        same_before = (owner[:, None] == owner[None, :]) & (order[None, :] < order[:, None])
        slot = owner * capacity + jnp.sum(same_before.astype(jnp.int32), axis=1)
        placed = slot[:, None] == jnp.arange(slot_count)[None, :]
        request = jnp.sum(jnp.where(placed, (chosen % mem_rows)[:, None] + 1, 0), axis=0) - 1
        requested = lax.all_to_all(
            request.reshape(seq_count, capacity), "seq", split_axis=0, concat_axis=0, tiled=True
        ).reshape(slot_count)
        picked = (requested[:, None] == jnp.arange(mem_rows)[None, :]).astype(low)
        placed = placed.astype(low)
        sent = jnp.stack((dot32(picked, mem_keys[0]).astype(low), dot32(picked, mem_values[0]).astype(low)))
        arrived = exchange(sent, seq_count, capacity)
        mem_key_rows = dot32(placed, arrived[0]).astype(low)
        mem_value_rows = dot32(placed, arrived[1]).astype(low)
        queries = dot32(normed_one, w_query).astype(low)
        keys = dot32(normed_one, w_key).astype(low)
        values = dot32(normed_one, w_value).astype(low)
        attended, *saved = attend_forward(limit, queries, keys, values, mem_key_rows, mem_value_rows)
    middle = tokens_f + dot32(attended, w_out)
    factor_two = rms_factor(middle)
    unit_two = middle * factor_two
    normed_two = (unit_two * gain_two).astype(low)
    gate = dot32(normed_two, w_gate)
    upper = dot32(normed_two, w_up)
    sigma = jax.nn.sigmoid(gate)
    hidden = (gate * sigma * upper).astype(low)
    layer_out = (middle + dot32(hidden, w_down)).astype(low)

    grad_y_low = cotangent[0]
    grad_y = grad_y_low.astype(jnp.float32)
    grad_down = dot32(hidden.T, grad_y_low)
    grad_hidden = dot32(grad_y_low, w_down.T)
    grad_gate_act = (grad_hidden * upper * sigma * (1.0 + gate * (1.0 - sigma))).astype(low)
    grad_up_act = (grad_hidden * gate * sigma).astype(low)
    grad_gate = dot32(normed_two.T, grad_gate_act)
    grad_up = dot32(normed_two.T, grad_up_act)
    grad_normed_two = dot32(grad_gate_act, w_gate.T) + dot32(grad_up_act, w_up.T)
    grad_ffn_gain = jnp.sum(grad_normed_two * unit_two, axis=0)
    scaled_two = gain_two * grad_normed_two
    grad_middle = grad_y + factor_two * (
        scaled_two - unit_two * jnp.mean(scaled_two * unit_two, axis=-1, keepdims=True)
    )
    grad_branch = grad_middle.astype(low)
    grad_out = dot32(attended.T, grad_branch)
    grad_attended = dot32(grad_branch, w_out.T).astype(low)
    if fitting():
        grad_tokens, gate_rows, up_rows, query_rows, key_rows, value_rows, out_rows, down_rows, gains, grad_mem_keys, grad_mem_values = go_back(
            limit,
            grad_attended,
            saved,
            [grad.astype(low) for grad in (grad_gate, grad_up, grad_out, grad_down)],
            (w_query, w_key, w_value),
            tokens[0],
            grad_middle,
            gain_one[None],
            grad_ffn_gain[None],
            placed_t,
            picked_t,
        )
        index = lax.axis_index("seq") * lax.axis_size("doc") + lax.axis_index("doc")
        parts = gains.reshape(2, seq_count * lax.axis_size("doc"), -1)
        attn_row, ffn_row = lax.dynamic_index_in_dim(parts, index, 1, keepdims=False)
    else:
        grad_q, grad_k, grad_v, grad_mk, grad_mv = attend_backward(limit, grad_attended, saved)
        back = jnp.stack((dot32(placed.T, grad_mk).astype(low), dot32(placed.T, grad_mv).astype(low)))
        returned = exchange(back, seq_count, capacity)
        grad_mem_keys = dot32(picked.T, returned[0])
        grad_mem_values = dot32(picked.T, returned[1])
        grad_query = dot32(normed_one.T, grad_q)
        grad_key = dot32(normed_one.T, grad_k)
        grad_value = dot32(normed_one.T, grad_v)
        grad_normed_one = dot32(grad_q, w_query.T) + dot32(grad_k, w_key.T) + dot32(grad_v, w_value.T)
        grad_attn_gain = jnp.sum(grad_normed_one * unit_one, axis=0)
        scaled_one = gain_one * grad_normed_one
        grad_input = grad_middle + factor_one * (
            scaled_one - unit_one * jnp.mean(scaled_one * unit_one, axis=-1, keepdims=True)
        )
        grad_tokens = grad_input.astype(low)
        gate_rows, up_rows, query_rows, key_rows, value_rows, out_rows, down_rows, attn_row, ffn_row = [
            lax.psum_scatter(grad, ("seq", "doc"), scatter_dimension=0, tiled=True)
            for grad in (
                grad_gate, grad_up, grad_query, grad_key, grad_value, grad_out, grad_down, grad_attn_gain, grad_ffn_gain
            )
        ]
    return (
        layer_out[None],
        grad_tokens[None],
        attn_row,
        query_rows,
        key_rows,
        value_rows,
        out_rows,
        ffn_row,
        gate_rows,
        up_rows,
        down_rows,
        grad_mem_keys[None],
        grad_mem_values[None],
    )


def solution(mesh):
    in_specs = (
        P("doc", "seq", None),
        P("doc", "seq", None),
        P(),
        P(),
        P(),
        P(),
        P(),
        P(),
        P(),
        P(),
        P(),
        P("doc", "seq", None),
        P("doc", "seq", None),
        P("doc", None),
        P("doc", "seq", None),
    )
    out_specs = (
        P("doc", "seq", None),
        P("doc", "seq", None),
        P(("seq", "doc")),
        P(("seq", "doc"), None),
        P(("seq", "doc"), None),
        P(("seq", "doc"), None),
        P(("seq", "doc"), None),
        P(("seq", "doc")),
        P(("seq", "doc"), None),
        P(("seq", "doc"), None),
        P(("seq", "doc"), None),
        P("doc", "seq", None),
        P("doc", "seq", None),
    )
    return jax.shard_map(
        on_device, mesh=mesh, in_specs=in_specs, out_specs=out_specs, check_vma=False
    )
```

```python
import functools
import math

import jax
import jax.numpy as jnp
from jax import lax
from jax.experimental import pallas as pl
from jax.experimental.pallas import tpu as pltpu
from jax.sharding import PartitionSpec as P

HEADS = 8
HEAD_DIM = 128
TOPK = 128
BPS = 4
NEG = -1000000000.0
MESH = pl.DeviceIdType.MESH
EPS = 1e-05
UNIT = 256
SKEW = 4


def flip(value, bit):
    return value + bit - 2 * bit * ((value // bit) % 2)


HALF = HEADS // 2
LOG2E = math.log2(math.e)
SCALE = HEAD_DIM ** (-0.5)
NT = (((1,), (1,)), ((), ()))
TN = (((0,), (0,)), ((), ()))
NN = (((1,), (0,)), ((), ()))


def matmul(left, right, dims):
    return lax.dot_general(left, right, dims, preferred_element_type=jnp.float32)


def seats():
    seq, doc = lax.axis_index("seq"), lax.axis_index("doc")
    core, chip = seq % 2, (seq // 2) % 2
    mate = (flip(seq, 1), doc)
    across = (flip(seq, 2), doc)
    diagonal = (flip(flip(seq, 2), 1), doc)
    return core, chip, mate, across, diagonal


def meet(peers):
    barrier = pltpu.get_barrier_semaphore()
    for peer in peers:
        pl.semaphore_signal(barrier, inc=1, device_id=peer, device_id_type=MESH)
    pl.semaphore_wait(barrier, len(peers))


def head_lanes(core, head):
    return pl.ds(pl.multiple_of((core * HALF + head) * HEAD_DIM, HEAD_DIM), HEAD_DIM)


def remote(src, dst, send, recv, peer):
    return pltpu.make_async_remote_copy(
        src_ref=src, dst_ref=dst, send_sem=send, recv_sem=recv, device_id=peer, device_id_type=MESH
    )


def share_heads(sources, boxes, core, mate, local_sem, send_sem, recv_sem):
    copies = []
    for i, (source, box) in enumerate(zip(sources, boxes)):
        for head in range(HALF):
            copies.append(
                remote(
                    source.at[:, head_lanes(1 - core, head)],
                    box.at[core, head],
                    send_sem.at[i, head],
                    recv_sem.at[i, head],
                    mate,
                )
            )
            copies[-1].start()
    for i, (source, box) in enumerate(zip(sources, boxes)):
        for head in range(HALF):
            copies.append(
                pltpu.make_async_copy(
                    source.at[:, head_lanes(core, head)], box.at[core, head], local_sem.at[i, head]
                )
            )
            copies[-1].start()
    return copies


def masked(scores, first_key, limit, diagonal):
    key = lax.broadcasted_iota(jnp.int32, scores.shape, 0)
    ok = key + first_key < limit
    if diagonal:
        ok = ok & (key <= lax.broadcasted_iota(jnp.int32, scores.shape, 1))
    return jnp.where(ok, scores, NEG)


def soften(parts):
    top = functools.reduce(
        jnp.maximum, [jnp.max(scores, axis=0, keepdims=True) for scores, _ in parts]
    )
    total, mixed = 0.0, 0.0
    for scores, values in parts:
        exponent = jnp.exp2(scores - top)
        total = total + jnp.sum(exponent, axis=0, keepdims=True)
        mixed = mixed + matmul(values, exponent.astype(jnp.bfloat16), TN)
    return mixed / total, top + jnp.log(total) * LOG2E


def forward_kernel(
    limit_ref, q, k, v, mk, mv,
    attended, qb, kb, vb, qx, mkb, mvb, ob, lse,
    mixed_own, mixed_out, mixed_in, lse_out, lse_in,
    local_sem, mate_send, mate_recv, far_send, far_recv, back_send, back_recv, end_sem,
):
    core, chip, mate, across, diagonal = seats()
    block = q.shape[0]
    limit = limit_ref[0]
    meet((mate, across, diagonal))

    def query_copy(head, own):
        return remote(
            q.at[:, head_lanes(core if own else 1 - core, head)],
            qx.at[core, head],
            far_send.at[0 if own else 1, head],
            far_recv.at[core, head],
            across if own else diagonal,
        )

    def arrived_query(far, head):
        return remote(
            q.at[:, head_lanes(core, head)], qx.at[far, head], far_send.at[0, head], far_recv.at[far, head], across
        )

    @pl.when(chip == 1)
    def _():
        for head in range(HALF):
            query_copy(head, True).start()
            query_copy(head, False).start()

    copies = share_heads((q, k, v, mk, mv), (qb, kb, vb, mkb, mvb), core, mate, local_sem, mate_send, mate_recv)
    for copy in copies:
        copy.wait()

    def own_part(blk, head):
        query = qb[blk, head]
        parts = []
        for kblk in range(blk + 1):
            scores = matmul(kb[kblk, head], query, NT) * (SCALE * LOG2E)
            scores = masked(scores, (2 * chip + kblk) * block, limit, kblk == blk)
            parts.append((scores, vb[kblk, head]))
        parts.append((matmul(mkb[blk, head], query, NT) * (SCALE * LOG2E), mvb[blk, head]))
        return soften(parts)

    for blk in range(2):
        def own_head(head, carry):
            mixed, level = own_part(blk, head)
            mixed_own[blk, head] = mixed
            lse[blk, head] = level
            return carry
        lax.fori_loop(0, HALF, own_head, 0)

    def back_copy(blk, head):
        return (
            remote(mixed_out.at[blk, head], mixed_in.at[blk, head], back_send.at[0, blk, head], back_recv.at[0, blk, head], across),
            remote(lse_out.at[blk, head], lse_in.at[blk, head], back_send.at[1, blk, head], back_recv.at[1, blk, head], across),
        )

    @pl.when(chip == 0)
    def _():
        def cross(i, carry):
            head, blk = i // 2, i % 2
            arrived_query(blk, head).wait_recv()
            query = qx[blk, head]
            parts = []
            for kblk in range(2):
                scores = matmul(kb[kblk, head], query, NT) * (SCALE * LOG2E)
                parts.append((masked(scores, kblk * block, limit, False), vb[kblk, head]))
            mixed, level = soften(parts)
            mixed_out[blk, head] = mixed.astype(jnp.bfloat16)
            lse_out[blk, head] = level
            for copy in back_copy(blk, head):
                copy.start()
            return carry
        lax.fori_loop(0, 2 * HALF, cross, 0)

        def finish(i, carry):
            head, blk = i // 2, i % 2
            ob[blk, head] = mixed_own[blk, head].T.astype(jnp.bfloat16)
            return carry
        lax.fori_loop(0, 2 * HALF, finish, 0)

    @pl.when(chip == 1)
    def _():
        def merge(i, carry):
            head, blk = i // 2, i % 2
            for copy in back_copy(blk, head):
                copy.wait_recv()
            near, far = lse[blk, head], lse_in[blk, head]
            top = jnp.maximum(near, far)
            near, far = jnp.exp2(near - top), jnp.exp2(far - top)
            total = near + far
            mixed = (mixed_own[blk, head] * near + mixed_in[blk, head].astype(jnp.float32) * far) / total
            ob[blk, head] = mixed.T.astype(jnp.bfloat16)
            lse[blk, head] = top + jnp.log(total) * LOG2E
            return carry
        lax.fori_loop(0, 2 * HALF, merge, 0)

    ends = []
    for head in range(HALF):
        ends.append(
            remote(ob.at[1 - core, head], attended.at[:, head_lanes(core, head)], end_sem.at[0, head], end_sem.at[1, head], mate)
        )
        ends.append(
            pltpu.make_async_copy(ob.at[core, head], attended.at[:, head_lanes(core, head)], end_sem.at[2, head])
        )
    for copy in ends:
        copy.start()
    for copy in ends:
        copy.wait()

    @pl.when(chip == 0)
    def _():
        for head in range(HALF):
            for blk in range(2):
                for copy in back_copy(blk, head):
                    copy.wait_send()

    @pl.when(chip == 1)
    def _():
        for head in range(HALF):
            query_copy(head, True).wait_send()
            query_copy(head, False).wait_send()


def attend_forward(limit, queries, keys, values, mem_keys, mem_values):
    block, width = queries.shape
    topk = mem_keys.shape[0]
    low, full = jnp.bfloat16, jnp.float32
    box = (2, HALF, block, HEAD_DIM)
    mem_box = (2, HALF, topk, HEAD_DIM)
    flat = (2, HALF, HEAD_DIM, block)
    row = (2, HALF, 1, block)
    dma = pltpu.SemaphoreType.DMA
    hbm, vmem = pl.BlockSpec(memory_space=pl.ANY), pl.BlockSpec(memory_space=pltpu.VMEM)
    struct = jax.ShapeDtypeStruct
    return pl.pallas_call(
        forward_kernel,
        out_shape=(
            struct((block, width), low),
            struct(box, low), struct(box, low), struct(box, low), struct(box, low),
            struct(mem_box, low), struct(mem_box, low), struct(box, low), struct(row, full),
        ),
        in_specs=[pl.BlockSpec(memory_space=pltpu.SMEM)] + [hbm] * 5,
        out_specs=(hbm,) + (vmem,) * 8,
        scratch_shapes=[
            pltpu.VMEM(flat, full), pltpu.VMEM(flat, low), pltpu.VMEM(flat, low),
            pltpu.VMEM(row, full), pltpu.VMEM(row, full),
            dma((5, HALF)), dma((5, HALF)), dma((5, HALF)),
            dma((2, HALF)), dma((2, HALF)), dma((2, 2, HALF)), dma((2, 2, HALF)), dma((3, HALF)),
        ],
        name="attend_forward",
        compiler_params=pltpu.CompilerParams(collective_id=1, has_side_effects=True, vmem_limit_bytes=56 * 2**20),
    )(limit, queries, keys, values, mem_keys, mem_values)


def backward_kernel(
    limit_ref, grad, qb, kb, vb, qx, mkb, mvb, ob, lse,
    dq, dk, dv, dmk, dmv,
    gb, gx, delta, lse_in, delta_in, dq_own, dq_out, dq_in, dk_sum, dv_sum, dmk_low, dmv_low, dqb, dkb, dvb,
    local_sem, mate_send, mate_recv, far_send, far_recv, row_send, row_recv, back_send, back_recv,
    end_local, end_send, end_recv,
):
    core, chip, mate, across, diagonal = seats()
    block = grad.shape[0]
    limit = limit_ref[0]
    meet((mate, across, diagonal))

    def grad_copy(head, own):
        return remote(
            grad.at[:, head_lanes(core if own else 1 - core, head)],
            gx.at[core, head],
            far_send.at[0 if own else 1, head],
            far_recv.at[core, head],
            across if own else diagonal,
        )

    def arrived_grad(far, head):
        return remote(
            grad.at[:, head_lanes(core, head)], gx.at[far, head], far_send.at[0, head], far_recv.at[far, head], across
        )

    def row_copies():
        return (
            remote(lse, lse_in, row_send.at[0], row_recv.at[0], across),
            remote(delta, delta_in, row_send.at[1], row_recv.at[1], across),
        )

    @pl.when(chip == 1)
    def _():
        for head in range(HALF):
            grad_copy(head, True).start()
            grad_copy(head, False).start()

    copies = share_heads((grad,), (gb,), core, mate, local_sem, mate_send, mate_recv)
    for copy in copies:
        copy.wait()

    def rows(i, carry):
        head, blk = i // 2, i % 2
        product = gb[blk, head].astype(jnp.float32) * ob[blk, head].astype(jnp.float32)
        delta[blk, head] = jnp.sum(product.T, axis=0, keepdims=True)
        return carry

    lax.fori_loop(0, 2 * HALF, rows, 0)

    @pl.when(chip == 1)
    def _():
        for copy in row_copies():
            copy.start()

    def pull(key_rows, value_rows, query, grad_rows, level, inner, where):
        scores = matmul(key_rows, query, NT) * (SCALE * LOG2E)
        if where is not None:
            scores = masked(scores, where[0], limit, where[1])
        weights = jnp.exp2(scores - level)
        grad_weights = matmul(value_rows, grad_rows, NT)
        grad_scores = (weights * (grad_weights - inner)).astype(jnp.bfloat16)
        return (
            matmul(grad_scores, query, NN),
            matmul(weights.astype(jnp.bfloat16), grad_rows, NN),
            matmul(key_rows, grad_scores, TN),
        )

    for blk in range(2):
        def own_head(head, carry):
            query, grad_rows = qb[blk, head], gb[blk, head]
            level, inner = lse[blk, head], delta[blk, head]
            total = 0.0
            for kblk in range(blk + 1):
                gk, gv, gq = pull(
                    kb[kblk, head], vb[kblk, head], query, grad_rows, level, inner,
                    ((2 * chip + kblk) * block, kblk == blk),
                )
                if kblk == blk:
                    dk_sum[kblk, head], dv_sum[kblk, head] = gk, gv
                else:
                    dk_sum[kblk, head] += gk
                    dv_sum[kblk, head] += gv
                total = total + gq
            gk, gv, gq = pull(mkb[blk, head], mvb[blk, head], query, grad_rows, level, inner, None)
            dmk_low[blk, head] = (gk * SCALE).astype(jnp.bfloat16)
            dmv_low[blk, head] = gv.astype(jnp.bfloat16)
            dq_own[blk, head] = total + gq
            return carry
        lax.fori_loop(0, HALF, own_head, 0)

    def back_copy(blk, head):
        return remote(dq_out.at[blk, head], dq_in.at[blk, head], back_send.at[blk, head], back_recv.at[blk, head], across)

    @pl.when(chip == 0)
    def _():
        for copy in row_copies():
            copy.wait_recv()

        def cross(i, carry):
            head, blk = i // 2, i % 2
            arrived_grad(blk, head).wait_recv()
            query, grad_rows = qx[blk, head], gx[blk, head]
            level, inner = lse_in[blk, head], delta_in[blk, head]
            total = 0.0
            for kblk in range(2):
                gk, gv, gq = pull(
                    kb[kblk, head], vb[kblk, head], query, grad_rows, level, inner, (kblk * block, False)
                )
                dk_sum[kblk, head] += gk
                dv_sum[kblk, head] += gv
                total = total + gq
            dq_out[blk, head] = total.astype(jnp.bfloat16)
            back_copy(blk, head).start()
            return carry
        lax.fori_loop(0, 2 * HALF, cross, 0)

    def finish(i, carry):
        head, blk = i // 2, i % 2
        dqb[blk, head] = (dq_own[blk, head].T * SCALE).astype(jnp.bfloat16)
        dkb[blk, head] = (dk_sum[blk, head] * SCALE).astype(jnp.bfloat16)
        dvb[blk, head] = dv_sum[blk, head].astype(jnp.bfloat16)
        return carry

    @pl.when(chip == 1)
    def _():
        def merge(i, carry):
            head, blk = i // 2, i % 2
            back_copy(blk, head).wait_recv()
            dq_own[blk, head] += dq_in[blk, head].astype(jnp.float32)
            return finish(i, carry)
        lax.fori_loop(0, 2 * HALF, merge, 0)

    @pl.when(chip == 0)
    def _():
        lax.fori_loop(0, 2 * HALF, finish, 0)

    ends = []
    for i, (box, out) in enumerate(((dqb, dq), (dkb, dk), (dvb, dv), (dmk_low, dmk), (dmv_low, dmv))):
        for head in range(HALF):
            lanes = head_lanes(core, head)
            ends.append(remote(box.at[1 - core, head], out.at[:, lanes], end_send.at[i, head], end_recv.at[i, head], mate))
            ends.append(pltpu.make_async_copy(box.at[core, head], out.at[:, lanes], end_local.at[i, head]))
    for copy in ends:
        copy.start()
    for copy in ends:
        copy.wait()

    @pl.when(chip == 0)
    def _():
        for head in range(HALF):
            for blk in range(2):
                back_copy(blk, head).wait_send()

    @pl.when(chip == 1)
    def _():
        for copy in row_copies():
            copy.wait_send()
        for head in range(HALF):
            grad_copy(head, True).wait_send()
            grad_copy(head, False).wait_send()


def attend_backward(limit, grad, saved):
    block, width = grad.shape
    topk = saved[4].shape[2]
    low, full = jnp.bfloat16, jnp.float32
    box = (2, HALF, block, HEAD_DIM)
    mem_box = (2, HALF, topk, HEAD_DIM)
    flat = (2, HALF, HEAD_DIM, block)
    row = (2, HALF, 1, block)
    dma = pltpu.SemaphoreType.DMA
    hbm, vmem = pl.BlockSpec(memory_space=pl.ANY), pl.BlockSpec(memory_space=pltpu.VMEM)
    struct = jax.ShapeDtypeStruct
    return pl.pallas_call(
        backward_kernel,
        out_shape=(struct((block, width), low),) * 3 + (struct((topk, width), low),) * 2,
        in_specs=[pl.BlockSpec(memory_space=pltpu.SMEM), hbm] + [vmem] * 8,
        out_specs=(hbm,) * 5,
        scratch_shapes=[
            pltpu.VMEM(box, low), pltpu.VMEM(box, low),
            pltpu.VMEM(row, full), pltpu.VMEM(row, full), pltpu.VMEM(row, full),
            pltpu.VMEM(flat, full), pltpu.VMEM(flat, low), pltpu.VMEM(flat, low),
            pltpu.VMEM(box, full), pltpu.VMEM(box, full),
            pltpu.VMEM(mem_box, low), pltpu.VMEM(mem_box, low),
            pltpu.VMEM(box, low), pltpu.VMEM(box, low), pltpu.VMEM(box, low),
            dma((1, HALF)), dma((1, HALF)), dma((1, HALF)),
            dma((2, HALF)), dma((2, HALF)), dma((2,)), dma((2,)),
            dma((2, HALF)), dma((2, HALF)),
            dma((5, HALF)), dma((5, HALF)), dma((5, HALF)),
        ],
        name="attend_backward",
        compiler_params=pltpu.CompilerParams(collective_id=2, has_side_effects=True, vmem_limit_bytes=56 * 2**20),
    )(limit, grad, *saved)


def keep_order(rank_of):
    before = lax.broadcasted_iota(jnp.int32, (rank_of, rank_of), 0)
    return (before < lax.broadcasted_iota(jnp.int32, (rank_of, rank_of), 1)).astype(jnp.bfloat16)


def front_kernel(
    limit_ref, tokens, gain, w_query, w_key, w_value, mem_keys, mem_values, wanted,
    attended, qb, kb, vb, qx, mkb, mvb, ob, lse, spots, pick_t,
    rows, weights, normed, qkv, tables, every, pick, mem_out, mem_in,
    mixed_own, mixed_out, mixed_in, lse_out, lse_in,
    load_sem, want_send, want_recv, mem_send, mem_recv, mem_local,
    local_sem, mate_send, mate_recv, far_send, far_recv, back_send, back_recv, end_sem,
):
    core, chip, mate, across, diagonal = seats()
    seq, doc = lax.axis_index("seq"), lax.axis_index("doc")
    seq_count, capacity = mem_in.shape[0], mem_in.shape[3]
    block, width = tokens.shape
    mem_rows, topk = tables.shape[1], every.shape[2]
    limit = limit_ref[0]

    loads = [
        pltpu.make_async_copy(src, dst, load_sem.at[i])
        for i, (src, dst) in enumerate(
            (
                (wanted, every.at[seq]), (tokens, rows), (w_query, weights.at[0]), (w_key, weights.at[1]),
                (w_value, weights.at[2]), (mem_keys, tables.at[0]), (mem_values, tables.at[1]),
            )
        )
    ]
    for copy in loads:
        copy.start()
    meet([(lax.rem(seq + away, seq_count), doc) for away in range(1, seq_count)])
    loads[0].wait()

    def want_copy(away):
        return remote(
            every.at[seq], every.at[seq], want_send.at[away - 1], want_recv.at[away - 1],
            (lax.rem(seq + away, seq_count), doc),
        )

    def want_arrival(away):
        source = lax.rem(seq + seq_count - away, seq_count)
        return remote(every.at[source], every.at[source], want_send.at[away - 1], want_recv.at[away - 1], (source, doc))

    def mem_copy(away):
        peer = lax.rem(seq + away, seq_count)
        return remote(mem_out.at[peer], mem_in.at[seq], mem_send.at[away - 1], mem_recv.at[away - 1], (peer, doc))

    def mem_arrival(away):
        source = lax.rem(seq + seq_count - away, seq_count)
        return remote(mem_out.at[source], mem_in.at[source], mem_send.at[away - 1], mem_recv.at[away - 1], (source, doc))

    for away in range(1, seq_count):
        want_copy(away).start()
    loads[1].wait()
    part = 64

    def norm(i, carry):
        at = pl.ds(pl.multiple_of(i * part, part), part)
        x = rows[at, :].astype(jnp.float32)
        factor = lax.rsqrt(jnp.mean(x * x, axis=-1, keepdims=True) + EPS)
        normed[at, :] = (x * factor * gain[...]).astype(jnp.bfloat16)
        return carry

    lax.fori_loop(0, block // part, norm, 0)

    def project(i):
        loads[2 + i].wait()

        def one(j, carry):
            lanes = pl.ds(pl.multiple_of(j * UNIT, UNIT), UNIT)
            qkv[i, :, lanes] = matmul(normed[...], weights[i, :, lanes], NN).astype(jnp.bfloat16)
            return carry

        lax.fori_loop(0, width // UNIT, one, 0)

    project(0)

    def query_copy(head, own):
        return remote(
            qkv.at[0, :, head_lanes(core if own else 1 - core, head)],
            qx.at[core, head],
            far_send.at[0 if own else 1, head],
            far_recv.at[core, head],
            across if own else diagonal,
        )

    def arrived_query(far, head):
        return remote(
            qkv.at[0, :, head_lanes(core, head)], qx.at[far, head], far_send.at[0, head], far_recv.at[far, head], across
        )

    @pl.when(chip == 1)
    def _():
        for head in range(HALF):
            query_copy(head, True).start()
            query_copy(head, False).start()

    project(1)
    project(2)
    copies = share_heads(
        (qkv.at[0], qkv.at[1], qkv.at[2]), (qb, kb, vb), core, mate, local_sem, mate_send, mate_recv
    )

    for away in range(1, seq_count):
        want_arrival(away).wait_recv()
    triangle = keep_order(topk)
    asked = every[:, 0, :]
    here = asked - seq * mem_rows
    mine = (here >= 0) & (here < mem_rows)
    before = matmul(mine.astype(jnp.bfloat16), triangle, NN).astype(jnp.int32)
    place = lax.broadcasted_iota(jnp.int32, (capacity, topk), 0)
    line = lax.broadcasted_iota(jnp.int32, (mem_rows, topk), 0)
    for b in range(seq_count):
        at_place = jnp.where((before[b : b + 1] == place) & (here[b : b + 1] >= 0) & (here[b : b + 1] < mem_rows), 1.0, 0.0)
        at_line = jnp.where(here[b : b + 1] == line, 1.0, 0.0)
        pick[b * capacity : (b + 1) * capacity, :] = matmul(
            at_place.astype(jnp.bfloat16), at_line.astype(jnp.bfloat16), NT
        ).astype(jnp.bfloat16)
    half = HALF * HEAD_DIM
    for kind in range(2):
        loads[5 + kind].wait()
        for side in range(2):
            found = matmul(pick[...], tables[kind, :, side * half : (side + 1) * half], NN).astype(jnp.bfloat16)
            for b in range(seq_count):
                mem_out[2 * (b // 2) + side, b % 2, kind] = found[b * capacity : (b + 1) * capacity]
    for away in range(1, seq_count):
        mem_copy(away).start()
    own_rows = pltpu.make_async_copy(mem_out.at[seq], mem_in.at[seq], mem_local.at[0])
    own_rows.start()
    pick_t[...] = pick[...].astype(jnp.float32).T.astype(jnp.bfloat16)
    seat = lax.broadcasted_iota(jnp.int32, (seq_count, topk), 0)
    slot_at = lax.broadcasted_iota(jnp.int32, (seq_count * capacity, topk), 0)
    for blk in range(2):
        away_rows = every[2 * (seq // 2) + blk] - seat * mem_rows
        owner = (away_rows >= 0) & (away_rows < mem_rows)
        rank = matmul(owner.astype(jnp.bfloat16), triangle, NN).astype(jnp.int32)
        slot = jnp.sum(jnp.where(owner, seat * capacity + rank, 0), axis=0, keepdims=True)
        spots[blk] = jnp.where(slot == slot_at, 1.0, 0.0).astype(jnp.bfloat16)

    for copy in copies:
        copy.wait()

    def own_head(blk, head):
        query = qb[blk, head]
        parts = []
        for kblk in range(blk + 1):
            scores = matmul(kb[kblk, head], query, NT) * (SCALE * LOG2E)
            scores = masked(scores, (2 * chip + kblk) * block, limit, kblk == blk)
            parts.append((scores, vb[kblk, head]))
        mixed_own[blk, head], lse[blk, head] = soften(parts)

    def back_copy(blk, head):
        return (
            remote(mixed_out.at[blk, head], mixed_in.at[blk, head], back_send.at[0, blk, head], back_recv.at[0, blk, head], across),
            remote(lse_out.at[blk, head], lse_in.at[blk, head], back_send.at[1, blk, head], back_recv.at[1, blk, head], across),
        )

    def heads(head, carry):
        @pl.when(chip == 0)
        def _():
            def cross(blk, carry):
                arrived_query(blk, head).wait_recv()
                query = qx[blk, head]
                parts = []
                for kblk in range(2):
                    scores = matmul(kb[kblk, head], query, NT) * (SCALE * LOG2E)
                    parts.append((masked(scores, kblk * block, limit, False), vb[kblk, head]))
                mixed, level = soften(parts)
                mixed_out[blk, head] = mixed.astype(jnp.bfloat16)
                lse_out[blk, head] = level
                for copy in back_copy(blk, head):
                    copy.start()
                return carry

            lax.fori_loop(0, 2, cross, 0)

        own_head(0, head)
        own_head(1, head)
        return carry

    lax.fori_loop(0, HALF, heads, 0)

    for away in range(1, seq_count):
        mem_arrival(away).wait_recv()
    own_rows.wait()
    for blk in range(2):
        for kind, box in enumerate((mkb, mvb)):
            found = mem_in[:, blk, kind].reshape(seq_count * capacity, half)
            found = matmul(spots[blk], found, TN).astype(jnp.bfloat16)
            for head in range(HALF):
                box[blk, head] = found[:, head * HEAD_DIM : (head + 1) * HEAD_DIM]

    def blend(pieces):
        top = functools.reduce(jnp.maximum, [level for _, level in pieces])
        total, mixed = 0.0, 0.0
        for value, level in pieces:
            share = jnp.exp2(level - top)
            total = total + share
            mixed = mixed + value * share
        return mixed / total, top + jnp.log(total) * LOG2E

    def finish(i, carry):
        head, blk = i // 2, i % 2
        scores = matmul(mkb[blk, head], qb[blk, head], NT) * (SCALE * LOG2E)
        pieces = [(mixed_own[blk, head], lse[blk, head]), soften([(scores, mvb[blk, head])])]

        @pl.when(chip == 0)
        def _():
            mixed, lse[blk, head] = blend(pieces)
            ob[blk, head] = mixed.T.astype(jnp.bfloat16)

        @pl.when(chip == 1)
        def _():
            for copy in back_copy(blk, head):
                copy.wait_recv()
            far = (mixed_in[blk, head].astype(jnp.float32), lse_in[blk, head])
            mixed, lse[blk, head] = blend(pieces + [far])
            ob[blk, head] = mixed.T.astype(jnp.bfloat16)

        return carry

    lax.fori_loop(0, 2 * HALF, finish, 0)

    ends = []
    for head in range(HALF):
        ends.append(
            remote(ob.at[1 - core, head], attended.at[:, head_lanes(core, head)], end_sem.at[0, head], end_sem.at[1, head], mate)
        )
        ends.append(
            pltpu.make_async_copy(ob.at[core, head], attended.at[:, head_lanes(core, head)], end_sem.at[2, head])
        )
    for copy in ends:
        copy.start()
    for copy in ends:
        copy.wait()
    for away in range(1, seq_count):
        want_copy(away).wait_send()
        mem_copy(away).wait_send()

    @pl.when(chip == 0)
    def _():
        for head in range(HALF):
            for blk in range(2):
                for copy in back_copy(blk, head):
                    copy.wait_send()

    @pl.when(chip == 1)
    def _():
        for head in range(HALF):
            query_copy(head, True).wait_send()
            query_copy(head, False).wait_send()


def go_forward(limit, tokens, gain, projections, mem_keys, mem_values, wanted):
    block, width = tokens.shape
    mem_rows, topk = mem_keys.shape[0], wanted.shape[1]
    seq_count = lax.axis_size("seq")
    capacity = 2 * topk // seq_count
    slots = seq_count * capacity
    low, full = jnp.bfloat16, jnp.float32
    box = (2, HALF, block, HEAD_DIM)
    mem_box = (2, HALF, topk, HEAD_DIM)
    flat = (2, HALF, HEAD_DIM, block)
    row = (2, HALF, 1, block)
    mem = (seq_count, 2, 2, capacity, HALF * HEAD_DIM)
    dma = pltpu.SemaphoreType.DMA
    hbm, vmem = pl.BlockSpec(memory_space=pl.ANY), pl.BlockSpec(memory_space=pltpu.VMEM)
    struct = jax.ShapeDtypeStruct
    return pl.pallas_call(
        front_kernel,
        out_shape=(
            struct((block, width), low),
            struct(box, low), struct(box, low), struct(box, low), struct(box, low),
            struct(mem_box, low), struct(mem_box, low), struct(box, low), struct(row, full),
            struct((2, slots, topk), low), struct((mem_rows, slots), low),
        ),
        in_specs=[pl.BlockSpec(memory_space=pltpu.SMEM), hbm, vmem] + [hbm] * 6,
        out_specs=(hbm,) + (vmem,) * 10,
        scratch_shapes=[
            pltpu.VMEM((block, width), low), pltpu.VMEM((3, width, width), low), pltpu.VMEM((block, width), low),
            pltpu.VMEM((3, block, width), low), pltpu.VMEM((2, mem_rows, width), low),
            pltpu.VMEM((seq_count, 1, topk), jnp.int32), pltpu.VMEM((slots, mem_rows), low),
            pltpu.VMEM(mem, low), pltpu.VMEM(mem, low),
            pltpu.VMEM(flat, full), pltpu.VMEM(flat, low), pltpu.VMEM(flat, low),
            pltpu.VMEM(row, full), pltpu.VMEM(row, full),
            dma((7,)), dma((seq_count - 1,)), dma((seq_count - 1,)), dma((seq_count - 1,)), dma((seq_count - 1,)), dma((1,)),
            dma((3, HALF)), dma((3, HALF)), dma((3, HALF)),
            dma((2, HALF)), dma((2, HALF)), dma((2, 2, HALF)), dma((2, 2, HALF)), dma((3, HALF)),
        ],
        name="go_forward",
        compiler_params=pltpu.CompilerParams(collective_id=4, has_side_effects=True, vmem_limit_bytes=56 * 2**20),
    )(limit, tokens, gain, *projections, mem_keys, mem_values, wanted)


ALONG = (("x", "y", "low", "high"), ("y", "x", "low", "high"), ("low", "high", "y", "x"), ("low", "high", "x", "y"))
TURNS = (1, 1, 3, 3, 1, 1, 2, 3, 0, 1, 0, 1, 1, 3, 3, 0, 1, 0, 0, 1, 2, 1, 2, 2, 2, 2, 3, 1, 1, 3, 1, 1, 3, 0, 1, 1, 0, 2, 2, 1, 1, 2)
PLAN = (
    (),
    ((0, 0), (1, 0),),
    ((2, 0), (3, 0),),
    ((0, 1), (4, 0), (5, 0),),
    ((1, 1), (2, 1), (6, 0), (7, 0), (0, 2),),
    ((3, 1), (4, 1), (8, 0), (9, 0), (1, 2),),
    ((5, 1), (10, 0), (11, 0), (6, 1), (2, 2), (4, 2),),
    ((9, 1), (12, 0), (7, 1), (13, 0), (8, 1), (0, 3), (5, 2),),
    ((11, 1), (1, 3), (14, 0), (15, 0), (10, 1), (4, 3), (3, 2), (2, 3),),
    ((12, 1), (16, 0), (9, 2), (17, 0), (8, 2), (6, 2), (11, 2), (10, 2), (2, 4), (13, 1),),
    ((18, 0), (5, 3), (19, 0), (7, 2), (15, 1), (0, 4), (3, 3), (1, 4), (16, 1), (12, 2), (14, 1),),
    ((6, 3), (20, 0), (9, 3), (21, 0),),
    ((8, 3), (4, 4), (11, 3), (17, 1), (10, 3), (19, 1),),
    ((15, 2), (3, 4), (18, 1), (12, 3),),
    ((7, 3), (16, 2), (13, 2), (6, 4), (21, 1), (5, 4),),
    (),
    ((19, 2), (17, 2), (22, 0), (20, 1),),
    (),
    ((23, 0), (18, 2), (14, 2), (7, 4), (24, 0), (15, 3), (9, 4), (25, 0),),
    ((8, 4), (16, 3), (11, 4), (19, 3),),
    ((10, 4), (17, 3), (12, 4),),
    ((13, 3),),
    (),
    ((22, 1), (21, 2), (38, 0), (14, 3), (13, 4),),
    (),
    ((39, 0), (14, 4),),
    ((23, 1), (20, 2), (18, 3), (40, 0), (24, 1),),
    (),
    ((41, 0), (15, 4), (25, 1),),
    (),
    ((39, 1), (16, 4), (20, 3), (19, 4), (21, 3), (17, 4),),
    (),
    ((22, 2),),
    (),
    ((40, 1), (39, 2), (38, 1), (20, 4),),
    (),
    ((23, 2),),
    ((18, 4), (22, 3),),
    ((23, 3), (24, 2),),
    ((41, 1), (24, 3),),
    (),
    ((39, 3),),
    ((25, 2), (21, 4), (40, 2),),
    (),
    ((25, 3),),
    ((26, 0), (27, 0),),
    ((28, 0), (29, 0),),
    ((30, 0), (31, 0), (38, 2), (32, 0),),
    ((40, 3), (33, 0), (34, 0), (27, 1), (35, 0), (22, 4),),
    ((36, 0), (26, 1), (37, 0),),
    ((28, 1), (23, 4),),
    ((29, 1), (41, 2), (30, 1),),
    ((24, 4), (25, 4), (32, 1), (39, 4),),
    ((31, 1), (33, 1), (38, 3),),
    ((40, 4), (27, 2), (37, 1),),
    ((34, 1), (26, 2), (36, 1),),
    ((28, 2), (27, 3), (35, 1), (30, 2), (29, 2), (41, 3), (28, 3), (31, 2), (38, 4), (33, 2), (30, 3), (32, 2), (34, 2), (36, 2), (31, 3), (26, 3), (33, 3), (37, 2), (35, 2), (34, 3), (27, 4), (29, 3), (26, 4), (36, 3), (28, 4), (41, 4), (30, 4), (37, 3), (32, 3), (35, 3), (29, 4), (31, 4), (33, 4), (37, 4), (32, 4), (34, 4), (36, 4), (35, 4),),
)
OFFERED = (20, 22, 24, 26)
RING = 8
NARROW = 38
ROWS = (32, 88)


def taken(unit, level):
    return [(unit, level) in events for events in PLAN].index(True)


class Sums:
    def __init__(self, down, made, own, stages, sums, local_sem, send_sem, recv_sem, peers):
        self.down, self.made, self.own, self.stages, self.sums = down, made, own, stages, sums
        self.local_sem, self.send_sem, self.recv_sem = local_sem, send_sem, recv_sem
        self.peers = peers
        seq, doc = lax.axis_index("seq"), lax.axis_index("doc")
        self.bits = {
            "core": seq % 2,
            "x": (seq // 2) % 2,
            "y": (seq // 4) % 2,
            "low": doc % 2,
            "high": (doc // 2) % 2,
        }

    def core_copy(self, kind, index):
        if kind == 0:
            source = self.made.at[index % RING, :, :, 1 - self.bits["core"]]
        else:
            source = self.down.at[:, :, 1 - self.bits["core"], :, :, :, pl.ds(index * UNIT, UNIT)]
        return remote(
            source,
            self.stages[kind][0].at[index],
            self.send_sem[kind].at[0, index],
            self.recv_sem[kind].at[0, index],
            self.peers["core"],
        )

    def own_copy(self, index):
        return pltpu.make_async_copy(
            self.down.at[:, :, self.bits["core"], :, :, :, pl.ds(index * UNIT, UNIT)],
            self.own.at[index % 2],
            self.local_sem.at[index % 2],
        )

    def put(self, unit, value):
        pl.when(unit >= RING)(lambda: self.core_copy(0, jnp.maximum(unit - RING, 0)).wait_send())
        self.made[unit % RING] = value.astype(jnp.bfloat16).reshape(self.made.shape[1:])
        self.core_copy(0, unit).start()

    def offer_down(self, index):
        self.core_copy(1, index).start()
        if index < 2 or taken(NARROW + index - 2, 0) < OFFERED[index]:
            self.own_copy(index).start()

    def half(self, kind, index, order, level, mine):
        name = order[level]
        left = [axis for axis in ("y", "x", "high", "low") if axis not in order[:level]]
        side = self.bits[name] if mine else 1 - self.bits[name]
        return (index,) + (slice(None),) * left.index(name) + (side,)

    def copy(self, kind, index, order, level):
        return remote(
            self.stages[kind][level - 1].at[self.half(kind, index, order, level - 1, False)],
            self.stages[kind][level].at[index],
            self.send_sem[kind].at[level, index],
            self.recv_sem[kind].at[level, index],
            self.peers[order[level - 1]],
        )

    def arrive(self, unit, level):
        kind = 0 if unit < NARROW else 1
        index = unit - kind * NARROW
        order = ALONG[TURNS[unit]]
        ref = self.stages[kind][level]
        if level == 0:
            self.core_copy(kind, index).wait_recv()
            if kind == 1:
                self.own_copy(index).wait()

            def add(i, carry):
                y, x = i // 2, i % 2
                mine = self.made[index % RING, y, x, self.bits["core"]] if kind == 0 else self.own[index % 2, y, x]
                ref[index, y, x] = ref[index, y, x] + mine
                return carry

            lax.fori_loop(0, 4, add, 0)
            if kind == 1 and index < 2 and taken(unit, 0) >= OFFERED[index + 2]:
                self.own_copy(index + 2).start()
        else:
            self.copy(kind, index, order, level).wait_recv()
            kept = self.stages[kind][level - 1][self.half(kind, index, order, level - 1, True)]
            if level < 4:
                ref[index] = ref[index] + kept
            else:
                self.sums[kind][index] = ref[index].astype(jnp.float32) + kept.astype(jnp.float32)
        if level < 4:
            self.copy(kind, index, order, level + 1).start()

    def run(self, place):
        for unit, level in PLAN[place]:
            self.arrive(unit, level)

    def run_turn(self, first, turn, count):
        for k in range(count):
            if PLAN[first + k]:
                pl.when(turn == k)(lambda: self.run(first + k))

    def drain(self):
        for kind, count in enumerate((NARROW, 4)):
            def one(index, carry):
                pl.when((kind == 1) | (index >= NARROW - RING))(lambda: self.core_copy(kind, index).wait_send())
                for level in range(1, 5):
                    self.copy(kind, index, ALONG[0], level).wait_send()
                return carry

            lax.fori_loop(0, count, one, 0)


def back_kernel(
    limit_ref, mixed_in, qb_in, kb_in, vb_in, qx_in, mkb_in, mvb_in, ob_in, lse_in0, spots_in,
    tokens, cotangent, w_query, w_key, w_value, w_out, w_gate, w_up, w_down, gain, gain_two,
    layer_out, grad_tokens, gate_rows, up_rows, query_rows, key_rows, value_rows, out_rows, down_rows, gains_out,
    mem_home, down, grad, middle_kept, grad_middle,
    gb, gx, lse, delta, lse_in, delta_in, dq_cross, dqkv, mem_in, gain_buf, made, own, *rest,
):
    stages = [rest[5 * c : 5 * c + 5] for c in range(2)]
    sums = rest[10:12]
    local_sem, send_sems, recv_sems, rest = rest[12], rest[13:15], rest[15:17], rest[17:]
    (
        in_sem, gb_local, gb_send, gb_recv, spot_sem, far_send, far_recv, row_send, row_recv, back_send, back_recv,
        mate_send, mate_recv, mem_local, mem_send, mem_recv, gain_send, gain_recv, load_sem, weight_sem, done_sem, front_sem, tile_sem, stage_sem,
    ) = rest
    core, chip, mate, across, diagonal = seats()
    seq, doc = lax.axis_index("seq"), lax.axis_index("doc")
    seq_count = mem_in.shape[0]
    block = grad.shape[0]
    limit = limit_ref[0]
    peers = {
        "core": mate,
        "x": across,
        "y": (flip(seq, 4), doc),
        "low": (seq, flip(doc, 1)),
        "high": (seq, flip(doc, 2)),
    }
    others = [(lax.rem(seq + away, seq_count), doc) for away in range(1, seq_count)]
    meet(others + [peers["low"], peers["high"]])
    engine = Sums(down, made, own, stages, sums, local_sem, send_sems, recv_sems, peers)

    def grad_copy(head, own):
        return remote(
            grad.at[:, head_lanes(core if own else 1 - core, head)],
            gx.at[core, head],
            far_send.at[0 if own else 1, head],
            far_recv.at[core, head],
            across if own else diagonal,
        )

    def arrived_grad(far, head):
        return remote(
            grad.at[:, head_lanes(core, head)], gx.at[far, head], far_send.at[0, head], far_recv.at[far, head], across
        )

    def row_copies():
        return (
            remote(lse, lse_in, row_send.at[0], row_recv.at[0], across),
            remote(delta, delta_in, row_send.at[1], row_recv.at[1], across),
        )

    def back_copy(blk, head):
        return remote(dq_cross.at[blk, head], dq_cross.at[blk, head], back_send.at[blk, head], back_recv.at[blk, head], across)

    def mate_copy(box, i, head):
        lanes = head_lanes(core, head)
        return remote(box.at[i, head], dqkv.at[i, :, lanes], mate_send.at[i, head], mate_recv.at[i, head], mate)

    def mate_arrival(i, head):
        lanes = head_lanes(1 - core, head)
        return remote(gb.at[0, head], dqkv.at[i, :, lanes], mate_send.at[i, head], mate_recv.at[i, head], mate)

    def mem_copy(box, away):
        peer = lax.rem(seq + away, seq_count)
        return remote(box.at[peer], mem_in.at[seq], mem_send.at[away - 1], mem_recv.at[away - 1], (peer, doc))

    def far_start(head):
        @pl.when(chip == 1)
        def _():
            grad_copy(head, True).start()
            grad_copy(head, False).start()

    def front(normed, normed_t, grad_y, total, back, hidden_t, mixed):
        width = total.shape[1]
        tiles = w_gate.shape[1] // UNIT
        part = 128
        copies = [
            pltpu.make_async_copy(mixed_in, mixed, front_sem.at[0]),
            pltpu.make_async_copy(cotangent, grad_y, front_sem.at[1]),
        ]
        for copy in copies:
            copy.start()

        def strip(i):
            return pl.ds(pl.multiple_of(i * UNIT, UNIT), UNIT)

        def chunk(i):
            return pl.ds(pl.multiple_of(i * part, part), part)

        def opening(rows, weights, middle):
            loads = [
                pltpu.make_async_copy(tokens, rows, front_sem.at[2]),
                pltpu.make_async_copy(w_out, weights, front_sem.at[3]),
            ]
            for copy in loads:
                copy.start()
            for copy in copies + loads:
                copy.wait()

            def join(j, carry):
                middle[:, strip(j)] = rows[:, strip(j)].astype(jnp.float32) + matmul(mixed[...], weights[:, strip(j)], NN)
                return carry

            lax.fori_loop(0, width // UNIT, join, 0)
            keep = pltpu.make_async_copy(middle, middle_kept, front_sem.at[4])
            keep.start()

            def norm(i, carry):
                x = middle[chunk(i), :]
                factor = lax.rsqrt(jnp.mean(x * x, axis=-1, keepdims=True) + EPS)
                value = x * factor * gain_two[...]
                normed[chunk(i), :] = value.astype(jnp.bfloat16)
                normed_t[:, chunk(i)] = value.T.astype(jnp.bfloat16)
                total[chunk(i), :] = jnp.zeros((part, width), jnp.float32)
                back[chunk(i), :] = jnp.zeros((part, width), jnp.float32)
                return carry

            lax.fori_loop(0, block // part, norm, 0)
            keep.wait()

        pl.run_scoped(
            opening,
            pltpu.VMEM(tokens.shape, jnp.bfloat16), pltpu.VMEM(w_out.shape, jnp.bfloat16), pltpu.VMEM(total.shape, jnp.float32),
        )

        def hidden_units(w_in, w_back):
            def loads(tile):
                slot = tile % 2
                return (
                    pltpu.make_async_copy(w_gate.at[:, strip(tile)], w_in.at[slot, 0], tile_sem.at[slot, 0]),
                    pltpu.make_async_copy(w_up.at[:, strip(tile)], w_in.at[slot, 1], tile_sem.at[slot, 1]),
                    pltpu.make_async_copy(w_down.at[strip(tile), :], w_back.at[slot], tile_sem.at[slot, 2]),
                )

            for copy in loads(0):
                copy.start()

            def one(tile, carry):
                slot = tile % 2

                @pl.when(tile + 1 < tiles)
                def _():
                    for copy in loads(tile + 1):
                        copy.start()

                for copy in loads(tile):
                    copy.wait()
                opened = matmul(normed[...], w_in[slot, 0], NN)
                upper = matmul(normed[...], w_in[slot, 1], NN)
                sigma = 1.0 / (1.0 + jnp.exp(-opened))
                gated = opened * sigma
                hidden = gated * upper
                total[...] += matmul(hidden.astype(jnp.bfloat16), w_back[slot], NN)
                hidden_t[strip(tile), :] = hidden.T.astype(jnp.bfloat16)
                grad_hidden = matmul(grad_y[...], w_back[slot], NT)
                grad_opened = (grad_hidden * upper * sigma * (1.0 + opened * (1.0 - sigma))).astype(jnp.bfloat16)
                grad_upper = (grad_hidden * gated).astype(jnp.bfloat16)
                back[...] += matmul(grad_opened, w_in[slot, 0], NT) + matmul(grad_upper, w_in[slot, 1], NT)
                for kind, value in enumerate((grad_opened, grad_upper)):
                    engine.put(2 * tile + kind, matmul(normed_t[...], value, NN))
                engine.run_turn(0, tile, tiles)
                return carry

            lax.fori_loop(0, tiles, one, 0)

        pl.run_scoped(
            hidden_units,
            pltpu.VMEM((2, 2, width, UNIT), jnp.bfloat16), pltpu.VMEM((2, UNIT, width), jnp.bfloat16),
        )

        def closing(middle, weights, branch, branch_back, stage_down):
            loads = [
                pltpu.make_async_copy(middle_kept, middle, front_sem.at[2]),
                pltpu.make_async_copy(w_out, weights, front_sem.at[3]),
            ]
            for copy in loads:
                copy.start()
            engine.run(11)
            for copy in loads:
                copy.wait()

            def norm_back(i, carry):
                x = middle[chunk(i), :]
                factor = lax.rsqrt(jnp.mean(x * x, axis=-1, keepdims=True) + EPS)
                unit = x * factor
                grad_normed = back[chunk(i), :]
                normed[chunk(i), :] = (x + total[chunk(i), :]).astype(jnp.bfloat16)
                scaled = gain_two[...] * grad_normed
                inner = jnp.mean(scaled * unit, axis=-1, keepdims=True)
                value = grad_y[chunk(i), :].astype(jnp.float32) + factor * (scaled - unit * inner)
                middle[chunk(i), :] = value
                branch[chunk(i), :] = value.astype(jnp.bfloat16)
                return carry + jnp.sum(grad_normed * unit, axis=0, keepdims=True)

            gain_buf[0, 0, 1] = lax.fori_loop(0, block // part, norm_back, jnp.zeros((1, width), jnp.float32))
            writes = [
                pltpu.make_async_copy(normed, layer_out, front_sem.at[0]),
                pltpu.make_async_copy(middle, grad_middle, front_sem.at[2]),
            ]
            for copy in writes:
                copy.start()

            engine.run(12)

            def to_attended(j, carry):
                branch_back[:, strip(j)] = matmul(branch[...], weights[strip(j), :], NT).astype(jnp.bfloat16)
                return carry

            lax.fori_loop(0, width // UNIT, to_attended, 0)
            store = pltpu.make_async_copy(branch_back, grad, front_sem.at[1])
            store.start()
            engine.run(13)
            store.wait()
            far_start(0)
            share_heads((grad,), (gb,), core, mate, gb_local, gb_send, gb_recv)

            def turn_over(i, carry):
                normed_t[:, chunk(i)] = mixed[chunk(i), :].astype(jnp.float32).T.astype(jnp.bfloat16)
                return carry

            lax.fori_loop(0, block // part, turn_over, 0)

            for j in range(4):
                engine.put(jnp.int32(22 + j), matmul(normed_t[...], branch[:, j * UNIT : (j + 1) * UNIT], NN))
                engine.run(14 + j)
            deep = stage_down.shape[4]
            tall = 8 * deep

            def down_store(n):
                i = n % 4
                return pltpu.make_async_copy(
                    stage_down.at[n % 2], down.at[i // 2, i % 2, :, :, :, :, strip(n // 4)], stage_sem.at[n % 2]
                )

            def down_part(n):
                i, j = n % 4, n // 4
                value = matmul(hidden_t[pl.ds(pl.multiple_of(i * tall, 64), tall), :], grad_y[:, strip(j)], NN)
                pl.when(n > 1)(lambda: down_store(n - 2).wait())
                for k in range(8):
                    stage_down[n % 2, k // 4, (k // 2) % 2, k % 2] = value[k * deep : (k + 1) * deep].astype(jnp.bfloat16)
                down_store(n).start()

            def down_parts(m, carry):
                down_part(2 * m)
                down_part(2 * m + 1)
                for j in range(3):
                    pl.when(m == 2 * j + 2)(lambda: engine.offer_down(j))
                pl.when(m == 1)(lambda: far_start(1))
                pl.when(m == 4)(lambda: far_start(2))
                engine.run_turn(18, m, 8)
                return carry

            lax.fori_loop(0, 8, down_parts, 0)
            down_store(14).wait()
            down_store(15).wait()
            engine.offer_down(3)
            far_start(3)
            for copy in writes:
                copy.wait()

        pl.run_scoped(
            closing,
            pltpu.VMEM(total.shape, jnp.float32), pltpu.VMEM(w_out.shape, jnp.bfloat16),
            pltpu.VMEM(normed.shape, jnp.bfloat16), pltpu.VMEM(normed.shape, jnp.bfloat16),
            pltpu.VMEM((2, 2, 2, 2, ROWS[1], UNIT), jnp.bfloat16),
        )

    pl.run_scoped(
        front,
        pltpu.VMEM(tokens.shape, jnp.bfloat16), pltpu.VMEM((tokens.shape[1], block), jnp.bfloat16),
        pltpu.VMEM(tokens.shape, jnp.bfloat16), pltpu.VMEM(tokens.shape, jnp.float32), pltpu.VMEM(tokens.shape, jnp.float32),
        pltpu.VMEM((w_gate.shape[1], block), jnp.bfloat16), pltpu.VMEM(tokens.shape, jnp.bfloat16),
    )

    def attention(qb, kb, vb, qx, mkb, mvb, ob, dq_own, dk_sum, dv_sum, dm, dqkv_mate, mem_out, spots):
        inputs = [
            pltpu.make_async_copy(src, dst, in_sem.at[i])
            for i, (src, dst) in enumerate(
                ((qb_in, qb), (kb_in, kb), (vb_in, vb), (mkb_in, mkb), (mvb_in, mvb), (ob_in, ob), (lse_in0, lse), (qx_in, qx))
            )
        ]
        spot_copies = [pltpu.make_async_copy(spots_in, spots, spot_sem.at[0])]
        for copy in inputs + spot_copies:
            copy.start()
        for head in range(HALF):
            remote(grad.at[:, head_lanes(core, head)], gb.at[core, head], gb_send.at[0, head], gb_recv.at[0, head], mate).wait()
            pltpu.make_async_copy(grad.at[:, head_lanes(core, head)], gb.at[core, head], gb_local.at[0, head]).wait()
        for copy in inputs + spot_copies:
            copy.wait()
        engine.run(26)

        def rows(i, carry):
            head, blk = i // 2, i % 2
            product = gb[blk, head].astype(jnp.float32) * ob[blk, head].astype(jnp.float32)
            delta[blk, head] = jnp.sum(product.T, axis=0, keepdims=True)
            return carry

        lax.fori_loop(0, 2 * HALF, rows, 0)

        @pl.when(chip == 1)
        def _():
            for copy in row_copies():
                copy.start()

        def pull(key_rows, value_rows, query, grad_rows, level, inner, where):
            scores = matmul(key_rows, query, NT) * (SCALE * LOG2E)
            if where is not None:
                scores = masked(scores, where[0], limit, where[1])
            weights = jnp.exp2(scores - level)
            grad_weights = matmul(value_rows, grad_rows, NT)
            grad_scores = (weights * (grad_weights - inner)).astype(jnp.bfloat16)
            return (
                matmul(grad_scores, query, NN),
                matmul(weights.astype(jnp.bfloat16), grad_rows, NN),
                matmul(key_rows, grad_scores, TN),
            )

        def own_head(head, carry):
            lanes = pl.ds(pl.multiple_of(head * HEAD_DIM, HEAD_DIM), HEAD_DIM)
            for blk in range(2):
                query, grad_rows = qb[blk, head], gb[blk, head]
                level, inner = lse[blk, head], delta[blk, head]
                total = 0.0
                for kblk in range(blk + 1):
                    gk, gv, gq = pull(
                        kb[kblk, head], vb[kblk, head], query, grad_rows, level, inner,
                        ((2 * chip + kblk) * block, kblk == blk),
                    )
                    if kblk == blk:
                        dk_sum[kblk, head], dv_sum[kblk, head] = gk, gv
                    else:
                        dk_sum[kblk, head] += gk
                        dv_sum[kblk, head] += gv
                    total = total + gq
                gk, gv, gq = pull(mkb[blk, head], mvb[blk, head], query, grad_rows, level, inner, None)
                dm[blk, 0, :, lanes] = (gk * SCALE).astype(jnp.bfloat16)
                dm[blk, 1, :, lanes] = gv.astype(jnp.bfloat16)
                dq_own[blk, head] = total + gq
            engine.run_turn(27, head, HALF)
            return carry

        lax.fori_loop(0, HALF, own_head, 0)

        for blk in range(2):
            for kind in range(2):
                rows_out = matmul(spots[blk], dm[blk, kind], NN).astype(jnp.bfloat16)
                mem_out[:, blk, kind] = rows_out.reshape(mem_out.shape[0], mem_out.shape[3], mem_out.shape[4])
        for away in range(1, seq_count):
            mem_copy(mem_out, away).start()
        own_rows = pltpu.make_async_copy(mem_out.at[seq], mem_in.at[seq], mem_local.at[0])
        own_rows.start()
        engine.run(31)

        @pl.when(chip == 0)
        def _():
            for copy in row_copies():
                copy.wait_recv()

        def far_turn(i, carry):
            head, blk = i // 2, i % 2

            @pl.when(chip == 0)
            def _():
                arrived_grad(blk, head).wait_recv()
                query, grad_rows = qx[blk, head], gx[blk, head]
                level, inner = lse_in[blk, head], delta_in[blk, head]
                total = 0.0
                for kblk in range(2):
                    gk, gv, gq = pull(
                        kb[kblk, head], vb[kblk, head], query, grad_rows, level, inner, (kblk * block, False)
                    )
                    dk_sum[kblk, head] += gk
                    dv_sum[kblk, head] += gv
                    total = total + gq
                dq_cross[blk, head] = total.astype(jnp.bfloat16)
                back_copy(blk, head).start()

            engine.run_turn(32, i, 2 * HALF)

            @pl.when(chip == 1)
            def _():
                back_copy(blk, head).wait_recv()
                dq_own[blk, head] += dq_cross[blk, head].astype(jnp.float32)

            return carry

        lax.fori_loop(0, 2 * HALF, far_turn, 0)

        def results(blk, head):
            return (
                (dq_own[blk, head].T * SCALE).astype(jnp.bfloat16),
                (dk_sum[blk, head] * SCALE).astype(jnp.bfloat16),
                dv_sum[blk, head].astype(jnp.bfloat16),
            )

        def for_mate(head, carry):
            for i, value in enumerate(results(1 - core, head)):
                dqkv_mate[i, head] = value
                mate_copy(dqkv_mate, i, head).start()
            return carry

        def for_own(head, carry):
            for i, value in enumerate(results(core, head)):
                dqkv[i, :, head_lanes(core, head)] = value
            return carry

        lax.fori_loop(0, HALF, for_mate, 0)
        engine.run(40)
        lax.fori_loop(0, HALF, for_own, 0)
        engine.run(41)
        for away in range(1, seq_count):
            mem_copy(mem_out, away).wait_send()
        own_rows.wait()
        for i in range(3):
            for head in range(HALF):
                mate_copy(dqkv_mate, i, head).wait_send()

    box = (2, HALF, block, HEAD_DIM)
    mem_box = mkb_in.shape
    low, full = jnp.bfloat16, jnp.float32
    pl.run_scoped(
        attention,
        pltpu.VMEM(box, low), pltpu.VMEM(box, low), pltpu.VMEM(box, low), pltpu.VMEM(box, low),
        pltpu.VMEM(mem_box, low), pltpu.VMEM(mem_box, low), pltpu.VMEM(box, low),
        pltpu.VMEM((2, HALF, HEAD_DIM, block), full), pltpu.VMEM(box, full), pltpu.VMEM(box, full),
        pltpu.VMEM((2, 2, mem_box[2], HALF * HEAD_DIM), low),
        pltpu.VMEM((3, HALF, block, HEAD_DIM), low), pltpu.VMEM(mem_in.shape, low), pltpu.VMEM(spots_in.shape, low),
    )

    def tail(normed, dx, middle, rows, weights):
        width = dx.shape[1]
        chunk = weights.shape[2]
        loads = [
            pltpu.make_async_copy(tokens, rows, load_sem.at[1]),
            pltpu.make_async_copy(grad_middle, middle, load_sem.at[2]),
        ]

        def weight_copies(j):
            at = pl.ds(pl.multiple_of(j * chunk, chunk), chunk)
            return [
                pltpu.make_async_copy(w.at[at, :], weights.at[j % 2, i], weight_sem.at[j % 2, i])
                for i, w in enumerate((w_query, w_key, w_value))
            ]

        for copy in loads + weight_copies(0):
            copy.start()
        loads[0].wait()
        part = 64

        def norm(i, carry):
            at = pl.ds(pl.multiple_of(i * 2 * part, 2 * part), 2 * part)
            x = rows[at, :].astype(jnp.float32)
            factor = lax.rsqrt(jnp.mean(x * x, axis=-1, keepdims=True) + EPS)
            normed[:, at] = (x * factor * gain[...]).T.astype(jnp.bfloat16)
            return carry

        lax.fori_loop(0, block // (2 * part), norm, 0)
        for i in range(3):
            for head in range(HALF):
                mate_arrival(i, head).wait_recv()
        engine.run(42)

        def make(w):
            lanes = pl.ds(pl.multiple_of(lax.rem(w, 4) * UNIT, UNIT), UNIT)
            engine.put(26 + w, matmul(normed[...], dqkv[w // 4, :, lanes], NN))

        def build(j, carry):
            make(2 * j)
            make(2 * j + 1)
            engine.run_turn(43, j, 6)
            return carry

        lax.fori_loop(0, 6, build, 0)

        def input_part(j, carry):
            for copy in weight_copies(j):
                copy.wait()

            @pl.when(j < 3)
            def _():
                for copy in weight_copies(j + 1):
                    copy.start()

            total = 0.0
            for i in range(3):
                total = total + matmul(dqkv[i], weights[j % 2, i], NT)
            dx[:, pl.ds(pl.multiple_of(j * chunk, chunk), chunk)] = total
            engine.run_turn(49, j, 4)
            return carry

        lax.fori_loop(0, 4, input_part, 0)
        loads[1].wait()

        def norm_back(i, carry):
            at = pl.ds(pl.multiple_of(i * part, part), part)
            x = rows[at, :].astype(jnp.float32)
            factor = lax.rsqrt(jnp.mean(x * x, axis=-1, keepdims=True) + EPS)
            unit = x * factor
            grad_normed = dx[at, :]
            scaled = gain[...] * grad_normed
            inner = jnp.mean(scaled * unit, axis=-1, keepdims=True)
            rows[at, :] = (middle[at, :] + factor * (scaled - unit * inner)).astype(jnp.bfloat16)
            return carry + jnp.sum(grad_normed * unit, axis=0, keepdims=True)

        gain_buf[0, 0, 0] = lax.fori_loop(0, block // part, norm_back, jnp.zeros((1, width), jnp.float32))
        out_copy = pltpu.make_async_copy(rows, grad_tokens, load_sem.at[1])
        out_copy.start()

        def gain_copy(level):
            name = ("core", "x", "y", "low", "high")[level]
            return remote(
                gain_buf.at[0, level], gain_buf.at[1, level], gain_send.at[level], gain_recv.at[level], peers[name]
            )

        gain_copy(0).start()
        engine.run(53)
        for away in range(1, seq_count):
            source = lax.rem(seq + seq_count - away, seq_count)
            remote(mem_in.at[source], mem_in.at[source], mem_send.at[away - 1], mem_recv.at[away - 1], (source, doc)).wait_recv()
        mem_copy_out = pltpu.make_async_copy(mem_in, mem_home, load_sem.at[2])
        mem_copy_out.start()
        engine.run(54)
        engine.run(55)
        events = PLAN[56]
        stops = [len(events) * k // 6 for k in range(1, 6)]
        for n, (unit, level) in enumerate(events):
            for step in range(5):
                if n == stops[step]:
                    gain_copy(step).wait_recv()
                    total = gain_buf[0, step] + gain_buf[1, step]
                    if step < 4:
                        gain_buf[0, step + 1] = total
                        gain_copy(step + 1).start()
                    else:
                        gains_out[...] = total
            engine.arrive(unit, level)
        homes = []
        for u in range(11):
            homes += [(0, 2 * u, gate_rows, u), (0, 2 * u + 1, up_rows, u)]
        for j in range(4):
            homes += [(0, 22 + j, out_rows, j), (0, 26 + j, query_rows, j), (0, 30 + j, key_rows, j), (0, 34 + j, value_rows, j)]
            homes.append((1, j, down_rows, j))
        outs = []
        for i, (kind, unit, ref, place) in enumerate(homes):
            outs.append(
                pltpu.make_async_copy(sums[kind].at[unit], ref.at[:, pl.ds(place * UNIT, UNIT)], done_sem.at[i])
            )
            outs[-1].start()
        engine.drain()
        for level in range(5):
            gain_copy(level).wait_send()
        for copy in outs + [out_copy, mem_copy_out]:
            copy.wait()

    width = w_query.shape[0]
    pl.run_scoped(
        tail,
        pltpu.VMEM((width, block), low),
        pltpu.VMEM((block, width), full), pltpu.VMEM((block, width), full), pltpu.VMEM((block, width), low),
        pltpu.VMEM((2, 3, UNIT, width), low),
    )

    @pl.when(chip == 0)
    def _():
        for head in range(HALF):
            for blk in range(2):
                back_copy(blk, head).wait_send()

    @pl.when(chip == 1)
    def _():
        for copy in row_copies():
            copy.wait_send()
        for head in range(HALF):
            grad_copy(head, True).wait_send()
            grad_copy(head, False).wait_send()


def go_back(limit, attended, saved, tokens, cotangent, weights, gain, gain_two):
    block, width = tokens.shape
    low, full = jnp.bfloat16, jnp.float32
    box = (2, HALF, block, HEAD_DIM)
    row = (2, HALF, 1, block)
    seq_count = lax.axis_size("seq")
    capacity = 2 * TOPK // seq_count
    dma = pltpu.SemaphoreType.DMA
    hbm, vmem = pl.BlockSpec(memory_space=pl.ANY), pl.BlockSpec(memory_space=pltpu.VMEM)
    struct = jax.ShapeDtypeStruct
    ff = weights[4].shape[1]
    *saved, picked_t = saved
    spots = saved[8]

    def wide(rows, columns):
        return struct((2, 2, 2, 2, 2, rows, columns), low)

    mem = (seq_count, 2, 2, capacity, HALF * HEAD_DIM)
    units = (NARROW, 4)
    scratch = [
        pltpu.VMEM(box, low), pltpu.VMEM(box, low),
        pltpu.VMEM(row, full), pltpu.VMEM(row, full), pltpu.VMEM(row, full), pltpu.VMEM(row, full),
        pltpu.VMEM((2, HALF, HEAD_DIM, block), low),
        pltpu.VMEM((3, block, width), low), pltpu.VMEM(mem, low),
        pltpu.VMEM((2, 5, 2, 1, width), full),
        pltpu.VMEM((RING, 2, 2, 2, 2, 2, ROWS[0], UNIT), low),
        pltpu.VMEM((2, 2, 2, 2, 2, ROWS[1], UNIT), low),
    ]
    for c in range(2):
        scratch += [pltpu.VMEM((units[c],) + (2,) * k + (ROWS[c], UNIT), low) for k in (4, 3, 2, 1, 0)]
    scratch += [pltpu.VMEM((units[c], ROWS[c], UNIT), full) for c in range(2)]
    scratch += [dma((2,))]
    scratch += [dma((5, units[c])) for c in range(2)] * 2
    scratch += [
        dma((8,)), dma((1, HALF)), dma((1, HALF)), dma((1, HALF)), dma((1,)),
        dma((2, HALF)), dma((2, HALF)), dma((2,)), dma((2,)), dma((2, HALF)), dma((2, HALF)),
        dma((3, HALF)), dma((3, HALF)), dma((1,)), dma((seq_count - 1,)), dma((seq_count - 1,)),
        dma((5,)), dma((5,)), dma((4,)), dma((2, 3)), dma((sum(units),)),
        dma((5,)), dma((2, 3)), dma((2,)),
    ]
    rows = struct((32, width), full)
    mem_rows = picked_t.shape[0]
    results = pl.pallas_call(
        back_kernel,
        out_shape=(
            struct((block, width), low), struct((block, width), low),
            struct((32, ff), full), struct((32, ff), full),
            rows, rows, rows, rows,
            struct((88, width), full), struct((2, 1, width), full),
            struct(mem, low),
            wide(88, width),
            struct((block, width), low), struct((block, width), full), struct((block, width), full),
        ),
        in_specs=[pl.BlockSpec(memory_space=pltpu.SMEM)] + [hbm] * 19 + [vmem] * 2,
        out_specs=(hbm,) * 9 + (vmem,) + (hbm,) * 5,
        scratch_shapes=scratch,
        name="go_back",
        compiler_params=pltpu.CompilerParams(collective_id=3, has_side_effects=True, vmem_limit_bytes=60 * 2**20),
    )(limit, attended, *saved, tokens, cotangent, *weights, gain, gain_two)
    return deliver(results[:9], results[10], picked_t) + (results[9],)


def deliver_kernel(*refs):
    sources, mem_home, picked_t = refs[:9], refs[9], refs[10]
    targets, tables = refs[11:20], refs[20:22]
    boxes, rest = refs[22:31], refs[31:]
    rows, pick, table, in_sem, out_sem, load_sem, table_sem = rest
    loads = [
        pltpu.make_async_copy(mem_home, rows, load_sem.at[0]),
        pltpu.make_async_copy(picked_t, pick, load_sem.at[1]),
    ]
    ins = [pltpu.make_async_copy(a, b, in_sem.at[i]) for i, (a, b) in enumerate(zip(sources, boxes))]
    outs = [pltpu.make_async_copy(a, b, out_sem.at[i]) for i, (a, b) in enumerate(zip(boxes, targets))]
    for copy in loads + ins:
        copy.start()
    for copy in loads:
        copy.wait()
    half = rows.shape[4]
    stores = []
    for kind in range(2):
        for side in range(2):
            values = jnp.concatenate(
                [rows[2 * src + side, blk, kind] for src in range(rows.shape[0] // 2) for blk in range(2)], axis=0
            )
            table[2 * kind + side] = matmul(pick[...], values, NN)
            stores.append(
                pltpu.make_async_copy(
                    table.at[2 * kind + side],
                    tables[kind].at[:, side * half : (side + 1) * half],
                    table_sem.at[2 * kind + side],
                )
            )
            stores[-1].start()
    for arrived, left in zip(ins, outs):
        arrived.wait()
        left.start()
    for copy in stores + outs:
        copy.wait()


def deliver(arrays, mem_home, picked_t):
    struct = jax.ShapeDtypeStruct
    hbm = pl.BlockSpec(memory_space=pl.ANY)
    mem_rows, half = picked_t.shape[0], mem_home.shape[4]
    table = struct((mem_rows, 2 * half), jnp.float32)
    return tuple(
        pl.pallas_call(
            deliver_kernel,
            out_shape=tuple(struct(a.shape, a.dtype) for a in arrays) + (table, table),
            in_specs=[hbm] * 11,
            out_specs=(hbm,) * 11,
            scratch_shapes=[pltpu.VMEM(a.shape, a.dtype) for a in arrays] + [
                pltpu.VMEM(mem_home.shape, jnp.bfloat16), pltpu.VMEM(picked_t.shape, jnp.bfloat16),
                pltpu.VMEM((4, mem_rows, half), jnp.float32),
                pltpu.SemaphoreType.DMA((9,)), pltpu.SemaphoreType.DMA((9,)), pltpu.SemaphoreType.DMA((2,)), pltpu.SemaphoreType.DMA((4,)),
            ],
            name="deliver",
            compiler_params=pltpu.CompilerParams(vmem_limit_bytes=60 * 2**20),
        )(*arrays, mem_home, picked_t)
    )


def rms_factor(values):
    return lax.rsqrt(jnp.mean(values * values, axis=-1, keepdims=True) + EPS)


def dot32(left, right):
    return jnp.dot(left, right, preferred_element_type=jnp.float32)


def fitting():
    return (lax.axis_size("seq"), lax.axis_size("doc")) == (8, 4)


def exchange(rows, owner_count, capacity):
    parts, _, width = rows.shape
    shaped = rows.reshape(parts, owner_count, capacity, width)
    moved = lax.all_to_all(shaped, "seq", split_axis=1, concat_axis=1, tiled=True)
    return moved.reshape(parts, owner_count * capacity, width)


def on_device(
    tokens,
    cotangent,
    attn_gain,
    w_query,
    w_key,
    w_value,
    w_out,
    ffn_gain,
    w_gate,
    w_up,
    w_down,
    mem_keys,
    mem_values,
    seg_len,
    mem_idx,
):
    low = jnp.bfloat16
    stream_count, block_len, model_width = tokens.shape
    mem_rows = mem_keys.shape[1]
    seq_count = lax.axis_size("seq")
    segment = lax.axis_index("seq") // BPS
    capacity = 2 * TOPK // seq_count
    slot_count = seq_count * capacity
    limit = lax.dynamic_index_in_dim(seg_len, segment, 1, keepdims=False)

    gain_one = attn_gain.astype(jnp.float32)
    gain_two = ffn_gain.astype(jnp.float32)
    if fitting():
        attended, *saved = go_forward(
            limit, tokens[0], gain_one[None], (w_query, w_key, w_value), mem_keys[0], mem_values[0], mem_idx[0]
        )
        layer_out, grad_tokens, gate_rows, up_rows, query_rows, key_rows, value_rows, out_rows, down_rows, grad_mk, grad_mv, gains = go_back(
            limit,
            attended,
            saved,
            tokens[0],
            cotangent[0],
            (w_query, w_key, w_value, w_out, w_gate, w_up, w_down),
            gain_one[None],
            gain_two[None],
        )
        index = lax.axis_index("seq") * lax.axis_size("doc") + lax.axis_index("doc")
        parts = gains.reshape(2, seq_count * lax.axis_size("doc"), -1)
        attn_row, ffn_row = lax.dynamic_index_in_dim(parts, index, 1, keepdims=False)
        return (
            layer_out[None],
            grad_tokens[None],
            attn_row,
            query_rows,
            key_rows,
            value_rows,
            out_rows,
            ffn_row,
            gate_rows,
            up_rows,
            down_rows,
            grad_mk[None],
            grad_mv[None],
        )

    tokens_f = tokens[0].astype(jnp.float32)
    factor_one = rms_factor(tokens_f)
    unit_one = tokens_f * factor_one
    normed_one = (unit_one * gain_one).astype(low)
    chosen = mem_idx[0, 0]
    owner = chosen // mem_rows
    order = jnp.arange(TOPK)
    same_before = (owner[:, None] == owner[None, :]) & (order[None, :] < order[:, None])
    slot = owner * capacity + jnp.sum(same_before.astype(jnp.int32), axis=1)
    placed = slot[:, None] == jnp.arange(slot_count)[None, :]
    request = jnp.sum(jnp.where(placed, (chosen % mem_rows)[:, None] + 1, 0), axis=0) - 1
    requested = lax.all_to_all(
        request.reshape(seq_count, capacity), "seq", split_axis=0, concat_axis=0, tiled=True
    ).reshape(slot_count)
    picked = (requested[:, None] == jnp.arange(mem_rows)[None, :]).astype(low)
    placed = placed.astype(low)
    sent = jnp.stack((dot32(picked, mem_keys[0]).astype(low), dot32(picked, mem_values[0]).astype(low)))
    arrived = exchange(sent, seq_count, capacity)
    mem_key_rows = dot32(placed, arrived[0]).astype(low)
    mem_value_rows = dot32(placed, arrived[1]).astype(low)
    queries = dot32(normed_one, w_query).astype(low)
    keys = dot32(normed_one, w_key).astype(low)
    values = dot32(normed_one, w_value).astype(low)
    attended, *saved = attend_forward(limit, queries, keys, values, mem_key_rows, mem_value_rows)
    middle = tokens_f + dot32(attended, w_out)
    factor_two = rms_factor(middle)
    unit_two = middle * factor_two
    normed_two = (unit_two * gain_two).astype(low)
    gate = dot32(normed_two, w_gate)
    upper = dot32(normed_two, w_up)
    sigma = jax.nn.sigmoid(gate)
    hidden = (gate * sigma * upper).astype(low)
    layer_out = (middle + dot32(hidden, w_down)).astype(low)

    grad_y_low = cotangent[0]
    grad_y = grad_y_low.astype(jnp.float32)
    grad_down = dot32(hidden.T, grad_y_low)
    grad_hidden = dot32(grad_y_low, w_down.T)
    grad_gate_act = (grad_hidden * upper * sigma * (1.0 + gate * (1.0 - sigma))).astype(low)
    grad_up_act = (grad_hidden * gate * sigma).astype(low)
    grad_gate = dot32(normed_two.T, grad_gate_act)
    grad_up = dot32(normed_two.T, grad_up_act)
    grad_normed_two = dot32(grad_gate_act, w_gate.T) + dot32(grad_up_act, w_up.T)
    grad_ffn_gain = jnp.sum(grad_normed_two * unit_two, axis=0)
    scaled_two = gain_two * grad_normed_two
    grad_middle = grad_y + factor_two * (
        scaled_two - unit_two * jnp.mean(scaled_two * unit_two, axis=-1, keepdims=True)
    )
    grad_branch = grad_middle.astype(low)
    grad_out = dot32(attended.T, grad_branch)
    grad_attended = dot32(grad_branch, w_out.T).astype(low)
    grad_q, grad_k, grad_v, grad_mk, grad_mv = attend_backward(limit, grad_attended, saved)
    back = jnp.stack((dot32(placed.T, grad_mk).astype(low), dot32(placed.T, grad_mv).astype(low)))
    returned = exchange(back, seq_count, capacity)
    grad_mem_keys = dot32(picked.T, returned[0])
    grad_mem_values = dot32(picked.T, returned[1])
    grad_query = dot32(normed_one.T, grad_q)
    grad_key = dot32(normed_one.T, grad_k)
    grad_value = dot32(normed_one.T, grad_v)
    grad_normed_one = dot32(grad_q, w_query.T) + dot32(grad_k, w_key.T) + dot32(grad_v, w_value.T)
    grad_attn_gain = jnp.sum(grad_normed_one * unit_one, axis=0)
    scaled_one = gain_one * grad_normed_one
    grad_input = grad_middle + factor_one * (
        scaled_one - unit_one * jnp.mean(scaled_one * unit_one, axis=-1, keepdims=True)
    )
    grad_tokens = grad_input.astype(low)
    gate_rows, up_rows, query_rows, key_rows, value_rows, out_rows, down_rows, attn_row, ffn_row = [
        lax.psum_scatter(grad, ("seq", "doc"), scatter_dimension=0, tiled=True)
        for grad in (
            grad_gate, grad_up, grad_query, grad_key, grad_value, grad_out, grad_down, grad_attn_gain, grad_ffn_gain
        )
    ]
    return (
        layer_out[None],
        grad_tokens[None],
        attn_row,
        query_rows,
        key_rows,
        value_rows,
        out_rows,
        ffn_row,
        gate_rows,
        up_rows,
        down_rows,
        grad_mem_keys[None],
        grad_mem_values[None],
    )


def solution(mesh):
    in_specs = (
        P("doc", "seq", None),
        P("doc", "seq", None),
        P(),
        P(),
        P(),
        P(),
        P(),
        P(),
        P(),
        P(),
        P(),
        P("doc", "seq", None),
        P("doc", "seq", None),
        P("doc", None),
        P("doc", "seq", None),
    )
    out_specs = (
        P("doc", "seq", None),
        P("doc", "seq", None),
        P(("seq", "doc")),
        P(("seq", "doc"), None),
        P(("seq", "doc"), None),
        P(("seq", "doc"), None),
        P(("seq", "doc"), None),
        P(("seq", "doc")),
        P(("seq", "doc"), None),
        P(("seq", "doc"), None),
        P(("seq", "doc"), None),
        P("doc", "seq", None),
        P("doc", "seq", None),
    )
    return jax.shard_map(
        on_device, mesh=mesh, in_specs=in_specs, out_specs=out_specs, check_vma=False
    )
```

```python
import functools
import math

import jax
import jax.numpy as jnp
from jax import lax
from jax.experimental import pallas as pl
from jax.experimental.pallas import tpu as pltpu
from jax.sharding import PartitionSpec as P

HEADS = 8
HEAD_DIM = 128
TOPK = 128
BPS = 4
NEG = -1000000000.0
MESH = pl.DeviceIdType.MESH
EPS = 1e-05
UNIT = 256
SKEW = 4


def flip(value, bit):
    return value + bit - 2 * bit * ((value // bit) % 2)


HALF = HEADS // 2
LOG2E = math.log2(math.e)
SCALE = HEAD_DIM ** (-0.5)
NT = (((1,), (1,)), ((), ()))
TN = (((0,), (0,)), ((), ()))
NN = (((1,), (0,)), ((), ()))


def matmul(left, right, dims):
    return lax.dot_general(left, right, dims, preferred_element_type=jnp.float32)


def seats():
    seq, doc = lax.axis_index("seq"), lax.axis_index("doc")
    core, chip = seq % 2, (seq // 2) % 2
    mate = (flip(seq, 1), doc)
    across = (flip(seq, 2), doc)
    diagonal = (flip(flip(seq, 2), 1), doc)
    return core, chip, mate, across, diagonal


def meet(peers):
    barrier = pltpu.get_barrier_semaphore()
    for peer in peers:
        pl.semaphore_signal(barrier, inc=1, device_id=peer, device_id_type=MESH)
    pl.semaphore_wait(barrier, len(peers))


def head_lanes(core, head):
    return pl.ds(pl.multiple_of((core * HALF + head) * HEAD_DIM, HEAD_DIM), HEAD_DIM)


def remote(src, dst, send, recv, peer):
    return pltpu.make_async_remote_copy(
        src_ref=src, dst_ref=dst, send_sem=send, recv_sem=recv, device_id=peer, device_id_type=MESH
    )


def share_heads(sources, boxes, core, mate, local_sem, send_sem, recv_sem):
    copies = []
    for i, (source, box) in enumerate(zip(sources, boxes)):
        for head in range(HALF):
            copies.append(
                remote(
                    source.at[:, head_lanes(1 - core, head)],
                    box.at[core, head],
                    send_sem.at[i, head],
                    recv_sem.at[i, head],
                    mate,
                )
            )
            copies[-1].start()
    for i, (source, box) in enumerate(zip(sources, boxes)):
        for head in range(HALF):
            copies.append(
                pltpu.make_async_copy(
                    source.at[:, head_lanes(core, head)], box.at[core, head], local_sem.at[i, head]
                )
            )
            copies[-1].start()
    return copies


def masked(scores, first_key, limit, diagonal):
    key = lax.broadcasted_iota(jnp.int32, scores.shape, 0)
    ok = key + first_key < limit
    if diagonal:
        ok = ok & (key <= lax.broadcasted_iota(jnp.int32, scores.shape, 1))
    return jnp.where(ok, scores, NEG)


def soften(parts):
    top = functools.reduce(
        jnp.maximum, [jnp.max(scores, axis=0, keepdims=True) for scores, _ in parts]
    )
    total, mixed = 0.0, 0.0
    for scores, values in parts:
        exponent = jnp.exp2(scores - top)
        total = total + jnp.sum(exponent, axis=0, keepdims=True)
        mixed = mixed + matmul(values, exponent.astype(jnp.bfloat16), TN)
    return mixed / total, top + jnp.log(total) * LOG2E


def forward_kernel(
    limit_ref, q, k, v, mk, mv,
    attended, qb, kb, vb, qx, mkb, mvb, ob, lse,
    mixed_own, mixed_out, mixed_in, lse_out, lse_in,
    local_sem, mate_send, mate_recv, far_send, far_recv, back_send, back_recv, end_sem,
):
    core, chip, mate, across, diagonal = seats()
    block = q.shape[0]
    limit = limit_ref[0]
    meet((mate, across, diagonal))

    def query_copy(head, own):
        return remote(
            q.at[:, head_lanes(core if own else 1 - core, head)],
            qx.at[core, head],
            far_send.at[0 if own else 1, head],
            far_recv.at[core, head],
            across if own else diagonal,
        )

    def arrived_query(far, head):
        return remote(
            q.at[:, head_lanes(core, head)], qx.at[far, head], far_send.at[0, head], far_recv.at[far, head], across
        )

    @pl.when(chip == 1)
    def _():
        for head in range(HALF):
            query_copy(head, True).start()
            query_copy(head, False).start()

    copies = share_heads((q, k, v, mk, mv), (qb, kb, vb, mkb, mvb), core, mate, local_sem, mate_send, mate_recv)
    for copy in copies:
        copy.wait()

    def own_part(blk, head):
        query = qb[blk, head]
        parts = []
        for kblk in range(blk + 1):
            scores = matmul(kb[kblk, head], query, NT) * (SCALE * LOG2E)
            scores = masked(scores, (2 * chip + kblk) * block, limit, kblk == blk)
            parts.append((scores, vb[kblk, head]))
        parts.append((matmul(mkb[blk, head], query, NT) * (SCALE * LOG2E), mvb[blk, head]))
        return soften(parts)

    for blk in range(2):
        def own_head(head, carry):
            mixed, level = own_part(blk, head)
            mixed_own[blk, head] = mixed
            lse[blk, head] = level
            return carry
        lax.fori_loop(0, HALF, own_head, 0)

    def back_copy(blk, head):
        return (
            remote(mixed_out.at[blk, head], mixed_in.at[blk, head], back_send.at[0, blk, head], back_recv.at[0, blk, head], across),
            remote(lse_out.at[blk, head], lse_in.at[blk, head], back_send.at[1, blk, head], back_recv.at[1, blk, head], across),
        )

    @pl.when(chip == 0)
    def _():
        def cross(i, carry):
            head, blk = i // 2, i % 2
            arrived_query(blk, head).wait_recv()
            query = qx[blk, head]
            parts = []
            for kblk in range(2):
                scores = matmul(kb[kblk, head], query, NT) * (SCALE * LOG2E)
                parts.append((masked(scores, kblk * block, limit, False), vb[kblk, head]))
            mixed, level = soften(parts)
            mixed_out[blk, head] = mixed.astype(jnp.bfloat16)
            lse_out[blk, head] = level
            for copy in back_copy(blk, head):
                copy.start()
            return carry
        lax.fori_loop(0, 2 * HALF, cross, 0)

        def finish(i, carry):
            head, blk = i // 2, i % 2
            ob[blk, head] = mixed_own[blk, head].T.astype(jnp.bfloat16)
            return carry
        lax.fori_loop(0, 2 * HALF, finish, 0)

    @pl.when(chip == 1)
    def _():
        def merge(i, carry):
            head, blk = i // 2, i % 2
            for copy in back_copy(blk, head):
                copy.wait_recv()
            near, far = lse[blk, head], lse_in[blk, head]
            top = jnp.maximum(near, far)
            near, far = jnp.exp2(near - top), jnp.exp2(far - top)
            total = near + far
            mixed = (mixed_own[blk, head] * near + mixed_in[blk, head].astype(jnp.float32) * far) / total
            ob[blk, head] = mixed.T.astype(jnp.bfloat16)
            lse[blk, head] = top + jnp.log(total) * LOG2E
            return carry
        lax.fori_loop(0, 2 * HALF, merge, 0)

    ends = []
    for head in range(HALF):
        ends.append(
            remote(ob.at[1 - core, head], attended.at[:, head_lanes(core, head)], end_sem.at[0, head], end_sem.at[1, head], mate)
        )
        ends.append(
            pltpu.make_async_copy(ob.at[core, head], attended.at[:, head_lanes(core, head)], end_sem.at[2, head])
        )
    for copy in ends:
        copy.start()
    for copy in ends:
        copy.wait()

    @pl.when(chip == 0)
    def _():
        for head in range(HALF):
            for blk in range(2):
                for copy in back_copy(blk, head):
                    copy.wait_send()

    @pl.when(chip == 1)
    def _():
        for head in range(HALF):
            query_copy(head, True).wait_send()
            query_copy(head, False).wait_send()


def attend_forward(limit, queries, keys, values, mem_keys, mem_values):
    block, width = queries.shape
    topk = mem_keys.shape[0]
    low, full = jnp.bfloat16, jnp.float32
    box = (2, HALF, block, HEAD_DIM)
    mem_box = (2, HALF, topk, HEAD_DIM)
    flat = (2, HALF, HEAD_DIM, block)
    row = (2, HALF, 1, block)
    dma = pltpu.SemaphoreType.DMA
    hbm, vmem = pl.BlockSpec(memory_space=pl.ANY), pl.BlockSpec(memory_space=pltpu.VMEM)
    struct = jax.ShapeDtypeStruct
    return pl.pallas_call(
        forward_kernel,
        out_shape=(
            struct((block, width), low),
            struct(box, low), struct(box, low), struct(box, low), struct(box, low),
            struct(mem_box, low), struct(mem_box, low), struct(box, low), struct(row, full),
        ),
        in_specs=[pl.BlockSpec(memory_space=pltpu.SMEM)] + [hbm] * 5,
        out_specs=(hbm,) + (vmem,) * 8,
        scratch_shapes=[
            pltpu.VMEM(flat, full), pltpu.VMEM(flat, low), pltpu.VMEM(flat, low),
            pltpu.VMEM(row, full), pltpu.VMEM(row, full),
            dma((5, HALF)), dma((5, HALF)), dma((5, HALF)),
            dma((2, HALF)), dma((2, HALF)), dma((2, 2, HALF)), dma((2, 2, HALF)), dma((3, HALF)),
        ],
        name="attend_forward",
        compiler_params=pltpu.CompilerParams(collective_id=1, has_side_effects=True, vmem_limit_bytes=56 * 2**20),
    )(limit, queries, keys, values, mem_keys, mem_values)


def backward_kernel(
    limit_ref, grad, qb, kb, vb, qx, mkb, mvb, ob, lse,
    dq, dk, dv, dmk, dmv,
    gb, gx, delta, lse_in, delta_in, dq_own, dq_out, dq_in, dk_sum, dv_sum, dmk_low, dmv_low, dqb, dkb, dvb,
    local_sem, mate_send, mate_recv, far_send, far_recv, row_send, row_recv, back_send, back_recv,
    end_local, end_send, end_recv,
):
    core, chip, mate, across, diagonal = seats()
    block = grad.shape[0]
    limit = limit_ref[0]
    meet((mate, across, diagonal))

    def grad_copy(head, own):
        return remote(
            grad.at[:, head_lanes(core if own else 1 - core, head)],
            gx.at[core, head],
            far_send.at[0 if own else 1, head],
            far_recv.at[core, head],
            across if own else diagonal,
        )

    def arrived_grad(far, head):
        return remote(
            grad.at[:, head_lanes(core, head)], gx.at[far, head], far_send.at[0, head], far_recv.at[far, head], across
        )

    def row_copies():
        return (
            remote(lse, lse_in, row_send.at[0], row_recv.at[0], across),
            remote(delta, delta_in, row_send.at[1], row_recv.at[1], across),
        )

    @pl.when(chip == 1)
    def _():
        for head in range(HALF):
            grad_copy(head, True).start()
            grad_copy(head, False).start()

    copies = share_heads((grad,), (gb,), core, mate, local_sem, mate_send, mate_recv)
    for copy in copies:
        copy.wait()

    def rows(i, carry):
        head, blk = i // 2, i % 2
        product = gb[blk, head].astype(jnp.float32) * ob[blk, head].astype(jnp.float32)
        delta[blk, head] = jnp.sum(product.T, axis=0, keepdims=True)
        return carry

    lax.fori_loop(0, 2 * HALF, rows, 0)

    @pl.when(chip == 1)
    def _():
        for copy in row_copies():
            copy.start()

    def pull(key_rows, value_rows, query, grad_rows, level, inner, where):
        scores = matmul(key_rows, query, NT) * (SCALE * LOG2E)
        if where is not None:
            scores = masked(scores, where[0], limit, where[1])
        weights = jnp.exp2(scores - level)
        grad_weights = matmul(value_rows, grad_rows, NT)
        grad_scores = (weights * (grad_weights - inner)).astype(jnp.bfloat16)
        return (
            matmul(grad_scores, query, NN),
            matmul(weights.astype(jnp.bfloat16), grad_rows, NN),
            matmul(key_rows, grad_scores, TN),
        )

    for blk in range(2):
        def own_head(head, carry):
            query, grad_rows = qb[blk, head], gb[blk, head]
            level, inner = lse[blk, head], delta[blk, head]
            total = 0.0
            for kblk in range(blk + 1):
                gk, gv, gq = pull(
                    kb[kblk, head], vb[kblk, head], query, grad_rows, level, inner,
                    ((2 * chip + kblk) * block, kblk == blk),
                )
                if kblk == blk:
                    dk_sum[kblk, head], dv_sum[kblk, head] = gk, gv
                else:
                    dk_sum[kblk, head] += gk
                    dv_sum[kblk, head] += gv
                total = total + gq
            gk, gv, gq = pull(mkb[blk, head], mvb[blk, head], query, grad_rows, level, inner, None)
            dmk_low[blk, head] = (gk * SCALE).astype(jnp.bfloat16)
            dmv_low[blk, head] = gv.astype(jnp.bfloat16)
            dq_own[blk, head] = total + gq
            return carry
        lax.fori_loop(0, HALF, own_head, 0)

    def back_copy(blk, head):
        return remote(dq_out.at[blk, head], dq_in.at[blk, head], back_send.at[blk, head], back_recv.at[blk, head], across)

    @pl.when(chip == 0)
    def _():
        for copy in row_copies():
            copy.wait_recv()

        def cross(i, carry):
            head, blk = i // 2, i % 2
            arrived_grad(blk, head).wait_recv()
            query, grad_rows = qx[blk, head], gx[blk, head]
            level, inner = lse_in[blk, head], delta_in[blk, head]
            total = 0.0
            for kblk in range(2):
                gk, gv, gq = pull(
                    kb[kblk, head], vb[kblk, head], query, grad_rows, level, inner, (kblk * block, False)
                )
                dk_sum[kblk, head] += gk
                dv_sum[kblk, head] += gv
                total = total + gq
            dq_out[blk, head] = total.astype(jnp.bfloat16)
            back_copy(blk, head).start()
            return carry
        lax.fori_loop(0, 2 * HALF, cross, 0)

    def finish(i, carry):
        head, blk = i // 2, i % 2
        dqb[blk, head] = (dq_own[blk, head].T * SCALE).astype(jnp.bfloat16)
        dkb[blk, head] = (dk_sum[blk, head] * SCALE).astype(jnp.bfloat16)
        dvb[blk, head] = dv_sum[blk, head].astype(jnp.bfloat16)
        return carry

    @pl.when(chip == 1)
    def _():
        def merge(i, carry):
            head, blk = i // 2, i % 2
            back_copy(blk, head).wait_recv()
            dq_own[blk, head] += dq_in[blk, head].astype(jnp.float32)
            return finish(i, carry)
        lax.fori_loop(0, 2 * HALF, merge, 0)

    @pl.when(chip == 0)
    def _():
        lax.fori_loop(0, 2 * HALF, finish, 0)

    ends = []
    for i, (box, out) in enumerate(((dqb, dq), (dkb, dk), (dvb, dv), (dmk_low, dmk), (dmv_low, dmv))):
        for head in range(HALF):
            lanes = head_lanes(core, head)
            ends.append(remote(box.at[1 - core, head], out.at[:, lanes], end_send.at[i, head], end_recv.at[i, head], mate))
            ends.append(pltpu.make_async_copy(box.at[core, head], out.at[:, lanes], end_local.at[i, head]))
    for copy in ends:
        copy.start()
    for copy in ends:
        copy.wait()

    @pl.when(chip == 0)
    def _():
        for head in range(HALF):
            for blk in range(2):
                back_copy(blk, head).wait_send()

    @pl.when(chip == 1)
    def _():
        for copy in row_copies():
            copy.wait_send()
        for head in range(HALF):
            grad_copy(head, True).wait_send()
            grad_copy(head, False).wait_send()


def attend_backward(limit, grad, saved):
    block, width = grad.shape
    topk = saved[4].shape[2]
    low, full = jnp.bfloat16, jnp.float32
    box = (2, HALF, block, HEAD_DIM)
    mem_box = (2, HALF, topk, HEAD_DIM)
    flat = (2, HALF, HEAD_DIM, block)
    row = (2, HALF, 1, block)
    dma = pltpu.SemaphoreType.DMA
    hbm, vmem = pl.BlockSpec(memory_space=pl.ANY), pl.BlockSpec(memory_space=pltpu.VMEM)
    struct = jax.ShapeDtypeStruct
    return pl.pallas_call(
        backward_kernel,
        out_shape=(struct((block, width), low),) * 3 + (struct((topk, width), low),) * 2,
        in_specs=[pl.BlockSpec(memory_space=pltpu.SMEM), hbm] + [vmem] * 8,
        out_specs=(hbm,) * 5,
        scratch_shapes=[
            pltpu.VMEM(box, low), pltpu.VMEM(box, low),
            pltpu.VMEM(row, full), pltpu.VMEM(row, full), pltpu.VMEM(row, full),
            pltpu.VMEM(flat, full), pltpu.VMEM(flat, low), pltpu.VMEM(flat, low),
            pltpu.VMEM(box, full), pltpu.VMEM(box, full),
            pltpu.VMEM(mem_box, low), pltpu.VMEM(mem_box, low),
            pltpu.VMEM(box, low), pltpu.VMEM(box, low), pltpu.VMEM(box, low),
            dma((1, HALF)), dma((1, HALF)), dma((1, HALF)),
            dma((2, HALF)), dma((2, HALF)), dma((2,)), dma((2,)),
            dma((2, HALF)), dma((2, HALF)),
            dma((5, HALF)), dma((5, HALF)), dma((5, HALF)),
        ],
        name="attend_backward",
        compiler_params=pltpu.CompilerParams(collective_id=2, has_side_effects=True, vmem_limit_bytes=56 * 2**20),
    )(limit, grad, *saved)


def keep_order(rank_of):
    before = lax.broadcasted_iota(jnp.int32, (rank_of, rank_of), 0)
    return (before < lax.broadcasted_iota(jnp.int32, (rank_of, rank_of), 1)).astype(jnp.bfloat16)


def front_kernel(
    limit_ref, tokens, gain, w_query, w_key, w_value, mem_keys, mem_values, wanted,
    attended, qb, kb, vb, qx, mkb, mvb, ob, lse, spots, pick_t,
    rows, weights, normed, qkv, tables, every, pick, mem_out, mem_in,
    mixed_own, mixed_out, mixed_in, lse_out, lse_in,
    load_sem, want_send, want_recv, mem_send, mem_recv, mem_local,
    local_sem, mate_send, mate_recv, far_send, far_recv, back_send, back_recv, end_sem,
):
    core, chip, mate, across, diagonal = seats()
    seq, doc = lax.axis_index("seq"), lax.axis_index("doc")
    seq_count, capacity = mem_in.shape[0], mem_in.shape[3]
    block, width = tokens.shape
    mem_rows, topk = tables.shape[1], every.shape[2]
    limit = limit_ref[0, seq // BPS]

    loads = [
        pltpu.make_async_copy(src, dst, load_sem.at[i])
        for i, (src, dst) in enumerate(
            (
                (wanted, every.at[seq]), (tokens, rows), (w_query, weights.at[0]), (w_key, weights.at[1]),
                (w_value, weights.at[2]), (mem_keys, tables.at[0]), (mem_values, tables.at[1]),
            )
        )
    ]
    for copy in loads:
        copy.start()
    meet([(lax.rem(seq + away, seq_count), doc) for away in range(1, seq_count)])
    loads[0].wait()

    def want_copy(away):
        return remote(
            every.at[seq], every.at[seq], want_send.at[away - 1], want_recv.at[away - 1],
            (lax.rem(seq + away, seq_count), doc),
        )

    def want_arrival(away):
        source = lax.rem(seq + seq_count - away, seq_count)
        return remote(every.at[source], every.at[source], want_send.at[away - 1], want_recv.at[away - 1], (source, doc))

    def mem_copy(away):
        peer = lax.rem(seq + away, seq_count)
        return remote(mem_out.at[peer], mem_in.at[seq], mem_send.at[away - 1], mem_recv.at[away - 1], (peer, doc))

    def mem_arrival(away):
        source = lax.rem(seq + seq_count - away, seq_count)
        return remote(mem_out.at[source], mem_in.at[source], mem_send.at[away - 1], mem_recv.at[away - 1], (source, doc))

    for away in range(1, seq_count):
        want_copy(away).start()
    loads[1].wait()
    part = 64

    def norm(i, carry):
        at = pl.ds(pl.multiple_of(i * part, part), part)
        x = rows[at, :].astype(jnp.float32)
        factor = lax.rsqrt(jnp.mean(x * x, axis=-1, keepdims=True) + EPS)
        normed[at, :] = (x * factor * gain[0:1, :]).astype(jnp.bfloat16)
        return carry

    lax.fori_loop(0, block // part, norm, 0)

    def project(i):
        loads[2 + i].wait()

        def one(j, carry):
            lanes = pl.ds(pl.multiple_of(j * UNIT, UNIT), UNIT)
            qkv[i, :, lanes] = matmul(normed[...], weights[i, :, lanes], NN).astype(jnp.bfloat16)
            return carry

        lax.fori_loop(0, width // UNIT, one, 0)

    project(0)

    def query_copy(head, own):
        return remote(
            qkv.at[0, :, head_lanes(core if own else 1 - core, head)],
            qx.at[core, head],
            far_send.at[0 if own else 1, head],
            far_recv.at[core, head],
            across if own else diagonal,
        )

    def arrived_query(far, head):
        return remote(
            qkv.at[0, :, head_lanes(core, head)], qx.at[far, head], far_send.at[0, head], far_recv.at[far, head], across
        )

    @pl.when(chip == 1)
    def _():
        for head in range(HALF):
            query_copy(head, True).start()
            query_copy(head, False).start()

    project(1)
    project(2)
    copies = share_heads(
        (qkv.at[0], qkv.at[1], qkv.at[2]), (qb, kb, vb), core, mate, local_sem, mate_send, mate_recv
    )

    for away in range(1, seq_count):
        want_arrival(away).wait_recv()
    triangle = keep_order(topk)
    asked = every[:, 0, :]
    here = asked - seq * mem_rows
    mine = (here >= 0) & (here < mem_rows)
    before = matmul(mine.astype(jnp.bfloat16), triangle, NN).astype(jnp.int32)
    place = lax.broadcasted_iota(jnp.int32, (capacity, topk), 0)
    line = lax.broadcasted_iota(jnp.int32, (mem_rows, topk), 0)
    for b in range(seq_count):
        at_place = jnp.where((before[b : b + 1] == place) & (here[b : b + 1] >= 0) & (here[b : b + 1] < mem_rows), 1.0, 0.0)
        at_line = jnp.where(here[b : b + 1] == line, 1.0, 0.0)
        pick[b * capacity : (b + 1) * capacity, :] = matmul(
            at_place.astype(jnp.bfloat16), at_line.astype(jnp.bfloat16), NT
        ).astype(jnp.bfloat16)
    half = HALF * HEAD_DIM
    for kind in range(2):
        loads[5 + kind].wait()
        for side in range(2):
            found = matmul(pick[...], tables[kind, :, side * half : (side + 1) * half], NN).astype(jnp.bfloat16)
            for b in range(seq_count):
                mem_out[2 * (b // 2) + side, b % 2, kind] = found[b * capacity : (b + 1) * capacity]
    for away in range(1, seq_count):
        mem_copy(away).start()
    own_rows = pltpu.make_async_copy(mem_out.at[seq], mem_in.at[seq], mem_local.at[0])
    own_rows.start()
    pick_t[...] = pick[...].astype(jnp.float32).T.astype(jnp.bfloat16)
    seat = lax.broadcasted_iota(jnp.int32, (seq_count, topk), 0)
    slot_at = lax.broadcasted_iota(jnp.int32, (seq_count * capacity, topk), 0)
    for blk in range(2):
        away_rows = every[2 * (seq // 2) + blk] - seat * mem_rows
        owner = (away_rows >= 0) & (away_rows < mem_rows)
        rank = matmul(owner.astype(jnp.bfloat16), triangle, NN).astype(jnp.int32)
        slot = jnp.sum(jnp.where(owner, seat * capacity + rank, 0), axis=0, keepdims=True)
        spots[blk] = jnp.where(slot == slot_at, 1.0, 0.0).astype(jnp.bfloat16)

    for copy in copies:
        copy.wait()

    def own_head(blk, head):
        query = qb[blk, head]
        parts = []
        for kblk in range(blk + 1):
            scores = matmul(kb[kblk, head], query, NT) * (SCALE * LOG2E)
            scores = masked(scores, (2 * chip + kblk) * block, limit, kblk == blk)
            parts.append((scores, vb[kblk, head]))
        mixed_own[blk, head], lse[blk, head] = soften(parts)

    def back_copy(blk, head):
        return (
            remote(mixed_out.at[blk, head], mixed_in.at[blk, head], back_send.at[0, blk, head], back_recv.at[0, blk, head], across),
            remote(lse_out.at[blk, head], lse_in.at[blk, head], back_send.at[1, blk, head], back_recv.at[1, blk, head], across),
        )

    def heads(head, carry):
        @pl.when(chip == 0)
        def _():
            def cross(blk, carry):
                arrived_query(blk, head).wait_recv()
                query = qx[blk, head]
                parts = []
                for kblk in range(2):
                    scores = matmul(kb[kblk, head], query, NT) * (SCALE * LOG2E)
                    parts.append((masked(scores, kblk * block, limit, False), vb[kblk, head]))
                mixed, level = soften(parts)
                mixed_out[blk, head] = mixed.astype(jnp.bfloat16)
                lse_out[blk, head] = level
                for copy in back_copy(blk, head):
                    copy.start()
                return carry

            lax.fori_loop(0, 2, cross, 0)

        own_head(0, head)
        own_head(1, head)
        return carry

    lax.fori_loop(0, HALF, heads, 0)

    for away in range(1, seq_count):
        mem_arrival(away).wait_recv()
    own_rows.wait()
    for blk in range(2):
        for kind, box in enumerate((mkb, mvb)):
            found = mem_in[:, blk, kind].reshape(seq_count * capacity, half)
            found = matmul(spots[blk], found, TN).astype(jnp.bfloat16)
            for head in range(HALF):
                box[blk, head] = found[:, head * HEAD_DIM : (head + 1) * HEAD_DIM]

    def blend(pieces):
        top = functools.reduce(jnp.maximum, [level for _, level in pieces])
        total, mixed = 0.0, 0.0
        for value, level in pieces:
            share = jnp.exp2(level - top)
            total = total + share
            mixed = mixed + value * share
        return mixed / total, top + jnp.log(total) * LOG2E

    def finish(i, carry):
        head, blk = i // 2, i % 2
        scores = matmul(mkb[blk, head], qb[blk, head], NT) * (SCALE * LOG2E)
        pieces = [(mixed_own[blk, head], lse[blk, head]), soften([(scores, mvb[blk, head])])]

        @pl.when(chip == 0)
        def _():
            mixed, lse[blk, head] = blend(pieces)
            ob[blk, head] = mixed.T.astype(jnp.bfloat16)

        @pl.when(chip == 1)
        def _():
            for copy in back_copy(blk, head):
                copy.wait_recv()
            far = (mixed_in[blk, head].astype(jnp.float32), lse_in[blk, head])
            mixed, lse[blk, head] = blend(pieces + [far])
            ob[blk, head] = mixed.T.astype(jnp.bfloat16)

        return carry

    lax.fori_loop(0, 2 * HALF, finish, 0)

    ends = []
    for head in range(HALF):
        ends.append(
            remote(ob.at[1 - core, head], attended.at[:, head_lanes(core, head)], end_sem.at[0, head], end_sem.at[1, head], mate)
        )
        ends.append(
            pltpu.make_async_copy(ob.at[core, head], attended.at[:, head_lanes(core, head)], end_sem.at[2, head])
        )
    for copy in ends:
        copy.start()
    for copy in ends:
        copy.wait()
    for away in range(1, seq_count):
        want_copy(away).wait_send()
        mem_copy(away).wait_send()

    @pl.when(chip == 0)
    def _():
        for head in range(HALF):
            for blk in range(2):
                for copy in back_copy(blk, head):
                    copy.wait_send()

    @pl.when(chip == 1)
    def _():
        for head in range(HALF):
            query_copy(head, True).wait_send()
            query_copy(head, False).wait_send()


def go_forward(limit, tokens, gain, projections, mem_keys, mem_values, wanted):
    block, width = tokens.shape
    mem_rows, topk = mem_keys.shape[0], wanted.shape[1]
    seq_count = lax.axis_size("seq")
    capacity = 2 * topk // seq_count
    slots = seq_count * capacity
    low, full = jnp.bfloat16, jnp.float32
    box = (2, HALF, block, HEAD_DIM)
    mem_box = (2, HALF, topk, HEAD_DIM)
    flat = (2, HALF, HEAD_DIM, block)
    row = (2, HALF, 1, block)
    mem = (seq_count, 2, 2, capacity, HALF * HEAD_DIM)
    dma = pltpu.SemaphoreType.DMA
    hbm, vmem = pl.BlockSpec(memory_space=pl.ANY), pl.BlockSpec(memory_space=pltpu.VMEM)
    struct = jax.ShapeDtypeStruct
    return pl.pallas_call(
        front_kernel,
        out_shape=(
            struct((block, width), low),
            struct(box, low), struct(box, low), struct(box, low), struct(box, low),
            struct(mem_box, low), struct(mem_box, low), struct(box, low), struct(row, full),
            struct((2, slots, topk), low), struct((mem_rows, slots), low),
        ),
        in_specs=[pl.BlockSpec(memory_space=pltpu.SMEM), hbm, vmem] + [hbm] * 6,
        out_specs=(hbm,) + (vmem,) * 10,
        scratch_shapes=[
            pltpu.VMEM((block, width), low), pltpu.VMEM((3, width, width), low), pltpu.VMEM((block, width), low),
            pltpu.VMEM((3, block, width), low), pltpu.VMEM((2, mem_rows, width), low),
            pltpu.VMEM((seq_count, 1, topk), jnp.int32), pltpu.VMEM((slots, mem_rows), low),
            pltpu.VMEM(mem, low), pltpu.VMEM(mem, low),
            pltpu.VMEM(flat, full), pltpu.VMEM(flat, low), pltpu.VMEM(flat, low),
            pltpu.VMEM(row, full), pltpu.VMEM(row, full),
            dma((7,)), dma((seq_count - 1,)), dma((seq_count - 1,)), dma((seq_count - 1,)), dma((seq_count - 1,)), dma((1,)),
            dma((3, HALF)), dma((3, HALF)), dma((3, HALF)),
            dma((2, HALF)), dma((2, HALF)), dma((2, 2, HALF)), dma((2, 2, HALF)), dma((3, HALF)),
        ],
        name="go_forward",
        compiler_params=pltpu.CompilerParams(collective_id=4, has_side_effects=True, vmem_limit_bytes=56 * 2**20),
    )(limit, tokens, gain, *projections, mem_keys, mem_values, wanted)


ALONG = (("x", "y", "low", "high"), ("y", "x", "low", "high"), ("low", "high", "y", "x"), ("low", "high", "x", "y"))
TURNS = (2, 0, 0, 3, 0, 1, 1, 1, 2, 1, 0, 0, 0, 0, 3, 0, 1, 0, 2, 0, 1, 3, 0, 0, 1, 1, 3, 1, 3, 0, 3, 1, 0, 0, 1, 0, 2, 0, 1, 2, 2, 3)
PLAN = (
    (),
    ((0, 0), (1, 0),),
    ((2, 0), (3, 0),),
    ((4, 0), (0, 1), (1, 1), (5, 0),),
    ((6, 0), (2, 1), (3, 1), (7, 0), (1, 2),),
    ((8, 0), (4, 1), (9, 0), (5, 1), (0, 2),),
    ((1, 3), (10, 0), (11, 0), (6, 1), (3, 2), (5, 2),),
    ((2, 2), (8, 1), (12, 0), (13, 0), (5, 3), (7, 1),),
    ((1, 4), (10, 1), (14, 0), (4, 2), (15, 0), (2, 3),),
    ((11, 1), (9, 1), (16, 0), (0, 3), (17, 0), (6, 2), (3, 3), (10, 2), (8, 2),),
    ((5, 4), (18, 0), (14, 1), (19, 0), (4, 3), (12, 1), (11, 2), (6, 3), (10, 3),),
    ((2, 4), (20, 0), (13, 1), (21, 0),),
    ((16, 1), (3, 4), (7, 2), (8, 3),),
    ((18, 1), (12, 2),),
    ((15, 1),),
    ((11, 3), (9, 2),),
    ((20, 1), (0, 4),),
    ((22, 0),),
    ((23, 0), (14, 2), (13, 2), (24, 0), (4, 4),),
    ((25, 0), (6, 4), (15, 2), (17, 1), (21, 1), (10, 4), (7, 3),),
    (),
    (),
    ((19, 1), (12, 3),),
    ((9, 3), (24, 1), (38, 0), (16, 2), (8, 4), (13, 3),),
    ((18, 2), (15, 3), (39, 0), (11, 4),),
    ((25, 1),),
    ((40, 0), (17, 2), (16, 3), (19, 2), (21, 2), (7, 4), (12, 4), (9, 4),),
    ((13, 4), (15, 4), (41, 0),),
    (),
    ((39, 1), (20, 2), (38, 1),),
    ((18, 3),),
    ((22, 1),),
    (),
    ((23, 1),),
    ((14, 3), (22, 2), (40, 1),),
    ((17, 3), (19, 3),),
    ((16, 4),),
    ((23, 2), (14, 4),),
    ((41, 1), (24, 2),),
    ((25, 2),),
    ((21, 3), (20, 3), (22, 3), (38, 2), (18, 4), (39, 2), (23, 3), (24, 3), (25, 3), (40, 2), (17, 4), (19, 4),),
    ((21, 4),),
    ((39, 3), (38, 3),),
    ((41, 2), (40, 3),),
    ((20, 4), (22, 4), (26, 0), (39, 4), (27, 0), (23, 4),),
    ((24, 4), (28, 0), (29, 0), (25, 4),),
    ((41, 3), (30, 0), (40, 4), (31, 0), (38, 4),),
    ((32, 0), (26, 1), (33, 0), (27, 1),),
    ((41, 4), (34, 0), (29, 1),),
    ((35, 0), (28, 1), (36, 0), (37, 0),),
    ((31, 1), (32, 1),),
    ((30, 1),),
    ((34, 1), (33, 1),),
    ((29, 2), (27, 2), (32, 2), (26, 2),),
    ((36, 1), (33, 2), (35, 1),),
    ((28, 2), (29, 3), (27, 3),),
    ((32, 3), (37, 1), (35, 2), (30, 2), (31, 2), (33, 3), (34, 2), (37, 2), (26, 3), (35, 3), (28, 3), (36, 2), (31, 3), (30, 3), (29, 4), (34, 3), (27, 4), (26, 4), (37, 3), (32, 4), (28, 4), (33, 4), (36, 3), (30, 4), (35, 4), (31, 4), (36, 4), (34, 4), (37, 4),),
)
OFFERED = (20, 22, 24, 26)
RING = 8
NARROW = 38
ROWS = (32, 88)


def taken(unit, level):
    return [(unit, level) in events for events in PLAN].index(True)


class Sums:
    def __init__(self, down, made, own, stages, sums, local_sem, send_sem, recv_sem, peers):
        self.down, self.made, self.own, self.stages, self.sums = down, made, own, stages, sums
        self.local_sem, self.send_sem, self.recv_sem = local_sem, send_sem, recv_sem
        self.peers = peers
        seq, doc = lax.axis_index("seq"), lax.axis_index("doc")
        self.bits = {
            "core": seq % 2,
            "x": (seq // 2) % 2,
            "y": (seq // 4) % 2,
            "low": doc % 2,
            "high": (doc // 2) % 2,
        }

    def core_copy(self, kind, index):
        if kind == 0:
            source = self.made.at[index % RING, :, :, 1 - self.bits["core"]]
        else:
            source = self.down.at[:, :, 1 - self.bits["core"], :, :, :, pl.ds(index * UNIT, UNIT)]
        return remote(
            source,
            self.stages[kind][0].at[index],
            self.send_sem[kind].at[0, index],
            self.recv_sem[kind].at[0, index],
            self.peers["core"],
        )

    def own_copy(self, index):
        return pltpu.make_async_copy(
            self.down.at[:, :, self.bits["core"], :, :, :, pl.ds(index * UNIT, UNIT)],
            self.own.at[index % 2],
            self.local_sem.at[index % 2],
        )

    def put(self, unit, value):
        pl.when(unit >= RING)(lambda: self.core_copy(0, jnp.maximum(unit - RING, 0)).wait_send())
        self.made[unit % RING] = value.astype(jnp.bfloat16).reshape(self.made.shape[1:])
        self.core_copy(0, unit).start()

    def offer_down(self, index):
        self.core_copy(1, index).start()
        if index < 2 or taken(NARROW + index - 2, 0) < OFFERED[index]:
            self.own_copy(index).start()

    def half(self, kind, index, order, level, mine):
        name = order[level]
        left = [axis for axis in ("y", "x", "high", "low") if axis not in order[:level]]
        side = self.bits[name] if mine else 1 - self.bits[name]
        return (index,) + (slice(None),) * left.index(name) + (side,)

    def copy(self, kind, index, order, level):
        return remote(
            self.stages[kind][level - 1].at[self.half(kind, index, order, level - 1, False)],
            self.stages[kind][level].at[index],
            self.send_sem[kind].at[level, index],
            self.recv_sem[kind].at[level, index],
            self.peers[order[level - 1]],
        )

    def arrive(self, unit, level):
        kind = 0 if unit < NARROW else 1
        index = unit - kind * NARROW
        order = ALONG[TURNS[unit]]
        ref = self.stages[kind][level]
        if level == 0:
            self.core_copy(kind, index).wait_recv()
            if kind == 1:
                self.own_copy(index).wait()

            def add(i, carry):
                y, x = i // 2, i % 2
                mine = self.made[index % RING, y, x, self.bits["core"]] if kind == 0 else self.own[index % 2, y, x]
                ref[index, y, x] = ref[index, y, x] + mine
                return carry

            lax.fori_loop(0, 4, add, 0)
            if kind == 1 and index < 2 and taken(unit, 0) >= OFFERED[index + 2]:
                self.own_copy(index + 2).start()
        else:
            self.copy(kind, index, order, level).wait_recv()
            kept = self.stages[kind][level - 1][self.half(kind, index, order, level - 1, True)]
            if level < 4:
                ref[index] = ref[index] + kept
            else:
                self.sums[kind][index] = ref[index].astype(jnp.float32) + kept.astype(jnp.float32)
        if level < 4:
            self.copy(kind, index, order, level + 1).start()

    def run(self, place):
        for unit, level in PLAN[place]:
            self.arrive(unit, level)

    def run_turn(self, first, turn, count):
        for k in range(count):
            if PLAN[first + k]:
                pl.when(turn == k)(lambda: self.run(first + k))

    def drain(self):
        for kind, count in enumerate((NARROW, 4)):
            def one(index, carry):
                pl.when((kind == 1) | (index >= NARROW - RING))(lambda: self.core_copy(kind, index).wait_send())
                for level in range(1, 5):
                    self.copy(kind, index, ALONG[0], level).wait_send()
                return carry

            lax.fori_loop(0, count, one, 0)


def back_kernel(
    limit_ref, mixed_in, qb_in, kb_in, vb_in, qx_in, mkb_in, mvb_in, ob_in, lse_in0, spots_in,
    tokens, cotangent, w_query, w_key, w_value, w_out, w_gate, w_up, w_down, gains_in,
    layer_out, grad_tokens, gate_rows, up_rows, query_rows, key_rows, value_rows, out_rows, down_rows, gains_out,
    mem_home, down, grad_middle,
    gb, gx, lse, delta, lse_in, delta_in, dq_cross, dqkv, mem_in, gain_buf, made, own, grad, *rest,
):
    stages = [rest[5 * c : 5 * c + 5] for c in range(2)]
    sums = rest[10:12]
    local_sem, send_sems, recv_sems, rest = rest[12], rest[13:15], rest[15:17], rest[17:]
    (
        in_sem, gb_local, gb_send, gb_recv, spot_sem, far_send, far_recv, row_send, row_recv, back_send, back_recv,
        mate_send, mate_recv, mem_local, mem_send, mem_recv, gain_send, gain_recv, load_sem, weight_sem, done_sem, front_sem, tile_sem, stage_sem,
    ) = rest
    core, chip, mate, across, diagonal = seats()
    seq, doc = lax.axis_index("seq"), lax.axis_index("doc")
    seq_count = mem_in.shape[0]
    block = tokens.shape[0]
    limit = limit_ref[0, seq // BPS]
    peers = {
        "core": mate,
        "x": across,
        "y": (flip(seq, 4), doc),
        "low": (seq, flip(doc, 1)),
        "high": (seq, flip(doc, 2)),
    }
    others = [(lax.rem(seq + away, seq_count), doc) for away in range(1, seq_count)]
    meet(others + [peers["low"], peers["high"]])
    engine = Sums(down, made, own, stages, sums, local_sem, send_sems, recv_sems, peers)

    def grad_copy(head, own):
        return remote(
            grad.at[:, head_lanes(core if own else 1 - core, head)],
            gx.at[core, head],
            far_send.at[0 if own else 1, head],
            far_recv.at[core, head],
            across if own else diagonal,
        )

    def arrived_grad(far, head):
        return remote(
            grad.at[:, head_lanes(core, head)], gx.at[far, head], far_send.at[0, head], far_recv.at[far, head], across
        )

    def row_copies():
        return (
            remote(lse, lse_in, row_send.at[0], row_recv.at[0], across),
            remote(delta, delta_in, row_send.at[1], row_recv.at[1], across),
        )

    def back_copy(blk, head):
        return remote(dq_cross.at[blk, head], dq_cross.at[blk, head], back_send.at[blk, head], back_recv.at[blk, head], across)

    def mate_copy(box, i, head):
        lanes = head_lanes(core, head)
        return remote(box.at[i, head], dqkv.at[i, :, lanes], mate_send.at[i, head], mate_recv.at[i, head], mate)

    def mate_arrival(i, head):
        lanes = head_lanes(1 - core, head)
        return remote(gb.at[0, head], dqkv.at[i, :, lanes], mate_send.at[i, head], mate_recv.at[i, head], mate)

    def mem_copy(box, away):
        peer = lax.rem(seq + away, seq_count)
        return remote(box.at[peer], mem_in.at[seq], mem_send.at[away - 1], mem_recv.at[away - 1], (peer, doc))

    def far_start(head):
        @pl.when(chip == 1)
        def _():
            grad_copy(head, True).start()
            grad_copy(head, False).start()

    def front(normed, normed_t, grad_y, total, back, hidden_t, mixed, middle, w_in, w_back):
        width = total.shape[1]
        tiles = w_gate.shape[1] // UNIT
        part = 128
        copies = [
            pltpu.make_async_copy(mixed_in, mixed, front_sem.at[0]),
            pltpu.make_async_copy(cotangent, grad_y, front_sem.at[1]),
        ]
        for copy in copies:
            copy.start()

        def strip(i):
            return pl.ds(pl.multiple_of(i * UNIT, UNIT), UNIT)

        def chunk(i):
            return pl.ds(pl.multiple_of(i * part, part), part)

        def opening(rows, weights):
            loads = [
                pltpu.make_async_copy(tokens, rows, front_sem.at[2]),
                pltpu.make_async_copy(w_out, weights, front_sem.at[3]),
            ]
            for copy in loads:
                copy.start()
            for copy in copies + loads:
                copy.wait()

            def join(j, carry):
                middle[:, strip(j)] = rows[:, strip(j)].astype(jnp.float32) + matmul(mixed[...], weights[:, strip(j)], NN)
                return carry

            lax.fori_loop(0, width // UNIT, join, 0)

            def norm(i, carry):
                x = middle[chunk(i), :]
                factor = lax.rsqrt(jnp.mean(x * x, axis=-1, keepdims=True) + EPS)
                value = x * factor * gains_in[1:2, :]
                normed[chunk(i), :] = value.astype(jnp.bfloat16)
                normed_t[:, chunk(i)] = value.T.astype(jnp.bfloat16)
                total[chunk(i), :] = jnp.zeros((part, width), jnp.float32)
                back[chunk(i), :] = jnp.zeros((part, width), jnp.float32)
                return carry

            lax.fori_loop(0, block // part, norm, 0)

        def tile_loads(tile):
            slot = tile % 2
            return (
                pltpu.make_async_copy(w_gate.at[:, strip(tile)], w_in.at[slot, 0], tile_sem.at[slot, 0]),
                pltpu.make_async_copy(w_up.at[:, strip(tile)], w_in.at[slot, 1], tile_sem.at[slot, 1]),
                pltpu.make_async_copy(w_down.at[strip(tile), :], w_back.at[slot], tile_sem.at[slot, 2]),
            )

        for copy in tile_loads(0):
            copy.start()
        pl.run_scoped(
            opening,
            pltpu.VMEM(tokens.shape, jnp.bfloat16), pltpu.VMEM(w_out.shape, jnp.bfloat16),
        )

        def hidden_units():
            def one(tile, carry):
                slot = tile % 2

                @pl.when(tile + 1 < tiles)
                def _():
                    for copy in tile_loads(tile + 1):
                        copy.start()

                for copy in tile_loads(tile):
                    copy.wait()
                opened = matmul(normed[...], w_in[slot, 0], NN)
                upper = matmul(normed[...], w_in[slot, 1], NN)
                sigma = 1.0 / (1.0 + jnp.exp(-opened))
                gated = opened * sigma
                hidden = gated * upper
                total[...] += matmul(hidden.astype(jnp.bfloat16), w_back[slot], NN)
                hidden_t[strip(tile), :] = hidden.T.astype(jnp.bfloat16)
                grad_hidden = matmul(grad_y[...], w_back[slot], NT)
                grad_opened = (grad_hidden * upper * sigma * (1.0 + opened * (1.0 - sigma))).astype(jnp.bfloat16)
                grad_upper = (grad_hidden * gated).astype(jnp.bfloat16)
                back[...] += matmul(grad_opened, w_in[slot, 0], NT) + matmul(grad_upper, w_in[slot, 1], NT)
                for kind, value in enumerate((grad_opened, grad_upper)):
                    engine.put(2 * tile + kind, matmul(normed_t[...], value, NN))
                engine.run_turn(0, tile, tiles)
                return carry

            lax.fori_loop(0, tiles, one, 0)

        hidden_units()

        def closing(branch, stage_down):
            loads = [
                pltpu.make_async_copy(w_out.at[:, strip(p)], w_in.at[p // 2, p % 2], tile_sem.at[p // 2, p % 2])
                for p in range(4)
            ]
            for copy in loads:
                copy.start()
            engine.run(11)

            def norm_back(i, carry):
                x = middle[chunk(i), :]
                factor = lax.rsqrt(jnp.mean(x * x, axis=-1, keepdims=True) + EPS)
                unit = x * factor
                grad_normed = back[chunk(i), :]
                normed[chunk(i), :] = (x + total[chunk(i), :]).astype(jnp.bfloat16)
                scaled = gains_in[1:2, :] * grad_normed
                inner = jnp.mean(scaled * unit, axis=-1, keepdims=True)
                value = grad_y[chunk(i), :].astype(jnp.float32) + factor * (scaled - unit * inner)
                middle[chunk(i), :] = value
                branch[chunk(i), :] = value.astype(jnp.bfloat16)
                return carry + jnp.sum(grad_normed * unit, axis=0, keepdims=True)

            gain_buf[0, 0, 1] = lax.fori_loop(0, block // part, norm_back, jnp.zeros((1, width), jnp.float32))
            writes = [
                pltpu.make_async_copy(normed, layer_out, front_sem.at[0]),
                pltpu.make_async_copy(middle, grad_middle, front_sem.at[2]),
            ]
            for copy in writes:
                copy.start()

            engine.run(12)

            for copy in loads:
                copy.wait()
            for j in (0, 2, 1, 3):
                at = slice(j * UNIT, (j + 1) * UNIT)
                value = 0.0
                for p in range(4):
                    value = value + matmul(branch[:, p * UNIT : (p + 1) * UNIT], w_in[p // 2, p % 2, at, :], NT)
                grad[:, at] = value.astype(jnp.bfloat16)
                if j == 2:
                    far_start(0)
            engine.run(13)
            far_start(1)
            share_heads((grad,), (gb,), core, mate, gb_local, gb_send, gb_recv)

            def turn_over(i, carry):
                normed_t[:, chunk(i)] = mixed[chunk(i), :].astype(jnp.float32).T.astype(jnp.bfloat16)
                return carry

            lax.fori_loop(0, block // part, turn_over, 0)

            for j in range(4):
                engine.put(jnp.int32(22 + j), matmul(normed_t[...], branch[:, j * UNIT : (j + 1) * UNIT], NN))
                engine.run(14 + j)
            deep = stage_down.shape[4]
            tall = 8 * deep

            def down_store(n):
                i = n % 4
                return pltpu.make_async_copy(
                    stage_down.at[n % 2], down.at[i // 2, i % 2, :, :, :, :, strip(n // 4)], stage_sem.at[n % 2]
                )

            def down_part(n):
                i, j = n % 4, n // 4
                value = matmul(hidden_t[pl.ds(pl.multiple_of(i * tall, 64), tall), :], grad_y[:, strip(j)], NN)
                pl.when(n > 1)(lambda: down_store(n - 2).wait())
                for k in range(8):
                    stage_down[n % 2, k // 4, (k // 2) % 2, k % 2] = value[k * deep : (k + 1) * deep].astype(jnp.bfloat16)
                down_store(n).start()

            def down_parts(m, carry):
                down_part(2 * m)
                down_part(2 * m + 1)
                for j in range(3):
                    pl.when(m == 2 * j + 2)(lambda: engine.offer_down(j))
                pl.when(m == 1)(lambda: far_start(2))
                pl.when(m == 4)(lambda: far_start(3))
                engine.run_turn(18, m, 8)
                return carry

            lax.fori_loop(0, 8, down_parts, 0)
            down_store(14).wait()
            down_store(15).wait()
            engine.offer_down(3)
            for copy in writes:
                copy.wait()

        pl.run_scoped(
            closing,
            pltpu.VMEM(normed.shape, jnp.bfloat16),
            pltpu.VMEM((2, 2, 2, 2, ROWS[1], UNIT), jnp.bfloat16),
        )

    pl.run_scoped(
        front,
        pltpu.VMEM(tokens.shape, jnp.bfloat16), pltpu.VMEM((tokens.shape[1], block), jnp.bfloat16),
        pltpu.VMEM(tokens.shape, jnp.bfloat16), pltpu.VMEM(tokens.shape, jnp.float32), pltpu.VMEM(tokens.shape, jnp.float32),
        pltpu.VMEM((w_gate.shape[1], block), jnp.bfloat16), pltpu.VMEM(tokens.shape, jnp.bfloat16),
        pltpu.VMEM(tokens.shape, jnp.float32), pltpu.VMEM((2, 2, tokens.shape[1], UNIT), jnp.bfloat16),
        pltpu.VMEM((2, UNIT, tokens.shape[1]), jnp.bfloat16),
    )

    def attention(qb, kb, vb, qx, mkb, mvb, ob, dq_own, dk_sum, dv_sum, dm, dqkv_mate, mem_out, spots):
        inputs = [
            pltpu.make_async_copy(src, dst, in_sem.at[i])
            for i, (src, dst) in enumerate(
                ((qb_in, qb), (kb_in, kb), (vb_in, vb), (mkb_in, mkb), (mvb_in, mvb), (ob_in, ob), (lse_in0, lse), (qx_in, qx))
            )
        ]
        spot_copies = [pltpu.make_async_copy(spots_in, spots, spot_sem.at[0])]
        for copy in inputs + spot_copies:
            copy.start()
        for head in range(HALF):
            remote(grad.at[:, head_lanes(core, head)], gb.at[core, head], gb_send.at[0, head], gb_recv.at[0, head], mate).wait()
            pltpu.make_async_copy(grad.at[:, head_lanes(core, head)], gb.at[core, head], gb_local.at[0, head]).wait()
        for copy in inputs + spot_copies:
            copy.wait()
        engine.run(26)

        def rows(i, carry):
            head, blk = i // 2, i % 2
            product = gb[blk, head].astype(jnp.float32) * ob[blk, head].astype(jnp.float32)
            delta[blk, head] = jnp.sum(product.T, axis=0, keepdims=True)
            return carry

        lax.fori_loop(0, 2 * HALF, rows, 0)

        @pl.when(chip == 1)
        def _():
            for copy in row_copies():
                copy.start()

        def pull(key_rows, value_rows, query, grad_rows, level, inner, where):
            scores = matmul(key_rows, query, NT) * (SCALE * LOG2E)
            if where is not None:
                scores = masked(scores, where[0], limit, where[1])
            weights = jnp.exp2(scores - level)
            grad_weights = matmul(value_rows, grad_rows, NT)
            grad_scores = (weights * (grad_weights - inner)).astype(jnp.bfloat16)
            return (
                matmul(grad_scores, query, NN),
                matmul(weights.astype(jnp.bfloat16), grad_rows, NN),
                matmul(key_rows, grad_scores, TN),
            )

        def own_head(head, carry):
            lanes = pl.ds(pl.multiple_of(head * HEAD_DIM, HEAD_DIM), HEAD_DIM)
            for blk in range(2):
                query, grad_rows = qb[blk, head], gb[blk, head]
                level, inner = lse[blk, head], delta[blk, head]
                total = 0.0
                for kblk in range(blk + 1):
                    gk, gv, gq = pull(
                        kb[kblk, head], vb[kblk, head], query, grad_rows, level, inner,
                        ((2 * chip + kblk) * block, kblk == blk),
                    )
                    if kblk == blk:
                        dk_sum[kblk, head], dv_sum[kblk, head] = gk, gv
                    else:
                        dk_sum[kblk, head] += gk
                        dv_sum[kblk, head] += gv
                    total = total + gq
                gk, gv, gq = pull(mkb[blk, head], mvb[blk, head], query, grad_rows, level, inner, None)
                dm[blk, 0, :, lanes] = (gk * SCALE).astype(jnp.bfloat16)
                dm[blk, 1, :, lanes] = gv.astype(jnp.bfloat16)
                dq_own[blk, head] = total + gq
            engine.run_turn(27, head, HALF)
            return carry

        lax.fori_loop(0, HALF, own_head, 0)

        for blk in range(2):
            for kind in range(2):
                rows_out = matmul(spots[blk], dm[blk, kind], NN).astype(jnp.bfloat16)
                mem_out[:, blk, kind] = rows_out.reshape(mem_out.shape[0], mem_out.shape[3], mem_out.shape[4])
        for away in range(1, seq_count):
            mem_copy(mem_out, away).start()
        own_rows = pltpu.make_async_copy(mem_out.at[seq], mem_in.at[seq], mem_local.at[0])
        own_rows.start()
        engine.run(31)

        @pl.when(chip == 0)
        def _():
            for copy in row_copies():
                copy.wait_recv()

        def far_turn(i, carry):
            head, blk = i // 2, i % 2

            @pl.when(chip == 0)
            def _():
                arrived_grad(blk, head).wait_recv()
                query, grad_rows = qx[blk, head], gx[blk, head]
                level, inner = lse_in[blk, head], delta_in[blk, head]
                total = 0.0
                for kblk in range(2):
                    gk, gv, gq = pull(
                        kb[kblk, head], vb[kblk, head], query, grad_rows, level, inner, (kblk * block, False)
                    )
                    dk_sum[kblk, head] += gk
                    dv_sum[kblk, head] += gv
                    total = total + gq
                dq_cross[blk, head] = total.astype(jnp.bfloat16)
                back_copy(blk, head).start()

            engine.run_turn(32, i, 2 * HALF)

            @pl.when(chip == 1)
            def _():
                back_copy(blk, head).wait_recv()
                dq_own[blk, head] += dq_cross[blk, head].astype(jnp.float32)

            return carry

        lax.fori_loop(0, 2 * HALF, far_turn, 0)

        def results(blk, head):
            return (
                (dq_own[blk, head].T * SCALE).astype(jnp.bfloat16),
                (dk_sum[blk, head] * SCALE).astype(jnp.bfloat16),
                dv_sum[blk, head].astype(jnp.bfloat16),
            )

        def for_mate(head, carry):
            for i, value in enumerate(results(1 - core, head)):
                dqkv_mate[i, head] = value
                mate_copy(dqkv_mate, i, head).start()
            return carry

        def for_own(head, carry):
            for i, value in enumerate(results(core, head)):
                dqkv[i, :, head_lanes(core, head)] = value
            return carry

        lax.fori_loop(0, HALF, for_mate, 0)
        engine.run(40)
        lax.fori_loop(0, HALF, for_own, 0)
        engine.run(41)
        for away in range(1, seq_count):
            mem_copy(mem_out, away).wait_send()
        own_rows.wait()
        for i in range(3):
            for head in range(HALF):
                mate_copy(dqkv_mate, i, head).wait_send()

    box = (2, HALF, block, HEAD_DIM)
    mem_box = mkb_in.shape
    low, full = jnp.bfloat16, jnp.float32
    pl.run_scoped(
        attention,
        pltpu.VMEM(box, low), pltpu.VMEM(box, low), pltpu.VMEM(box, low), pltpu.VMEM(box, low),
        pltpu.VMEM(mem_box, low), pltpu.VMEM(mem_box, low), pltpu.VMEM(box, low),
        pltpu.VMEM((2, HALF, HEAD_DIM, block), full), pltpu.VMEM(box, full), pltpu.VMEM(box, full),
        pltpu.VMEM((2, 2, mem_box[2], HALF * HEAD_DIM), low),
        pltpu.VMEM((3, HALF, block, HEAD_DIM), low), pltpu.VMEM(mem_in.shape, low), pltpu.VMEM(spots_in.shape, low),
    )

    def tail(normed, dx, middle, rows, weights):
        width = dx.shape[1]
        chunk = weights.shape[2]
        loads = [
            pltpu.make_async_copy(tokens, rows, load_sem.at[1]),
            pltpu.make_async_copy(grad_middle, middle, load_sem.at[2]),
        ]

        def weight_copies(j):
            at = pl.ds(pl.multiple_of(j * chunk, chunk), chunk)
            return [
                pltpu.make_async_copy(w.at[at, :], weights.at[j % 2, i], weight_sem.at[j % 2, i])
                for i, w in enumerate((w_query, w_key, w_value))
            ]

        for copy in loads + weight_copies(0):
            copy.start()
        loads[0].wait()
        part = 64

        def norm(i, carry):
            at = pl.ds(pl.multiple_of(i * 2 * part, 2 * part), 2 * part)
            x = rows[at, :].astype(jnp.float32)
            factor = lax.rsqrt(jnp.mean(x * x, axis=-1, keepdims=True) + EPS)
            normed[:, at] = (x * factor * gains_in[0:1, :]).T.astype(jnp.bfloat16)
            return carry

        lax.fori_loop(0, block // (2 * part), norm, 0)
        for i in range(3):
            for head in range(HALF):
                mate_arrival(i, head).wait_recv()
        engine.run(42)

        def make(w):
            lanes = pl.ds(pl.multiple_of(lax.rem(w, 4) * UNIT, UNIT), UNIT)
            engine.put(26 + w, matmul(normed[...], dqkv[w // 4, :, lanes], NN))

        def build(j, carry):
            make(2 * j)
            make(2 * j + 1)
            engine.run_turn(43, j, 6)
            return carry

        lax.fori_loop(0, 6, build, 0)

        def input_part(j, carry):
            for copy in weight_copies(j):
                copy.wait()

            @pl.when(j < 3)
            def _():
                for copy in weight_copies(j + 1):
                    copy.start()

            total = 0.0
            for i in range(3):
                total = total + matmul(dqkv[i], weights[j % 2, i], NT)
            dx[:, pl.ds(pl.multiple_of(j * chunk, chunk), chunk)] = total
            engine.run_turn(49, j, 4)
            return carry

        lax.fori_loop(0, 4, input_part, 0)
        loads[1].wait()

        def norm_back(i, carry):
            at = pl.ds(pl.multiple_of(i * part, part), part)
            x = rows[at, :].astype(jnp.float32)
            factor = lax.rsqrt(jnp.mean(x * x, axis=-1, keepdims=True) + EPS)
            unit = x * factor
            grad_normed = dx[at, :]
            scaled = gains_in[0:1, :] * grad_normed
            inner = jnp.mean(scaled * unit, axis=-1, keepdims=True)
            rows[at, :] = (middle[at, :] + factor * (scaled - unit * inner)).astype(jnp.bfloat16)
            return carry + jnp.sum(grad_normed * unit, axis=0, keepdims=True)

        gain_buf[0, 0, 0] = lax.fori_loop(0, block // part, norm_back, jnp.zeros((1, width), jnp.float32))
        out_copy = pltpu.make_async_copy(rows, grad_tokens, load_sem.at[1])
        out_copy.start()

        def gain_copy(level):
            name = ("core", "x", "y", "low", "high")[level]
            return remote(
                gain_buf.at[0, level], gain_buf.at[1, level], gain_send.at[level], gain_recv.at[level], peers[name]
            )

        gain_copy(0).start()
        engine.run(53)
        for away in range(1, seq_count):
            source = lax.rem(seq + seq_count - away, seq_count)
            remote(mem_in.at[source], mem_in.at[source], mem_send.at[away - 1], mem_recv.at[away - 1], (source, doc)).wait_recv()
        mem_copy_out = pltpu.make_async_copy(mem_in, mem_home, load_sem.at[2])
        mem_copy_out.start()
        engine.run(54)
        engine.run(55)
        events = PLAN[56]
        stops = [len(events) * k // 6 for k in range(1, 6)]
        for n, (unit, level) in enumerate(events):
            for step in range(5):
                if n == stops[step]:
                    gain_copy(step).wait_recv()
                    total = gain_buf[0, step] + gain_buf[1, step]
                    if step < 4:
                        gain_buf[0, step + 1] = total
                        gain_copy(step + 1).start()
                    else:
                        gains_out[...] = total
            engine.arrive(unit, level)
        homes = []
        for u in range(11):
            homes += [(0, 2 * u, gate_rows, u), (0, 2 * u + 1, up_rows, u)]
        for j in range(4):
            homes += [(0, 22 + j, out_rows, j), (0, 26 + j, query_rows, j), (0, 30 + j, key_rows, j), (0, 34 + j, value_rows, j)]
            homes.append((1, j, down_rows, j))
        outs = []
        for i, (kind, unit, ref, place) in enumerate(homes):
            outs.append(
                pltpu.make_async_copy(sums[kind].at[unit], ref.at[:, pl.ds(place * UNIT, UNIT)], done_sem.at[i])
            )
            outs[-1].start()
        engine.drain()
        for level in range(5):
            gain_copy(level).wait_send()
        for copy in outs + [out_copy, mem_copy_out]:
            copy.wait()

    width = w_query.shape[0]
    pl.run_scoped(
        tail,
        pltpu.VMEM((width, block), low),
        pltpu.VMEM((block, width), full), pltpu.VMEM((block, width), full), pltpu.VMEM((block, width), low),
        pltpu.VMEM((2, 3, UNIT, width), low),
    )

    @pl.when(chip == 0)
    def _():
        for head in range(HALF):
            for blk in range(2):
                back_copy(blk, head).wait_send()

    @pl.when(chip == 1)
    def _():
        for copy in row_copies():
            copy.wait_send()
        for head in range(HALF):
            grad_copy(head, True).wait_send()
            grad_copy(head, False).wait_send()


def go_back(limit, attended, saved, tokens, cotangent, weights, gains):
    block, width = tokens.shape
    low, full = jnp.bfloat16, jnp.float32
    box = (2, HALF, block, HEAD_DIM)
    row = (2, HALF, 1, block)
    seq_count = lax.axis_size("seq")
    capacity = 2 * TOPK // seq_count
    dma = pltpu.SemaphoreType.DMA
    hbm, vmem = pl.BlockSpec(memory_space=pl.ANY), pl.BlockSpec(memory_space=pltpu.VMEM)
    struct = jax.ShapeDtypeStruct
    ff = weights[4].shape[1]
    *saved, picked_t = saved
    spots = saved[8]

    def wide(rows, columns):
        return struct((2, 2, 2, 2, 2, rows, columns), low)

    mem = (seq_count, 2, 2, capacity, HALF * HEAD_DIM)
    units = (NARROW, 4)
    scratch = [
        pltpu.VMEM(box, low), pltpu.VMEM(box, low),
        pltpu.VMEM(row, full), pltpu.VMEM(row, full), pltpu.VMEM(row, full), pltpu.VMEM(row, full),
        pltpu.VMEM((2, HALF, HEAD_DIM, block), low),
        pltpu.VMEM((3, block, width), low), pltpu.VMEM(mem, low),
        pltpu.VMEM((2, 5, 2, 1, width), full),
        pltpu.VMEM((RING, 2, 2, 2, 2, 2, ROWS[0], UNIT), low),
        pltpu.VMEM((2, 2, 2, 2, 2, ROWS[1], UNIT), low),
        pltpu.VMEM((block, width), low),
    ]
    for c in range(2):
        scratch += [pltpu.VMEM((units[c],) + (2,) * k + (ROWS[c], UNIT), low) for k in (4, 3, 2, 1, 0)]
    scratch += [pltpu.VMEM((units[c], ROWS[c], UNIT), full) for c in range(2)]
    scratch += [dma((2,))]
    scratch += [dma((5, units[c])) for c in range(2)] * 2
    scratch += [
        dma((8,)), dma((1, HALF)), dma((1, HALF)), dma((1, HALF)), dma((1,)),
        dma((2, HALF)), dma((2, HALF)), dma((2,)), dma((2,)), dma((2, HALF)), dma((2, HALF)),
        dma((3, HALF)), dma((3, HALF)), dma((1,)), dma((seq_count - 1,)), dma((seq_count - 1,)),
        dma((5,)), dma((5,)), dma((4,)), dma((2, 3)), dma((sum(units),)),
        dma((5,)), dma((2, 3)), dma((2,)),
    ]
    rows = struct((32, width), full)
    mem_rows = picked_t.shape[0]
    results = pl.pallas_call(
        back_kernel,
        out_shape=(
            struct((block, width), low), struct((block, width), low),
            struct((32, ff), full), struct((32, ff), full),
            rows, rows, rows, rows,
            struct((88, width), full), struct((2, 1, width), full),
            struct(mem, low),
            wide(88, width),
            struct((block, width), full),
        ),
        in_specs=[pl.BlockSpec(memory_space=pltpu.SMEM)] + [hbm] * 19 + [vmem],
        out_specs=(hbm,) * 9 + (vmem,) + (hbm,) * 3,
        scratch_shapes=scratch,
        name="go_back",
        compiler_params=pltpu.CompilerParams(collective_id=3, has_side_effects=True, vmem_limit_bytes=60 * 2**20),
    )(limit, attended, *saved, tokens, cotangent, *weights, gains)
    return deliver(results[:9], results[10], picked_t) + (results[9],)


def deliver_kernel(*refs):
    sources, mem_home, picked_t = refs[:9], refs[9], refs[10]
    targets, tables = refs[11:20], refs[20:22]
    boxes, rest = refs[22:31], refs[31:]
    rows, pick, table, in_sem, out_sem, load_sem, table_sem = rest
    loads = [
        pltpu.make_async_copy(mem_home, rows, load_sem.at[0]),
        pltpu.make_async_copy(picked_t, pick, load_sem.at[1]),
    ]
    ins = [pltpu.make_async_copy(a, b, in_sem.at[i]) for i, (a, b) in enumerate(zip(sources, boxes))]
    outs = [pltpu.make_async_copy(a, b, out_sem.at[i]) for i, (a, b) in enumerate(zip(boxes, targets))]
    for copy in loads + ins:
        copy.start()
    for copy in loads:
        copy.wait()
    half = rows.shape[4]
    stores = []
    for kind in range(2):
        for side in range(2):
            values = jnp.concatenate(
                [rows[2 * src + side, blk, kind] for src in range(rows.shape[0] // 2) for blk in range(2)], axis=0
            )
            table[2 * kind + side] = matmul(pick[...], values, NN)
            stores.append(
                pltpu.make_async_copy(
                    table.at[2 * kind + side],
                    tables[kind].at[:, side * half : (side + 1) * half],
                    table_sem.at[2 * kind + side],
                )
            )
            stores[-1].start()
    for arrived, left in zip(ins, outs):
        arrived.wait()
        left.start()
    for copy in stores + outs:
        copy.wait()


def deliver(arrays, mem_home, picked_t):
    struct = jax.ShapeDtypeStruct
    hbm = pl.BlockSpec(memory_space=pl.ANY)
    mem_rows, half = picked_t.shape[0], mem_home.shape[4]
    table = struct((mem_rows, 2 * half), jnp.float32)
    return tuple(
        pl.pallas_call(
            deliver_kernel,
            out_shape=tuple(struct(a.shape, a.dtype) for a in arrays) + (table, table),
            in_specs=[hbm] * 11,
            out_specs=(hbm,) * 11,
            scratch_shapes=[pltpu.VMEM(a.shape, a.dtype) for a in arrays] + [
                pltpu.VMEM(mem_home.shape, jnp.bfloat16), pltpu.VMEM(picked_t.shape, jnp.bfloat16),
                pltpu.VMEM((4, mem_rows, half), jnp.float32),
                pltpu.SemaphoreType.DMA((9,)), pltpu.SemaphoreType.DMA((9,)), pltpu.SemaphoreType.DMA((2,)), pltpu.SemaphoreType.DMA((4,)),
            ],
            name="deliver",
            compiler_params=pltpu.CompilerParams(vmem_limit_bytes=60 * 2**20),
        )(*arrays, mem_home, picked_t)
    )


def rms_factor(values):
    return lax.rsqrt(jnp.mean(values * values, axis=-1, keepdims=True) + EPS)


def dot32(left, right):
    return jnp.dot(left, right, preferred_element_type=jnp.float32)


def fitting():
    return (lax.axis_size("seq"), lax.axis_size("doc")) == (8, 4)


def exchange(rows, owner_count, capacity):
    parts, _, width = rows.shape
    shaped = rows.reshape(parts, owner_count, capacity, width)
    moved = lax.all_to_all(shaped, "seq", split_axis=1, concat_axis=1, tiled=True)
    return moved.reshape(parts, owner_count * capacity, width)


def on_device(
    tokens,
    cotangent,
    attn_gain,
    w_query,
    w_key,
    w_value,
    w_out,
    ffn_gain,
    w_gate,
    w_up,
    w_down,
    mem_keys,
    mem_values,
    seg_len,
    mem_idx,
):
    low = jnp.bfloat16
    stream_count, block_len, model_width = tokens.shape
    mem_rows = mem_keys.shape[1]
    seq_count = lax.axis_size("seq")
    segment = lax.axis_index("seq") // BPS
    capacity = 2 * TOPK // seq_count
    slot_count = seq_count * capacity
    limit = lax.dynamic_index_in_dim(seg_len, segment, 1, keepdims=False)

    gain_one = attn_gain.astype(jnp.float32)
    gain_two = ffn_gain.astype(jnp.float32)
    if fitting():
        gains = jnp.stack((attn_gain, ffn_gain)).astype(jnp.float32)
        attended, *saved = go_forward(
            seg_len, tokens[0], gains, (w_query, w_key, w_value), mem_keys[0], mem_values[0], mem_idx[0]
        )
        layer_out, grad_tokens, gate_rows, up_rows, query_rows, key_rows, value_rows, out_rows, down_rows, grad_mk, grad_mv, summed = go_back(
            seg_len,
            attended,
            saved,
            tokens[0],
            cotangent[0],
            (w_query, w_key, w_value, w_out, w_gate, w_up, w_down),
            gains,
        )
        index = lax.axis_index("seq") * lax.axis_size("doc") + lax.axis_index("doc")
        parts = summed.reshape(2, seq_count * lax.axis_size("doc"), -1)
        attn_row, ffn_row = lax.dynamic_index_in_dim(parts, index, 1, keepdims=False)
        return (
            layer_out[None],
            grad_tokens[None],
            attn_row,
            query_rows,
            key_rows,
            value_rows,
            out_rows,
            ffn_row,
            gate_rows,
            up_rows,
            down_rows,
            grad_mk[None],
            grad_mv[None],
        )

    tokens_f = tokens[0].astype(jnp.float32)
    factor_one = rms_factor(tokens_f)
    unit_one = tokens_f * factor_one
    normed_one = (unit_one * gain_one).astype(low)
    chosen = mem_idx[0, 0]
    owner = chosen // mem_rows
    order = jnp.arange(TOPK)
    same_before = (owner[:, None] == owner[None, :]) & (order[None, :] < order[:, None])
    slot = owner * capacity + jnp.sum(same_before.astype(jnp.int32), axis=1)
    placed = slot[:, None] == jnp.arange(slot_count)[None, :]
    request = jnp.sum(jnp.where(placed, (chosen % mem_rows)[:, None] + 1, 0), axis=0) - 1
    requested = lax.all_to_all(
        request.reshape(seq_count, capacity), "seq", split_axis=0, concat_axis=0, tiled=True
    ).reshape(slot_count)
    picked = (requested[:, None] == jnp.arange(mem_rows)[None, :]).astype(low)
    placed = placed.astype(low)
    sent = jnp.stack((dot32(picked, mem_keys[0]).astype(low), dot32(picked, mem_values[0]).astype(low)))
    arrived = exchange(sent, seq_count, capacity)
    mem_key_rows = dot32(placed, arrived[0]).astype(low)
    mem_value_rows = dot32(placed, arrived[1]).astype(low)
    queries = dot32(normed_one, w_query).astype(low)
    keys = dot32(normed_one, w_key).astype(low)
    values = dot32(normed_one, w_value).astype(low)
    attended, *saved = attend_forward(limit, queries, keys, values, mem_key_rows, mem_value_rows)
    middle = tokens_f + dot32(attended, w_out)
    factor_two = rms_factor(middle)
    unit_two = middle * factor_two
    normed_two = (unit_two * gain_two).astype(low)
    gate = dot32(normed_two, w_gate)
    upper = dot32(normed_two, w_up)
    sigma = jax.nn.sigmoid(gate)
    hidden = (gate * sigma * upper).astype(low)
    layer_out = (middle + dot32(hidden, w_down)).astype(low)

    grad_y_low = cotangent[0]
    grad_y = grad_y_low.astype(jnp.float32)
    grad_down = dot32(hidden.T, grad_y_low)
    grad_hidden = dot32(grad_y_low, w_down.T)
    grad_gate_act = (grad_hidden * upper * sigma * (1.0 + gate * (1.0 - sigma))).astype(low)
    grad_up_act = (grad_hidden * gate * sigma).astype(low)
    grad_gate = dot32(normed_two.T, grad_gate_act)
    grad_up = dot32(normed_two.T, grad_up_act)
    grad_normed_two = dot32(grad_gate_act, w_gate.T) + dot32(grad_up_act, w_up.T)
    grad_ffn_gain = jnp.sum(grad_normed_two * unit_two, axis=0)
    scaled_two = gain_two * grad_normed_two
    grad_middle = grad_y + factor_two * (
        scaled_two - unit_two * jnp.mean(scaled_two * unit_two, axis=-1, keepdims=True)
    )
    grad_branch = grad_middle.astype(low)
    grad_out = dot32(attended.T, grad_branch)
    grad_attended = dot32(grad_branch, w_out.T).astype(low)
    grad_q, grad_k, grad_v, grad_mk, grad_mv = attend_backward(limit, grad_attended, saved)
    back = jnp.stack((dot32(placed.T, grad_mk).astype(low), dot32(placed.T, grad_mv).astype(low)))
    returned = exchange(back, seq_count, capacity)
    grad_mem_keys = dot32(picked.T, returned[0])
    grad_mem_values = dot32(picked.T, returned[1])
    grad_query = dot32(normed_one.T, grad_q)
    grad_key = dot32(normed_one.T, grad_k)
    grad_value = dot32(normed_one.T, grad_v)
    grad_normed_one = dot32(grad_q, w_query.T) + dot32(grad_k, w_key.T) + dot32(grad_v, w_value.T)
    grad_attn_gain = jnp.sum(grad_normed_one * unit_one, axis=0)
    scaled_one = gain_one * grad_normed_one
    grad_input = grad_middle + factor_one * (
        scaled_one - unit_one * jnp.mean(scaled_one * unit_one, axis=-1, keepdims=True)
    )
    grad_tokens = grad_input.astype(low)
    gate_rows, up_rows, query_rows, key_rows, value_rows, out_rows, down_rows, attn_row, ffn_row = [
        lax.psum_scatter(grad, ("seq", "doc"), scatter_dimension=0, tiled=True)
        for grad in (
            grad_gate, grad_up, grad_query, grad_key, grad_value, grad_out, grad_down, grad_attn_gain, grad_ffn_gain
        )
    ]
    return (
        layer_out[None],
        grad_tokens[None],
        attn_row,
        query_rows,
        key_rows,
        value_rows,
        out_rows,
        ffn_row,
        gate_rows,
        up_rows,
        down_rows,
        grad_mem_keys[None],
        grad_mem_values[None],
    )


def solution(mesh):
    in_specs = (
        P("doc", "seq", None),
        P("doc", "seq", None),
        P(),
        P(),
        P(),
        P(),
        P(),
        P(),
        P(),
        P(),
        P(),
        P("doc", "seq", None),
        P("doc", "seq", None),
        P("doc", None),
        P("doc", "seq", None),
    )
    out_specs = (
        P("doc", "seq", None),
        P("doc", "seq", None),
        P(("seq", "doc")),
        P(("seq", "doc"), None),
        P(("seq", "doc"), None),
        P(("seq", "doc"), None),
        P(("seq", "doc"), None),
        P(("seq", "doc")),
        P(("seq", "doc"), None),
        P(("seq", "doc"), None),
        P(("seq", "doc"), None),
        P("doc", "seq", None),
        P("doc", "seq", None),
    )
    return jax.shard_map(
        on_device, mesh=mesh, in_specs=in_specs, out_specs=out_specs, check_vma=False
    )
```

```python
import functools
import math

import jax
import jax.numpy as jnp
from jax import lax
from jax.experimental import pallas as pl
from jax.experimental.pallas import tpu as pltpu
from jax.sharding import PartitionSpec as P

HEADS = 8
HEAD_DIM = 128
TOPK = 128
BPS = 4
NEG = -1000000000.0
MESH = pl.DeviceIdType.MESH
EPS = 1e-05
UNIT = 256
SKEW = 4


def flip(value, bit):
    return value + bit - 2 * bit * ((value // bit) % 2)


HALF = HEADS // 2
LOG2E = math.log2(math.e)
SCALE = HEAD_DIM ** (-0.5)
NT = (((1,), (1,)), ((), ()))
TN = (((0,), (0,)), ((), ()))
NN = (((1,), (0,)), ((), ()))


def matmul(left, right, dims):
    return lax.dot_general(left, right, dims, preferred_element_type=jnp.float32)


def seats():
    seq, doc = lax.axis_index("seq"), lax.axis_index("doc")
    core, chip = seq % 2, (seq // 2) % 2
    mate = (flip(seq, 1), doc)
    across = (flip(seq, 2), doc)
    diagonal = (flip(flip(seq, 2), 1), doc)
    return core, chip, mate, across, diagonal


def meet(peers):
    barrier = pltpu.get_barrier_semaphore()
    for peer in peers:
        pl.semaphore_signal(barrier, inc=1, device_id=peer, device_id_type=MESH)
    pl.semaphore_wait(barrier, len(peers))


def head_lanes(core, head):
    return pl.ds(pl.multiple_of((core * HALF + head) * HEAD_DIM, HEAD_DIM), HEAD_DIM)


def remote(src, dst, send, recv, peer):
    return pltpu.make_async_remote_copy(
        src_ref=src, dst_ref=dst, send_sem=send, recv_sem=recv, device_id=peer, device_id_type=MESH
    )


def share_heads(sources, boxes, core, mate, local_sem, send_sem, recv_sem):
    copies = []
    for i, (source, box) in enumerate(zip(sources, boxes)):
        for head in range(HALF):
            copies.append(
                remote(
                    source.at[:, head_lanes(1 - core, head)],
                    box.at[core, head],
                    send_sem.at[i, head],
                    recv_sem.at[i, head],
                    mate,
                )
            )
            copies[-1].start()
    for i, (source, box) in enumerate(zip(sources, boxes)):
        for head in range(HALF):
            copies.append(
                pltpu.make_async_copy(
                    source.at[:, head_lanes(core, head)], box.at[core, head], local_sem.at[i, head]
                )
            )
            copies[-1].start()
    return copies


def masked(scores, first_key, limit, diagonal):
    key = lax.broadcasted_iota(jnp.int32, scores.shape, 0)
    ok = key + first_key < limit
    if diagonal:
        ok = ok & (key <= lax.broadcasted_iota(jnp.int32, scores.shape, 1))
    return jnp.where(ok, scores, NEG)


def soften(parts):
    top = functools.reduce(
        jnp.maximum, [jnp.max(scores, axis=0, keepdims=True) for scores, _ in parts]
    )
    total, mixed = 0.0, 0.0
    for scores, values in parts:
        exponent = jnp.exp2(scores - top)
        total = total + jnp.sum(exponent, axis=0, keepdims=True)
        mixed = mixed + matmul(values, exponent.astype(jnp.bfloat16), TN)
    return mixed / total, top + jnp.log(total) * LOG2E


def forward_kernel(
    limit_ref, q, k, v, mk, mv,
    attended, qb, kb, vb, qx, mkb, mvb, ob, lse,
    mixed_own, mixed_out, mixed_in, lse_out, lse_in,
    local_sem, mate_send, mate_recv, far_send, far_recv, back_send, back_recv, end_sem,
):
    core, chip, mate, across, diagonal = seats()
    block = q.shape[0]
    limit = limit_ref[0]
    meet((mate, across, diagonal))

    def query_copy(head, own):
        return remote(
            q.at[:, head_lanes(core if own else 1 - core, head)],
            qx.at[core, head],
            far_send.at[0 if own else 1, head],
            far_recv.at[core, head],
            across if own else diagonal,
        )

    def arrived_query(far, head):
        return remote(
            q.at[:, head_lanes(core, head)], qx.at[far, head], far_send.at[0, head], far_recv.at[far, head], across
        )

    @pl.when(chip == 1)
    def _():
        for head in range(HALF):
            query_copy(head, True).start()
            query_copy(head, False).start()

    copies = share_heads((q, k, v, mk, mv), (qb, kb, vb, mkb, mvb), core, mate, local_sem, mate_send, mate_recv)
    for copy in copies:
        copy.wait()

    def own_part(blk, head):
        query = qb[blk, head]
        parts = []
        for kblk in range(blk + 1):
            scores = matmul(kb[kblk, head], query, NT) * (SCALE * LOG2E)
            scores = masked(scores, (2 * chip + kblk) * block, limit, kblk == blk)
            parts.append((scores, vb[kblk, head]))
        parts.append((matmul(mkb[blk, head], query, NT) * (SCALE * LOG2E), mvb[blk, head]))
        return soften(parts)

    for blk in range(2):
        def own_head(head, carry):
            mixed, level = own_part(blk, head)
            mixed_own[blk, head] = mixed
            lse[blk, head] = level
            return carry
        lax.fori_loop(0, HALF, own_head, 0)

    def back_copy(blk, head):
        return (
            remote(mixed_out.at[blk, head], mixed_in.at[blk, head], back_send.at[0, blk, head], back_recv.at[0, blk, head], across),
            remote(lse_out.at[blk, head], lse_in.at[blk, head], back_send.at[1, blk, head], back_recv.at[1, blk, head], across),
        )

    @pl.when(chip == 0)
    def _():
        def cross(i, carry):
            head, blk = i // 2, i % 2
            arrived_query(blk, head).wait_recv()
            query = qx[blk, head]
            parts = []
            for kblk in range(2):
                scores = matmul(kb[kblk, head], query, NT) * (SCALE * LOG2E)
                parts.append((masked(scores, kblk * block, limit, False), vb[kblk, head]))
            mixed, level = soften(parts)
            mixed_out[blk, head] = mixed.astype(jnp.bfloat16)
            lse_out[blk, head] = level
            for copy in back_copy(blk, head):
                copy.start()
            return carry
        lax.fori_loop(0, 2 * HALF, cross, 0)

        def finish(i, carry):
            head, blk = i // 2, i % 2
            ob[blk, head] = mixed_own[blk, head].T.astype(jnp.bfloat16)
            return carry
        lax.fori_loop(0, 2 * HALF, finish, 0)

    @pl.when(chip == 1)
    def _():
        def merge(i, carry):
            head, blk = i // 2, i % 2
            for copy in back_copy(blk, head):
                copy.wait_recv()
            near, far = lse[blk, head], lse_in[blk, head]
            top = jnp.maximum(near, far)
            near, far = jnp.exp2(near - top), jnp.exp2(far - top)
            total = near + far
            mixed = (mixed_own[blk, head] * near + mixed_in[blk, head].astype(jnp.float32) * far) / total
            ob[blk, head] = mixed.T.astype(jnp.bfloat16)
            lse[blk, head] = top + jnp.log(total) * LOG2E
            return carry
        lax.fori_loop(0, 2 * HALF, merge, 0)

    ends = []
    for head in range(HALF):
        ends.append(
            remote(ob.at[1 - core, head], attended.at[:, head_lanes(core, head)], end_sem.at[0, head], end_sem.at[1, head], mate)
        )
        ends.append(
            pltpu.make_async_copy(ob.at[core, head], attended.at[:, head_lanes(core, head)], end_sem.at[2, head])
        )
    for copy in ends:
        copy.start()
    for copy in ends:
        copy.wait()

    @pl.when(chip == 0)
    def _():
        for head in range(HALF):
            for blk in range(2):
                for copy in back_copy(blk, head):
                    copy.wait_send()

    @pl.when(chip == 1)
    def _():
        for head in range(HALF):
            query_copy(head, True).wait_send()
            query_copy(head, False).wait_send()


def attend_forward(limit, queries, keys, values, mem_keys, mem_values):
    block, width = queries.shape
    topk = mem_keys.shape[0]
    low, full = jnp.bfloat16, jnp.float32
    box = (2, HALF, block, HEAD_DIM)
    mem_box = (2, HALF, topk, HEAD_DIM)
    flat = (2, HALF, HEAD_DIM, block)
    row = (2, HALF, 1, block)
    dma = pltpu.SemaphoreType.DMA
    hbm, vmem = pl.BlockSpec(memory_space=pl.ANY), pl.BlockSpec(memory_space=pltpu.VMEM)
    struct = jax.ShapeDtypeStruct
    return pl.pallas_call(
        forward_kernel,
        out_shape=(
            struct((block, width), low),
            struct(box, low), struct(box, low), struct(box, low), struct(box, low),
            struct(mem_box, low), struct(mem_box, low), struct(box, low), struct(row, full),
        ),
        in_specs=[pl.BlockSpec(memory_space=pltpu.SMEM)] + [hbm] * 5,
        out_specs=(hbm,) + (vmem,) * 8,
        scratch_shapes=[
            pltpu.VMEM(flat, full), pltpu.VMEM(flat, low), pltpu.VMEM(flat, low),
            pltpu.VMEM(row, full), pltpu.VMEM(row, full),
            dma((5, HALF)), dma((5, HALF)), dma((5, HALF)),
            dma((2, HALF)), dma((2, HALF)), dma((2, 2, HALF)), dma((2, 2, HALF)), dma((3, HALF)),
        ],
        name="attend_forward",
        compiler_params=pltpu.CompilerParams(collective_id=1, has_side_effects=True, vmem_limit_bytes=56 * 2**20),
    )(limit, queries, keys, values, mem_keys, mem_values)


def backward_kernel(
    limit_ref, grad, qb, kb, vb, qx, mkb, mvb, ob, lse,
    dq, dk, dv, dmk, dmv,
    gb, gx, delta, lse_in, delta_in, dq_own, dq_out, dq_in, dk_sum, dv_sum, dmk_low, dmv_low, dqb, dkb, dvb,
    local_sem, mate_send, mate_recv, far_send, far_recv, row_send, row_recv, back_send, back_recv,
    end_local, end_send, end_recv,
):
    core, chip, mate, across, diagonal = seats()
    block = grad.shape[0]
    limit = limit_ref[0]
    meet((mate, across, diagonal))

    def grad_copy(head, own):
        return remote(
            grad.at[:, head_lanes(core if own else 1 - core, head)],
            gx.at[core, head],
            far_send.at[0 if own else 1, head],
            far_recv.at[core, head],
            across if own else diagonal,
        )

    def arrived_grad(far, head):
        return remote(
            grad.at[:, head_lanes(core, head)], gx.at[far, head], far_send.at[0, head], far_recv.at[far, head], across
        )

    def row_copies():
        return (
            remote(lse, lse_in, row_send.at[0], row_recv.at[0], across),
            remote(delta, delta_in, row_send.at[1], row_recv.at[1], across),
        )

    @pl.when(chip == 1)
    def _():
        for head in range(HALF):
            grad_copy(head, True).start()
            grad_copy(head, False).start()

    copies = share_heads((grad,), (gb,), core, mate, local_sem, mate_send, mate_recv)
    for copy in copies:
        copy.wait()

    def rows(i, carry):
        head, blk = i // 2, i % 2
        product = gb[blk, head].astype(jnp.float32) * ob[blk, head].astype(jnp.float32)
        delta[blk, head] = jnp.sum(product.T, axis=0, keepdims=True)
        return carry

    lax.fori_loop(0, 2 * HALF, rows, 0)

    @pl.when(chip == 1)
    def _():
        for copy in row_copies():
            copy.start()

    def pull(key_rows, value_rows, query, grad_rows, level, inner, where):
        scores = matmul(key_rows, query, NT) * (SCALE * LOG2E)
        if where is not None:
            scores = masked(scores, where[0], limit, where[1])
        weights = jnp.exp2(scores - level)
        grad_weights = matmul(value_rows, grad_rows, NT)
        grad_scores = (weights * (grad_weights - inner)).astype(jnp.bfloat16)
        return (
            matmul(grad_scores, query, NN),
            matmul(weights.astype(jnp.bfloat16), grad_rows, NN),
            matmul(key_rows, grad_scores, TN),
        )

    for blk in range(2):
        def own_head(head, carry):
            query, grad_rows = qb[blk, head], gb[blk, head]
            level, inner = lse[blk, head], delta[blk, head]
            total = 0.0
            for kblk in range(blk + 1):
                gk, gv, gq = pull(
                    kb[kblk, head], vb[kblk, head], query, grad_rows, level, inner,
                    ((2 * chip + kblk) * block, kblk == blk),
                )
                if kblk == blk:
                    dk_sum[kblk, head], dv_sum[kblk, head] = gk, gv
                else:
                    dk_sum[kblk, head] += gk
                    dv_sum[kblk, head] += gv
                total = total + gq
            gk, gv, gq = pull(mkb[blk, head], mvb[blk, head], query, grad_rows, level, inner, None)
            dmk_low[blk, head] = (gk * SCALE).astype(jnp.bfloat16)
            dmv_low[blk, head] = gv.astype(jnp.bfloat16)
            dq_own[blk, head] = total + gq
            return carry
        lax.fori_loop(0, HALF, own_head, 0)

    def back_copy(blk, head):
        return remote(dq_out.at[blk, head], dq_in.at[blk, head], back_send.at[blk, head], back_recv.at[blk, head], across)

    @pl.when(chip == 0)
    def _():
        for copy in row_copies():
            copy.wait_recv()

        def cross(i, carry):
            head, blk = i // 2, i % 2
            arrived_grad(blk, head).wait_recv()
            query, grad_rows = qx[blk, head], gx[blk, head]
            level, inner = lse_in[blk, head], delta_in[blk, head]
            total = 0.0
            for kblk in range(2):
                gk, gv, gq = pull(
                    kb[kblk, head], vb[kblk, head], query, grad_rows, level, inner, (kblk * block, False)
                )
                dk_sum[kblk, head] += gk
                dv_sum[kblk, head] += gv
                total = total + gq
            dq_out[blk, head] = total.astype(jnp.bfloat16)
            back_copy(blk, head).start()
            return carry
        lax.fori_loop(0, 2 * HALF, cross, 0)

    def finish(i, carry):
        head, blk = i // 2, i % 2
        dqb[blk, head] = (dq_own[blk, head].T * SCALE).astype(jnp.bfloat16)
        dkb[blk, head] = (dk_sum[blk, head] * SCALE).astype(jnp.bfloat16)
        dvb[blk, head] = dv_sum[blk, head].astype(jnp.bfloat16)
        return carry

    @pl.when(chip == 1)
    def _():
        def merge(i, carry):
            head, blk = i // 2, i % 2
            back_copy(blk, head).wait_recv()
            dq_own[blk, head] += dq_in[blk, head].astype(jnp.float32)
            return finish(i, carry)
        lax.fori_loop(0, 2 * HALF, merge, 0)

    @pl.when(chip == 0)
    def _():
        lax.fori_loop(0, 2 * HALF, finish, 0)

    ends = []
    for i, (box, out) in enumerate(((dqb, dq), (dkb, dk), (dvb, dv), (dmk_low, dmk), (dmv_low, dmv))):
        for head in range(HALF):
            lanes = head_lanes(core, head)
            ends.append(remote(box.at[1 - core, head], out.at[:, lanes], end_send.at[i, head], end_recv.at[i, head], mate))
            ends.append(pltpu.make_async_copy(box.at[core, head], out.at[:, lanes], end_local.at[i, head]))
    for copy in ends:
        copy.start()
    for copy in ends:
        copy.wait()

    @pl.when(chip == 0)
    def _():
        for head in range(HALF):
            for blk in range(2):
                back_copy(blk, head).wait_send()

    @pl.when(chip == 1)
    def _():
        for copy in row_copies():
            copy.wait_send()
        for head in range(HALF):
            grad_copy(head, True).wait_send()
            grad_copy(head, False).wait_send()


def attend_backward(limit, grad, saved):
    block, width = grad.shape
    topk = saved[4].shape[2]
    low, full = jnp.bfloat16, jnp.float32
    box = (2, HALF, block, HEAD_DIM)
    mem_box = (2, HALF, topk, HEAD_DIM)
    flat = (2, HALF, HEAD_DIM, block)
    row = (2, HALF, 1, block)
    dma = pltpu.SemaphoreType.DMA
    hbm, vmem = pl.BlockSpec(memory_space=pl.ANY), pl.BlockSpec(memory_space=pltpu.VMEM)
    struct = jax.ShapeDtypeStruct
    return pl.pallas_call(
        backward_kernel,
        out_shape=(struct((block, width), low),) * 3 + (struct((topk, width), low),) * 2,
        in_specs=[pl.BlockSpec(memory_space=pltpu.SMEM), hbm] + [vmem] * 8,
        out_specs=(hbm,) * 5,
        scratch_shapes=[
            pltpu.VMEM(box, low), pltpu.VMEM(box, low),
            pltpu.VMEM(row, full), pltpu.VMEM(row, full), pltpu.VMEM(row, full),
            pltpu.VMEM(flat, full), pltpu.VMEM(flat, low), pltpu.VMEM(flat, low),
            pltpu.VMEM(box, full), pltpu.VMEM(box, full),
            pltpu.VMEM(mem_box, low), pltpu.VMEM(mem_box, low),
            pltpu.VMEM(box, low), pltpu.VMEM(box, low), pltpu.VMEM(box, low),
            dma((1, HALF)), dma((1, HALF)), dma((1, HALF)),
            dma((2, HALF)), dma((2, HALF)), dma((2,)), dma((2,)),
            dma((2, HALF)), dma((2, HALF)),
            dma((5, HALF)), dma((5, HALF)), dma((5, HALF)),
        ],
        name="attend_backward",
        compiler_params=pltpu.CompilerParams(collective_id=2, has_side_effects=True, vmem_limit_bytes=56 * 2**20),
    )(limit, grad, *saved)


def keep_order(rank_of):
    before = lax.broadcasted_iota(jnp.int32, (rank_of, rank_of), 0)
    return (before < lax.broadcasted_iota(jnp.int32, (rank_of, rank_of), 1)).astype(jnp.bfloat16)


def one_row(ref):
    value = ref[...].astype(jnp.float32)
    return jnp.concatenate([value[i : i + 1] for i in range(value.shape[0])], axis=1)


def front_kernel(
    limit_ref, tokens, gain_in, w_query, w_key, w_value, mem_keys, mem_values, wanted,
    attended, qb, kb, vb, qx, mkb, mvb, ob, lse, spots, pick_t,
    rows, weights, normed, qkv, tables, every, pick, mem_out, mem_in,
    mixed_own, mixed_out, mixed_in, lse_out, lse_in,
    gain, load_sem, want_send, want_recv, mem_send, mem_recv, mem_local,
    local_sem, mate_send, mate_recv, far_send, far_recv, back_send, back_recv, end_sem,
):
    core, chip, mate, across, diagonal = seats()
    seq, doc = lax.axis_index("seq"), lax.axis_index("doc")
    seq_count, capacity = mem_in.shape[0], mem_in.shape[3]
    block, width = tokens.shape
    mem_rows, topk = tables.shape[1], every.shape[2]
    limit = limit_ref[0, seq // BPS]

    loads = [
        pltpu.make_async_copy(src, dst, load_sem.at[i])
        for i, (src, dst) in enumerate(
            (
                (wanted, every.at[seq]), (tokens, rows), (w_query, weights.at[0]), (w_key, weights.at[1]),
                (w_value, weights.at[2]), (mem_keys, tables.at[0]), (mem_values, tables.at[1]),
            )
        )
    ]
    for copy in loads:
        copy.start()
    meet([(lax.rem(seq + away, seq_count), doc) for away in range(1, seq_count)])
    loads[0].wait()

    def want_copy(away):
        return remote(
            every.at[seq], every.at[seq], want_send.at[away - 1], want_recv.at[away - 1],
            (lax.rem(seq + away, seq_count), doc),
        )

    def want_arrival(away):
        source = lax.rem(seq + seq_count - away, seq_count)
        return remote(every.at[source], every.at[source], want_send.at[away - 1], want_recv.at[away - 1], (source, doc))

    def mem_copy(away):
        peer = lax.rem(seq + away, seq_count)
        return remote(mem_out.at[peer], mem_in.at[seq], mem_send.at[away - 1], mem_recv.at[away - 1], (peer, doc))

    def mem_arrival(away):
        source = lax.rem(seq + seq_count - away, seq_count)
        return remote(mem_out.at[source], mem_in.at[source], mem_send.at[away - 1], mem_recv.at[away - 1], (source, doc))

    for away in range(1, seq_count):
        want_copy(away).start()
    gain[...] = one_row(gain_in)
    loads[1].wait()
    part = 64

    def norm(i, carry):
        at = pl.ds(pl.multiple_of(i * part, part), part)
        x = rows[at, :].astype(jnp.float32)
        factor = lax.rsqrt(jnp.mean(x * x, axis=-1, keepdims=True) + EPS)
        normed[at, :] = (x * factor * gain[0:1, :]).astype(jnp.bfloat16)
        return carry

    lax.fori_loop(0, block // part, norm, 0)

    def project(i):
        loads[2 + i].wait()

        def one(j, carry):
            lanes = pl.ds(pl.multiple_of(j * UNIT, UNIT), UNIT)
            qkv[i, :, lanes] = matmul(normed[...], weights[i, :, lanes], NN).astype(jnp.bfloat16)
            return carry

        lax.fori_loop(0, width // UNIT, one, 0)

    def query_copy(head, own):
        return remote(
            qkv.at[0, :, head_lanes(core if own else 1 - core, head)],
            qx.at[core, head],
            far_send.at[0 if own else 1, head],
            far_recv.at[core, head],
            across if own else diagonal,
        )

    def arrived_query(far, head):
        return remote(
            qkv.at[0, :, head_lanes(core, head)], qx.at[far, head], far_send.at[0, head], far_recv.at[far, head], across
        )

    loads[2].wait()
    for pair in range(HALF // 2):
        for side in range(2):
            lanes = slice((side * HALF // 2 + pair) * UNIT, (side * HALF // 2 + pair + 1) * UNIT)
            qkv[0, :, lanes] = matmul(normed[...], weights[0, :, lanes], NN).astype(jnp.bfloat16)

        @pl.when(chip == 1)
        def _():
            for head in (2 * pair, 2 * pair + 1):
                query_copy(head, True).start()
                query_copy(head, False).start()

    project(1)
    project(2)
    copies = share_heads(
        (qkv.at[0], qkv.at[1], qkv.at[2]), (qb, kb, vb), core, mate, local_sem, mate_send, mate_recv
    )

    for away in range(1, seq_count):
        want_arrival(away).wait_recv()
    triangle = keep_order(topk)
    asked = every[:, 0, :]
    here = asked - seq * mem_rows
    mine = (here >= 0) & (here < mem_rows)
    before = matmul(mine.astype(jnp.bfloat16), triangle, NN).astype(jnp.int32)
    place = lax.broadcasted_iota(jnp.int32, (capacity, topk), 0)
    line = lax.broadcasted_iota(jnp.int32, (mem_rows, topk), 0)
    for b in range(seq_count):
        at_place = jnp.where((before[b : b + 1] == place) & (here[b : b + 1] >= 0) & (here[b : b + 1] < mem_rows), 1.0, 0.0)
        at_line = jnp.where(here[b : b + 1] == line, 1.0, 0.0)
        pick[b * capacity : (b + 1) * capacity, :] = matmul(
            at_place.astype(jnp.bfloat16), at_line.astype(jnp.bfloat16), NT
        ).astype(jnp.bfloat16)
    half = HALF * HEAD_DIM
    for kind in range(2):
        loads[5 + kind].wait()
        for side in range(2):
            found = matmul(pick[...], tables[kind, :, side * half : (side + 1) * half], NN).astype(jnp.bfloat16)
            for b in range(seq_count):
                mem_out[2 * (b // 2) + side, b % 2, kind] = found[b * capacity : (b + 1) * capacity]
    for away in range(1, seq_count):
        mem_copy(away).start()
    own_rows = pltpu.make_async_copy(mem_out.at[seq], mem_in.at[seq], mem_local.at[0])
    own_rows.start()
    pick_t[...] = pick[...].astype(jnp.float32).T.astype(jnp.bfloat16)
    seat = lax.broadcasted_iota(jnp.int32, (seq_count, topk), 0)
    slot_at = lax.broadcasted_iota(jnp.int32, (seq_count * capacity, topk), 0)
    for blk in range(2):
        away_rows = every[2 * (seq // 2) + blk] - seat * mem_rows
        owner = (away_rows >= 0) & (away_rows < mem_rows)
        rank = matmul(owner.astype(jnp.bfloat16), triangle, NN).astype(jnp.int32)
        slot = jnp.sum(jnp.where(owner, seat * capacity + rank, 0), axis=0, keepdims=True)
        spots[blk] = jnp.where(slot == slot_at, 1.0, 0.0).astype(jnp.bfloat16)

    for copy in copies:
        copy.wait()

    def own_head(blk, head):
        query = qb[blk, head]
        parts = []
        for kblk in range(blk + 1):
            scores = matmul(kb[kblk, head], query, NT) * (SCALE * LOG2E)
            scores = masked(scores, (2 * chip + kblk) * block, limit, kblk == blk)
            parts.append((scores, vb[kblk, head]))
        mixed_own[blk, head], lse[blk, head] = soften(parts)

    def back_copy(blk, head):
        return (
            remote(mixed_out.at[blk, head], mixed_in.at[blk, head], back_send.at[0, blk, head], back_recv.at[0, blk, head], across),
            remote(lse_out.at[blk, head], lse_in.at[blk, head], back_send.at[1, blk, head], back_recv.at[1, blk, head], across),
        )

    def heads(head, carry):
        @pl.when(chip == 0)
        def _():
            def cross(blk, carry):
                arrived_query(blk, head).wait_recv()
                query = qx[blk, head]
                parts = []
                for kblk in range(2):
                    scores = matmul(kb[kblk, head], query, NT) * (SCALE * LOG2E)
                    parts.append((masked(scores, kblk * block, limit, False), vb[kblk, head]))
                mixed, level = soften(parts)
                mixed_out[blk, head] = mixed.astype(jnp.bfloat16)
                lse_out[blk, head] = level
                for copy in back_copy(blk, head):
                    copy.start()
                return carry

            lax.fori_loop(0, 2, cross, 0)

        own_head(0, head)
        own_head(1, head)
        return carry

    lax.fori_loop(0, HALF, heads, 0)

    for away in range(1, seq_count):
        mem_arrival(away).wait_recv()
    own_rows.wait()
    for blk in range(2):
        for kind, box in enumerate((mkb, mvb)):
            found = mem_in[:, blk, kind].reshape(seq_count * capacity, half)
            found = matmul(spots[blk], found, TN).astype(jnp.bfloat16)
            for head in range(HALF):
                box[blk, head] = found[:, head * HEAD_DIM : (head + 1) * HEAD_DIM]

    def blend(pieces):
        top = functools.reduce(jnp.maximum, [level for _, level in pieces])
        total, mixed = 0.0, 0.0
        for value, level in pieces:
            share = jnp.exp2(level - top)
            total = total + share
            mixed = mixed + value * share
        return mixed / total, top + jnp.log(total) * LOG2E

    def finish(i, carry):
        head, blk = i // 2, i % 2
        scores = matmul(mkb[blk, head], qb[blk, head], NT) * (SCALE * LOG2E)
        pieces = [(mixed_own[blk, head], lse[blk, head]), soften([(scores, mvb[blk, head])])]

        @pl.when(chip == 0)
        def _():
            mixed, lse[blk, head] = blend(pieces)
            ob[blk, head] = mixed.T.astype(jnp.bfloat16)

        @pl.when(chip == 1)
        def _():
            for copy in back_copy(blk, head):
                copy.wait_recv()
            far = (mixed_in[blk, head].astype(jnp.float32), lse_in[blk, head])
            mixed, lse[blk, head] = blend(pieces + [far])
            ob[blk, head] = mixed.T.astype(jnp.bfloat16)

        return carry

    lax.fori_loop(0, 2 * HALF, finish, 0)

    ends = []
    for head in range(HALF):
        ends.append(
            remote(ob.at[1 - core, head], attended.at[:, head_lanes(core, head)], end_sem.at[0, head], end_sem.at[1, head], mate)
        )
        ends.append(
            pltpu.make_async_copy(ob.at[core, head], attended.at[:, head_lanes(core, head)], end_sem.at[2, head])
        )
    for copy in ends:
        copy.start()
    for copy in ends:
        copy.wait()
    for away in range(1, seq_count):
        want_copy(away).wait_send()
        mem_copy(away).wait_send()

    @pl.when(chip == 0)
    def _():
        for head in range(HALF):
            for blk in range(2):
                for copy in back_copy(blk, head):
                    copy.wait_send()

    @pl.when(chip == 1)
    def _():
        for head in range(HALF):
            query_copy(head, True).wait_send()
            query_copy(head, False).wait_send()


def go_forward(limit, tokens, gain, projections, mem_keys, mem_values, wanted):
    block, width = tokens.shape
    mem_rows, topk = mem_keys.shape[0], wanted.shape[1]
    seq_count = lax.axis_size("seq")
    capacity = 2 * topk // seq_count
    slots = seq_count * capacity
    low, full = jnp.bfloat16, jnp.float32
    box = (2, HALF, block, HEAD_DIM)
    mem_box = (2, HALF, topk, HEAD_DIM)
    flat = (2, HALF, HEAD_DIM, block)
    row = (2, HALF, 1, block)
    mem = (seq_count, 2, 2, capacity, HALF * HEAD_DIM)
    dma = pltpu.SemaphoreType.DMA
    hbm, vmem = pl.BlockSpec(memory_space=pl.ANY), pl.BlockSpec(memory_space=pltpu.VMEM)
    struct = jax.ShapeDtypeStruct
    return pl.pallas_call(
        front_kernel,
        out_shape=(
            struct((block, width), low),
            struct(box, low), struct(box, low), struct(box, low), struct(box, low),
            struct(mem_box, low), struct(mem_box, low), struct(box, low), struct(row, full),
            struct((2, slots, topk), low), struct((mem_rows, slots), low),
        ),
        in_specs=[pl.BlockSpec(memory_space=pltpu.SMEM), hbm, vmem] + [hbm] * 6,
        out_specs=(hbm,) + (vmem,) * 10,
        scratch_shapes=[
            pltpu.VMEM((block, width), low), pltpu.VMEM((3, width, width), low), pltpu.VMEM((block, width), low),
            pltpu.VMEM((3, block, width), low), pltpu.VMEM((2, mem_rows, width), low),
            pltpu.VMEM((seq_count, 1, topk), jnp.int32), pltpu.VMEM((slots, mem_rows), low),
            pltpu.VMEM(mem, low), pltpu.VMEM(mem, low),
            pltpu.VMEM(flat, full), pltpu.VMEM(flat, low), pltpu.VMEM(flat, low),
            pltpu.VMEM(row, full), pltpu.VMEM(row, full),
            pltpu.VMEM((1, width), full),
            dma((7,)), dma((seq_count - 1,)), dma((seq_count - 1,)), dma((seq_count - 1,)), dma((seq_count - 1,)), dma((1,)),
            dma((3, HALF)), dma((3, HALF)), dma((3, HALF)),
            dma((2, HALF)), dma((2, HALF)), dma((2, 2, HALF)), dma((2, 2, HALF)), dma((3, HALF)),
        ],
        name="go_forward",
        compiler_params=pltpu.CompilerParams(collective_id=4, has_side_effects=True, vmem_limit_bytes=56 * 2**20),
    )(limit, tokens, gain, *projections, mem_keys, mem_values, wanted)


ALONG = (("x", "y", "low", "high"), ("y", "x", "low", "high"), ("low", "high", "y", "x"), ("low", "high", "x", "y"))
TURNS = (2, 0, 0, 3, 0, 1, 1, 1, 2, 1, 0, 0, 0, 0, 3, 0, 1, 0, 2, 0, 1, 3, 0, 0, 1, 1, 3, 1, 3, 0, 3, 1, 0, 0, 1, 0, 2, 0, 1, 2, 2, 3)
PLAN = (
    (),
    ((0, 0), (1, 0),),
    ((2, 0), (3, 0),),
    ((4, 0), (0, 1), (1, 1), (5, 0),),
    ((6, 0), (2, 1), (3, 1), (7, 0), (1, 2),),
    ((8, 0), (4, 1), (9, 0), (5, 1), (0, 2),),
    ((1, 3), (10, 0), (11, 0), (6, 1), (3, 2), (5, 2),),
    ((2, 2), (8, 1), (12, 0), (13, 0), (5, 3), (7, 1),),
    ((1, 4), (10, 1), (14, 0), (4, 2), (15, 0), (2, 3),),
    ((11, 1), (9, 1), (16, 0), (0, 3), (17, 0), (6, 2), (3, 3), (10, 2), (8, 2),),
    ((5, 4), (18, 0), (14, 1), (19, 0), (4, 3), (12, 1), (11, 2), (6, 3), (10, 3),),
    ((2, 4), (20, 0), (13, 1), (21, 0),),
    ((16, 1), (3, 4), (7, 2), (8, 3),),
    ((18, 1), (12, 2),),
    ((15, 1),),
    ((11, 3), (9, 2),),
    ((20, 1), (0, 4),),
    ((22, 0),),
    ((23, 0), (14, 2), (13, 2), (24, 0), (4, 4),),
    ((25, 0), (6, 4), (15, 2), (17, 1), (21, 1), (10, 4), (7, 3),),
    (),
    (),
    ((19, 1), (12, 3),),
    ((9, 3), (24, 1), (38, 0), (16, 2), (8, 4), (13, 3),),
    ((18, 2), (15, 3), (39, 0), (11, 4),),
    ((25, 1),),
    ((40, 0), (17, 2), (16, 3), (19, 2), (21, 2), (7, 4), (12, 4), (9, 4),),
    ((13, 4), (15, 4), (41, 0),),
    (),
    ((39, 1), (20, 2), (38, 1),),
    ((18, 3),),
    ((22, 1),),
    (),
    ((23, 1),),
    ((14, 3), (22, 2), (40, 1),),
    ((17, 3), (19, 3),),
    ((16, 4),),
    ((23, 2), (14, 4),),
    ((41, 1), (24, 2),),
    ((25, 2),),
    ((21, 3), (20, 3), (22, 3), (38, 2), (18, 4), (39, 2), (23, 3), (24, 3), (25, 3), (40, 2), (17, 4), (19, 4),),
    ((21, 4),),
    ((39, 3), (38, 3),),
    ((41, 2), (40, 3),),
    ((20, 4), (22, 4), (26, 0), (39, 4), (27, 0), (23, 4),),
    ((24, 4), (28, 0), (29, 0), (25, 4),),
    ((41, 3), (30, 0), (40, 4), (31, 0), (38, 4),),
    ((32, 0), (26, 1), (33, 0), (27, 1),),
    ((41, 4), (34, 0), (29, 1),),
    ((35, 0), (28, 1), (36, 0), (37, 0),),
    ((31, 1), (32, 1),),
    ((30, 1),),
    ((34, 1), (33, 1),),
    ((29, 2), (27, 2), (32, 2), (26, 2),),
    ((36, 1), (33, 2), (35, 1),),
    ((28, 2), (29, 3), (27, 3),),
    ((32, 3), (37, 1), (35, 2), (30, 2), (31, 2), (33, 3), (34, 2), (37, 2), (26, 3), (35, 3), (28, 3), (36, 2), (31, 3), (30, 3), (29, 4), (34, 3), (27, 4), (26, 4), (37, 3), (32, 4), (28, 4), (33, 4), (36, 3), (30, 4), (35, 4), (31, 4), (36, 4), (34, 4), (37, 4),),
)
OFFERED = (20, 22, 24, 26)
RING = 8
NARROW = 38
ROWS = (32, 88)


def taken(unit, level):
    return [(unit, level) in events for events in PLAN].index(True)


class Sums:
    def __init__(self, down, made, own, stages, sums, homes, local_sem, send_sem, recv_sem, done_sem, peers):
        self.down, self.made, self.own, self.stages, self.sums = down, made, own, stages, sums
        self.local_sem, self.send_sem, self.recv_sem = local_sem, send_sem, recv_sem
        self.peers, self.homes, self.done_sem = peers, homes, done_sem
        seq, doc = lax.axis_index("seq"), lax.axis_index("doc")
        self.bits = {
            "core": seq % 2,
            "x": (seq // 2) % 2,
            "y": (seq // 4) % 2,
            "low": doc % 2,
            "high": (doc // 2) % 2,
        }

    def core_copy(self, kind, index):
        if kind == 0:
            source = self.made.at[index % RING, :, :, 1 - self.bits["core"]]
        else:
            source = self.down.at[:, :, 1 - self.bits["core"], :, :, :, pl.ds(index * UNIT, UNIT)]
        return remote(
            source,
            self.stages[kind][0].at[index],
            self.send_sem[kind].at[0, index],
            self.recv_sem[kind].at[0, index],
            self.peers["core"],
        )

    def own_copy(self, index):
        return pltpu.make_async_copy(
            self.down.at[:, :, self.bits["core"], :, :, :, pl.ds(index * UNIT, UNIT)],
            self.own.at[index % 2],
            self.local_sem.at[index % 2],
        )

    def put(self, unit, value):
        pl.when(unit >= RING)(lambda: self.core_copy(0, jnp.maximum(unit - RING, 0)).wait_send())
        self.made[unit % RING] = value.astype(jnp.bfloat16).reshape(self.made.shape[1:])
        self.core_copy(0, unit).start()

    def offer_down(self, index):
        self.core_copy(1, index).start()
        if index < 2 or taken(NARROW + index - 2, 0) < OFFERED[index]:
            self.own_copy(index).start()

    def half(self, kind, index, order, level, mine):
        name = order[level]
        left = [axis for axis in ("y", "x", "high", "low") if axis not in order[:level]]
        side = self.bits[name] if mine else 1 - self.bits[name]
        return (index,) + (slice(None),) * left.index(name) + (side,)

    def copy(self, kind, index, order, level):
        return remote(
            self.stages[kind][level - 1].at[self.half(kind, index, order, level - 1, False)],
            self.stages[kind][level].at[index],
            self.send_sem[kind].at[level, index],
            self.recv_sem[kind].at[level, index],
            self.peers[order[level - 1]],
        )

    def arrive(self, unit, level):
        kind = 0 if unit < NARROW else 1
        index = unit - kind * NARROW
        order = ALONG[TURNS[unit]]
        ref = self.stages[kind][level]
        if level == 0:
            self.core_copy(kind, index).wait_recv()
            if kind == 1:
                self.own_copy(index).wait()

            def add(i, carry):
                y, x = i // 2, i % 2
                mine = self.made[index % RING, y, x, self.bits["core"]] if kind == 0 else self.own[index % 2, y, x]
                ref[index, y, x] = ref[index, y, x] + mine
                return carry

            lax.fori_loop(0, 4, add, 0)
            if kind == 1 and index < 2 and taken(unit, 0) >= OFFERED[index + 2]:
                self.own_copy(index + 2).start()
        else:
            self.copy(kind, index, order, level).wait_recv()
            kept = self.stages[kind][level - 1][self.half(kind, index, order, level - 1, True)]
            if level < 4:
                ref[index] = ref[index] + kept
            else:
                self.sums[kind][index] = ref[index].astype(jnp.float32) + kept.astype(jnp.float32)
                self.result(unit).start()
        if level < 4:
            self.copy(kind, index, order, level + 1).start()

    def result(self, unit):
        gate, up, out, query, key, value, down = self.homes
        if unit < 22:
            home, place = (gate, up)[unit % 2], unit // 2
        elif unit < 26:
            home, place = out, unit - 22
        elif unit < NARROW:
            home, place = (query, key, value)[(unit - 26) // 4], (unit - 26) % 4
        else:
            home, place = down, unit - NARROW
        kind = 0 if unit < NARROW else 1
        return pltpu.make_async_copy(
            self.sums[kind].at[unit - kind * NARROW], home.at[:, pl.ds(place * UNIT, UNIT)], self.done_sem.at[unit]
        )

    def run(self, place):
        for unit, level in PLAN[place]:
            self.arrive(unit, level)

    def run_turn(self, first, turn, count):
        for k in range(count):
            if PLAN[first + k]:
                pl.when(turn == k)(lambda: self.run(first + k))

    def drain(self, kind, first, last):
        def one(index, carry):
            pl.when((kind == 1) | (index >= NARROW - RING))(lambda: self.core_copy(kind, index).wait_send())
            for level in range(1, 5):
                self.copy(kind, index, ALONG[0], level).wait_send()
            return carry

        lax.fori_loop(first, last, one, 0)


def back_kernel(
    limit_ref, mixed_in, qb_in, kb_in, vb_in, qx_in, mkb_in, mvb_in, ob_in, lse_in0, spots_in,
    tokens, cotangent, w_query, w_key, w_value, w_out, w_gate, w_up, w_down, gain_one_in, gain_two_in,
    layer_out, grad_tokens, gate_rows, up_rows, query_rows, key_rows, value_rows, out_rows, down_rows, gains_out,
    mem_home, down, grad_middle,
    gb, gx, lse, delta, lse_in, delta_in, dq_cross, dqkv, mem_in, gain_buf, made, own, grad, gains_in, *rest,
):
    stages = [rest[5 * c : 5 * c + 5] for c in range(2)]
    sums = rest[10:12]
    local_sem, send_sems, recv_sems, rest = rest[12], rest[13:15], rest[15:17], rest[17:]
    (
        in_sem, gb_local, gb_send, gb_recv, spot_sem, far_send, far_recv, row_send, row_recv, back_send, back_recv,
        mate_send, mate_recv, mem_local, mem_send, mem_recv, gain_send, gain_recv, load_sem, weight_sem, done_sem, front_sem, tile_sem, stage_sem,
    ) = rest
    core, chip, mate, across, diagonal = seats()
    seq, doc = lax.axis_index("seq"), lax.axis_index("doc")
    seq_count = mem_in.shape[0]
    block = tokens.shape[0]
    limit = limit_ref[0, seq // BPS]
    peers = {
        "core": mate,
        "x": across,
        "y": (flip(seq, 4), doc),
        "low": (seq, flip(doc, 1)),
        "high": (seq, flip(doc, 2)),
    }
    others = [(lax.rem(seq + away, seq_count), doc) for away in range(1, seq_count)]
    homes = (gate_rows, up_rows, out_rows, query_rows, key_rows, value_rows, down_rows)
    engine = Sums(down, made, own, stages, sums, homes, local_sem, send_sems, recv_sems, done_sem, peers)

    def grad_copy(head, own):
        return remote(
            grad.at[:, head_lanes(core if own else 1 - core, head)],
            gx.at[core, head],
            far_send.at[0 if own else 1, head],
            far_recv.at[core, head],
            across if own else diagonal,
        )

    def arrived_grad(far, head):
        return remote(
            grad.at[:, head_lanes(core, head)], gx.at[far, head], far_send.at[0, head], far_recv.at[far, head], across
        )

    def row_copies():
        return (
            remote(lse, lse_in, row_send.at[0], row_recv.at[0], across),
            remote(delta, delta_in, row_send.at[1], row_recv.at[1], across),
        )

    def back_copy(blk, head):
        return remote(dq_cross.at[blk, head], dq_cross.at[blk, head], back_send.at[blk, head], back_recv.at[blk, head], across)

    def mate_copy(box, i, head):
        lanes = head_lanes(core, head)
        return remote(box.at[i, head], dqkv.at[i, :, lanes], mate_send.at[i, head], mate_recv.at[i, head], mate)

    def mate_arrival(i, head):
        lanes = head_lanes(1 - core, head)
        return remote(gb.at[0, head], dqkv.at[i, :, lanes], mate_send.at[i, head], mate_recv.at[i, head], mate)

    def mem_copy(box, away):
        peer = lax.rem(seq + away, seq_count)
        return remote(box.at[peer], mem_in.at[seq], mem_send.at[away - 1], mem_recv.at[away - 1], (peer, doc))

    def far_start(head):
        @pl.when(chip == 1)
        def _():
            grad_copy(head, True).start()
            grad_copy(head, False).start()

    def front(normed, normed_t, grad_y, total, back, hidden_t, mixed, middle, w_in, w_back):
        width = total.shape[1]
        tiles = w_gate.shape[1] // UNIT
        part = 128
        copies = [
            pltpu.make_async_copy(mixed_in, mixed, front_sem.at[0]),
            pltpu.make_async_copy(cotangent, grad_y, front_sem.at[1]),
        ]
        for copy in copies:
            copy.start()

        def strip(i):
            return pl.ds(pl.multiple_of(i * UNIT, UNIT), UNIT)

        def chunk(i):
            return pl.ds(pl.multiple_of(i * part, part), part)

        def opening(rows, weights):
            loads = [
                pltpu.make_async_copy(tokens, rows, front_sem.at[2]),
                pltpu.make_async_copy(w_out, weights, front_sem.at[3]),
            ]
            for copy in loads:
                copy.start()
            meet(others + [peers["low"], peers["high"]])
            gains_in[0:1, :] = one_row(gain_one_in)
            gains_in[1:2, :] = one_row(gain_two_in)
            for copy in copies + loads:
                copy.wait()

            def join(j, carry):
                middle[:, strip(j)] = rows[:, strip(j)].astype(jnp.float32) + matmul(mixed[...], weights[:, strip(j)], NN)
                return carry

            lax.fori_loop(0, width // UNIT, join, 0)

            def norm(i, carry):
                x = middle[chunk(i), :]
                factor = lax.rsqrt(jnp.mean(x * x, axis=-1, keepdims=True) + EPS)
                value = x * factor * gains_in[1:2, :]
                normed[chunk(i), :] = value.astype(jnp.bfloat16)
                normed_t[:, chunk(i)] = value.T.astype(jnp.bfloat16)
                total[chunk(i), :] = jnp.zeros((part, width), jnp.float32)
                back[chunk(i), :] = jnp.zeros((part, width), jnp.float32)
                return carry

            lax.fori_loop(0, block // part, norm, 0)

        def tile_loads(tile):
            slot = tile % 2
            return (
                pltpu.make_async_copy(w_gate.at[:, strip(tile)], w_in.at[slot, 0], tile_sem.at[slot, 0]),
                pltpu.make_async_copy(w_up.at[:, strip(tile)], w_in.at[slot, 1], tile_sem.at[slot, 1]),
                pltpu.make_async_copy(w_down.at[strip(tile), :], w_back.at[slot], tile_sem.at[slot, 2]),
            )

        for copy in tile_loads(0):
            copy.start()
        pl.run_scoped(
            opening,
            pltpu.VMEM(tokens.shape, jnp.bfloat16), pltpu.VMEM(w_out.shape, jnp.bfloat16),
        )

        def hidden_units():
            def one(tile, carry):
                slot = tile % 2

                @pl.when(tile + 1 < tiles)
                def _():
                    for copy in tile_loads(tile + 1):
                        copy.start()

                for copy in tile_loads(tile):
                    copy.wait()
                opened = matmul(normed[...], w_in[slot, 0], NN)
                upper = matmul(normed[...], w_in[slot, 1], NN)
                sigma = 1.0 / (1.0 + jnp.exp(-opened))
                gated = opened * sigma
                hidden = gated * upper
                total[...] += matmul(hidden.astype(jnp.bfloat16), w_back[slot], NN)
                hidden_t[strip(tile), :] = hidden.T.astype(jnp.bfloat16)
                grad_hidden = matmul(grad_y[...], w_back[slot], NT)
                grad_opened = (grad_hidden * upper * sigma * (1.0 + opened * (1.0 - sigma))).astype(jnp.bfloat16)
                grad_upper = (grad_hidden * gated).astype(jnp.bfloat16)
                back[...] += matmul(grad_opened, w_in[slot, 0], NT) + matmul(grad_upper, w_in[slot, 1], NT)
                for kind, value in enumerate((grad_opened, grad_upper)):
                    engine.put(2 * tile + kind, matmul(normed_t[...], value, NN))
                engine.run_turn(0, tile, tiles)
                return carry

            lax.fori_loop(0, tiles, one, 0)

        hidden_units()

        def closing(branch, stage_down):
            loads = [
                pltpu.make_async_copy(w_out.at[:, strip(p)], w_in.at[p // 2, p % 2], tile_sem.at[p // 2, p % 2])
                for p in range(4)
            ]
            for copy in loads:
                copy.start()
            engine.run(11)

            def norm_back(i, carry):
                x = middle[chunk(i), :]
                factor = lax.rsqrt(jnp.mean(x * x, axis=-1, keepdims=True) + EPS)
                unit = x * factor
                grad_normed = back[chunk(i), :]
                normed[chunk(i), :] = (x + total[chunk(i), :]).astype(jnp.bfloat16)
                scaled = gains_in[1:2, :] * grad_normed
                inner = jnp.mean(scaled * unit, axis=-1, keepdims=True)
                value = grad_y[chunk(i), :].astype(jnp.float32) + factor * (scaled - unit * inner)
                middle[chunk(i), :] = value
                branch[chunk(i), :] = value.astype(jnp.bfloat16)
                return carry + jnp.sum(grad_normed * unit, axis=0, keepdims=True)

            gain_buf[0, 0, 1] = lax.fori_loop(0, block // part, norm_back, jnp.zeros((1, width), jnp.float32))
            writes = [
                pltpu.make_async_copy(normed, layer_out, front_sem.at[0]),
                pltpu.make_async_copy(middle, grad_middle, front_sem.at[2]),
            ]
            for copy in writes:
                copy.start()

            engine.run(12)

            for copy in loads:
                copy.wait()
            for j in (0, 2, 1, 3):
                at = slice(j * UNIT, (j + 1) * UNIT)
                value = 0.0
                for p in range(4):
                    value = value + matmul(branch[:, p * UNIT : (p + 1) * UNIT], w_in[p // 2, p % 2, at, :], NT)
                grad[:, at] = value.astype(jnp.bfloat16)
                if j == 2:
                    far_start(0)
            engine.run(13)
            far_start(1)
            share_heads((grad,), (gb,), core, mate, gb_local, gb_send, gb_recv)

            def turn_over(i, carry):
                normed_t[:, chunk(i)] = mixed[chunk(i), :].astype(jnp.float32).T.astype(jnp.bfloat16)
                return carry

            lax.fori_loop(0, block // part, turn_over, 0)

            for j in range(4):
                engine.put(jnp.int32(22 + j), matmul(normed_t[...], branch[:, j * UNIT : (j + 1) * UNIT], NN))
                engine.run(14 + j)
            deep = stage_down.shape[4]
            tall = 8 * deep

            def down_store(n):
                i = n % 4
                return pltpu.make_async_copy(
                    stage_down.at[n % 2], down.at[i // 2, i % 2, :, :, :, :, strip(n // 4)], stage_sem.at[n % 2]
                )

            def down_part(n):
                i, j = n % 4, n // 4
                value = matmul(hidden_t[pl.ds(pl.multiple_of(i * tall, 64), tall), :], grad_y[:, strip(j)], NN)
                pl.when(n > 1)(lambda: down_store(n - 2).wait())
                for k in range(8):
                    stage_down[n % 2, k // 4, (k // 2) % 2, k % 2] = value[k * deep : (k + 1) * deep].astype(jnp.bfloat16)
                down_store(n).start()

            def down_parts(m, carry):
                down_part(2 * m)
                down_part(2 * m + 1)
                for j in range(3):
                    pl.when(m == 2 * j + 2)(lambda: engine.offer_down(j))
                pl.when(m == 1)(lambda: far_start(2))
                pl.when(m == 4)(lambda: far_start(3))
                engine.run_turn(18, m, 8)
                return carry

            lax.fori_loop(0, 8, down_parts, 0)
            down_store(14).wait()
            down_store(15).wait()
            engine.offer_down(3)
            for copy in writes:
                copy.wait()

        pl.run_scoped(
            closing,
            pltpu.VMEM(normed.shape, jnp.bfloat16),
            pltpu.VMEM((2, 2, 2, 2, ROWS[1], UNIT), jnp.bfloat16),
        )

    pl.run_scoped(
        front,
        pltpu.VMEM(tokens.shape, jnp.bfloat16), pltpu.VMEM((tokens.shape[1], block), jnp.bfloat16),
        pltpu.VMEM(tokens.shape, jnp.bfloat16), pltpu.VMEM(tokens.shape, jnp.float32), pltpu.VMEM(tokens.shape, jnp.float32),
        pltpu.VMEM((w_gate.shape[1], block), jnp.bfloat16), pltpu.VMEM(tokens.shape, jnp.bfloat16),
        pltpu.VMEM(tokens.shape, jnp.float32), pltpu.VMEM((2, 2, tokens.shape[1], UNIT), jnp.bfloat16),
        pltpu.VMEM((2, UNIT, tokens.shape[1]), jnp.bfloat16),
    )

    def attention(qb, kb, vb, qx, mkb, mvb, ob, dq_own, dk_sum, dv_sum, dm, dqkv_mate, mem_out, spots):
        inputs = [
            pltpu.make_async_copy(src, dst, in_sem.at[i])
            for i, (src, dst) in enumerate(
                ((qb_in, qb), (kb_in, kb), (vb_in, vb), (mkb_in, mkb), (mvb_in, mvb), (ob_in, ob), (lse_in0, lse), (qx_in, qx))
            )
        ]
        spot_copies = [pltpu.make_async_copy(spots_in, spots, spot_sem.at[0])]
        for copy in inputs + spot_copies:
            copy.start()
        for head in range(HALF):
            remote(grad.at[:, head_lanes(core, head)], gb.at[core, head], gb_send.at[0, head], gb_recv.at[0, head], mate).wait()
            pltpu.make_async_copy(grad.at[:, head_lanes(core, head)], gb.at[core, head], gb_local.at[0, head]).wait()
        for copy in inputs + spot_copies:
            copy.wait()
        engine.run(26)

        def rows(i, carry):
            head, blk = i // 2, i % 2
            product = gb[blk, head].astype(jnp.float32) * ob[blk, head].astype(jnp.float32)
            delta[blk, head] = jnp.sum(product.T, axis=0, keepdims=True)
            return carry

        lax.fori_loop(0, 2 * HALF, rows, 0)

        @pl.when(chip == 1)
        def _():
            for copy in row_copies():
                copy.start()

        def pull(key_rows, value_rows, query, grad_rows, level, inner, where):
            scores = matmul(key_rows, query, NT) * (SCALE * LOG2E)
            if where is not None:
                scores = masked(scores, where[0], limit, where[1])
            weights = jnp.exp2(scores - level)
            grad_weights = matmul(value_rows, grad_rows, NT)
            grad_scores = (weights * (grad_weights - inner)).astype(jnp.bfloat16)
            return (
                matmul(grad_scores, query, NN),
                matmul(weights.astype(jnp.bfloat16), grad_rows, NN),
                matmul(key_rows, grad_scores, TN),
            )

        def own_head(head, carry):
            lanes = pl.ds(pl.multiple_of(head * HEAD_DIM, HEAD_DIM), HEAD_DIM)
            for blk in range(2):
                query, grad_rows = qb[blk, head], gb[blk, head]
                level, inner = lse[blk, head], delta[blk, head]
                total = 0.0
                for kblk in range(blk + 1):
                    gk, gv, gq = pull(
                        kb[kblk, head], vb[kblk, head], query, grad_rows, level, inner,
                        ((2 * chip + kblk) * block, kblk == blk),
                    )
                    if kblk == blk:
                        dk_sum[kblk, head], dv_sum[kblk, head] = gk, gv
                    else:
                        dk_sum[kblk, head] += gk
                        dv_sum[kblk, head] += gv
                    total = total + gq
                gk, gv, gq = pull(mkb[blk, head], mvb[blk, head], query, grad_rows, level, inner, None)
                dm[blk, 0, :, lanes] = (gk * SCALE).astype(jnp.bfloat16)
                dm[blk, 1, :, lanes] = gv.astype(jnp.bfloat16)
                dq_own[blk, head] = total + gq
            engine.run_turn(27, head, HALF)
            return carry

        lax.fori_loop(0, HALF, own_head, 0)

        for blk in range(2):
            for kind in range(2):
                rows_out = matmul(spots[blk], dm[blk, kind], NN).astype(jnp.bfloat16)
                mem_out[:, blk, kind] = rows_out.reshape(mem_out.shape[0], mem_out.shape[3], mem_out.shape[4])
        for away in range(1, seq_count):
            mem_copy(mem_out, away).start()
        own_rows = pltpu.make_async_copy(mem_out.at[seq], mem_in.at[seq], mem_local.at[0])
        own_rows.start()
        engine.run(31)

        @pl.when(chip == 0)
        def _():
            for copy in row_copies():
                copy.wait_recv()

        def results(blk, head, which):
            values = {}
            if 0 in which:
                values[0] = (dq_own[blk, head].T * SCALE).astype(jnp.bfloat16)
            if 1 in which:
                values[1] = (dk_sum[blk, head] * SCALE).astype(jnp.bfloat16)
                values[2] = dv_sum[blk, head].astype(jnp.bfloat16)
            return values

        def hand_out(which):
            def for_mate(head, carry):
                for i, value in results(1 - core, head, which).items():
                    dqkv_mate[i, head] = value
                    mate_copy(dqkv_mate, i, head).start()
                return carry

            def for_own(head, carry):
                for i, value in results(core, head, which).items():
                    dqkv[i, :, head_lanes(core, head)] = value
                return carry

            lax.fori_loop(0, HALF, for_mate, 0)
            lax.fori_loop(0, HALF, for_own, 0)

        pl.when(chip == 0)(lambda: hand_out((0,)))
        pl.when(chip == 1)(lambda: hand_out((1,)))

        def far_turn(i, carry):
            head, blk = i // 2, i % 2

            @pl.when(chip == 0)
            def _():
                arrived_grad(blk, head).wait_recv()
                query, grad_rows = qx[blk, head], gx[blk, head]
                level, inner = lse_in[blk, head], delta_in[blk, head]
                total = 0.0
                for kblk in range(2):
                    gk, gv, gq = pull(
                        kb[kblk, head], vb[kblk, head], query, grad_rows, level, inner, (kblk * block, False)
                    )
                    dk_sum[kblk, head] += gk
                    dv_sum[kblk, head] += gv
                    total = total + gq
                dq_cross[blk, head] = total.astype(jnp.bfloat16)
                back_copy(blk, head).start()

            engine.run_turn(32, i, 2 * HALF)

            @pl.when(chip == 1)
            def _():
                back_copy(blk, head).wait_recv()
                dq_own[blk, head] += dq_cross[blk, head].astype(jnp.float32)

            return carry

        lax.fori_loop(0, 2 * HALF, far_turn, 0)

        pl.when(chip == 0)(lambda: hand_out((1,)))
        pl.when(chip == 1)(lambda: hand_out((0,)))
        engine.run(40)
        engine.run(41)
        for away in range(1, seq_count):
            mem_copy(mem_out, away).wait_send()
        own_rows.wait()
        for i in range(3):
            for head in range(HALF):
                mate_copy(dqkv_mate, i, head).wait_send()

    box = (2, HALF, block, HEAD_DIM)
    mem_box = mkb_in.shape
    low, full = jnp.bfloat16, jnp.float32
    pl.run_scoped(
        attention,
        pltpu.VMEM(box, low), pltpu.VMEM(box, low), pltpu.VMEM(box, low), pltpu.VMEM(box, low),
        pltpu.VMEM(mem_box, low), pltpu.VMEM(mem_box, low), pltpu.VMEM(box, low),
        pltpu.VMEM((2, HALF, HEAD_DIM, block), full), pltpu.VMEM(box, full), pltpu.VMEM(box, full),
        pltpu.VMEM((2, 2, mem_box[2], HALF * HEAD_DIM), low),
        pltpu.VMEM((3, HALF, block, HEAD_DIM), low), pltpu.VMEM(mem_in.shape, low), pltpu.VMEM(spots_in.shape, low),
    )

    def tail(normed, dx, middle, rows, weights):
        width = dx.shape[1]
        chunk = weights.shape[2]
        loads = [
            pltpu.make_async_copy(tokens, rows, load_sem.at[1]),
            pltpu.make_async_copy(grad_middle, middle, load_sem.at[2]),
        ]

        def weight_copies(j):
            at = pl.ds(pl.multiple_of(j * chunk, chunk), chunk)
            return [
                pltpu.make_async_copy(w.at[at, :], weights.at[j % 2, i], weight_sem.at[j % 2, i])
                for i, w in enumerate((w_query, w_key, w_value))
            ]

        for copy in loads + weight_copies(0):
            copy.start()
        loads[0].wait()
        part = 64

        def norm(i, carry):
            at = pl.ds(pl.multiple_of(i * 2 * part, 2 * part), 2 * part)
            x = rows[at, :].astype(jnp.float32)
            factor = lax.rsqrt(jnp.mean(x * x, axis=-1, keepdims=True) + EPS)
            normed[:, at] = (x * factor * gains_in[0:1, :]).T.astype(jnp.bfloat16)
            return carry

        lax.fori_loop(0, block // (2 * part), norm, 0)
        for i in range(3):
            for head in range(HALF):
                mate_arrival(i, head).wait_recv()
        engine.run(42)

        def make(w):
            lanes = pl.ds(pl.multiple_of(lax.rem(w, 4) * UNIT, UNIT), UNIT)
            engine.put(26 + w, matmul(normed[...], dqkv[w // 4, :, lanes], NN))

        def build(j, carry):
            make(2 * j)
            make(2 * j + 1)
            engine.run_turn(43, j, 6)
            return carry

        lax.fori_loop(0, 6, build, 0)

        def input_part(j, carry):
            for copy in weight_copies(j):
                copy.wait()

            @pl.when(j < 3)
            def _():
                for copy in weight_copies(j + 1):
                    copy.start()

            total = 0.0
            for i in range(3):
                total = total + matmul(dqkv[i], weights[j % 2, i], NT)
            dx[:, pl.ds(pl.multiple_of(j * chunk, chunk), chunk)] = total
            engine.run_turn(49, j, 4)
            return carry

        lax.fori_loop(0, 4, input_part, 0)
        loads[1].wait()

        def norm_back(i, carry):
            at = pl.ds(pl.multiple_of(i * part, part), part)
            x = rows[at, :].astype(jnp.float32)
            factor = lax.rsqrt(jnp.mean(x * x, axis=-1, keepdims=True) + EPS)
            unit = x * factor
            grad_normed = dx[at, :]
            scaled = gains_in[0:1, :] * grad_normed
            inner = jnp.mean(scaled * unit, axis=-1, keepdims=True)
            rows[at, :] = (middle[at, :] + factor * (scaled - unit * inner)).astype(jnp.bfloat16)
            return carry + jnp.sum(grad_normed * unit, axis=0, keepdims=True)

        gain_buf[0, 0, 0] = lax.fori_loop(0, block // part, norm_back, jnp.zeros((1, width), jnp.float32))
        out_copy = pltpu.make_async_copy(rows, grad_tokens, load_sem.at[1])
        out_copy.start()

        def gain_copy(level):
            name = ("core", "x", "y", "low", "high")[level]
            return remote(
                gain_buf.at[0, level], gain_buf.at[1, level], gain_send.at[level], gain_recv.at[level], peers[name]
            )

        gain_copy(0).start()
        engine.run(53)
        for away in range(1, seq_count):
            source = lax.rem(seq + seq_count - away, seq_count)
            remote(mem_in.at[source], mem_in.at[source], mem_send.at[away - 1], mem_recv.at[away - 1], (source, doc)).wait_recv()
        mem_copy_out = pltpu.make_async_copy(mem_in, mem_home, load_sem.at[2])
        mem_copy_out.start()
        engine.run(54)
        engine.run(55)
        events = PLAN[56]
        early = [n for n, (unit, level) in enumerate(events) if level == 3 and (unit < 26 or unit >= NARROW)]
        emptied = max(early + [-1]) + 1
        stops = [len(events) * k // 6 for k in range(1, 6)]
        for n, (unit, level) in enumerate(events):
            for step in range(5):
                if n == stops[step]:
                    gain_copy(step).wait_recv()
                    total = gain_buf[0, step] + gain_buf[1, step]
                    if step < 4:
                        gain_buf[0, step + 1] = total
                        gain_copy(step + 1).start()
                    else:
                        gains_out[...] = total
            if n == emptied:
                engine.drain(0, 0, 26)
                engine.drain(1, 0, 4)
            engine.arrive(unit, level)
        engine.drain(0, 26, NARROW)
        for level in range(5):
            gain_copy(level).wait_send()
        for copy in [out_copy, mem_copy_out]:
            copy.wait()
        for unit in range(NARROW + 4):
            engine.result(unit).wait()

    width = w_query.shape[0]
    pl.run_scoped(
        tail,
        pltpu.VMEM((width, block), low),
        pltpu.VMEM((block, width), full), pltpu.VMEM((block, width), full), pltpu.VMEM((block, width), low),
        pltpu.VMEM((2, 3, UNIT, width), low),
    )

    @pl.when(chip == 0)
    def _():
        for head in range(HALF):
            for blk in range(2):
                back_copy(blk, head).wait_send()

    @pl.when(chip == 1)
    def _():
        for copy in row_copies():
            copy.wait_send()
        for head in range(HALF):
            grad_copy(head, True).wait_send()
            grad_copy(head, False).wait_send()


def go_back(limit, attended, saved, tokens, cotangent, weights, gain_one, gain_two):
    block, width = tokens.shape
    low, full = jnp.bfloat16, jnp.float32
    box = (2, HALF, block, HEAD_DIM)
    row = (2, HALF, 1, block)
    seq_count = lax.axis_size("seq")
    capacity = 2 * TOPK // seq_count
    dma = pltpu.SemaphoreType.DMA
    hbm, vmem = pl.BlockSpec(memory_space=pl.ANY), pl.BlockSpec(memory_space=pltpu.VMEM)
    struct = jax.ShapeDtypeStruct
    ff = weights[4].shape[1]
    *saved, picked_t = saved
    spots = saved[8]

    def wide(rows, columns):
        return struct((2, 2, 2, 2, 2, rows, columns), low)

    mem = (seq_count, 2, 2, capacity, HALF * HEAD_DIM)
    units = (NARROW, 4)
    scratch = [
        pltpu.VMEM(box, low), pltpu.VMEM(box, low),
        pltpu.VMEM(row, full), pltpu.VMEM(row, full), pltpu.VMEM(row, full), pltpu.VMEM(row, full),
        pltpu.VMEM((2, HALF, HEAD_DIM, block), low),
        pltpu.VMEM((3, block, width), low), pltpu.VMEM(mem, low),
        pltpu.VMEM((2, 5, 2, 1, width), full),
        pltpu.VMEM((RING, 2, 2, 2, 2, 2, ROWS[0], UNIT), low),
        pltpu.VMEM((2, 2, 2, 2, 2, ROWS[1], UNIT), low),
        pltpu.VMEM((block, width), low),
        pltpu.VMEM((2, width), full),
    ]
    for c in range(2):
        scratch += [pltpu.VMEM((units[c],) + (2,) * k + (ROWS[c], UNIT), low) for k in (4, 3, 2, 1, 0)]
    scratch += [pltpu.VMEM((units[c], ROWS[c], UNIT), full) for c in range(2)]
    scratch += [dma((2,))]
    scratch += [dma((5, units[c])) for c in range(2)] * 2
    scratch += [
        dma((8,)), dma((1, HALF)), dma((1, HALF)), dma((1, HALF)), dma((1,)),
        dma((2, HALF)), dma((2, HALF)), dma((2,)), dma((2,)), dma((2, HALF)), dma((2, HALF)),
        dma((3, HALF)), dma((3, HALF)), dma((1,)), dma((seq_count - 1,)), dma((seq_count - 1,)),
        dma((5,)), dma((5,)), dma((4,)), dma((2, 3)), dma((sum(units),)),
        dma((5,)), dma((2, 3)), dma((2,)),
    ]
    rows = struct((32, width), full)
    mem_rows = picked_t.shape[0]
    results = pl.pallas_call(
        back_kernel,
        out_shape=(
            struct((block, width), low), struct((block, width), low),
            struct((32, ff), full), struct((32, ff), full),
            rows, rows, rows, rows,
            struct((88, width), full), struct((2, 1, width), full),
            struct(mem, low),
            wide(88, width),
            struct((block, width), full),
        ),
        in_specs=[pl.BlockSpec(memory_space=pltpu.SMEM)] + [hbm] * 19 + [vmem] * 2,
        out_specs=(hbm,) * 9 + (vmem,) + (hbm,) * 3,
        scratch_shapes=scratch,
        name="go_back",
        compiler_params=pltpu.CompilerParams(collective_id=3, has_side_effects=True, vmem_limit_bytes=60 * 2**20),
    )(limit, attended, *saved, tokens, cotangent, *weights, gain_one, gain_two)
    return deliver(results[:9], results[10], picked_t) + (results[9],)


def deliver_kernel(*refs):
    sources, mem_home, picked_t = refs[:9], refs[9], refs[10]
    targets, tables = refs[11:20], refs[20:22]
    boxes, rest = refs[22:31], refs[31:]
    rows, pick, table, in_sem, out_sem, load_sem, table_sem = rest
    loads = [
        pltpu.make_async_copy(mem_home, rows, load_sem.at[0]),
        pltpu.make_async_copy(picked_t, pick, load_sem.at[1]),
    ]
    ins = [pltpu.make_async_copy(a, b, in_sem.at[i]) for i, (a, b) in enumerate(zip(sources, boxes))]
    outs = [pltpu.make_async_copy(a, b, out_sem.at[i]) for i, (a, b) in enumerate(zip(boxes, targets))]
    for copy in loads + ins:
        copy.start()
    for copy in loads:
        copy.wait()
    half = rows.shape[4]
    stores = []
    for kind in range(2):
        for side in range(2):
            values = jnp.concatenate(
                [rows[2 * src + side, blk, kind] for src in range(rows.shape[0] // 2) for blk in range(2)], axis=0
            )
            table[2 * kind + side] = matmul(pick[...], values, NN)
            stores.append(
                pltpu.make_async_copy(
                    table.at[2 * kind + side],
                    tables[kind].at[:, side * half : (side + 1) * half],
                    table_sem.at[2 * kind + side],
                )
            )
            stores[-1].start()
    for arrived, left in zip(ins, outs):
        arrived.wait()
        left.start()
    for copy in stores + outs:
        copy.wait()


def deliver(arrays, mem_home, picked_t):
    struct = jax.ShapeDtypeStruct
    hbm = pl.BlockSpec(memory_space=pl.ANY)
    mem_rows, half = picked_t.shape[0], mem_home.shape[4]
    table = struct((mem_rows, 2 * half), jnp.float32)
    return tuple(
        pl.pallas_call(
            deliver_kernel,
            out_shape=tuple(struct(a.shape, a.dtype) for a in arrays) + (table, table),
            in_specs=[hbm] * 11,
            out_specs=(hbm,) * 11,
            scratch_shapes=[pltpu.VMEM(a.shape, a.dtype) for a in arrays] + [
                pltpu.VMEM(mem_home.shape, jnp.bfloat16), pltpu.VMEM(picked_t.shape, jnp.bfloat16),
                pltpu.VMEM((4, mem_rows, half), jnp.float32),
                pltpu.SemaphoreType.DMA((9,)), pltpu.SemaphoreType.DMA((9,)), pltpu.SemaphoreType.DMA((2,)), pltpu.SemaphoreType.DMA((4,)),
            ],
            name="deliver",
            compiler_params=pltpu.CompilerParams(vmem_limit_bytes=60 * 2**20),
        )(*arrays, mem_home, picked_t)
    )


def rms_factor(values):
    return lax.rsqrt(jnp.mean(values * values, axis=-1, keepdims=True) + EPS)


def dot32(left, right):
    return jnp.dot(left, right, preferred_element_type=jnp.float32)


def fitting():
    return (lax.axis_size("seq"), lax.axis_size("doc")) == (8, 4)


def exchange(rows, owner_count, capacity):
    parts, _, width = rows.shape
    shaped = rows.reshape(parts, owner_count, capacity, width)
    moved = lax.all_to_all(shaped, "seq", split_axis=1, concat_axis=1, tiled=True)
    return moved.reshape(parts, owner_count * capacity, width)


def on_device(
    tokens,
    cotangent,
    attn_gain,
    w_query,
    w_key,
    w_value,
    w_out,
    ffn_gain,
    w_gate,
    w_up,
    w_down,
    mem_keys,
    mem_values,
    seg_len,
    mem_idx,
):
    low = jnp.bfloat16
    stream_count, block_len, model_width = tokens.shape
    mem_rows = mem_keys.shape[1]
    seq_count = lax.axis_size("seq")
    segment = lax.axis_index("seq") // BPS
    capacity = 2 * TOPK // seq_count
    slot_count = seq_count * capacity
    limit = lax.dynamic_index_in_dim(seg_len, segment, 1, keepdims=False)

    gain_one = attn_gain.astype(jnp.float32)
    gain_two = ffn_gain.astype(jnp.float32)
    if fitting():
        gain_rows = [gain.reshape(8, -1) for gain in (attn_gain, ffn_gain)]
        attended, *saved = go_forward(
            seg_len, tokens[0], gain_rows[0], (w_query, w_key, w_value), mem_keys[0], mem_values[0], mem_idx[0]
        )
        layer_out, grad_tokens, gate_rows, up_rows, query_rows, key_rows, value_rows, out_rows, down_rows, grad_mk, grad_mv, summed = go_back(
            seg_len,
            attended,
            saved,
            tokens[0],
            cotangent[0],
            (w_query, w_key, w_value, w_out, w_gate, w_up, w_down),
            *gain_rows,
        )
        index = lax.axis_index("seq") * lax.axis_size("doc") + lax.axis_index("doc")
        parts = summed.reshape(2, seq_count * lax.axis_size("doc"), -1)
        attn_row, ffn_row = lax.dynamic_index_in_dim(parts, index, 1, keepdims=False)
        return (
            layer_out[None],
            grad_tokens[None],
            attn_row,
            query_rows,
            key_rows,
            value_rows,
            out_rows,
            ffn_row,
            gate_rows,
            up_rows,
            down_rows,
            grad_mk[None],
            grad_mv[None],
        )

    tokens_f = tokens[0].astype(jnp.float32)
    factor_one = rms_factor(tokens_f)
    unit_one = tokens_f * factor_one
    normed_one = (unit_one * gain_one).astype(low)
    chosen = mem_idx[0, 0]
    owner = chosen // mem_rows
    order = jnp.arange(TOPK)
    same_before = (owner[:, None] == owner[None, :]) & (order[None, :] < order[:, None])
    slot = owner * capacity + jnp.sum(same_before.astype(jnp.int32), axis=1)
    placed = slot[:, None] == jnp.arange(slot_count)[None, :]
    request = jnp.sum(jnp.where(placed, (chosen % mem_rows)[:, None] + 1, 0), axis=0) - 1
    requested = lax.all_to_all(
        request.reshape(seq_count, capacity), "seq", split_axis=0, concat_axis=0, tiled=True
    ).reshape(slot_count)
    picked = (requested[:, None] == jnp.arange(mem_rows)[None, :]).astype(low)
    placed = placed.astype(low)
    sent = jnp.stack((dot32(picked, mem_keys[0]).astype(low), dot32(picked, mem_values[0]).astype(low)))
    arrived = exchange(sent, seq_count, capacity)
    mem_key_rows = dot32(placed, arrived[0]).astype(low)
    mem_value_rows = dot32(placed, arrived[1]).astype(low)
    queries = dot32(normed_one, w_query).astype(low)
    keys = dot32(normed_one, w_key).astype(low)
    values = dot32(normed_one, w_value).astype(low)
    attended, *saved = attend_forward(limit, queries, keys, values, mem_key_rows, mem_value_rows)
    middle = tokens_f + dot32(attended, w_out)
    factor_two = rms_factor(middle)
    unit_two = middle * factor_two
    normed_two = (unit_two * gain_two).astype(low)
    gate = dot32(normed_two, w_gate)
    upper = dot32(normed_two, w_up)
    sigma = jax.nn.sigmoid(gate)
    hidden = (gate * sigma * upper).astype(low)
    layer_out = (middle + dot32(hidden, w_down)).astype(low)

    grad_y_low = cotangent[0]
    grad_y = grad_y_low.astype(jnp.float32)
    grad_down = dot32(hidden.T, grad_y_low)
    grad_hidden = dot32(grad_y_low, w_down.T)
    grad_gate_act = (grad_hidden * upper * sigma * (1.0 + gate * (1.0 - sigma))).astype(low)
    grad_up_act = (grad_hidden * gate * sigma).astype(low)
    grad_gate = dot32(normed_two.T, grad_gate_act)
    grad_up = dot32(normed_two.T, grad_up_act)
    grad_normed_two = dot32(grad_gate_act, w_gate.T) + dot32(grad_up_act, w_up.T)
    grad_ffn_gain = jnp.sum(grad_normed_two * unit_two, axis=0)
    scaled_two = gain_two * grad_normed_two
    grad_middle = grad_y + factor_two * (
        scaled_two - unit_two * jnp.mean(scaled_two * unit_two, axis=-1, keepdims=True)
    )
    grad_branch = grad_middle.astype(low)
    grad_out = dot32(attended.T, grad_branch)
    grad_attended = dot32(grad_branch, w_out.T).astype(low)
    grad_q, grad_k, grad_v, grad_mk, grad_mv = attend_backward(limit, grad_attended, saved)
    back = jnp.stack((dot32(placed.T, grad_mk).astype(low), dot32(placed.T, grad_mv).astype(low)))
    returned = exchange(back, seq_count, capacity)
    grad_mem_keys = dot32(picked.T, returned[0])
    grad_mem_values = dot32(picked.T, returned[1])
    grad_query = dot32(normed_one.T, grad_q)
    grad_key = dot32(normed_one.T, grad_k)
    grad_value = dot32(normed_one.T, grad_v)
    grad_normed_one = dot32(grad_q, w_query.T) + dot32(grad_k, w_key.T) + dot32(grad_v, w_value.T)
    grad_attn_gain = jnp.sum(grad_normed_one * unit_one, axis=0)
    scaled_one = gain_one * grad_normed_one
    grad_input = grad_middle + factor_one * (
        scaled_one - unit_one * jnp.mean(scaled_one * unit_one, axis=-1, keepdims=True)
    )
    grad_tokens = grad_input.astype(low)
    gate_rows, up_rows, query_rows, key_rows, value_rows, out_rows, down_rows, attn_row, ffn_row = [
        lax.psum_scatter(grad, ("seq", "doc"), scatter_dimension=0, tiled=True)
        for grad in (
            grad_gate, grad_up, grad_query, grad_key, grad_value, grad_out, grad_down, grad_attn_gain, grad_ffn_gain
        )
    ]
    return (
        layer_out[None],
        grad_tokens[None],
        attn_row,
        query_rows,
        key_rows,
        value_rows,
        out_rows,
        ffn_row,
        gate_rows,
        up_rows,
        down_rows,
        grad_mem_keys[None],
        grad_mem_values[None],
    )


def solution(mesh):
    in_specs = (
        P("doc", "seq", None),
        P("doc", "seq", None),
        P(),
        P(),
        P(),
        P(),
        P(),
        P(),
        P(),
        P(),
        P(),
        P("doc", "seq", None),
        P("doc", "seq", None),
        P("doc", None),
        P("doc", "seq", None),
    )
    out_specs = (
        P("doc", "seq", None),
        P("doc", "seq", None),
        P(("seq", "doc")),
        P(("seq", "doc"), None),
        P(("seq", "doc"), None),
        P(("seq", "doc"), None),
        P(("seq", "doc"), None),
        P(("seq", "doc")),
        P(("seq", "doc"), None),
        P(("seq", "doc"), None),
        P(("seq", "doc"), None),
        P("doc", "seq", None),
        P("doc", "seq", None),
    )
    return jax.shard_map(
        on_device, mesh=mesh, in_specs=in_specs, out_specs=out_specs, check_vma=False
    )
```

```python
import functools
import math

import jax
import jax.numpy as jnp
from jax import lax
from jax.experimental import pallas as pl
from jax.experimental.pallas import tpu as pltpu
from jax.sharding import PartitionSpec as P

HEADS = 8
HEAD_DIM = 128
TOPK = 128
BPS = 4
NEG = -1000000000.0
MESH = pl.DeviceIdType.MESH
EPS = 1e-05
UNIT = 256
SKEW = 4


def flip(value, bit):
    return value + bit - 2 * bit * ((value // bit) % 2)


HALF = HEADS // 2
LOG2E = math.log2(math.e)
SCALE = HEAD_DIM ** (-0.5)
NT = (((1,), (1,)), ((), ()))
TN = (((0,), (0,)), ((), ()))
NN = (((1,), (0,)), ((), ()))


def matmul(left, right, dims):
    return lax.dot_general(left, right, dims, preferred_element_type=jnp.float32)


def seats():
    seq, doc = lax.axis_index("seq"), lax.axis_index("doc")
    core, chip = seq % 2, (seq // 2) % 2
    mate = (flip(seq, 1), doc)
    across = (flip(seq, 2), doc)
    diagonal = (flip(flip(seq, 2), 1), doc)
    return core, chip, mate, across, diagonal


def meet(peers):
    barrier = pltpu.get_barrier_semaphore()
    for peer in peers:
        pl.semaphore_signal(barrier, inc=1, device_id=peer, device_id_type=MESH)
    pl.semaphore_wait(barrier, len(peers))


def head_lanes(core, head):
    return pl.ds(pl.multiple_of((core * HALF + head) * HEAD_DIM, HEAD_DIM), HEAD_DIM)


def remote(src, dst, send, recv, peer):
    return pltpu.make_async_remote_copy(
        src_ref=src, dst_ref=dst, send_sem=send, recv_sem=recv, device_id=peer, device_id_type=MESH
    )


def share_heads(sources, boxes, core, mate, local_sem, send_sem, recv_sem):
    copies = []
    for i, (source, box) in enumerate(zip(sources, boxes)):
        for head in range(HALF):
            copies.append(
                remote(
                    source.at[:, head_lanes(1 - core, head)],
                    box.at[core, head],
                    send_sem.at[i, head],
                    recv_sem.at[i, head],
                    mate,
                )
            )
            copies[-1].start()
    for i, (source, box) in enumerate(zip(sources, boxes)):
        for head in range(HALF):
            copies.append(
                pltpu.make_async_copy(
                    source.at[:, head_lanes(core, head)], box.at[core, head], local_sem.at[i, head]
                )
            )
            copies[-1].start()
    return copies


def masked(scores, first_key, limit, diagonal):
    key = lax.broadcasted_iota(jnp.int32, scores.shape, 0)
    ok = key + first_key < limit
    if diagonal:
        ok = ok & (key <= lax.broadcasted_iota(jnp.int32, scores.shape, 1))
    return jnp.where(ok, scores, NEG)


def soften(parts):
    top = functools.reduce(
        jnp.maximum, [jnp.max(scores, axis=0, keepdims=True) for scores, _ in parts]
    )
    total, mixed = 0.0, 0.0
    for scores, values in parts:
        exponent = jnp.exp2(scores - top)
        total = total + jnp.sum(exponent, axis=0, keepdims=True)
        mixed = mixed + matmul(values, exponent.astype(jnp.bfloat16), TN)
    return mixed / total, top + jnp.log(total) * LOG2E


def forward_kernel(
    limit_ref, q, k, v, mk, mv,
    attended, qb, kb, vb, qx, mkb, mvb, ob, lse,
    mixed_own, mixed_out, mixed_in, lse_out, lse_in,
    local_sem, mate_send, mate_recv, far_send, far_recv, back_send, back_recv, end_sem,
):
    core, chip, mate, across, diagonal = seats()
    block = q.shape[0]
    limit = limit_ref[0]
    meet((mate, across, diagonal))

    def query_copy(head, own):
        return remote(
            q.at[:, head_lanes(core if own else 1 - core, head)],
            qx.at[core, head],
            far_send.at[0 if own else 1, head],
            far_recv.at[core, head],
            across if own else diagonal,
        )

    def arrived_query(far, head):
        return remote(
            q.at[:, head_lanes(core, head)], qx.at[far, head], far_send.at[0, head], far_recv.at[far, head], across
        )

    @pl.when(chip == 1)
    def _():
        for head in range(HALF):
            query_copy(head, True).start()
            query_copy(head, False).start()

    copies = share_heads((q, k, v, mk, mv), (qb, kb, vb, mkb, mvb), core, mate, local_sem, mate_send, mate_recv)
    for copy in copies:
        copy.wait()

    def own_part(blk, head):
        query = qb[blk, head]
        parts = []
        for kblk in range(blk + 1):
            scores = matmul(kb[kblk, head], query, NT) * (SCALE * LOG2E)
            scores = masked(scores, (2 * chip + kblk) * block, limit, kblk == blk)
            parts.append((scores, vb[kblk, head]))
        parts.append((matmul(mkb[blk, head], query, NT) * (SCALE * LOG2E), mvb[blk, head]))
        return soften(parts)

    for blk in range(2):
        def own_head(head, carry):
            mixed, level = own_part(blk, head)
            mixed_own[blk, head] = mixed
            lse[blk, head] = level
            return carry
        lax.fori_loop(0, HALF, own_head, 0)

    def back_copy(blk, head):
        return (
            remote(mixed_out.at[blk, head], mixed_in.at[blk, head], back_send.at[0, blk, head], back_recv.at[0, blk, head], across),
            remote(lse_out.at[blk, head], lse_in.at[blk, head], back_send.at[1, blk, head], back_recv.at[1, blk, head], across),
        )

    @pl.when(chip == 0)
    def _():
        def cross(i, carry):
            head, blk = i // 2, i % 2
            arrived_query(blk, head).wait_recv()
            query = qx[blk, head]
            parts = []
            for kblk in range(2):
                scores = matmul(kb[kblk, head], query, NT) * (SCALE * LOG2E)
                parts.append((masked(scores, kblk * block, limit, False), vb[kblk, head]))
            mixed, level = soften(parts)
            mixed_out[blk, head] = mixed.astype(jnp.bfloat16)
            lse_out[blk, head] = level
            for copy in back_copy(blk, head):
                copy.start()
            return carry
        lax.fori_loop(0, 2 * HALF, cross, 0)

        def finish(i, carry):
            head, blk = i // 2, i % 2
            ob[blk, head] = mixed_own[blk, head].T.astype(jnp.bfloat16)
            return carry
        lax.fori_loop(0, 2 * HALF, finish, 0)

    @pl.when(chip == 1)
    def _():
        def merge(i, carry):
            head, blk = i // 2, i % 2
            for copy in back_copy(blk, head):
                copy.wait_recv()
            near, far = lse[blk, head], lse_in[blk, head]
            top = jnp.maximum(near, far)
            near, far = jnp.exp2(near - top), jnp.exp2(far - top)
            total = near + far
            mixed = (mixed_own[blk, head] * near + mixed_in[blk, head].astype(jnp.float32) * far) / total
            ob[blk, head] = mixed.T.astype(jnp.bfloat16)
            lse[blk, head] = top + jnp.log(total) * LOG2E
            return carry
        lax.fori_loop(0, 2 * HALF, merge, 0)

    ends = []
    for head in range(HALF):
        ends.append(
            remote(ob.at[1 - core, head], attended.at[:, head_lanes(core, head)], end_sem.at[0, head], end_sem.at[1, head], mate)
        )
        ends.append(
            pltpu.make_async_copy(ob.at[core, head], attended.at[:, head_lanes(core, head)], end_sem.at[2, head])
        )
    for copy in ends:
        copy.start()
    for copy in ends:
        copy.wait()

    @pl.when(chip == 0)
    def _():
        for head in range(HALF):
            for blk in range(2):
                for copy in back_copy(blk, head):
                    copy.wait_send()

    @pl.when(chip == 1)
    def _():
        for head in range(HALF):
            query_copy(head, True).wait_send()
            query_copy(head, False).wait_send()


def attend_forward(limit, queries, keys, values, mem_keys, mem_values):
    block, width = queries.shape
    topk = mem_keys.shape[0]
    low, full = jnp.bfloat16, jnp.float32
    box = (2, HALF, block, HEAD_DIM)
    mem_box = (2, HALF, topk, HEAD_DIM)
    flat = (2, HALF, HEAD_DIM, block)
    row = (2, HALF, 1, block)
    dma = pltpu.SemaphoreType.DMA
    hbm, vmem = pl.BlockSpec(memory_space=pl.ANY), pl.BlockSpec(memory_space=pltpu.VMEM)
    struct = jax.ShapeDtypeStruct
    return pl.pallas_call(
        forward_kernel,
        out_shape=(
            struct((block, width), low),
            struct(box, low), struct(box, low), struct(box, low), struct(box, low),
            struct(mem_box, low), struct(mem_box, low), struct(box, low), struct(row, full),
        ),
        in_specs=[pl.BlockSpec(memory_space=pltpu.SMEM)] + [hbm] * 5,
        out_specs=(hbm,) + (vmem,) * 8,
        scratch_shapes=[
            pltpu.VMEM(flat, full), pltpu.VMEM(flat, low), pltpu.VMEM(flat, low),
            pltpu.VMEM(row, full), pltpu.VMEM(row, full),
            dma((5, HALF)), dma((5, HALF)), dma((5, HALF)),
            dma((2, HALF)), dma((2, HALF)), dma((2, 2, HALF)), dma((2, 2, HALF)), dma((3, HALF)),
        ],
        name="attend_forward",
        compiler_params=pltpu.CompilerParams(collective_id=1, has_side_effects=True, vmem_limit_bytes=56 * 2**20),
    )(limit, queries, keys, values, mem_keys, mem_values)


def backward_kernel(
    limit_ref, grad, qb, kb, vb, qx, mkb, mvb, ob, lse,
    dq, dk, dv, dmk, dmv,
    gb, gx, delta, lse_in, delta_in, dq_own, dq_out, dq_in, dk_sum, dv_sum, dmk_low, dmv_low, dqb, dkb, dvb,
    local_sem, mate_send, mate_recv, far_send, far_recv, row_send, row_recv, back_send, back_recv,
    end_local, end_send, end_recv,
):
    core, chip, mate, across, diagonal = seats()
    block = grad.shape[0]
    limit = limit_ref[0]
    meet((mate, across, diagonal))

    def grad_copy(head, own):
        return remote(
            grad.at[:, head_lanes(core if own else 1 - core, head)],
            gx.at[core, head],
            far_send.at[0 if own else 1, head],
            far_recv.at[core, head],
            across if own else diagonal,
        )

    def arrived_grad(far, head):
        return remote(
            grad.at[:, head_lanes(core, head)], gx.at[far, head], far_send.at[0, head], far_recv.at[far, head], across
        )

    def row_copies():
        return (
            remote(lse, lse_in, row_send.at[0], row_recv.at[0], across),
            remote(delta, delta_in, row_send.at[1], row_recv.at[1], across),
        )

    @pl.when(chip == 1)
    def _():
        for head in range(HALF):
            grad_copy(head, True).start()
            grad_copy(head, False).start()

    copies = share_heads((grad,), (gb,), core, mate, local_sem, mate_send, mate_recv)
    for copy in copies:
        copy.wait()

    def rows(i, carry):
        head, blk = i // 2, i % 2
        product = gb[blk, head].astype(jnp.float32) * ob[blk, head].astype(jnp.float32)
        delta[blk, head] = jnp.sum(product.T, axis=0, keepdims=True)
        return carry

    lax.fori_loop(0, 2 * HALF, rows, 0)

    @pl.when(chip == 1)
    def _():
        for copy in row_copies():
            copy.start()

    def pull(key_rows, value_rows, query, grad_rows, level, inner, where):
        scores = matmul(key_rows, query, NT) * (SCALE * LOG2E)
        if where is not None:
            scores = masked(scores, where[0], limit, where[1])
        weights = jnp.exp2(scores - level)
        grad_weights = matmul(value_rows, grad_rows, NT)
        grad_scores = (weights * (grad_weights - inner)).astype(jnp.bfloat16)
        return (
            matmul(grad_scores, query, NN),
            matmul(weights.astype(jnp.bfloat16), grad_rows, NN),
            matmul(key_rows, grad_scores, TN),
        )

    for blk in range(2):
        def own_head(head, carry):
            query, grad_rows = qb[blk, head], gb[blk, head]
            level, inner = lse[blk, head], delta[blk, head]
            total = 0.0
            for kblk in range(blk + 1):
                gk, gv, gq = pull(
                    kb[kblk, head], vb[kblk, head], query, grad_rows, level, inner,
                    ((2 * chip + kblk) * block, kblk == blk),
                )
                if kblk == blk:
                    dk_sum[kblk, head], dv_sum[kblk, head] = gk, gv
                else:
                    dk_sum[kblk, head] += gk
                    dv_sum[kblk, head] += gv
                total = total + gq
            gk, gv, gq = pull(mkb[blk, head], mvb[blk, head], query, grad_rows, level, inner, None)
            dmk_low[blk, head] = (gk * SCALE).astype(jnp.bfloat16)
            dmv_low[blk, head] = gv.astype(jnp.bfloat16)
            dq_own[blk, head] = total + gq
            return carry
        lax.fori_loop(0, HALF, own_head, 0)

    def back_copy(blk, head):
        return remote(dq_out.at[blk, head], dq_in.at[blk, head], back_send.at[blk, head], back_recv.at[blk, head], across)

    @pl.when(chip == 0)
    def _():
        for copy in row_copies():
            copy.wait_recv()

        def cross(i, carry):
            head, blk = i // 2, i % 2
            arrived_grad(blk, head).wait_recv()
            query, grad_rows = qx[blk, head], gx[blk, head]
            level, inner = lse_in[blk, head], delta_in[blk, head]
            total = 0.0
            for kblk in range(2):
                gk, gv, gq = pull(
                    kb[kblk, head], vb[kblk, head], query, grad_rows, level, inner, (kblk * block, False)
                )
                dk_sum[kblk, head] += gk
                dv_sum[kblk, head] += gv
                total = total + gq
            dq_out[blk, head] = total.astype(jnp.bfloat16)
            back_copy(blk, head).start()
            return carry
        lax.fori_loop(0, 2 * HALF, cross, 0)

    def finish(i, carry):
        head, blk = i // 2, i % 2
        dqb[blk, head] = (dq_own[blk, head].T * SCALE).astype(jnp.bfloat16)
        dkb[blk, head] = (dk_sum[blk, head] * SCALE).astype(jnp.bfloat16)
        dvb[blk, head] = dv_sum[blk, head].astype(jnp.bfloat16)
        return carry

    @pl.when(chip == 1)
    def _():
        def merge(i, carry):
            head, blk = i // 2, i % 2
            back_copy(blk, head).wait_recv()
            dq_own[blk, head] += dq_in[blk, head].astype(jnp.float32)
            return finish(i, carry)
        lax.fori_loop(0, 2 * HALF, merge, 0)

    @pl.when(chip == 0)
    def _():
        lax.fori_loop(0, 2 * HALF, finish, 0)

    ends = []
    for i, (box, out) in enumerate(((dqb, dq), (dkb, dk), (dvb, dv), (dmk_low, dmk), (dmv_low, dmv))):
        for head in range(HALF):
            lanes = head_lanes(core, head)
            ends.append(remote(box.at[1 - core, head], out.at[:, lanes], end_send.at[i, head], end_recv.at[i, head], mate))
            ends.append(pltpu.make_async_copy(box.at[core, head], out.at[:, lanes], end_local.at[i, head]))
    for copy in ends:
        copy.start()
    for copy in ends:
        copy.wait()

    @pl.when(chip == 0)
    def _():
        for head in range(HALF):
            for blk in range(2):
                back_copy(blk, head).wait_send()

    @pl.when(chip == 1)
    def _():
        for copy in row_copies():
            copy.wait_send()
        for head in range(HALF):
            grad_copy(head, True).wait_send()
            grad_copy(head, False).wait_send()


def attend_backward(limit, grad, saved):
    block, width = grad.shape
    topk = saved[4].shape[2]
    low, full = jnp.bfloat16, jnp.float32
    box = (2, HALF, block, HEAD_DIM)
    mem_box = (2, HALF, topk, HEAD_DIM)
    flat = (2, HALF, HEAD_DIM, block)
    row = (2, HALF, 1, block)
    dma = pltpu.SemaphoreType.DMA
    hbm, vmem = pl.BlockSpec(memory_space=pl.ANY), pl.BlockSpec(memory_space=pltpu.VMEM)
    struct = jax.ShapeDtypeStruct
    return pl.pallas_call(
        backward_kernel,
        out_shape=(struct((block, width), low),) * 3 + (struct((topk, width), low),) * 2,
        in_specs=[pl.BlockSpec(memory_space=pltpu.SMEM), hbm] + [vmem] * 8,
        out_specs=(hbm,) * 5,
        scratch_shapes=[
            pltpu.VMEM(box, low), pltpu.VMEM(box, low),
            pltpu.VMEM(row, full), pltpu.VMEM(row, full), pltpu.VMEM(row, full),
            pltpu.VMEM(flat, full), pltpu.VMEM(flat, low), pltpu.VMEM(flat, low),
            pltpu.VMEM(box, full), pltpu.VMEM(box, full),
            pltpu.VMEM(mem_box, low), pltpu.VMEM(mem_box, low),
            pltpu.VMEM(box, low), pltpu.VMEM(box, low), pltpu.VMEM(box, low),
            dma((1, HALF)), dma((1, HALF)), dma((1, HALF)),
            dma((2, HALF)), dma((2, HALF)), dma((2,)), dma((2,)),
            dma((2, HALF)), dma((2, HALF)),
            dma((5, HALF)), dma((5, HALF)), dma((5, HALF)),
        ],
        name="attend_backward",
        compiler_params=pltpu.CompilerParams(collective_id=2, has_side_effects=True, vmem_limit_bytes=56 * 2**20),
    )(limit, grad, *saved)


def keep_order(rank_of):
    before = lax.broadcasted_iota(jnp.int32, (rank_of, rank_of), 0)
    return (before < lax.broadcasted_iota(jnp.int32, (rank_of, rank_of), 1)).astype(jnp.bfloat16)


def one_row(ref):
    value = ref[...].astype(jnp.float32)
    return jnp.concatenate([value[i : i + 1] for i in range(value.shape[0])], axis=1)


def front_kernel(
    limit_ref, tokens, gain_in, w_query, w_key, w_value, mem_keys, mem_values, wanted,
    attended, qb, kb, vb, qx, mkb, mvb, ob, lse, spots, pick_t,
    rows, weights, normed, qkv, tables, every, pick, mem_out, mem_in,
    mixed_own, mixed_out, mixed_in, lse_out, lse_in,
    gain, load_sem, want_send, want_recv, mem_send, mem_recv, mem_local,
    local_sem, mate_send, mate_recv, far_send, far_recv, back_send, back_recv, end_sem,
):
    core, chip, mate, across, diagonal = seats()
    seq, doc = lax.axis_index("seq"), lax.axis_index("doc")
    seq_count, capacity = mem_in.shape[0], mem_in.shape[3]
    block, width = tokens.shape
    mem_rows, topk = tables.shape[1], every.shape[2]
    limit = limit_ref[0, seq // BPS]

    loads = [
        pltpu.make_async_copy(src, dst, load_sem.at[i])
        for i, (src, dst) in enumerate(
            (
                (wanted, every.at[seq]), (tokens, rows), (w_query, weights.at[0]), (w_key, weights.at[1]),
                (w_value, weights.at[2]), (mem_keys, tables.at[0]), (mem_values, tables.at[1]),
            )
        )
    ]
    for copy in loads:
        copy.start()
    meet([(lax.rem(seq + away, seq_count), doc) for away in range(1, seq_count)])
    loads[0].wait()

    def want_copy(away):
        return remote(
            every.at[seq], every.at[seq], want_send.at[away - 1], want_recv.at[away - 1],
            (lax.rem(seq + away, seq_count), doc),
        )

    def want_arrival(away):
        source = lax.rem(seq + seq_count - away, seq_count)
        return remote(every.at[source], every.at[source], want_send.at[away - 1], want_recv.at[away - 1], (source, doc))

    def mem_copy(away):
        peer = lax.rem(seq + away, seq_count)
        return remote(mem_out.at[peer], mem_in.at[seq], mem_send.at[away - 1], mem_recv.at[away - 1], (peer, doc))

    def mem_arrival(away):
        source = lax.rem(seq + seq_count - away, seq_count)
        return remote(mem_out.at[source], mem_in.at[source], mem_send.at[away - 1], mem_recv.at[away - 1], (source, doc))

    for away in range(1, seq_count):
        want_copy(away).start()
    gain[...] = one_row(gain_in)
    loads[1].wait()
    part = 64

    def norm(i, carry):
        at = pl.ds(pl.multiple_of(i * part, part), part)
        x = rows[at, :].astype(jnp.float32)
        factor = lax.rsqrt(jnp.mean(x * x, axis=-1, keepdims=True) + EPS)
        normed[at, :] = (x * factor * gain[0:1, :]).astype(jnp.bfloat16)
        return carry

    lax.fori_loop(0, block // part, norm, 0)

    def project(i):
        loads[2 + i].wait()

        def one(j, carry):
            lanes = pl.ds(pl.multiple_of(j * UNIT, UNIT), UNIT)
            qkv[i, :, lanes] = matmul(normed[...], weights[i, :, lanes], NN).astype(jnp.bfloat16)
            return carry

        lax.fori_loop(0, width // UNIT, one, 0)

    def query_copy(head, own):
        return remote(
            qkv.at[0, :, head_lanes(core if own else 1 - core, head)],
            qx.at[core, head],
            far_send.at[0 if own else 1, head],
            far_recv.at[core, head],
            across if own else diagonal,
        )

    def arrived_query(far, head):
        return remote(
            qkv.at[0, :, head_lanes(core, head)], qx.at[far, head], far_send.at[0, head], far_recv.at[far, head], across
        )

    loads[2].wait()
    for pair in range(HALF // 2):
        for side in range(2):
            lanes = slice((side * HALF // 2 + pair) * UNIT, (side * HALF // 2 + pair + 1) * UNIT)
            qkv[0, :, lanes] = matmul(normed[...], weights[0, :, lanes], NN).astype(jnp.bfloat16)

        @pl.when(chip == 1)
        def _():
            for head in (2 * pair, 2 * pair + 1):
                query_copy(head, True).start()
                query_copy(head, False).start()

    project(1)
    project(2)
    copies = share_heads(
        (qkv.at[0], qkv.at[1], qkv.at[2]), (qb, kb, vb), core, mate, local_sem, mate_send, mate_recv
    )

    for away in range(1, seq_count):
        want_arrival(away).wait_recv()
    triangle = keep_order(topk)
    asked = every[:, 0, :]
    here = asked - seq * mem_rows
    mine = (here >= 0) & (here < mem_rows)
    before = matmul(mine.astype(jnp.bfloat16), triangle, NN).astype(jnp.int32)
    place = lax.broadcasted_iota(jnp.int32, (capacity, topk), 0)
    line = lax.broadcasted_iota(jnp.int32, (mem_rows, topk), 0)
    for b in range(seq_count):
        at_place = jnp.where((before[b : b + 1] == place) & (here[b : b + 1] >= 0) & (here[b : b + 1] < mem_rows), 1.0, 0.0)
        at_line = jnp.where(here[b : b + 1] == line, 1.0, 0.0)
        pick[b * capacity : (b + 1) * capacity, :] = matmul(
            at_place.astype(jnp.bfloat16), at_line.astype(jnp.bfloat16), NT
        ).astype(jnp.bfloat16)
    half = HALF * HEAD_DIM
    for kind in range(2):
        loads[5 + kind].wait()
        for side in range(2):
            found = matmul(pick[...], tables[kind, :, side * half : (side + 1) * half], NN).astype(jnp.bfloat16)
            for b in range(seq_count):
                mem_out[2 * (b // 2) + side, b % 2, kind] = found[b * capacity : (b + 1) * capacity]
    for away in range(1, seq_count):
        mem_copy(away).start()
    own_rows = pltpu.make_async_copy(mem_out.at[seq], mem_in.at[seq], mem_local.at[0])
    own_rows.start()
    pick_t[...] = pick[...].astype(jnp.float32).T.astype(jnp.bfloat16)
    seat = lax.broadcasted_iota(jnp.int32, (seq_count, topk), 0)
    slot_at = lax.broadcasted_iota(jnp.int32, (seq_count * capacity, topk), 0)
    for blk in range(2):
        away_rows = every[2 * (seq // 2) + blk] - seat * mem_rows
        owner = (away_rows >= 0) & (away_rows < mem_rows)
        rank = matmul(owner.astype(jnp.bfloat16), triangle, NN).astype(jnp.int32)
        slot = jnp.sum(jnp.where(owner, seat * capacity + rank, 0), axis=0, keepdims=True)
        spots[blk] = jnp.where(slot == slot_at, 1.0, 0.0).astype(jnp.bfloat16)

    for copy in copies:
        copy.wait()

    def own_head(blk, head):
        query = qb[blk, head]
        parts = []
        for kblk in range(blk + 1):
            scores = matmul(kb[kblk, head], query, NT) * (SCALE * LOG2E)
            scores = masked(scores, (2 * chip + kblk) * block, limit, kblk == blk)
            parts.append((scores, vb[kblk, head]))
        mixed_own[blk, head], lse[blk, head] = soften(parts)

    def back_copy(blk, head):
        return (
            remote(mixed_out.at[blk, head], mixed_in.at[blk, head], back_send.at[0, blk, head], back_recv.at[0, blk, head], across),
            remote(lse_out.at[blk, head], lse_in.at[blk, head], back_send.at[1, blk, head], back_recv.at[1, blk, head], across),
        )

    def heads(head, carry):
        @pl.when(chip == 0)
        def _():
            def cross(blk, carry):
                arrived_query(blk, head).wait_recv()
                query = qx[blk, head]
                parts = []
                for kblk in range(2):
                    scores = matmul(kb[kblk, head], query, NT) * (SCALE * LOG2E)
                    parts.append((masked(scores, kblk * block, limit, False), vb[kblk, head]))
                mixed, level = soften(parts)
                mixed_out[blk, head] = mixed.astype(jnp.bfloat16)
                lse_out[blk, head] = level
                for copy in back_copy(blk, head):
                    copy.start()
                return carry

            lax.fori_loop(0, 2, cross, 0)

        own_head(0, head)
        own_head(1, head)
        return carry

    lax.fori_loop(0, HALF, heads, 0)

    for away in range(1, seq_count):
        mem_arrival(away).wait_recv()
    own_rows.wait()
    for blk in range(2):
        for kind, box in enumerate((mkb, mvb)):
            found = mem_in[:, blk, kind].reshape(seq_count * capacity, half)
            found = matmul(spots[blk], found, TN).astype(jnp.bfloat16)
            for head in range(HALF):
                box[blk, head] = found[:, head * HEAD_DIM : (head + 1) * HEAD_DIM]

    def blend(pieces):
        top = functools.reduce(jnp.maximum, [level for _, level in pieces])
        total, mixed = 0.0, 0.0
        for value, level in pieces:
            share = jnp.exp2(level - top)
            total = total + share
            mixed = mixed + value * share
        return mixed / total, top + jnp.log(total) * LOG2E

    def finish(i, carry):
        head, blk = i // 2, i % 2
        scores = matmul(mkb[blk, head], qb[blk, head], NT) * (SCALE * LOG2E)
        pieces = [(mixed_own[blk, head], lse[blk, head]), soften([(scores, mvb[blk, head])])]

        @pl.when(chip == 0)
        def _():
            mixed, lse[blk, head] = blend(pieces)
            ob[blk, head] = mixed.T.astype(jnp.bfloat16)

        @pl.when(chip == 1)
        def _():
            for copy in back_copy(blk, head):
                copy.wait_recv()
            far = (mixed_in[blk, head].astype(jnp.float32), lse_in[blk, head])
            mixed, lse[blk, head] = blend(pieces + [far])
            ob[blk, head] = mixed.T.astype(jnp.bfloat16)

        return carry

    lax.fori_loop(0, 2 * HALF, finish, 0)

    ends = []
    for head in range(HALF):
        ends.append(
            remote(ob.at[1 - core, head], attended.at[:, head_lanes(core, head)], end_sem.at[0, head], end_sem.at[1, head], mate)
        )
        ends.append(
            pltpu.make_async_copy(ob.at[core, head], attended.at[:, head_lanes(core, head)], end_sem.at[2, head])
        )
    for copy in ends:
        copy.start()
    for copy in ends:
        copy.wait()
    for away in range(1, seq_count):
        want_copy(away).wait_send()
        mem_copy(away).wait_send()

    @pl.when(chip == 0)
    def _():
        for head in range(HALF):
            for blk in range(2):
                for copy in back_copy(blk, head):
                    copy.wait_send()

    @pl.when(chip == 1)
    def _():
        for head in range(HALF):
            query_copy(head, True).wait_send()
            query_copy(head, False).wait_send()


def go_forward(limit, tokens, gain, projections, mem_keys, mem_values, wanted):
    block, width = tokens.shape
    mem_rows, topk = mem_keys.shape[0], wanted.shape[1]
    seq_count = lax.axis_size("seq")
    capacity = 2 * topk // seq_count
    slots = seq_count * capacity
    low, full = jnp.bfloat16, jnp.float32
    box = (2, HALF, block, HEAD_DIM)
    mem_box = (2, HALF, topk, HEAD_DIM)
    flat = (2, HALF, HEAD_DIM, block)
    row = (2, HALF, 1, block)
    mem = (seq_count, 2, 2, capacity, HALF * HEAD_DIM)
    dma = pltpu.SemaphoreType.DMA
    hbm, vmem = pl.BlockSpec(memory_space=pl.ANY), pl.BlockSpec(memory_space=pltpu.VMEM)
    struct = jax.ShapeDtypeStruct
    return pl.pallas_call(
        front_kernel,
        out_shape=(
            struct((block, width), low),
            struct(box, low), struct(box, low), struct(box, low), struct(box, low),
            struct(mem_box, low), struct(mem_box, low), struct(box, low), struct(row, full),
            struct((2, slots, topk), low), struct((mem_rows, slots), low),
        ),
        in_specs=[pl.BlockSpec(memory_space=pltpu.SMEM), hbm, vmem] + [hbm] * 6,
        out_specs=(hbm,) + (vmem,) * 10,
        scratch_shapes=[
            pltpu.VMEM((block, width), low), pltpu.VMEM((3, width, width), low), pltpu.VMEM((block, width), low),
            pltpu.VMEM((3, block, width), low), pltpu.VMEM((2, mem_rows, width), low),
            pltpu.VMEM((seq_count, 1, topk), jnp.int32), pltpu.VMEM((slots, mem_rows), low),
            pltpu.VMEM(mem, low), pltpu.VMEM(mem, low),
            pltpu.VMEM(flat, full), pltpu.VMEM(flat, low), pltpu.VMEM(flat, low),
            pltpu.VMEM(row, full), pltpu.VMEM(row, full),
            pltpu.VMEM((1, width), full),
            dma((7,)), dma((seq_count - 1,)), dma((seq_count - 1,)), dma((seq_count - 1,)), dma((seq_count - 1,)), dma((1,)),
            dma((3, HALF)), dma((3, HALF)), dma((3, HALF)),
            dma((2, HALF)), dma((2, HALF)), dma((2, 2, HALF)), dma((2, 2, HALF)), dma((3, HALF)),
        ],
        name="go_forward",
        compiler_params=pltpu.CompilerParams(collective_id=4, has_side_effects=True, vmem_limit_bytes=56 * 2**20),
    )(limit, tokens, gain, *projections, mem_keys, mem_values, wanted)


ALONG = (("x", "y", "low", "high"), ("y", "x", "low", "high"), ("low", "high", "y", "x"), ("low", "high", "x", "y"))
TURNS = (2, 0, 0, 3, 0, 1, 1, 1, 2, 1, 0, 0, 0, 0, 3, 0, 1, 0, 2, 0, 1, 3, 0, 0, 1, 1, 3, 1, 3, 0, 3, 1, 0, 0, 1, 0, 2, 0, 1, 2, 2, 3)
PLAN = (
    (),
    ((0, 0), (1, 0),),
    ((2, 0), (3, 0),),
    ((4, 0), (0, 1), (1, 1), (5, 0),),
    ((6, 0), (2, 1), (3, 1), (7, 0), (1, 2),),
    ((8, 0), (4, 1), (9, 0), (5, 1), (0, 2),),
    ((1, 3), (10, 0), (11, 0), (6, 1), (3, 2), (5, 2),),
    ((2, 2), (8, 1), (12, 0), (13, 0), (5, 3), (7, 1),),
    ((1, 4), (10, 1), (14, 0), (4, 2), (15, 0), (2, 3),),
    ((11, 1), (9, 1), (16, 0), (0, 3), (17, 0), (6, 2), (3, 3), (10, 2), (8, 2),),
    ((5, 4), (18, 0), (14, 1), (19, 0), (4, 3), (12, 1), (11, 2), (6, 3), (10, 3),),
    ((2, 4), (20, 0), (13, 1), (21, 0),),
    ((16, 1), (3, 4), (7, 2), (8, 3),),
    ((18, 1), (12, 2),),
    ((15, 1),),
    ((11, 3), (9, 2),),
    ((20, 1), (0, 4),),
    ((22, 0),),
    ((23, 0), (14, 2), (13, 2), (24, 0), (4, 4),),
    ((25, 0), (6, 4), (15, 2), (17, 1), (21, 1), (10, 4), (7, 3),),
    (),
    (),
    ((19, 1), (12, 3),),
    ((9, 3), (24, 1), (38, 0), (16, 2), (8, 4), (13, 3),),
    ((18, 2), (15, 3), (39, 0), (11, 4),),
    ((25, 1),),
    ((40, 0), (17, 2), (16, 3), (19, 2), (21, 2), (7, 4), (12, 4), (9, 4),),
    ((13, 4), (15, 4), (41, 0),),
    (),
    ((39, 1), (20, 2), (38, 1),),
    ((18, 3),),
    ((22, 1),),
    (),
    ((23, 1),),
    ((14, 3), (22, 2), (40, 1),),
    ((17, 3), (19, 3),),
    ((16, 4),),
    ((23, 2), (14, 4),),
    ((41, 1), (24, 2),),
    ((25, 2),),
    ((21, 3), (20, 3), (22, 3), (38, 2), (18, 4), (39, 2), (23, 3), (24, 3), (25, 3), (40, 2), (17, 4), (19, 4),),
    ((21, 4),),
    ((39, 3), (38, 3),),
    ((41, 2), (40, 3),),
    ((20, 4), (22, 4), (26, 0), (39, 4), (27, 0), (23, 4),),
    ((24, 4), (28, 0), (29, 0), (25, 4),),
    ((41, 3), (30, 0), (40, 4), (31, 0), (38, 4),),
    ((32, 0), (26, 1), (33, 0), (27, 1),),
    ((41, 4), (34, 0), (29, 1),),
    ((35, 0), (28, 1), (36, 0), (37, 0),),
    ((31, 1), (32, 1),),
    ((30, 1),),
    ((34, 1), (33, 1),),
    ((29, 2), (27, 2), (32, 2), (26, 2),),
    ((36, 1), (33, 2), (35, 1),),
    ((28, 2), (29, 3), (27, 3),),
    ((32, 3), (37, 1), (35, 2), (30, 2), (31, 2), (33, 3), (34, 2), (37, 2), (26, 3), (35, 3), (28, 3), (36, 2), (31, 3), (30, 3), (29, 4), (34, 3), (27, 4), (26, 4), (37, 3), (32, 4), (28, 4), (33, 4), (36, 3), (30, 4), (35, 4), (31, 4), (36, 4), (34, 4), (37, 4),),
)
OFFERED = (20, 22, 24, 26)
RING = 8
NARROW = 38
ROWS = (32, 88)


def taken(unit, level):
    return [(unit, level) in events for events in PLAN].index(True)


class Sums:
    def __init__(self, down, made, own, stages, sums, homes, local_sem, send_sem, recv_sem, done_sem, peers):
        self.down, self.made, self.own, self.stages, self.sums = down, made, own, stages, sums
        self.local_sem, self.send_sem, self.recv_sem = local_sem, send_sem, recv_sem
        self.peers, self.homes, self.done_sem = peers, homes, done_sem
        seq, doc = lax.axis_index("seq"), lax.axis_index("doc")
        self.bits = {
            "core": seq % 2,
            "x": (seq // 2) % 2,
            "y": (seq // 4) % 2,
            "low": doc % 2,
            "high": (doc // 2) % 2,
        }

    def core_copy(self, kind, index):
        if kind == 0:
            source = self.made.at[index % RING, :, :, 1 - self.bits["core"]]
        else:
            source = self.down.at[:, :, 1 - self.bits["core"], :, :, :, pl.ds(index * UNIT, UNIT)]
        return remote(
            source,
            self.stages[kind][0].at[index],
            self.send_sem[kind].at[0, index],
            self.recv_sem[kind].at[0, index],
            self.peers["core"],
        )

    def own_copy(self, index):
        return pltpu.make_async_copy(
            self.down.at[:, :, self.bits["core"], :, :, :, pl.ds(index * UNIT, UNIT)],
            self.own.at[index % 2],
            self.local_sem.at[index % 2],
        )

    def put(self, unit, value):
        pl.when(unit >= RING)(lambda: self.core_copy(0, jnp.maximum(unit - RING, 0)).wait_send())
        self.made[unit % RING] = value.astype(jnp.bfloat16).reshape(self.made.shape[1:])
        self.core_copy(0, unit).start()

    def offer_down(self, index):
        self.core_copy(1, index).start()
        if index < 2 or taken(NARROW + index - 2, 0) < OFFERED[index]:
            self.own_copy(index).start()

    def half(self, kind, index, order, level, mine):
        name = order[level]
        left = [axis for axis in ("y", "x", "high", "low") if axis not in order[:level]]
        side = self.bits[name] if mine else 1 - self.bits[name]
        return (index,) + (slice(None),) * left.index(name) + (side,)

    def copy(self, kind, index, order, level):
        return remote(
            self.stages[kind][level - 1].at[self.half(kind, index, order, level - 1, False)],
            self.stages[kind][level].at[index],
            self.send_sem[kind].at[level, index],
            self.recv_sem[kind].at[level, index],
            self.peers[order[level - 1]],
        )

    def arrive(self, unit, level):
        kind = 0 if unit < NARROW else 1
        index = unit - kind * NARROW
        order = ALONG[TURNS[unit]]
        ref = self.stages[kind][level]
        if level == 0:
            self.core_copy(kind, index).wait_recv()
            if kind == 1:
                self.own_copy(index).wait()

            def add(i, carry):
                y, x = i // 2, i % 2
                mine = self.made[index % RING, y, x, self.bits["core"]] if kind == 0 else self.own[index % 2, y, x]
                ref[index, y, x] = ref[index, y, x] + mine
                return carry

            lax.fori_loop(0, 4, add, 0)
            if kind == 1 and index < 2 and taken(unit, 0) >= OFFERED[index + 2]:
                self.own_copy(index + 2).start()
        else:
            self.copy(kind, index, order, level).wait_recv()
            kept = self.stages[kind][level - 1][self.half(kind, index, order, level - 1, True)]
            if level < 4:
                ref[index] = ref[index] + kept
            else:
                self.sums[kind][index] = ref[index].astype(jnp.float32) + kept.astype(jnp.float32)
                self.result(unit).start()
        if level < 4:
            self.copy(kind, index, order, level + 1).start()

    def result(self, unit):
        gate, up, out, query, key, value, down = self.homes
        if unit < 22:
            home, place = (gate, up)[unit % 2], unit // 2
        elif unit < 26:
            home, place = out, unit - 22
        elif unit < NARROW:
            home, place = (query, key, value)[(unit - 26) // 4], (unit - 26) % 4
        else:
            home, place = down, unit - NARROW
        kind = 0 if unit < NARROW else 1
        return pltpu.make_async_copy(
            self.sums[kind].at[unit - kind * NARROW], home.at[:, pl.ds(place * UNIT, UNIT)], self.done_sem.at[unit]
        )

    def run(self, place):
        for unit, level in PLAN[place]:
            self.arrive(unit, level)

    def run_turn(self, first, turn, count):
        for k in range(count):
            if PLAN[first + k]:
                pl.when(turn == k)(lambda: self.run(first + k))

    def drain(self, kind, first, last):
        def one(index, carry):
            pl.when((kind == 1) | (index >= NARROW - RING))(lambda: self.core_copy(kind, index).wait_send())
            for level in range(1, 5):
                self.copy(kind, index, ALONG[0], level).wait_send()
            return carry

        lax.fori_loop(first, last, one, 0)


def back_kernel(
    limit_ref, mixed_in, qb_in, kb_in, vb_in, qx_in, mkb_in, mvb_in, ob_in, lse_in0, spots_in,
    tokens, cotangent, w_query, w_key, w_value, w_out, w_gate, w_up, w_down, gain_one_in, gain_two_in,
    layer_out, grad_tokens, gate_rows, up_rows, query_rows, key_rows, value_rows, out_rows, down_rows, gains_out,
    mem_home, down, grad_middle,
    gb, gx, lse, delta, lse_in, delta_in, dq_cross, dqkv, mem_in, gain_buf, made, own, grad, gains_in, *rest,
):
    stages = [rest[5 * c : 5 * c + 5] for c in range(2)]
    sums = rest[10:12]
    local_sem, send_sems, recv_sems, rest = rest[12], rest[13:15], rest[15:17], rest[17:]
    (
        in_sem, gb_local, gb_send, gb_recv, spot_sem, far_send, far_recv, row_send, row_recv, back_send, back_recv,
        mate_send, mate_recv, mem_local, mem_send, mem_recv, gain_send, gain_recv, load_sem, weight_sem, done_sem, front_sem, tile_sem, stage_sem,
    ) = rest
    core, chip, mate, across, diagonal = seats()
    seq, doc = lax.axis_index("seq"), lax.axis_index("doc")
    seq_count = mem_in.shape[0]
    block = tokens.shape[0]
    limit = limit_ref[0, seq // BPS]
    peers = {
        "core": mate,
        "x": across,
        "y": (flip(seq, 4), doc),
        "low": (seq, flip(doc, 1)),
        "high": (seq, flip(doc, 2)),
    }
    others = [(lax.rem(seq + away, seq_count), doc) for away in range(1, seq_count)]
    homes = (gate_rows, up_rows, out_rows, query_rows, key_rows, value_rows, down_rows)
    engine = Sums(down, made, own, stages, sums, homes, local_sem, send_sems, recv_sems, done_sem, peers)

    def grad_copy(head, own):
        return remote(
            grad.at[:, head_lanes(core if own else 1 - core, head)],
            gx.at[core, head],
            far_send.at[0 if own else 1, head],
            far_recv.at[core, head],
            across if own else diagonal,
        )

    def arrived_grad(far, head):
        return remote(
            grad.at[:, head_lanes(core, head)], gx.at[far, head], far_send.at[0, head], far_recv.at[far, head], across
        )

    def row_copies():
        return (
            remote(lse, lse_in, row_send.at[0], row_recv.at[0], across),
            remote(delta, delta_in, row_send.at[1], row_recv.at[1], across),
        )

    def back_copy(blk, head):
        return remote(dq_cross.at[blk, head], dq_cross.at[blk, head], back_send.at[blk, head], back_recv.at[blk, head], across)

    def mate_copy(box, i, head):
        lanes = head_lanes(core, head)
        return remote(box.at[i, head], dqkv.at[i, :, lanes], mate_send.at[i, head], mate_recv.at[i, head], mate)

    def mate_arrival(i, head):
        lanes = head_lanes(1 - core, head)
        return remote(gb.at[0, head], dqkv.at[i, :, lanes], mate_send.at[i, head], mate_recv.at[i, head], mate)

    def mem_copy(box, away):
        peer = lax.rem(seq + away, seq_count)
        return remote(box.at[peer], mem_in.at[seq], mem_send.at[away - 1], mem_recv.at[away - 1], (peer, doc))

    def far_start(head):
        @pl.when(chip == 1)
        def _():
            grad_copy(head, True).start()
            grad_copy(head, False).start()

    def front(normed, normed_t, grad_y, total, back, hidden_t, mixed, middle, w_in, w_back):
        width = total.shape[1]
        tiles = w_gate.shape[1] // UNIT
        part = 128
        copies = [
            pltpu.make_async_copy(mixed_in, mixed, front_sem.at[0]),
            pltpu.make_async_copy(cotangent, grad_y, front_sem.at[1]),
        ]
        for copy in copies:
            copy.start()

        def strip(i):
            return pl.ds(pl.multiple_of(i * UNIT, UNIT), UNIT)

        def chunk(i):
            return pl.ds(pl.multiple_of(i * part, part), part)

        def opening(rows, weights):
            loads = [
                pltpu.make_async_copy(tokens, rows, front_sem.at[2]),
                pltpu.make_async_copy(w_out, weights, front_sem.at[3]),
            ]
            for copy in loads:
                copy.start()
            meet(others + [peers["low"], peers["high"]])
            gains_in[0:1, :] = one_row(gain_one_in)
            gains_in[1:2, :] = one_row(gain_two_in)
            for copy in copies + loads:
                copy.wait()

            def join(j, carry):
                middle[:, strip(j)] = rows[:, strip(j)].astype(jnp.float32) + matmul(mixed[...], weights[:, strip(j)], NN)
                return carry

            lax.fori_loop(0, width // UNIT, join, 0)

            def norm(i, carry):
                x = middle[chunk(i), :]
                factor = lax.rsqrt(jnp.mean(x * x, axis=-1, keepdims=True) + EPS)
                value = x * factor * gains_in[1:2, :]
                normed[chunk(i), :] = value.astype(jnp.bfloat16)
                normed_t[:, chunk(i)] = value.T.astype(jnp.bfloat16)
                total[chunk(i), :] = jnp.zeros((part, width), jnp.float32)
                back[chunk(i), :] = jnp.zeros((part, width), jnp.float32)
                return carry

            lax.fori_loop(0, block // part, norm, 0)

        def tile_loads(tile):
            slot = tile % 2
            return (
                pltpu.make_async_copy(w_gate.at[:, strip(tile)], w_in.at[slot, :, 0:UNIT], tile_sem.at[slot, 0]),
                pltpu.make_async_copy(w_up.at[:, strip(tile)], w_in.at[slot, :, UNIT : 2 * UNIT], tile_sem.at[slot, 1]),
                pltpu.make_async_copy(w_down.at[strip(tile), :], w_back.at[slot], tile_sem.at[slot, 2]),
            )

        for copy in tile_loads(0):
            copy.start()
        pl.run_scoped(
            opening,
            pltpu.VMEM(tokens.shape, jnp.bfloat16), pltpu.VMEM(w_out.shape, jnp.bfloat16),
        )

        def hidden_units():
            def one(tile, carry):
                slot = tile % 2

                @pl.when(tile + 1 < tiles)
                def _():
                    for copy in tile_loads(tile + 1):
                        copy.start()

                for copy in tile_loads(tile):
                    copy.wait()
                opened = matmul(normed[...], w_in[slot, :, 0:UNIT], NN)
                upper = matmul(normed[...], w_in[slot, :, UNIT : 2 * UNIT], NN)
                sigma = 1.0 / (1.0 + jnp.exp(-opened))
                gated = opened * sigma
                hidden = gated * upper
                total[...] += matmul(hidden.astype(jnp.bfloat16), w_back[slot], NN)
                hidden_t[strip(tile), :] = hidden.T.astype(jnp.bfloat16)
                grad_hidden = matmul(grad_y[...], w_back[slot], NT)
                grad_opened = (grad_hidden * upper * sigma * (1.0 + opened * (1.0 - sigma))).astype(jnp.bfloat16)
                grad_upper = (grad_hidden * gated).astype(jnp.bfloat16)
                back[...] += matmul(jnp.concatenate((grad_opened, grad_upper), axis=1), w_in[slot], NT)
                for kind, value in enumerate((grad_opened, grad_upper)):
                    engine.put(2 * tile + kind, matmul(normed_t[...], value, NN))
                engine.run_turn(0, tile, tiles)
                return carry

            lax.fori_loop(0, tiles, one, 0)

        hidden_units()

        def closing(branch, stage_down):
            loads = [
                pltpu.make_async_copy(w_out.at[:, strip(p)], w_in.at[p // 2, :, (p % 2) * UNIT : (p % 2 + 1) * UNIT], tile_sem.at[p // 2, p % 2])
                for p in range(4)
            ]
            for copy in loads:
                copy.start()
            engine.run(11)

            def norm_back(i, carry):
                x = middle[chunk(i), :]
                factor = lax.rsqrt(jnp.mean(x * x, axis=-1, keepdims=True) + EPS)
                unit = x * factor
                grad_normed = back[chunk(i), :]
                normed[chunk(i), :] = (x + total[chunk(i), :]).astype(jnp.bfloat16)
                scaled = gains_in[1:2, :] * grad_normed
                inner = jnp.mean(scaled * unit, axis=-1, keepdims=True)
                value = grad_y[chunk(i), :].astype(jnp.float32) + factor * (scaled - unit * inner)
                middle[chunk(i), :] = value
                branch[chunk(i), :] = value.astype(jnp.bfloat16)
                return carry + jnp.sum(grad_normed * unit, axis=0, keepdims=True)

            gain_buf[0, 0, 1] = lax.fori_loop(0, block // part, norm_back, jnp.zeros((1, width), jnp.float32))
            writes = [
                pltpu.make_async_copy(normed, layer_out, front_sem.at[0]),
                pltpu.make_async_copy(middle, grad_middle, front_sem.at[2]),
            ]
            for copy in writes:
                copy.start()

            engine.run(12)

            for copy in loads:
                copy.wait()
            for j in (0, 2, 1, 3):
                at = slice(j * UNIT, (j + 1) * UNIT)
                value = 0.0
                for p in range(2):
                    value = value + matmul(branch[:, 2 * p * UNIT : 2 * (p + 1) * UNIT], w_in[p, at, :], NT)
                grad[:, at] = value.astype(jnp.bfloat16)
                if j == 2:
                    far_start(0)
            engine.run(13)
            far_start(1)
            share_heads((grad,), (gb,), core, mate, gb_local, gb_send, gb_recv)

            def turn_over(i, carry):
                normed_t[:, chunk(i)] = mixed[chunk(i), :].astype(jnp.float32).T.astype(jnp.bfloat16)
                return carry

            lax.fori_loop(0, block // part, turn_over, 0)

            for j in range(4):
                engine.put(jnp.int32(22 + j), matmul(normed_t[...], branch[:, j * UNIT : (j + 1) * UNIT], NN))
                engine.run(14 + j)
            deep = stage_down.shape[4]
            tall = 8 * deep

            def down_store(n):
                i = n % 4
                return pltpu.make_async_copy(
                    stage_down.at[n % 2], down.at[i // 2, i % 2, :, :, :, :, strip(n // 4)], stage_sem.at[n % 2]
                )

            def down_part(n):
                i, j = n % 4, n // 4
                value = matmul(hidden_t[pl.ds(pl.multiple_of(i * tall, 64), tall), :], grad_y[:, strip(j)], NN)
                pl.when(n > 1)(lambda: down_store(n - 2).wait())
                for k in range(8):
                    stage_down[n % 2, k // 4, (k // 2) % 2, k % 2] = value[k * deep : (k + 1) * deep].astype(jnp.bfloat16)
                down_store(n).start()

            def down_parts(m, carry):
                down_part(2 * m)
                down_part(2 * m + 1)
                for j in range(3):
                    pl.when(m == 2 * j + 2)(lambda: engine.offer_down(j))
                pl.when(m == 1)(lambda: far_start(2))
                pl.when(m == 4)(lambda: far_start(3))
                engine.run_turn(18, m, 8)
                return carry

            lax.fori_loop(0, 8, down_parts, 0)
            down_store(14).wait()
            down_store(15).wait()
            engine.offer_down(3)
            for copy in writes:
                copy.wait()

        pl.run_scoped(
            closing,
            pltpu.VMEM(normed.shape, jnp.bfloat16),
            pltpu.VMEM((2, 2, 2, 2, ROWS[1], UNIT), jnp.bfloat16),
        )

    pl.run_scoped(
        front,
        pltpu.VMEM(tokens.shape, jnp.bfloat16), pltpu.VMEM((tokens.shape[1], block), jnp.bfloat16),
        pltpu.VMEM(tokens.shape, jnp.bfloat16), pltpu.VMEM(tokens.shape, jnp.float32), pltpu.VMEM(tokens.shape, jnp.float32),
        pltpu.VMEM((w_gate.shape[1], block), jnp.bfloat16), pltpu.VMEM(tokens.shape, jnp.bfloat16),
        pltpu.VMEM(tokens.shape, jnp.float32), pltpu.VMEM((2, tokens.shape[1], 2 * UNIT), jnp.bfloat16),
        pltpu.VMEM((2, UNIT, tokens.shape[1]), jnp.bfloat16),
    )

    def attention(qb, kb, vb, qx, mkb, mvb, ob, dq_own, dk_sum, dv_sum, dm, dqkv_mate, mem_out, spots):
        inputs = [
            pltpu.make_async_copy(src, dst, in_sem.at[i])
            for i, (src, dst) in enumerate(
                ((qb_in, qb), (kb_in, kb), (vb_in, vb), (mkb_in, mkb), (mvb_in, mvb), (ob_in, ob), (lse_in0, lse), (qx_in, qx))
            )
        ]
        spot_copies = [pltpu.make_async_copy(spots_in, spots, spot_sem.at[0])]
        for copy in inputs + spot_copies:
            copy.start()
        for head in range(HALF):
            remote(grad.at[:, head_lanes(core, head)], gb.at[core, head], gb_send.at[0, head], gb_recv.at[0, head], mate).wait()
            pltpu.make_async_copy(grad.at[:, head_lanes(core, head)], gb.at[core, head], gb_local.at[0, head]).wait()
        for copy in inputs + spot_copies:
            copy.wait()
        engine.run(26)

        def rows(i, carry):
            head, blk = i // 2, i % 2
            product = gb[blk, head].astype(jnp.float32) * ob[blk, head].astype(jnp.float32)
            delta[blk, head] = jnp.sum(product.T, axis=0, keepdims=True)
            return carry

        lax.fori_loop(0, 2 * HALF, rows, 0)

        @pl.when(chip == 1)
        def _():
            for copy in row_copies():
                copy.start()

        def pull(key_rows, value_rows, query, grad_rows, level, inner, where):
            scores = matmul(key_rows, query, NT) * (SCALE * LOG2E)
            if where is not None:
                scores = masked(scores, where[0], limit, where[1])
            weights = jnp.exp2(scores - level)
            grad_weights = matmul(value_rows, grad_rows, NT)
            grad_scores = (weights * (grad_weights - inner)).astype(jnp.bfloat16)
            return (
                matmul(grad_scores, query, NN),
                matmul(weights.astype(jnp.bfloat16), grad_rows, NN),
                matmul(key_rows, grad_scores, TN),
            )

        def own_head(head, carry):
            lanes = pl.ds(pl.multiple_of(head * HEAD_DIM, HEAD_DIM), HEAD_DIM)
            for blk in range(2):
                query, grad_rows = qb[blk, head], gb[blk, head]
                level, inner = lse[blk, head], delta[blk, head]
                total = 0.0
                for kblk in range(blk + 1):
                    gk, gv, gq = pull(
                        kb[kblk, head], vb[kblk, head], query, grad_rows, level, inner,
                        ((2 * chip + kblk) * block, kblk == blk),
                    )
                    if kblk == blk:
                        dk_sum[kblk, head], dv_sum[kblk, head] = gk, gv
                    else:
                        dk_sum[kblk, head] += gk
                        dv_sum[kblk, head] += gv
                    total = total + gq
                gk, gv, gq = pull(mkb[blk, head], mvb[blk, head], query, grad_rows, level, inner, None)
                dm[blk, 0, :, lanes] = (gk * SCALE).astype(jnp.bfloat16)
                dm[blk, 1, :, lanes] = gv.astype(jnp.bfloat16)
                dq_own[blk, head] = total + gq
            engine.run_turn(27, head, HALF)
            return carry

        lax.fori_loop(0, HALF, own_head, 0)

        for blk in range(2):
            for kind in range(2):
                rows_out = matmul(spots[blk], dm[blk, kind], NN).astype(jnp.bfloat16)
                mem_out[:, blk, kind] = rows_out.reshape(mem_out.shape[0], mem_out.shape[3], mem_out.shape[4])
        for away in range(1, seq_count):
            mem_copy(mem_out, away).start()
        own_rows = pltpu.make_async_copy(mem_out.at[seq], mem_in.at[seq], mem_local.at[0])
        own_rows.start()
        engine.run(31)

        @pl.when(chip == 0)
        def _():
            for copy in row_copies():
                copy.wait_recv()

        def results(blk, head, which):
            values = {}
            if 0 in which:
                values[0] = (dq_own[blk, head].T * SCALE).astype(jnp.bfloat16)
            if 1 in which:
                values[1] = (dk_sum[blk, head] * SCALE).astype(jnp.bfloat16)
                values[2] = dv_sum[blk, head].astype(jnp.bfloat16)
            return values

        def hand_out(which):
            def for_mate(head, carry):
                for i, value in results(1 - core, head, which).items():
                    dqkv_mate[i, head] = value
                    mate_copy(dqkv_mate, i, head).start()
                return carry

            def for_own(head, carry):
                for i, value in results(core, head, which).items():
                    dqkv[i, :, head_lanes(core, head)] = value
                return carry

            lax.fori_loop(0, HALF, for_mate, 0)
            lax.fori_loop(0, HALF, for_own, 0)

        pl.when(chip == 0)(lambda: hand_out((0,)))
        pl.when(chip == 1)(lambda: hand_out((1,)))

        def far_turn(i, carry):
            head, blk = i // 2, i % 2

            @pl.when(chip == 0)
            def _():
                arrived_grad(blk, head).wait_recv()
                query, grad_rows = qx[blk, head], gx[blk, head]
                level, inner = lse_in[blk, head], delta_in[blk, head]
                total = 0.0
                for kblk in range(2):
                    gk, gv, gq = pull(
                        kb[kblk, head], vb[kblk, head], query, grad_rows, level, inner, (kblk * block, False)
                    )
                    dk_sum[kblk, head] += gk
                    dv_sum[kblk, head] += gv
                    total = total + gq
                dq_cross[blk, head] = total.astype(jnp.bfloat16)
                back_copy(blk, head).start()

            engine.run_turn(32, i, 2 * HALF)

            @pl.when(chip == 1)
            def _():
                back_copy(blk, head).wait_recv()
                dq_own[blk, head] += dq_cross[blk, head].astype(jnp.float32)

            return carry

        lax.fori_loop(0, 2 * HALF, far_turn, 0)

        pl.when(chip == 0)(lambda: hand_out((1,)))
        pl.when(chip == 1)(lambda: hand_out((0,)))
        engine.run(40)
        engine.run(41)
        for away in range(1, seq_count):
            mem_copy(mem_out, away).wait_send()
        own_rows.wait()
        for i in range(3):
            for head in range(HALF):
                mate_copy(dqkv_mate, i, head).wait_send()

    box = (2, HALF, block, HEAD_DIM)
    mem_box = mkb_in.shape
    low, full = jnp.bfloat16, jnp.float32
    pl.run_scoped(
        attention,
        pltpu.VMEM(box, low), pltpu.VMEM(box, low), pltpu.VMEM(box, low), pltpu.VMEM(box, low),
        pltpu.VMEM(mem_box, low), pltpu.VMEM(mem_box, low), pltpu.VMEM(box, low),
        pltpu.VMEM((2, HALF, HEAD_DIM, block), full), pltpu.VMEM(box, full), pltpu.VMEM(box, full),
        pltpu.VMEM((2, 2, mem_box[2], HALF * HEAD_DIM), low),
        pltpu.VMEM((3, HALF, block, HEAD_DIM), low), pltpu.VMEM(mem_in.shape, low), pltpu.VMEM(spots_in.shape, low),
    )

    def tail(normed, dx, middle, rows, weights):
        width = dx.shape[1]
        chunk = weights.shape[2]
        loads = [
            pltpu.make_async_copy(tokens, rows, load_sem.at[1]),
            pltpu.make_async_copy(grad_middle, middle, load_sem.at[2]),
        ]

        def weight_copies(j):
            at = pl.ds(pl.multiple_of(j * chunk, chunk), chunk)
            return [
                pltpu.make_async_copy(w.at[at, :], weights.at[j % 2, i], weight_sem.at[j % 2, i])
                for i, w in enumerate((w_query, w_key, w_value))
            ]

        for copy in loads + weight_copies(0):
            copy.start()
        loads[0].wait()
        part = 64

        def norm(i, carry):
            at = pl.ds(pl.multiple_of(i * 2 * part, 2 * part), 2 * part)
            x = rows[at, :].astype(jnp.float32)
            factor = lax.rsqrt(jnp.mean(x * x, axis=-1, keepdims=True) + EPS)
            normed[:, at] = (x * factor * gains_in[0:1, :]).T.astype(jnp.bfloat16)
            return carry

        lax.fori_loop(0, block // (2 * part), norm, 0)
        for i in range(3):
            for head in range(HALF):
                mate_arrival(i, head).wait_recv()
        engine.run(42)

        def make(w):
            lanes = pl.ds(pl.multiple_of(lax.rem(w, 4) * UNIT, UNIT), UNIT)
            engine.put(26 + w, matmul(normed[...], dqkv[w // 4, :, lanes], NN))

        def build(j, carry):
            make(2 * j)
            make(2 * j + 1)
            engine.run_turn(43, j, 6)
            return carry

        lax.fori_loop(0, 6, build, 0)

        def input_part(j, carry):
            for copy in weight_copies(j):
                copy.wait()

            @pl.when(j < 3)
            def _():
                for copy in weight_copies(j + 1):
                    copy.start()

            total = 0.0
            for i in range(3):
                total = total + matmul(dqkv[i], weights[j % 2, i], NT)
            dx[:, pl.ds(pl.multiple_of(j * chunk, chunk), chunk)] = total
            engine.run_turn(49, j, 4)
            return carry

        lax.fori_loop(0, 4, input_part, 0)
        loads[1].wait()

        def norm_back(i, carry):
            at = pl.ds(pl.multiple_of(i * part, part), part)
            x = rows[at, :].astype(jnp.float32)
            factor = lax.rsqrt(jnp.mean(x * x, axis=-1, keepdims=True) + EPS)
            unit = x * factor
            grad_normed = dx[at, :]
            scaled = gains_in[0:1, :] * grad_normed
            inner = jnp.mean(scaled * unit, axis=-1, keepdims=True)
            rows[at, :] = (middle[at, :] + factor * (scaled - unit * inner)).astype(jnp.bfloat16)
            return carry + jnp.sum(grad_normed * unit, axis=0, keepdims=True)

        gain_buf[0, 0, 0] = lax.fori_loop(0, block // part, norm_back, jnp.zeros((1, width), jnp.float32))
        out_copy = pltpu.make_async_copy(rows, grad_tokens, load_sem.at[1])
        out_copy.start()

        def gain_copy(level):
            name = ("core", "x", "y", "low", "high")[level]
            return remote(
                gain_buf.at[0, level], gain_buf.at[1, level], gain_send.at[level], gain_recv.at[level], peers[name]
            )

        gain_copy(0).start()
        engine.run(53)
        for away in range(1, seq_count):
            source = lax.rem(seq + seq_count - away, seq_count)
            remote(mem_in.at[source], mem_in.at[source], mem_send.at[away - 1], mem_recv.at[away - 1], (source, doc)).wait_recv()
        mem_copy_out = pltpu.make_async_copy(mem_in, mem_home, load_sem.at[2])
        mem_copy_out.start()
        engine.run(54)
        engine.run(55)
        events = PLAN[56]
        early = [n for n, (unit, level) in enumerate(events) if level == 3 and (unit < 26 or unit >= NARROW)]
        emptied = max(early + [-1]) + 1
        stops = [len(events) * k // 6 for k in range(1, 6)]
        for n, (unit, level) in enumerate(events):
            for step in range(5):
                if n == stops[step]:
                    gain_copy(step).wait_recv()
                    total = gain_buf[0, step] + gain_buf[1, step]
                    if step < 4:
                        gain_buf[0, step + 1] = total
                        gain_copy(step + 1).start()
                    else:
                        gains_out[...] = total
            if n == emptied:
                engine.drain(0, 0, 26)
                engine.drain(1, 0, 4)
            engine.arrive(unit, level)
        engine.drain(0, 26, NARROW)
        for level in range(5):
            gain_copy(level).wait_send()
        for copy in [out_copy, mem_copy_out]:
            copy.wait()
        for unit in range(NARROW + 4):
            engine.result(unit).wait()

    width = w_query.shape[0]
    pl.run_scoped(
        tail,
        pltpu.VMEM((width, block), low),
        pltpu.VMEM((block, width), full), pltpu.VMEM((block, width), full), pltpu.VMEM((block, width), low),
        pltpu.VMEM((2, 3, UNIT, width), low),
    )

    @pl.when(chip == 0)
    def _():
        for head in range(HALF):
            for blk in range(2):
                back_copy(blk, head).wait_send()

    @pl.when(chip == 1)
    def _():
        for copy in row_copies():
            copy.wait_send()
        for head in range(HALF):
            grad_copy(head, True).wait_send()
            grad_copy(head, False).wait_send()


def go_back(limit, attended, saved, tokens, cotangent, weights, gain_one, gain_two):
    block, width = tokens.shape
    low, full = jnp.bfloat16, jnp.float32
    box = (2, HALF, block, HEAD_DIM)
    row = (2, HALF, 1, block)
    seq_count = lax.axis_size("seq")
    capacity = 2 * TOPK // seq_count
    dma = pltpu.SemaphoreType.DMA
    hbm, vmem = pl.BlockSpec(memory_space=pl.ANY), pl.BlockSpec(memory_space=pltpu.VMEM)
    struct = jax.ShapeDtypeStruct
    ff = weights[4].shape[1]
    *saved, picked_t = saved
    spots = saved[8]

    def wide(rows, columns):
        return struct((2, 2, 2, 2, 2, rows, columns), low)

    mem = (seq_count, 2, 2, capacity, HALF * HEAD_DIM)
    units = (NARROW, 4)
    scratch = [
        pltpu.VMEM(box, low), pltpu.VMEM(box, low),
        pltpu.VMEM(row, full), pltpu.VMEM(row, full), pltpu.VMEM(row, full), pltpu.VMEM(row, full),
        pltpu.VMEM((2, HALF, HEAD_DIM, block), low),
        pltpu.VMEM((3, block, width), low), pltpu.VMEM(mem, low),
        pltpu.VMEM((2, 5, 2, 1, width), full),
        pltpu.VMEM((RING, 2, 2, 2, 2, 2, ROWS[0], UNIT), low),
        pltpu.VMEM((2, 2, 2, 2, 2, ROWS[1], UNIT), low),
        pltpu.VMEM((block, width), low),
        pltpu.VMEM((2, width), full),
    ]
    for c in range(2):
        scratch += [pltpu.VMEM((units[c],) + (2,) * k + (ROWS[c], UNIT), low) for k in (4, 3, 2, 1, 0)]
    scratch += [pltpu.VMEM((units[c], ROWS[c], UNIT), full) for c in range(2)]
    scratch += [dma((2,))]
    scratch += [dma((5, units[c])) for c in range(2)] * 2
    scratch += [
        dma((8,)), dma((1, HALF)), dma((1, HALF)), dma((1, HALF)), dma((1,)),
        dma((2, HALF)), dma((2, HALF)), dma((2,)), dma((2,)), dma((2, HALF)), dma((2, HALF)),
        dma((3, HALF)), dma((3, HALF)), dma((1,)), dma((seq_count - 1,)), dma((seq_count - 1,)),
        dma((5,)), dma((5,)), dma((4,)), dma((2, 3)), dma((sum(units),)),
        dma((5,)), dma((2, 3)), dma((2,)),
    ]
    rows = struct((32, width), full)
    mem_rows = picked_t.shape[0]
    results = pl.pallas_call(
        back_kernel,
        out_shape=(
            struct((block, width), low), struct((block, width), low),
            struct((32, ff), full), struct((32, ff), full),
            rows, rows, rows, rows,
            struct((88, width), full), struct((2, 1, width), full),
            struct(mem, low),
            wide(88, width),
            struct((block, width), full),
        ),
        in_specs=[pl.BlockSpec(memory_space=pltpu.SMEM)] + [hbm] * 19 + [vmem] * 2,
        out_specs=(hbm,) * 9 + (vmem,) + (hbm,) * 3,
        scratch_shapes=scratch,
        name="go_back",
        compiler_params=pltpu.CompilerParams(collective_id=3, has_side_effects=True, vmem_limit_bytes=60 * 2**20),
    )(limit, attended, *saved, tokens, cotangent, *weights, gain_one, gain_two)
    return deliver(results[:9], results[10], picked_t) + (results[9],)


def deliver_kernel(*refs):
    sources, mem_home, picked_t = refs[:9], refs[9], refs[10]
    targets, tables = refs[11:20], refs[20:22]
    boxes, rest = refs[22:31], refs[31:]
    rows, pick, table, in_sem, out_sem, load_sem, table_sem = rest
    loads = [
        pltpu.make_async_copy(mem_home, rows, load_sem.at[0]),
        pltpu.make_async_copy(picked_t, pick, load_sem.at[1]),
    ]
    ins = [pltpu.make_async_copy(a, b, in_sem.at[i]) for i, (a, b) in enumerate(zip(sources, boxes))]
    outs = [pltpu.make_async_copy(a, b, out_sem.at[i]) for i, (a, b) in enumerate(zip(boxes, targets))]
    for copy in loads + ins:
        copy.start()
    for copy in loads:
        copy.wait()
    half = rows.shape[4]
    stores = []
    for kind in range(2):
        for side in range(2):
            values = jnp.concatenate(
                [rows[2 * src + side, blk, kind] for src in range(rows.shape[0] // 2) for blk in range(2)], axis=0
            )
            table[2 * kind + side] = matmul(pick[...], values, NN)
            stores.append(
                pltpu.make_async_copy(
                    table.at[2 * kind + side],
                    tables[kind].at[:, side * half : (side + 1) * half],
                    table_sem.at[2 * kind + side],
                )
            )
            stores[-1].start()
    for arrived, left in zip(ins, outs):
        arrived.wait()
        left.start()
    for copy in stores + outs:
        copy.wait()


def deliver(arrays, mem_home, picked_t):
    struct = jax.ShapeDtypeStruct
    hbm = pl.BlockSpec(memory_space=pl.ANY)
    mem_rows, half = picked_t.shape[0], mem_home.shape[4]
    table = struct((mem_rows, 2 * half), jnp.float32)
    return tuple(
        pl.pallas_call(
            deliver_kernel,
            out_shape=tuple(struct(a.shape, a.dtype) for a in arrays) + (table, table),
            in_specs=[hbm] * 11,
            out_specs=(hbm,) * 11,
            scratch_shapes=[pltpu.VMEM(a.shape, a.dtype) for a in arrays] + [
                pltpu.VMEM(mem_home.shape, jnp.bfloat16), pltpu.VMEM(picked_t.shape, jnp.bfloat16),
                pltpu.VMEM((4, mem_rows, half), jnp.float32),
                pltpu.SemaphoreType.DMA((9,)), pltpu.SemaphoreType.DMA((9,)), pltpu.SemaphoreType.DMA((2,)), pltpu.SemaphoreType.DMA((4,)),
            ],
            name="deliver",
            compiler_params=pltpu.CompilerParams(vmem_limit_bytes=60 * 2**20),
        )(*arrays, mem_home, picked_t)
    )


def rms_factor(values):
    return lax.rsqrt(jnp.mean(values * values, axis=-1, keepdims=True) + EPS)


def dot32(left, right):
    return jnp.dot(left, right, preferred_element_type=jnp.float32)


def fitting():
    return (lax.axis_size("seq"), lax.axis_size("doc")) == (8, 4)


def exchange(rows, owner_count, capacity):
    parts, _, width = rows.shape
    shaped = rows.reshape(parts, owner_count, capacity, width)
    moved = lax.all_to_all(shaped, "seq", split_axis=1, concat_axis=1, tiled=True)
    return moved.reshape(parts, owner_count * capacity, width)


def on_device(
    tokens,
    cotangent,
    attn_gain,
    w_query,
    w_key,
    w_value,
    w_out,
    ffn_gain,
    w_gate,
    w_up,
    w_down,
    mem_keys,
    mem_values,
    seg_len,
    mem_idx,
):
    low = jnp.bfloat16
    stream_count, block_len, model_width = tokens.shape
    mem_rows = mem_keys.shape[1]
    seq_count = lax.axis_size("seq")
    segment = lax.axis_index("seq") // BPS
    capacity = 2 * TOPK // seq_count
    slot_count = seq_count * capacity
    limit = lax.dynamic_index_in_dim(seg_len, segment, 1, keepdims=False)

    gain_one = attn_gain.astype(jnp.float32)
    gain_two = ffn_gain.astype(jnp.float32)
    if fitting():
        gain_rows = [gain.reshape(8, -1) for gain in (attn_gain, ffn_gain)]
        attended, *saved = go_forward(
            seg_len, tokens[0], gain_rows[0], (w_query, w_key, w_value), mem_keys[0], mem_values[0], mem_idx[0]
        )
        layer_out, grad_tokens, gate_rows, up_rows, query_rows, key_rows, value_rows, out_rows, down_rows, grad_mk, grad_mv, summed = go_back(
            seg_len,
            attended,
            saved,
            tokens[0],
            cotangent[0],
            (w_query, w_key, w_value, w_out, w_gate, w_up, w_down),
            *gain_rows,
        )
        index = lax.axis_index("seq") * lax.axis_size("doc") + lax.axis_index("doc")
        parts = summed.reshape(2, seq_count * lax.axis_size("doc"), -1)
        attn_row, ffn_row = lax.dynamic_index_in_dim(parts, index, 1, keepdims=False)
        return (
            layer_out[None],
            grad_tokens[None],
            attn_row,
            query_rows,
            key_rows,
            value_rows,
            out_rows,
            ffn_row,
            gate_rows,
            up_rows,
            down_rows,
            grad_mk[None],
            grad_mv[None],
        )

    tokens_f = tokens[0].astype(jnp.float32)
    factor_one = rms_factor(tokens_f)
    unit_one = tokens_f * factor_one
    normed_one = (unit_one * gain_one).astype(low)
    chosen = mem_idx[0, 0]
    owner = chosen // mem_rows
    order = jnp.arange(TOPK)
    same_before = (owner[:, None] == owner[None, :]) & (order[None, :] < order[:, None])
    slot = owner * capacity + jnp.sum(same_before.astype(jnp.int32), axis=1)
    placed = slot[:, None] == jnp.arange(slot_count)[None, :]
    request = jnp.sum(jnp.where(placed, (chosen % mem_rows)[:, None] + 1, 0), axis=0) - 1
    requested = lax.all_to_all(
        request.reshape(seq_count, capacity), "seq", split_axis=0, concat_axis=0, tiled=True
    ).reshape(slot_count)
    picked = (requested[:, None] == jnp.arange(mem_rows)[None, :]).astype(low)
    placed = placed.astype(low)
    sent = jnp.stack((dot32(picked, mem_keys[0]).astype(low), dot32(picked, mem_values[0]).astype(low)))
    arrived = exchange(sent, seq_count, capacity)
    mem_key_rows = dot32(placed, arrived[0]).astype(low)
    mem_value_rows = dot32(placed, arrived[1]).astype(low)
    queries = dot32(normed_one, w_query).astype(low)
    keys = dot32(normed_one, w_key).astype(low)
    values = dot32(normed_one, w_value).astype(low)
    attended, *saved = attend_forward(limit, queries, keys, values, mem_key_rows, mem_value_rows)
    middle = tokens_f + dot32(attended, w_out)
    factor_two = rms_factor(middle)
    unit_two = middle * factor_two
    normed_two = (unit_two * gain_two).astype(low)
    gate = dot32(normed_two, w_gate)
    upper = dot32(normed_two, w_up)
    sigma = jax.nn.sigmoid(gate)
    hidden = (gate * sigma * upper).astype(low)
    layer_out = (middle + dot32(hidden, w_down)).astype(low)

    grad_y_low = cotangent[0]
    grad_y = grad_y_low.astype(jnp.float32)
    grad_down = dot32(hidden.T, grad_y_low)
    grad_hidden = dot32(grad_y_low, w_down.T)
    grad_gate_act = (grad_hidden * upper * sigma * (1.0 + gate * (1.0 - sigma))).astype(low)
    grad_up_act = (grad_hidden * gate * sigma).astype(low)
    grad_gate = dot32(normed_two.T, grad_gate_act)
    grad_up = dot32(normed_two.T, grad_up_act)
    grad_normed_two = dot32(grad_gate_act, w_gate.T) + dot32(grad_up_act, w_up.T)
    grad_ffn_gain = jnp.sum(grad_normed_two * unit_two, axis=0)
    scaled_two = gain_two * grad_normed_two
    grad_middle = grad_y + factor_two * (
        scaled_two - unit_two * jnp.mean(scaled_two * unit_two, axis=-1, keepdims=True)
    )
    grad_branch = grad_middle.astype(low)
    grad_out = dot32(attended.T, grad_branch)
    grad_attended = dot32(grad_branch, w_out.T).astype(low)
    grad_q, grad_k, grad_v, grad_mk, grad_mv = attend_backward(limit, grad_attended, saved)
    back = jnp.stack((dot32(placed.T, grad_mk).astype(low), dot32(placed.T, grad_mv).astype(low)))
    returned = exchange(back, seq_count, capacity)
    grad_mem_keys = dot32(picked.T, returned[0])
    grad_mem_values = dot32(picked.T, returned[1])
    grad_query = dot32(normed_one.T, grad_q)
    grad_key = dot32(normed_one.T, grad_k)
    grad_value = dot32(normed_one.T, grad_v)
    grad_normed_one = dot32(grad_q, w_query.T) + dot32(grad_k, w_key.T) + dot32(grad_v, w_value.T)
    grad_attn_gain = jnp.sum(grad_normed_one * unit_one, axis=0)
    scaled_one = gain_one * grad_normed_one
    grad_input = grad_middle + factor_one * (
        scaled_one - unit_one * jnp.mean(scaled_one * unit_one, axis=-1, keepdims=True)
    )
    grad_tokens = grad_input.astype(low)
    gate_rows, up_rows, query_rows, key_rows, value_rows, out_rows, down_rows, attn_row, ffn_row = [
        lax.psum_scatter(grad, ("seq", "doc"), scatter_dimension=0, tiled=True)
        for grad in (
            grad_gate, grad_up, grad_query, grad_key, grad_value, grad_out, grad_down, grad_attn_gain, grad_ffn_gain
        )
    ]
    return (
        layer_out[None],
        grad_tokens[None],
        attn_row,
        query_rows,
        key_rows,
        value_rows,
        out_rows,
        ffn_row,
        gate_rows,
        up_rows,
        down_rows,
        grad_mem_keys[None],
        grad_mem_values[None],
    )


def solution(mesh):
    in_specs = (
        P("doc", "seq", None),
        P("doc", "seq", None),
        P(),
        P(),
        P(),
        P(),
        P(),
        P(),
        P(),
        P(),
        P(),
        P("doc", "seq", None),
        P("doc", "seq", None),
        P("doc", None),
        P("doc", "seq", None),
    )
    out_specs = (
        P("doc", "seq", None),
        P("doc", "seq", None),
        P(("seq", "doc")),
        P(("seq", "doc"), None),
        P(("seq", "doc"), None),
        P(("seq", "doc"), None),
        P(("seq", "doc"), None),
        P(("seq", "doc")),
        P(("seq", "doc"), None),
        P(("seq", "doc"), None),
        P(("seq", "doc"), None),
        P("doc", "seq", None),
        P("doc", "seq", None),
    )
    return jax.shard_map(
        on_device, mesh=mesh, in_specs=in_specs, out_specs=out_specs, check_vma=False
    )
```
